32 devices in a mesh: grp: 4 (over y, x), ctx: 8 (over z, core).
Axes of the slice: x: 2, y: 2, z: 4, core: 2. Of those that a mesh axis runs over, the one named last changes fastest.
Arguments:
- tokens_in: bfloat16 [16384, 2304], P(('grp', 'ctx')), may hold values from -6 to 6
- cotangent: bfloat16 [16384, 2304], P(('grp', 'ctx')), may hold values from -6 to 6
- w_query: bfloat16 [2304, 2304], P(('grp', 'ctx')), as said below
- w_key: bfloat16 [2304, 2304], P(('grp', 'ctx')), may hold values from -0.125 to 0.125
- w_value: bfloat16 [2304, 2304], P(('grp', 'ctx')), may hold values from -0.125 to 0.125
- w_output: bfloat16 [2304, 2304], P(('grp', 'ctx')), may hold values from -6 to 6
- w_gate: bfloat16 [2304, 5760], P('grp', 'ctx'), may hold values from -0.125 to 0.125
- w_up: bfloat16 [2304, 5760], P('grp', 'ctx'), may hold values from -0.125 to 0.125
- w_down: bfloat16 [5760, 2304], P('ctx', 'grp'), may hold values from -0.3125 to 0.3125
- attn_gain: bfloat16 [2304], P(('grp', 'ctx')), may hold values from 0.5 to 1.5
- ffn_gain: bfloat16 [2304], P(('grp', 'ctx')), may hold values from 0.5 to 1.5
- cont_len: int32 [4, 8], P('grp'), may hold values from 64 to 256
- deal_order: int32 [4, 64], P('grp'), may hold values from 0 to 63, as said below
- clip_threshold: int32 [1], replicated, may hold values from 2 to 4
Outputs:
- output: bfloat16 [16384, 2304], P(('grp', 'ctx'))
- grad_input: float32 [16384, 2304], P(('grp', 'ctx'))
- grad_w_query: float32 [2304, 2304], P(('grp', 'ctx'))
- grad_w_key: float32 [2304, 2304], P(('grp', 'ctx'))
- grad_w_value: float32 [2304, 2304], P(('grp', 'ctx'))
- grad_w_output: float32 [2304, 2304], P(('grp', 'ctx'))
- grad_w_gate: float32 [2304, 5760], P('grp', 'ctx')
- grad_w_up: float32 [2304, 5760], P('grp', 'ctx')
- grad_w_down: float32 [5760, 2304], P('ctx', 'grp')
- grad_attn_gain: float32 [2304], P(('grp', 'ctx'))
- grad_ffn_gain: float32 [2304], P(('grp', 'ctx'))
- logit_max: float32 [36], replicated
- clip_factor: float32 [36], replicated
- clipped_query: float32 [2304, 2304], P(('grp', 'ctx'))
- clipped_key: float32 [2304, 2304], P(('grp', 'ctx'))
The draws below stay inside these ranges and needn't reach their ends.
Inputs may be any that keep to these rules, and one draw needn't show every extreme that they name: Each row of deal_order lists every tile of the group once. The stored slots of one device along ctx are 8 in a row; the first half of them hold prompt tiles and the second half continuation tiles. `w_query`: normal entries of deviation 2304^-0.5, unclipped, with all 64 columns of a head multiplied by one factor between 1 and 2.5.
All inputs are finite; a program needn't handle non-finite values.
Results may differ from the reference program's by a relative error of at most 0.02.
Values may be sent and summed in bfloat16 or wider, within the bound.
No kernel may reach another device: no remote copies, remote signals or barrier semaphores. Data moves between devices by JAX's collectives and lax.ppermute only.
A program may use at most 448 MiB of HBM per device.

```python
import math
import jax
import jax.numpy as jnp
from jax import lax

D = 2304
HEADS = 36
HDIM = 64
FF = 5760
PLEN = 2048
CLEN = 256
NCONT = 8
BLK = 64
FAMTOK = 4096
FAMS = 1
GTOK = 4096
NTILE = 64
TILES_DEV = 8
GROUPS = 4
TOKENS = 16384


def draw_w_query(key, part):
    base = jax.random.normal(jax.random.fold_in(key, 11), (D, D), jnp.float32) * D ** (-0.5)
    head_scale = jnp.exp(jax.random.uniform(jax.random.fold_in(key, 12), (HEADS,), jnp.float32, 0.0, math.log(2.5)))
    return (base * jnp.repeat(head_scale, HDIM)[None, :]).astype(jnp.bfloat16)


def draw_deal_order(key, part):
    half_tiles = NTILE // 2
    ctx_count = NTILE // TILES_DEV
    per_family = PLEN // BLK
    index = jnp.arange(half_tiles, dtype=jnp.int32)
    prompt_ids = index // per_family * (FAMTOK // BLK) + index % per_family
    cont_ids = prompt_ids + per_family
    group_rows = []
    for group_index in range(GROUPS):
        group_key = jax.random.fold_in(key, 100 + group_index)
        prompt_perm = prompt_ids[jax.random.permutation(jax.random.fold_in(group_key, 1), half_tiles)]
        cont_perm = cont_ids[jax.random.permutation(jax.random.fold_in(group_key, 2), half_tiles)]
        joined = jnp.concatenate([prompt_perm.reshape(ctx_count, TILES_DEV // 2), cont_perm.reshape(ctx_count, TILES_DEV // 2)], axis=1)
        group_rows.append(joined.reshape(NTILE))
    return jnp.stack(group_rows).astype(jnp.int32)


def set_ends(array, rng, least, largest):
    extent = array.shape
    place = [jax.random.randint(jax.random.fold_in(rng, axis), (), 0, extent[axis]) for axis in range(len(extent))]
    array = array.at[tuple(place)].set(least)
    longest = extent.index(max(extent))
    place[longest] = (place[longest] + 1) % extent[longest]
    return array.at[tuple(place)].set(largest)


def level_of(key, shape, pieces, least, high):
    level, own = 1.0, jax.random.fold_in(key, 6)
    for axis_at, blocks in pieces:
        steps = jnp.exp(jax.random.uniform(jax.random.fold_in(own, axis_at), (blocks,), jnp.float32, least / len(pieces), high / len(pieces)))
        level = level * jnp.repeat(steps, shape[axis_at] // blocks).reshape([-1 if axis == axis_at else 1 for axis in range(len(shape))])
    return level


def centred(key, dims, scale, reach, pieces=(), kind=jnp.bfloat16):
    values = jax.random.normal(key, dims, jnp.float32) * scale
    if len(pieces) > 0:
        values = level_of(key, dims, pieces, -0.22, 0.18) * values
    return jnp.clip(values, min=-reach, max=reach).astype(kind)


def setup_inputs(seed: int = 0) -> dict:
    key_of = jax.random.split(jax.random.key(seed), 15)
    return {
        "tokens_in": centred(key_of[0], (TOKENS, D), 1.0, 6.0, ((0, 32),)),
        "cotangent": centred(key_of[1], (TOKENS, D), 1.0, 6.0, ((0, 32),)),
        "w_query": draw_w_query(jax.random.fold_in(key_of[14], 71), 0),
        "w_key": centred(key_of[3], (D, D), D ** -0.5, 0.125, ((0, 32),)),
        "w_value": centred(key_of[4], (D, D), D ** -0.5, 0.125, ((0, 32),)),
        "w_output": centred(key_of[5], (D, D), 1 ** -0.5, 6.0, ((0, 32),)),
        "w_gate": centred(key_of[6], (D, FF), D ** -0.5, 0.125, ((0, 4), (1, 8))),
        "w_up": centred(key_of[7], (D, FF), D ** -0.5, 0.125, ((0, 4), (1, 8))),
        "w_down": centred(key_of[8], (FF, D), (FF // 16) ** -0.5, 0.3125, ((0, 8), (1, 4))),
        "attn_gain": jnp.clip(1.0 + 0.1 * jax.random.normal(key_of[9], (D,), jnp.float32), 0.5, 1.5).astype(jnp.bfloat16),
        "ffn_gain": jnp.clip(1.0 + 0.1 * jax.random.normal(key_of[10], (D,), jnp.float32), 0.5, 1.5).astype(jnp.bfloat16),
        "cont_len": set_ends(jax.random.randint(key_of[11], (GROUPS, FAMS * NCONT), CLEN // 4, CLEN + 1), jax.random.fold_in(key_of[11], 1), CLEN // 4, CLEN).astype(jnp.int32),
        "deal_order": draw_deal_order(jax.random.fold_in(key_of[14], 71), 0),
        "clip_threshold": jax.random.randint(key_of[13], (1,), 2, 5).astype(jnp.int32),
    }


branch_scale = 1.4 / math.sqrt(40.0)
norm_eps = 1e-05
rope_base = 10000.0
masked_value = -1e+30
highest = lax.Precision.HIGHEST

@jax.custom_vjp
def low(v):
    return lax.optimization_barrier(v.astype(jnp.bfloat16)).astype(jnp.float32)

@jax.custom_vjp
def low_back(v):
    return v

def low_keep(v):
    return (low(v), None)

def low_pass(kept, grad):
    return (grad,)

def back_keep(v):
    return (v, None)

def back_low(kept, grad):
    return (low(grad),)
low.defvjp(low_keep, low_pass)
low_back.defvjp(back_keep, back_low)

def matmul(left, right):
    return jnp.dot(left, right, preferred_element_type=jnp.float32, precision=highest)

def rms_norm(values, gain):
    return values * lax.rsqrt(lax.optimization_barrier(jnp.mean(values * values, axis=-1, keepdims=True)) + norm_eps) * gain

def rope_angles(position):
    half_dim = HDIM // 2
    frequency = rope_base ** (-(jnp.arange(half_dim, dtype=jnp.float32) * (2.0 / HDIM)))
    angles = position.astype(jnp.float32)[:, None] * frequency[None, :]
    return (jnp.cos(angles)[:, None, :], jnp.sin(angles)[:, None, :])

def rotate(values, cosine, sine_vals):
    row_count = values.shape[0]
    shaped = values.reshape(row_count, HEADS, HDIM)
    leading = shaped[..., :HDIM // 2]
    trailing = shaped[..., HDIM // 2:]
    turned = jnp.concatenate([leading * cosine - trailing * sine_vals, trailing * cosine + leading * sine_vals], axis=-1)
    return turned.reshape(row_count, HEADS * HDIM)

def family_facts(lengths):
    offset = jnp.arange(FAMTOK, dtype=jnp.int32)
    prompt = offset < PLEN
    member = jnp.clip((offset - PLEN) // CLEN, 0, NCONT - 1)
    inside = offset - PLEN - member * CLEN
    seq_id = jnp.where(prompt, -1, member)
    numbers = jnp.arange(NCONT, dtype=jnp.int32)
    live_len = lax.optimization_barrier(jnp.sum(jnp.where(member[:, None] == numbers[None, :], lengths[None, :], 0), axis=1))
    is_live = prompt | (inside < live_len)
    position = jnp.where(prompt, offset, PLEN + inside)
    return (offset, prompt, seq_id, is_live, position)

def family_attention(query_rot, key_rot, value_low, offset, prompt, seq_id, is_live):
    query_heads = query_rot.reshape(FAMTOK, HEADS, HDIM)
    key_heads = key_rot.reshape(FAMTOK, HEADS, HDIM)
    value_heads = value_low.reshape(FAMTOK, HEADS, HDIM)
    block_rows = math.gcd(FAMTOK, 512)

    def one_block(first_row):
        query_block = lax.dynamic_slice_in_dim(query_heads, first_row, block_rows, 0)
        query_offset = lax.dynamic_slice_in_dim(offset, first_row, block_rows, 0)
        query_seq = lax.dynamic_slice_in_dim(seq_id, first_row, block_rows, 0)
        visible_mask = (offset[None, :] <= query_offset[:, None]) & (prompt[None, :] | (seq_id[None, :] == query_seq[:, None]) & is_live[None, :])
        scores = low_back(jnp.einsum('qhd,khd->hqk', query_block, key_heads, precision=highest) * HDIM ** (-0.5))
        masked = jnp.where(visible_mask[None], scores, masked_value)
        prob_low = low(jax.nn.softmax(masked, axis=-1))
        attended = jnp.einsum('hqk,khd->qhd', prob_low, value_heads, precision=highest)
        return (attended.reshape(block_rows, HEADS * HDIM), lax.optimization_barrier(jnp.max(masked, axis=(1, 2))))
    starts = jnp.arange(FAMTOK // block_rows, dtype=jnp.int32) * block_rows
    attended, block_max = lax.map(jax.checkpoint(one_block), starts)
    return (attended.reshape(FAMTOK, HEADS * HDIM), lax.optimization_barrier(jnp.max(block_max, axis=0)))

def reference(tokens_in, cotangent, w_query, w_key, w_value, w_output, w_gate, w_up, w_down, attn_gain, ffn_gain, cont_len, deal_order, clip_threshold):
    within = jnp.arange(BLK, dtype=jnp.int32)
    logical_of_stored = (deal_order[:, :, None] * BLK + within[None, None, :]).reshape(GROUPS, GTOK).astype(jnp.int32)
    stored_of_logical = jnp.argsort(logical_of_stored, axis=1).astype(jnp.int32)
    fam_lengths = cont_len.reshape(GROUPS * FAMS, NCONT)

    def forward(tokens, wq, wk, wv, wo, wg, wu, wd, gain_one, gain_two):
        grouped = tokens.reshape(GROUPS, GTOK, D)
        logical = jnp.take_along_axis(grouped, stored_of_logical[:, :, None], axis=1)
        flat_rows = logical.reshape(TOKENS, D)
        normed_one = low(rms_norm(flat_rows, gain_one))
        query_pre = low_back(matmul(normed_one, wq))
        key_pre = low_back(matmul(normed_one, wk))
        value_low = low(low_back(matmul(normed_one, wv)))

        def per_family(family_items):
            query_fam, key_fam, value_fam, lengths = family_items
            offset, prompt, seq_id, is_live, position = family_facts(lengths)
            cosine, sine_vals = rope_angles(position)
            query_rot = low(rotate(query_fam, cosine, sine_vals))
            key_rot = low(rotate(key_fam, cosine, sine_vals))
            return family_attention(query_rot, key_rot, value_fam, offset, prompt, seq_id, is_live)
        shape_fam = (GROUPS * FAMS, FAMTOK, D)
        attended, family_max = lax.map(per_family, (query_pre.reshape(shape_fam), key_pre.reshape(shape_fam), value_low.reshape(shape_fam), fam_lengths))
        attn_low = low(low_back(attended.reshape(TOKENS, D)))
        after_attn = flat_rows + branch_scale * low_back(matmul(attn_low, wo))
        normed_two = low(rms_norm(after_attn, gain_two))
        gate_pre = low_back(matmul(normed_two, wg))
        up_pre = low_back(matmul(normed_two, wu))
        mixed = low(jax.nn.silu(gate_pre) * up_pre)
        result = after_attn + branch_scale * low_back(matmul(mixed, wd))
        restored = jnp.take_along_axis(result.reshape(GROUPS, GTOK, D), logical_of_stored[:, :, None], axis=1)
        return (restored.reshape(TOKENS, D), lax.optimization_barrier(jnp.max(family_max, axis=0)))
    primals = (tokens_in.astype(jnp.float32), w_query.astype(jnp.float32), w_key.astype(jnp.float32), w_value.astype(jnp.float32), w_output.astype(jnp.float32), w_gate.astype(jnp.float32), w_up.astype(jnp.float32), w_down.astype(jnp.float32), attn_gain.astype(jnp.float32), ffn_gain.astype(jnp.float32))
    result, pullback, maxima = jax.vjp(forward, *primals, has_aux=True)
    gradients = pullback(cotangent.astype(jnp.float32))
    limit_value = clip_threshold[0].astype(jnp.float32)
    clip_factor = jnp.sqrt(limit_value / jnp.maximum(maxima, limit_value))
    column_factor = jnp.repeat(clip_factor, HDIM)
    return (result.astype(jnp.bfloat16), gradients[0], gradients[1], gradients[2], gradients[3], gradients[4], gradients[5], gradients[6], gradients[7], gradients[8], gradients[9], maxima, clip_factor, primals[1] * column_factor[None, :], primals[2] * column_factor[None, :])
```

```python
import functools
import math

import jax
import jax.numpy as jnp
from jax import lax
from jax.experimental import pallas as pl
from jax.experimental.pallas import tpu as pltpu
from jax.sharding import Mesh
from jax.sharding import PartitionSpec as P

HEADS = 36
HDIM = 64
PLEN = 2048
CLEN = 256
NCONT = 8
BLK = 64
FAMTOK = 4096

F32 = jnp.float32
BF = jnp.bfloat16
NH = HEADS // 4
PART = NH * HDIM
QB = 256
KB = 1024
KB_FWD = 512
HEAD_STEP = 9
NT = (((1,), (1,)), ((), ()))
NN = (((1,), (0,)), ((), ()))
TN = (((0,), (0,)), ((), ()))
VMEM_ROOM = 56 * 1024 * 1024


branch_scale = 1.4 / math.sqrt(40.0)
norm_eps = 1e-05
rope_base = 10000.0
masked_value = -1e30


def rope_angles(position):
    half_dim = HDIM // 2
    frequency = rope_base ** (-(jnp.arange(half_dim, dtype=jnp.float32) * (2.0 / HDIM)))
    angles = position.astype(jnp.float32)[:, None] * frequency[None, :]
    return (jnp.cos(angles)[:, None, :], jnp.sin(angles)[:, None, :])


def rotate(values, cosine, sine_vals, turn_sign):
    row_count = values.shape[0]
    shaped = values.reshape(row_count, HEADS, HDIM)
    leading = shaped[..., : HDIM // 2]
    trailing = shaped[..., HDIM // 2 :]
    turned = jnp.concatenate(
        [
            leading * cosine - turn_sign * trailing * sine_vals,
            trailing * cosine + turn_sign * leading * sine_vals,
        ],
        axis=-1,
    )
    return turned.reshape(row_count, HEADS * HDIM)


def token_facts(logical, lengths):
    family = logical // FAMTOK
    offset = logical % FAMTOK
    prompt = offset < PLEN
    member = jnp.clip((offset - PLEN) // CLEN, 0, NCONT - 1)
    inside = offset - PLEN - member * CLEN
    seq_id = jnp.where(prompt, -1, family * NCONT + member)
    numbers = jnp.arange(lengths.shape[0], dtype=jnp.int32)
    live_len = jnp.sum(jnp.where(seq_id[:, None] == numbers[None, :], lengths[None, :], 0), axis=1)
    is_live = prompt | (inside < live_len)
    position = jnp.where(prompt, offset, PLEN + inside)
    return (family, offset, prompt, seq_id, is_live, position)


def visible(query_facts, key_part):
    same_family = query_facts[0][:, None] == key_part[0][None, :]
    causal = key_part[1][None, :] <= query_facts[1][:, None]
    reaches = (
        key_part[2][None, :]
        | (key_part[3][None, :] == query_facts[3][:, None]) & key_part[4][None, :]
    )
    return same_family & causal & reaches


def key_slice(keys_heads, values_heads, key_facts, query_facts, first_row, span_rows):
    key_block = lax.dynamic_slice_in_dim(keys_heads, first_row, span_rows, 0)
    value_block = lax.dynamic_slice_in_dim(values_heads, first_row, span_rows, 0)
    key_part = tuple(
        (
            lax.dynamic_slice_in_dim(member_array, first_row, span_rows, 0)
            for member_array in key_facts
        )
    )
    return (key_block, value_block, visible(query_facts, key_part))


def block_scores(query_heads, key_block, visible_mask):
    scores = jnp.einsum(
        "qhd,khd->hqk", query_heads, key_block, preferred_element_type=jnp.float32
    ) * HDIM ** (-0.5)
    return jnp.where(visible_mask[None], scores, masked_value)


def score_grads(
    query_heads, grad_heads, log_total, row_delta, key_block, value_block, visible_mask
):
    scores = block_scores(query_heads, key_block, visible_mask)
    prob_table = jnp.where(visible_mask[None], jnp.exp(scores - log_total[:, :, None]), 0.0)
    grad_probs = jnp.einsum(
        "qhd,khd->hqk", grad_heads, value_block, preferred_element_type=jnp.float32
    )
    grad_scores = (prob_table * (grad_probs - row_delta[:, :, None])).astype(jnp.bfloat16)
    return (prob_table.astype(jnp.bfloat16), grad_scores)


def gate_grads(grad_mixed, gate_pre, up_pre):
    sigmoid = jax.nn.sigmoid(gate_pre)
    grad_gate = grad_mixed * up_pre * sigmoid * (1.0 + gate_pre * (1.0 - sigmoid))
    grad_up = grad_mixed * gate_pre * sigmoid
    return (grad_gate.astype(jnp.bfloat16), grad_up.astype(jnp.bfloat16))


def norm_backward(grad_normed, values, inverse, gain):
    scaled = grad_normed * gain[None, :]
    grad_gain = jnp.sum(grad_normed * values * inverse, axis=0)
    grad_values = inverse * scaled - values * inverse**3 * jnp.mean(
        scaled * values, axis=-1, keepdims=True
    )
    return (grad_gain, grad_values)


def attention_weights(w_query, w_key, w_value, w_output, attn_gain, ffn_gain):
    return (
        lax.all_gather(w_query, ("grp", "ctx"), axis=0, tiled=True),
        lax.all_gather(w_key, ("grp", "ctx"), axis=0, tiled=True),
        lax.all_gather(w_value, ("grp", "ctx"), axis=0, tiled=True),
        lax.all_gather(w_output, ("grp", "ctx"), axis=0, tiled=True),
        lax.all_gather(attn_gain, ("grp", "ctx"), axis=0, tiled=True),
        lax.all_gather(ffn_gain, ("grp", "ctx"), axis=0, tiled=True),
    )


def ffn_rows_gather(w_gate, w_up, w_down):
    return (
        lax.all_gather(w_gate, "grp", axis=0, tiled=True),
        lax.all_gather(w_up, "grp", axis=0, tiled=True),
        lax.all_gather(w_down, "grp", axis=1, tiled=True),
    )


def local(
    tokens_in,
    cotangent,
    w_query,
    w_key,
    w_value,
    w_output,
    w_gate,
    w_up,
    w_down,
    attn_gain,
    ffn_gain,
    cont_len,
    deal_order,
    clip_threshold,
):
    row_count = tokens_in.shape[0]
    model_width = tokens_in.shape[1]
    tile_count = deal_order.shape[1]
    group_rows = tile_count * BLK
    lengths = cont_len[0]
    my_index = lax.axis_index("ctx")
    tile_offsets = jnp.arange(BLK, dtype=jnp.int32)
    stored_logical = (deal_order[0][:, None] * BLK + tile_offsets[None, :]).reshape(group_rows)
    key_facts = token_facts(stored_logical, lengths)
    query_facts = tuple(
        (
            lax.dynamic_slice_in_dim(member_array, my_index * row_count, row_count, 0)
            for member_array in key_facts
        )
    )
    cosine, sine_vals = rope_angles(query_facts[5])
    key_step = math.gcd(group_rows, 512)
    key_blocks = group_rows // key_step
    full_query, full_key, full_value, full_output, gain_one, gain_two = attention_weights(
        w_query, w_key, w_value, w_output, attn_gain, ffn_gain
    )
    residual = tokens_in.astype(jnp.float32)
    inverse_one = lax.rsqrt(jnp.mean(residual * residual, axis=-1, keepdims=True) + norm_eps)
    gain_one_f = gain_one.astype(jnp.float32)
    gain_two_f = gain_two.astype(jnp.float32)
    normed_one = (residual * inverse_one * gain_one_f).astype(jnp.bfloat16)
    query_rot = rotate(
        jnp.dot(normed_one, full_query, preferred_element_type=jnp.float32), cosine, sine_vals, 1.0
    ).astype(jnp.bfloat16)
    key_rot = rotate(
        jnp.dot(normed_one, full_key, preferred_element_type=jnp.float32), cosine, sine_vals, 1.0
    ).astype(jnp.bfloat16)
    value_low = jnp.dot(normed_one, full_value, preferred_element_type=jnp.float32).astype(
        jnp.bfloat16
    )
    keys_all, values_all = (
        lax.all_gather(key_rot, "ctx", axis=0, tiled=True),
        lax.all_gather(value_low, "ctx", axis=0, tiled=True),
    )
    query_heads = query_rot.reshape(row_count, HEADS, HDIM)
    keys_heads = keys_all.reshape(group_rows, HEADS, HDIM)
    values_heads = values_all.reshape(group_rows, HEADS, HDIM)

    def stats_step(block_index, state_carry):
        key_block, value_block, visible_mask = key_slice(
            keys_heads, values_heads, key_facts, query_facts, block_index * key_step, key_step
        )

        def stats_busy(carry):
            run_max, run_sum, head_max = carry
            scores = block_scores(query_heads, key_block, visible_mask)
            block_max = jnp.max(scores, axis=2)
            new_max = jnp.maximum(run_max, block_max)
            exp_table = jnp.where(visible_mask[None], jnp.exp(scores - new_max[:, :, None]), 0.0)
            new_sum = run_sum * jnp.exp(run_max - new_max) + jnp.sum(exp_table, axis=2)
            return (new_max, new_sum, jnp.maximum(head_max, jnp.max(block_max, axis=1)))

        return lax.cond(jnp.any(visible_mask), stats_busy, lambda carry: carry, state_carry)

    start_state = (
        jnp.full((HEADS, row_count), masked_value, jnp.float32),
        jnp.zeros((HEADS, row_count), jnp.float32),
        jnp.full((HEADS,), masked_value, jnp.float32),
    )
    run_max, run_sum, head_max = lax.fori_loop(0, key_blocks, stats_step, start_state)
    log_total = run_max + jnp.log(run_sum)

    def output_step(block_index, running):
        key_block, value_block, visible_mask = key_slice(
            keys_heads, values_heads, key_facts, query_facts, block_index * key_step, key_step
        )

        def output_busy(total):
            scores = block_scores(query_heads, key_block, visible_mask)
            prob_low = jnp.where(
                visible_mask[None], jnp.exp(scores - log_total[:, :, None]), 0.0
            ).astype(jnp.bfloat16)
            return total + jnp.einsum(
                "hqk,khd->qhd", prob_low, value_block, preferred_element_type=jnp.float32
            )

        return lax.cond(jnp.any(visible_mask), output_busy, lambda total: total, running)

    attended = lax.fori_loop(
        0, key_blocks, output_step, jnp.zeros((row_count, HEADS, HDIM), jnp.float32)
    )
    attn_low = attended.reshape(row_count, model_width).astype(jnp.bfloat16)
    after_attn = residual + branch_scale * jnp.dot(
        attn_low, full_output, preferred_element_type=jnp.float32
    )
    inverse_two = lax.rsqrt(jnp.mean(after_attn * after_attn, axis=-1, keepdims=True) + norm_eps)
    normed_two = (after_attn * inverse_two * gain_two_f).astype(jnp.bfloat16)
    gate_cols, up_cols, down_cols = ffn_rows_gather(w_gate, w_up, w_down)
    normed_rows = lax.all_gather(normed_two, "ctx", axis=0, tiled=True)
    gate_pre = jnp.dot(normed_rows, gate_cols, preferred_element_type=jnp.float32)
    up_pre = jnp.dot(normed_rows, up_cols, preferred_element_type=jnp.float32)
    mixed = (jax.nn.silu(gate_pre) * up_pre).astype(jnp.bfloat16)
    branch_ffn = lax.psum_scatter(
        jnp.dot(mixed, down_cols, preferred_element_type=jnp.float32).astype(jnp.bfloat16),
        "ctx",
        scatter_dimension=0,
        tiled=True,
    ).astype(jnp.float32)
    output = (after_attn + branch_scale * branch_ffn).astype(jnp.bfloat16)
    grad_out = cotangent.astype(jnp.float32)
    grad_branch = (branch_scale * grad_out).astype(jnp.bfloat16)
    gate_again, up_again, down_again = ffn_rows_gather(w_gate, w_up, w_down)
    grad_rows = lax.all_gather(grad_branch, "ctx", axis=0, tiled=True)
    grad_mixed = jnp.dot(grad_rows, down_again.T, preferred_element_type=jnp.float32)
    grad_down = jnp.dot(mixed.T, grad_rows, preferred_element_type=jnp.float32)
    grad_gate_low, grad_up_low = gate_grads(grad_mixed, gate_pre, up_pre)
    grad_gate = jnp.dot(normed_rows.T, grad_gate_low, preferred_element_type=jnp.float32)
    grad_up = jnp.dot(normed_rows.T, grad_up_low, preferred_element_type=jnp.float32)
    grad_normed_two = lax.psum_scatter(
        (
            jnp.dot(grad_gate_low, gate_again.T, preferred_element_type=jnp.float32)
            + jnp.dot(grad_up_low, up_again.T, preferred_element_type=jnp.float32)
        ).astype(jnp.bfloat16),
        "ctx",
        scatter_dimension=0,
        tiled=True,
    ).astype(jnp.float32)
    ffn_stack = jnp.stack([grad_gate, grad_up, grad_down.T], axis=0)
    ffn_summed = lax.psum_scatter(
        ffn_stack.astype(jnp.bfloat16), "grp", scatter_dimension=1, tiled=True
    ).astype(jnp.float32)
    grad_gain_two, grad_second = norm_backward(grad_normed_two, after_attn, inverse_two, gain_two_f)
    grad_resid = grad_out + grad_second
    back_query, back_key, back_value, back_output, back_gain_one, back_gain_two = attention_weights(
        w_query, w_key, w_value, w_output, attn_gain, ffn_gain
    )
    grad_branch_attn = (branch_scale * grad_resid).astype(jnp.bfloat16)
    grad_w_output = jnp.dot(attn_low.T, grad_branch_attn, preferred_element_type=jnp.float32)
    grad_attn = jnp.dot(grad_branch_attn, back_output.T, preferred_element_type=jnp.float32).astype(
        jnp.bfloat16
    )
    grad_heads = grad_attn.reshape(row_count, HEADS, HDIM)
    row_delta = jnp.sum(grad_heads.astype(jnp.float32) * attended, axis=2).T

    def back_step(grad_q, block_index):
        key_block, value_block, visible_mask = key_slice(
            keys_heads, values_heads, key_facts, query_facts, block_index * key_step, key_step
        )

        def back_busy(current):
            prob_low, grad_scores = score_grads(
                query_heads, grad_heads, log_total, row_delta, key_block, value_block, visible_mask
            )
            updated = current + jnp.einsum(
                "hqk,khd->qhd", grad_scores, key_block, preferred_element_type=jnp.float32
            )
            grad_keys = jnp.einsum(
                "hqk,qhd->khd", grad_scores, query_heads, preferred_element_type=jnp.float32
            ) * HDIM ** (-0.5)
            grad_values = jnp.einsum(
                "hqk,qhd->khd", prob_low, grad_heads, preferred_element_type=jnp.float32
            )
            return (
                updated,
                (
                    grad_keys.reshape(key_step, model_width),
                    grad_values.reshape(key_step, model_width),
                ),
            )

        def quiet(current):
            empty = jnp.zeros((key_step, model_width), jnp.float32)
            return (current, (empty, empty))

        return lax.cond(jnp.any(visible_mask), back_busy, quiet, grad_q)

    grad_q_heads, key_terms = lax.scan(
        back_step,
        jnp.zeros((row_count, HEADS, HDIM), jnp.float32),
        jnp.arange(key_blocks, dtype=jnp.int32),
    )
    key_sum, value_sum = (
        lax.psum_scatter(
            key_terms[0].reshape(group_rows, model_width).astype(jnp.bfloat16),
            "ctx",
            scatter_dimension=0,
            tiled=True,
        ).astype(jnp.float32),
        lax.psum_scatter(
            key_terms[1].reshape(group_rows, model_width).astype(jnp.bfloat16),
            "ctx",
            scatter_dimension=0,
            tiled=True,
        ).astype(jnp.float32),
    )
    grad_query_rot = grad_q_heads.reshape(row_count, model_width) * HDIM ** (-0.5)
    grad_query = rotate(grad_query_rot, cosine, sine_vals, -1.0).astype(jnp.bfloat16)
    grad_key = rotate(key_sum, cosine, sine_vals, -1.0).astype(jnp.bfloat16)
    grad_value = value_sum.astype(jnp.bfloat16)
    grad_w_query = jnp.dot(normed_one.T, grad_query, preferred_element_type=jnp.float32)
    grad_w_key = jnp.dot(normed_one.T, grad_key, preferred_element_type=jnp.float32)
    grad_w_value = jnp.dot(normed_one.T, grad_value, preferred_element_type=jnp.float32)
    grad_normed_one = (
        jnp.dot(grad_query, back_query.T, preferred_element_type=jnp.float32)
        + jnp.dot(grad_key, back_key.T, preferred_element_type=jnp.float32)
        + jnp.dot(grad_value, back_value.T, preferred_element_type=jnp.float32)
    )
    grad_gain_one, grad_first = norm_backward(grad_normed_one, residual, inverse_one, gain_one_f)
    grad_input = grad_resid + grad_first
    gain_pair = jnp.stack([grad_gain_one, grad_gain_two], axis=1)
    summed = (
        lax.psum_scatter(grad_w_query, ("grp", "ctx"), scatter_dimension=0, tiled=True),
        lax.psum_scatter(grad_w_key, ("grp", "ctx"), scatter_dimension=0, tiled=True),
        lax.psum_scatter(grad_w_value, ("grp", "ctx"), scatter_dimension=0, tiled=True),
        lax.psum_scatter(grad_w_output, ("grp", "ctx"), scatter_dimension=0, tiled=True),
        lax.psum_scatter(gain_pair, ("grp", "ctx"), scatter_dimension=0, tiled=True),
    )
    maxima = lax.pmax(head_max, ("grp", "ctx"))
    limit_value = clip_threshold[0].astype(jnp.float32)
    clip_factor = jnp.sqrt(limit_value / jnp.maximum(maxima, limit_value))
    column_factor = jnp.repeat(clip_factor, HDIM)
    clipped_query = w_query.astype(jnp.float32) * column_factor[None, :]
    clipped_key = w_key.astype(jnp.float32) * column_factor[None, :]
    return (
        output,
        grad_input,
        summed[0],
        summed[1],
        summed[2],
        summed[3],
        ffn_summed[0],
        ffn_summed[1],
        ffn_summed[2].T,
        summed[4][:, 0],
        summed[4][:, 1],
        maxima,
        clip_factor,
        clipped_query,
        clipped_key,
    )


def mul(left, right, dims=NN):
    return lax.dot_general(left, right, dims, preferred_element_type=F32)


def room():
    return pltpu.CompilerParams(vmem_limit_bytes=VMEM_ROOM)


def straighten(w_ref, w_sc, thin):
    for i in range(4):
        for k in range(8):
            w_sc[(i * 8 + k) * thin : (i * 8 + k + 1) * thin, :] = w_ref[k, i, :thin, :]


def swing(values, cosine, sine_vals):
    lane = lax.broadcasted_iota(jnp.int32, values.shape, 1)
    other = jnp.where(
        lane % HDIM < HDIM // 2,
        pltpu.roll(values, 2 * HDIM - HDIM // 2, 1),
        pltpu.roll(values, HDIM // 2, 1),
    )
    return values * cosine + other * sine_vals


def project_kernel(x_ref, w_ref, cos_ref, sin_ref, q_ref, kv_ref, w_sc):
    thin = w_sc.shape[0] // 32

    @pl.when(pl.program_id(0) == 0)
    def _():
        straighten(w_ref, w_sc, thin)

    y = mul(x_ref[...], w_sc[...])
    cosine, sine_vals = cos_ref[...], sin_ref[...]
    for k in range(NH):
        piece = swing(y[:, k * 128 : (k + 1) * 128], cosine, sine_vals)
        for j in range(2):
            head = 2 * k + j
            if head < NH:
                q_ref[head] = (piece[:, j * HDIM : (j + 1) * HDIM] * 0.125).astype(BF)
        if 2 * k + 1 > NH:
            kv_ref[:, k * 128 : (k + 1) * 128] = piece.astype(BF)
        elif 2 * k + 1 == NH:
            kv_ref[:, k * 128 + HDIM : (k + 1) * 128] = piece[:, HDIM:].astype(BF)
    kv_ref[:, :PART] = y[:, 2 * PART :].astype(BF)


def project(normed, w_all, cosine, sine_vals):
    rows, width = normed.shape
    full = w_all.shape
    return pl.pallas_call(
        project_kernel,
        out_shape=[
            jax.ShapeDtypeStruct((NH, rows, HDIM), BF),
            jax.ShapeDtypeStruct((rows, 2 * PART), BF),
        ],
        grid=(rows // QB,),
        in_specs=[
            pl.BlockSpec((QB, width), lambda i: (i, 0)),
            pl.BlockSpec(full, lambda i: (0, 0, 0, 0), pipeline_mode=pl.Buffered(1)),
            pl.BlockSpec((QB, 128), lambda i: (i, 0)),
            pl.BlockSpec((QB, 128), lambda i: (i, 0)),
        ],
        out_specs=[
            pl.BlockSpec((NH, QB, HDIM), lambda i: (0, i, 0)),
            pl.BlockSpec((QB, 2 * PART), lambda i: (i, 0)),
        ],
        scratch_shapes=[pltpu.VMEM((width, full[3]), BF)],
        compiler_params=room(),
        name="project",
    )(normed, w_all, cosine, sine_vals)


def sort_kernel(order_ref, *refs):
    k_ref, v_ref = refs[8:]
    first = pl.program_id(0) * 4
    for j in range(4):
        from_mine = order_ref[first + j] < 32
        tile = jnp.where(from_mine, refs[j][0], refs[4 + j][0])
        rows = slice(j * BLK, (j + 1) * BLK)
        for h in range(NH):
            v_ref[h, rows, :] = tile[:, h * HDIM : (h + 1) * HDIM]
            k_ref[h, rows, :] = tile[:, PART + h * HDIM : PART + (h + 1) * HDIM]


def sort_keys(order, mine, theirs):
    count = order.shape[0]
    shape = (1, BLK, 2 * PART)
    near = lambda j: pl.BlockSpec(shape, lambda i, o: (jnp.minimum(o[i * 4 + j], 31), 0, 0))
    far = lambda j: pl.BlockSpec(shape, lambda i, o: (jnp.maximum(o[i * 4 + j] - 32, 0), 0, 0))
    return pl.pallas_call(
        sort_kernel,
        out_shape=[jax.ShapeDtypeStruct((NH, count * BLK, HDIM), BF)] * 2,
        grid_spec=pltpu.PrefetchScalarGridSpec(
            num_scalar_prefetch=1,
            grid=(count // 4,),
            in_specs=[near(j) for j in range(4)] + [far(j) for j in range(4)],
            out_specs=[pl.BlockSpec((NH, 4 * BLK, HDIM), lambda i, o: (0, i, 0))] * 2,
        ),
        compiler_params=room(),
        name="sort_keys",
    )(order, *([mine.reshape(32, BLK, 2 * PART)] * 4), *([theirs.reshape(32, BLK, 2 * PART)] * 4))


def lane_tile(vals):
    lane = lax.broadcasted_iota(jnp.int32, (1, QB), 1)
    out = jnp.full((1, QB), vals[3], jnp.int32)
    for j in (2, 1, 0):
        out = jnp.where(lane < (j + 1) * BLK, vals[j], out)
    return out, lane & (BLK - 1)


def block_facts(tiles_ref, len_ref, block, step):
    half_tiles = PLEN // BLK
    t = [tiles_ref[block * 4 + j] for j in range(4)]
    tile, within = lane_tile(t)
    qpos = tile * BLK + within
    tmax = jnp.maximum(jnp.maximum(t[0], t[1]), jnp.maximum(t[2], t[3]))
    tmin = jnp.minimum(jnp.minimum(t[0], t[1]), jnp.minimum(t[2], t[3]))
    per = step // BLK
    is_cont = t[0] >= half_tiles
    n_all = jnp.where(is_cont, PLEN // step, tmax // per + 1)
    n_free = jnp.where(is_cont, PLEN // step, tmin // per)
    conts = [jnp.maximum(t[j] - half_tiles, 0) // 4 for j in range(4)]
    lens = lane_tile([len_ref[conts[j]] for j in range(4)])[0]
    qin = qpos - PLEN - lane_tile(conts)[0] * CLEN
    starts = [pl.multiple_of(PLEN + conts[j] * CLEN, CLEN) for j in range(4)]
    kin = lax.broadcasted_iota(jnp.int32, (CLEN, QB), 0)
    seen = lambda: (kin <= qin) & (kin < lens)
    return qpos, is_cont, n_all, n_free, starts, seen


def forward_kernel(
    tiles_ref, len_ref, q_ref, k_ref, v_ref, o_ref, lse_ref, mx_ref, vt_sc, ot_sc
):
    block = pl.program_id(0)

    @pl.when(block == 0)
    def _():
        def flip_head(h, carry):
            vt_sc[h] = v_ref[h].T
            return carry

        lax.fori_loop(0, NH, flip_head, 0)

    qpos, is_cont, n_all, n_free, starts, seen = block_facts(tiles_ref, len_ref, block, KB_FWD)

    def heads(group, carry):
        hs = [group * HEAD_STEP + j for j in range(HEAD_STEP)]
        qs = [q_ref[h] for h in hs]

        def update(scores, states, weigh):
            out = []
            for n, (s, (m, l, acc)) in enumerate(zip(scores, states)):
                mn = jnp.maximum(m, jnp.max(s, axis=0, keepdims=True))
                p = jnp.exp(s - mn)
                al = jnp.exp(m - mn)
                out.append(
                    (
                        mn,
                        l * al + jnp.sum(p, axis=0, keepdims=True),
                        acc * al + weigh(n, p.astype(BF)),
                    )
                )
            return tuple(out)

        def step(kb, states, masked):
            base = pl.multiple_of(kb * KB_FWD, KB_FWD)
            rows = pl.ds(base, KB_FWD)
            scores = [mul(k_ref[h, rows, :], q, NT) for h, q in zip(hs, qs)]
            if masked:
                kpos = base + lax.broadcasted_iota(jnp.int32, (KB_FWD, QB), 0)
                vis = kpos <= qpos
                scores = [jnp.where(vis, s, masked_value) for s in scores]
            return update(scores, states, lambda n, p: mul(vt_sc[hs[n], :, rows], p))

        states = tuple(
            (
                jnp.full((1, QB), masked_value, F32),
                jnp.zeros((1, QB), F32),
                jnp.zeros((HDIM, QB), F32),
            )
            for _ in hs
        )
        states = lax.fori_loop(0, n_free, functools.partial(step, masked=False), states)
        states = lax.fori_loop(n_free, n_all, functools.partial(step, masked=True), states)

        def own(states):
            vis = seen()
            cols = lambda x, j: x[:, j * BLK : (j + 1) * BLK]
            scores = []
            for h, q in zip(hs, qs):
                s = [
                    mul(k_ref[h, pl.ds(starts[j], CLEN), :], q[j * BLK : (j + 1) * BLK], NT)
                    for j in range(4)
                ]
                scores.append(jnp.where(vis, jnp.concatenate(s, axis=1), masked_value))
            return update(
                scores,
                states,
                lambda n, p: jnp.concatenate(
                    [
                        mul(vt_sc[hs[n], :, pl.ds(starts[j], CLEN)], cols(p, j))
                        for j in range(4)
                    ],
                    axis=1,
                ),
            )

        states = lax.cond(is_cont, own, lambda s: s, states)
        for h, (m, l, acc) in zip(hs, states):
            ot_sc[h] = acc / l
            lse_ref[0, pl.ds(h, 1), :] = m + jnp.log(l)
            mx_ref[0, pl.ds(h, 1), :] = m
        return carry

    lax.fori_loop(0, NH // HEAD_STEP, heads, 0)
    for h in range(NH):
        o_ref[:, h * HDIM : (h + 1) * HDIM] = ot_sc[h].T.astype(BF)


def attention_forward(tiles, lengths, queries, keys, values):
    rows = queries.shape[1]
    count = rows // QB
    span = keys.shape[1]
    whole = pl.BlockSpec((NH, span, HDIM), lambda i, a, b: (0, 0, 0), pipeline_mode=pl.Buffered(1))
    stat = pl.BlockSpec((1, NH, QB), lambda i, a, b: (i, 0, 0))
    return pl.pallas_call(
        forward_kernel,
        out_shape=[
            jax.ShapeDtypeStruct((rows, PART), BF),
            jax.ShapeDtypeStruct((count, NH, QB), F32),
            jax.ShapeDtypeStruct((count, NH, QB), F32),
        ],
        grid_spec=pltpu.PrefetchScalarGridSpec(
            num_scalar_prefetch=2,
            grid=(count,),
            in_specs=[pl.BlockSpec((NH, QB, HDIM), lambda i, a, b: (0, i, 0)), whole, whole],
            out_specs=[pl.BlockSpec((QB, PART), lambda i, a, b: (i, 0)), stat, stat],
            scratch_shapes=[
                pltpu.VMEM((NH, HDIM, span), BF),
                pltpu.VMEM((NH, HDIM, QB), F32),
            ],
        ),
        compiler_params=room(),
        name="attention_forward",
    )(tiles, lengths, queries, keys, values)


def delta_kernel(g_ref, w_ref, o_ref, gh_ref, delta_ref):
    grad = mul(g_ref[...], w_ref[...], NT).astype(BF)
    ones = jnp.ones((8, HDIM), F32)
    for h in range(NH):
        cols = slice(h * HDIM, (h + 1) * HDIM)
        gh_ref[h] = grad[:, cols]
        prod = grad[:, cols].astype(F32) * o_ref[:, cols].astype(F32)
        total = lax.dot_general(
            ones, prod, NT, preferred_element_type=F32, precision=lax.Precision.HIGHEST
        )
        delta_ref[0, h : h + 1, :] = total[0:1]


def attention_delta(grad_branch, w_out, attended):
    rows, width = grad_branch.shape
    count = rows // QB
    return pl.pallas_call(
        delta_kernel,
        out_shape=[
            jax.ShapeDtypeStruct((NH, rows, HDIM), BF),
            jax.ShapeDtypeStruct((count, NH, QB), F32),
        ],
        grid=(count,),
        in_specs=[
            pl.BlockSpec((QB, width), lambda i: (i, 0)),
            pl.BlockSpec((PART, width), lambda i: (0, 0), pipeline_mode=pl.Buffered(1)),
            pl.BlockSpec((QB, PART), lambda i: (i, 0)),
        ],
        out_specs=[
            pl.BlockSpec((NH, QB, HDIM), lambda i: (0, i, 0)),
            pl.BlockSpec((1, NH, QB), lambda i: (i, 0, 0)),
        ],
        compiler_params=room(),
        name="attention_delta",
    )(grad_branch, w_out, attended)


def backward_kernel(
    tiles_ref, len_ref, q_ref, g_ref, lse_ref, delta_ref, k_ref, v_ref, dq_ref, dk_ref, dv_ref, kt_sc
):
    h = pl.program_id(0)
    block = pl.program_id(1)

    @pl.when(block == 0)
    def _():
        dk_ref[...] = jnp.zeros_like(dk_ref)
        dv_ref[...] = jnp.zeros_like(dv_ref)
        kt_sc[...] = k_ref[0].T

    qpos, is_cont, n_all, n_free, starts, seen = block_facts(tiles_ref, len_ref, block, KB)
    q = q_ref[0]
    g = g_ref[0]
    lse = lse_ref[0, pl.ds(h, 1), :]
    delta = delta_ref[0, pl.ds(h, 1), :]

    def step(kb, dqt, masked):
        base = pl.multiple_of(kb * KB, KB)
        rows = pl.ds(base, KB)
        s = mul(k_ref[0, rows, :], q, NT)
        dp = mul(v_ref[0, rows, :], g, NT)
        if masked:
            kpos = base + lax.broadcasted_iota(jnp.int32, (KB, QB), 0)
            s = jnp.where(kpos <= qpos, s, masked_value)
        p = jnp.exp(s - lse)
        ds = (p * (dp - delta)).astype(BF)
        dv_ref[0, rows, :] += mul(p.astype(BF), g)
        dk_ref[0, rows, :] += mul(ds, q)
        return dqt + mul(kt_sc[:, rows], ds)

    dqt = jnp.zeros((HDIM, QB), F32)
    dqt = lax.fori_loop(0, n_free, functools.partial(step, masked=False), dqt)
    dqt = lax.fori_loop(n_free, n_all, functools.partial(step, masked=True), dqt)
    dq_ref[0] = dqt.T * HDIM ** (-0.5)

    @pl.when(is_cont)
    def _():
        part = lambda x, j: x[j * BLK : (j + 1) * BLK]
        rows = [pl.ds(starts[j], CLEN) for j in range(4)]
        s = jnp.concatenate([mul(k_ref[0, rows[j], :], part(q, j), NT) for j in range(4)], axis=1)
        s = jnp.where(seen(), s, masked_value)
        p = jnp.exp(s - lse)
        dp = jnp.concatenate([mul(v_ref[0, rows[j], :], part(g, j), NT) for j in range(4)], axis=1)
        ds = (p * (dp - delta)).astype(BF)
        pb = p.astype(BF)
        dq = []
        for j in range(4):
            cols = slice(j * BLK, (j + 1) * BLK)
            dv_ref[0, rows[j], :] += mul(pb[:, cols], part(g, j))
            dk_ref[0, rows[j], :] += mul(ds[:, cols], part(q, j))
            dq.append(mul(kt_sc[:, rows[j]], ds[:, cols]))
        dq_ref[0] += jnp.concatenate(dq, axis=1).T * HDIM ** (-0.5)


def attention_backward(tiles, lengths, queries, grads, log_total, row_delta, keys, values):
    rows = queries.shape[1]
    count = rows // QB
    span = keys.shape[1]
    row = pl.BlockSpec((1, QB, HDIM), lambda h, i, a, b: (h, i, 0))
    stat = pl.BlockSpec((1, NH, QB), lambda h, i, a, b: (i, 0, 0))
    full = pl.BlockSpec((1, span, HDIM), lambda h, i, a, b: (h, 0, 0))
    return pl.pallas_call(
        backward_kernel,
        out_shape=[
            jax.ShapeDtypeStruct((NH, rows, HDIM), F32),
            jax.ShapeDtypeStruct((NH, span, HDIM), F32),
            jax.ShapeDtypeStruct((NH, span, HDIM), F32),
        ],
        grid_spec=pltpu.PrefetchScalarGridSpec(
            num_scalar_prefetch=2,
            grid=(NH, count),
            in_specs=[row, row, stat, stat, full, full],
            out_specs=[row, full, full],
            scratch_shapes=[pltpu.VMEM((HDIM, span), BF)],
        ),
        compiler_params=room(),
        name="attention_backward",
    )(tiles, lengths, queries, grads, log_total, row_delta, keys, values)


def restore_kernel(tiles_ref, *refs):
    mine_ref, theirs_ref = refs[8:]

    def write(out_ref):
        for j in range(4):
            rows = slice(j * BLK, (j + 1) * BLK)
            for h in range(NH):
                cols = slice(h * HDIM, (h + 1) * HDIM)
                out_ref[rows, cols] = refs[4 + j][h].astype(BF)
                out_ref[rows, PART + h * HDIM : PART + (h + 1) * HDIM] = refs[j][h].astype(BF)

    @pl.when(pl.program_id(0) < 8)
    def _():
        write(theirs_ref)

    @pl.when(pl.program_id(0) >= 8)
    def _():
        write(mine_ref)


def restore_keys(tiles, grad_k, grad_v):
    spec = lambda j: pl.BlockSpec((NH, BLK, HDIM), lambda i, o: (0, o[i * 4 + j], 0))
    shape = (4 * BLK, 2 * PART)
    return pl.pallas_call(
        restore_kernel,
        out_shape=[jax.ShapeDtypeStruct((32 * BLK, 2 * PART), BF)] * 2,
        grid_spec=pltpu.PrefetchScalarGridSpec(
            num_scalar_prefetch=1,
            grid=(16,),
            in_specs=[spec(j) for j in range(4)] * 2,
            out_specs=[
                pl.BlockSpec(shape, lambda i, o: (jnp.maximum(i - 8, 0), 0)),
                pl.BlockSpec(shape, lambda i, o: (jnp.minimum(i, 7), 0)),
            ],
        ),
        compiler_params=room(),
        name="restore_keys",
    )(tiles, *([grad_k] * 4), *([grad_v] * 4))


def unproject_kernel(dq_ref, mine_ref, theirs_ref, w_ref, cos_ref, sin_ref, g_ref, x_ref, w_sc, y_sc):
    thin = w_sc.shape[0] // 32

    @pl.when(pl.program_id(0) == 0)
    def _():
        straighten(w_ref, w_sc, thin)

    kv = mine_ref[...].astype(F32) + theirs_ref[...].astype(F32)
    for h in range(NH):
        y_sc[:, h * HDIM : (h + 1) * HDIM] = dq_ref[h]
    y_sc[:, PART:] = kv[:, PART:]
    cosine, sine_vals = cos_ref[...], -sin_ref[...]
    for k in range(NH):
        cols = slice(k * 128, (k + 1) * 128)
        g_ref[:, cols] = swing(y_sc[:, cols], cosine, sine_vals).astype(BF)
    g_ref[:, 2 * PART :] = kv[:, :PART].astype(BF)
    x_ref[...] = mul(g_ref[...], w_sc[...], NT).astype(BF)


def unproject(grad_q, mine, theirs, w_all, cosine, sine_vals):
    rows = mine.shape[0]
    full = w_all.shape
    width = full[0] * full[1] * (full[2] - 8)
    row = lambda n: pl.BlockSpec((QB, n), lambda i: (i, 0))
    return pl.pallas_call(
        unproject_kernel,
        out_shape=[
            jax.ShapeDtypeStruct((rows, 3 * PART), BF),
            jax.ShapeDtypeStruct((rows, width), BF),
        ],
        grid=(rows // QB,),
        in_specs=[
            pl.BlockSpec((NH, QB, HDIM), lambda i: (0, i, 0)),
            row(2 * PART),
            row(2 * PART),
            pl.BlockSpec(full, lambda i: (0, 0, 0, 0), pipeline_mode=pl.Buffered(1)),
            row(128),
            row(128),
        ],
        out_specs=[row(3 * PART), row(width)],
        scratch_shapes=[
            pltpu.VMEM((width, full[3]), BF),
            pltpu.VMEM((QB, 2 * PART), F32),
        ],
        compiler_params=room(),
        name="unproject",
    )(grad_q, mine, theirs, w_all, cosine, sine_vals)


def to_plane(rows):
    blocks = rows.reshape(4, rows.shape[0] // 4, rows.shape[1])
    blocks = lax.all_to_all(blocks, "p", 0, 0, tiled=True)
    return lax.all_to_all(blocks, "z", 0, 0, tiled=True).reshape(rows.shape)


def from_plane(rows):
    blocks = rows.reshape(4, rows.shape[0] // 4, rows.shape[1])
    blocks = lax.all_to_all(blocks, "z", 0, 0, tiled=True)
    return lax.all_to_all(blocks, "p", 0, 0, tiled=True).reshape(rows.shape)


def flip(values, mask):
    return lax.ppermute(values, "p", [(k, k ^ mask) for k in range(4)])


def gather_slots(own):
    half = own.shape[0] // 2
    first = flip(own, 1)
    second = flip(own, 2)
    upper = flip(second[:half], 1)
    lower = flip(first[half:], 2)
    return jnp.concatenate([own, first, second, upper, lower], axis=0)


def scatter_slots(terms):
    size = terms.shape[0] // 4
    half = size // 2
    low = lambda v: v.astype(BF)
    upper = flip(low(terms[3 * size : 3 * size + half]), 1)
    lower = flip(low(terms[3 * size + half :]), 2)
    first = jnp.concatenate(
        [
            low(terms[size : size + half]),
            low(terms[size + half : 2 * size].astype(F32) + lower.astype(F32)),
        ],
        axis=0,
    )
    second = jnp.concatenate(
        [
            low(terms[2 * size : 2 * size + half].astype(F32) + upper.astype(F32)),
            low(terms[2 * size + half : 3 * size]),
        ],
        axis=0,
    )
    return terms[:size].astype(F32) + flip(first, 1).astype(F32) + flip(second, 2).astype(F32)


def hidden_cuts(hidden):
    steps = hidden // 8
    sizes = [8 * (steps // 4 + (k < steps % 4)) for k in range(4)]
    starts = [sum(sizes[:k]) for k in range(4)]
    return starts, sizes, max(sizes)


def inner(
    tokens_in,
    cotangent,
    w_query,
    w_key,
    w_value,
    w_output,
    w_gate,
    w_up,
    w_down,
    attn_gain,
    ffn_gain,
    cont_len,
    deal_order,
    clip_threshold,
):
    plane, depth, core = (lax.axis_index(name) for name in ("p", "z", "c"))
    line = ("z", "c")
    width = tokens_in.shape[1]
    thin = w_query.shape[0]
    hidden = w_down.shape[0]
    starts, sizes, share = hidden_cuts(hidden)
    gain_f = attn_gain.astype(F32)
    moved = to_plane(tokens_in)
    deal = lax.ppermute(deal_order[0], ("p", "z"), [(g * 4 + k, k * 4 + g) for g in range(4) for k in range(4)])
    lengths = lax.ppermute(cont_len[0], ("p", "z"), [(g * 4 + k, k * 4 + g) for g in range(4) for k in range(4)])

    scaled = [(w.astype(F32) * gain_f[:, None]).astype(BF) for w in (w_query, w_key, w_value)]
    blocks = jnp.stack(scaled).reshape(3, thin, 4, PART).transpose(2, 1, 0, 3)
    blocks = blocks.reshape(4, thin, 3 * PART)
    extra = jnp.zeros((4, 8, 3 * PART), BF).at[:, 0, :thin].set(ffn_gain[None, :])
    send = jnp.concatenate([blocks, extra], axis=1)
    w_qkv = lax.all_gather(lax.all_to_all(send, "p", 0, 0, tiled=True), line, axis=0)
    gain_two = w_qkv[:, :, thin, :thin].transpose(1, 0, 2).reshape(width).astype(F32)
    w_out = lax.all_gather(w_output, line, axis=0, tiled=True)
    stacked = jnp.stack([w_gate.T, w_up.T, w_down])
    stacked = jnp.stack(
        [
            jnp.pad(stacked[:, a : a + n], ((0, 0), (0, share - n), (0, 0)))
            for a, n in zip(starts, sizes)
        ]
    )
    stacked = lax.all_to_all(stacked, "p", 0, 0, tiled=True)
    stacked = stacked.transpose(1, 2, 0, 3).reshape(3, share, width)
    w_ffn = [lax.all_gather(stacked[k], line, axis=0, tiled=True) for k in range(3)]

    slot = jnp.arange(4)[:, None, None]
    source = jnp.arange(4)[None, :, None]
    pair = jnp.arange(2)[None, None, :]
    quarter = jnp.bitwise_xor(plane, slot)
    held = lambda which: deal[((source * 2 + which) * 8 + quarter * 2 + pair).reshape(-1)]
    tiles, tiles_far = held(core), held(1 - core)
    both = jnp.concatenate([tiles, tiles_far])
    numbers = jnp.arange(64, dtype=jnp.int32)
    order = jnp.sum(
        jnp.where(both[None, :] == numbers[:, None], numbers[None, :], 0), axis=1
    ).astype(jnp.int32)
    logical = (tiles[:, None] * BLK + jnp.arange(BLK, dtype=jnp.int32)[None, :]).reshape(-1)
    position = jnp.where(logical < PLEN, logical, PLEN + (logical - PLEN) % CLEN)
    cosine, sine_vals = (v[:, 0, :] for v in rope_angles(position))
    cosine = jnp.concatenate([cosine] * 4, axis=1)
    sine_vals = jnp.concatenate([-sine_vals, sine_vals] * 2, axis=1)

    residual = moved.astype(F32)
    inverse_one = lax.rsqrt(jnp.mean(residual * residual, axis=-1, keepdims=True) + norm_eps)
    normed = gather_slots((residual * inverse_one).astype(BF))
    queries, mine = project(normed, w_qkv, cosine, sine_vals)
    theirs = lax.ppermute(mine, "c", [(0, 1), (1, 0)])
    keys, values = sort_keys(order, mine, theirs)
    attended, log_total, peaks = attention_forward(tiles, lengths, queries, keys, values)
    after_attn = residual + branch_scale * scatter_slots(mul(attended, w_out))
    inverse_two = lax.rsqrt(jnp.mean(after_attn * after_attn, axis=-1, keepdims=True) + norm_eps)
    normed_two = gather_slots((after_attn * inverse_two * gain_two).astype(BF))

    grad_out = to_plane(cotangent).astype(F32)
    grad_rows = gather_slots((branch_scale * grad_out).astype(BF))
    gate_pre = mul(normed_two, w_ffn[0], NT)
    up_pre = mul(normed_two, w_ffn[1], NT)
    mixed = (jax.nn.silu(gate_pre) * up_pre).astype(BF)
    grad_mixed = mul(grad_rows, w_ffn[2], NT)
    grad_gate_low, grad_up_low = gate_grads(grad_mixed, gate_pre, up_pre)
    grad_normed_two = scatter_slots(mul(grad_gate_low, w_ffn[0]) + mul(grad_up_low, w_ffn[1]))
    branch_ffn = scatter_slots(mul(mixed, w_ffn[2]))
    output = from_plane((after_attn + branch_scale * branch_ffn).astype(BF))
    ffn_grads = jnp.stack(
        [
            lax.psum_scatter(mul(a, b, TN).astype(BF), line, scatter_dimension=0, tiled=True)
            for a, b in (
                (grad_gate_low, normed_two),
                (grad_up_low, normed_two),
                (mixed, grad_rows),
            )
        ]
    )
    ffn_grads = ffn_grads.reshape(3, share, 4, PART).transpose(2, 0, 1, 3)
    ffn_grads = lax.all_to_all(ffn_grads, "p", 0, 0, tiled=True).astype(F32)
    ffn_grads = jnp.concatenate([ffn_grads[k, :, :n] for k, n in enumerate(sizes)], axis=1)

    grad_gain_two, grad_second = norm_backward(grad_normed_two, after_attn, inverse_two, gain_two)
    grad_resid = grad_out + grad_second
    grad_branch = gather_slots((branch_scale * grad_resid).astype(BF))
    grad_w_output = mul(attended, grad_branch, TN).astype(BF)
    grad_w_output = lax.psum_scatter(grad_w_output, line, scatter_dimension=0, tiled=True)
    grad_heads, row_delta = attention_delta(grad_branch, w_out, attended)
    grad_q, grad_k, grad_v = attention_backward(
        tiles, lengths, queries, grad_heads, log_total, row_delta, keys, values
    )
    part_mine, part_far = restore_keys(jnp.concatenate([tiles_far, tiles]), grad_k, grad_v)
    received = lax.ppermute(part_far, "c", [(0, 1), (1, 0)])
    grad_qkv, scaled_one = unproject(grad_q, part_mine, received, w_qkv, cosine, sine_vals)
    scaled_one = scatter_slots(scaled_one)
    grad_first = inverse_one * scaled_one - residual * inverse_one**3 * jnp.mean(
        scaled_one * residual, axis=-1, keepdims=True
    )
    grad_input = from_plane((grad_resid + grad_first).astype(BF)).astype(F32)
    proj = mul(normed, grad_qkv, TN).astype(BF)
    proj = proj.reshape(4, 8, thin, 3 * PART).transpose(1, 0, 2, 3)
    gain_rows = grad_gain_two.astype(BF).reshape(4, 8, 1, thin).transpose(1, 0, 2, 3)
    gain_rows = jnp.pad(gain_rows, ((0, 0), (0, 0), (0, 7), (0, 3 * PART - thin)))
    proj = jnp.concatenate([proj, gain_rows], axis=2).reshape(8 * 4 * (thin + 8), 3 * PART)
    proj = lax.psum_scatter(proj, line, scatter_dimension=0, tiled=True)
    proj = proj.reshape(4, thin + 8, 3 * PART)
    proj = lax.all_to_all(proj, "p", 0, 0, tiled=True).astype(F32)
    grad_ffn_gain = jnp.sum(proj[:, thin, :thin], axis=0)
    proj = proj[:, :thin].reshape(4, thin, 3, PART).transpose(2, 1, 0, 3).reshape(3, thin, width)
    grad_attn_gain = sum(
        jnp.sum(w.astype(F32) * proj[k], axis=1) for k, w in enumerate((w_query, w_key, w_value))
    )
    proj = proj * gain_f[None, :, None]

    maxima = jnp.where(
        jnp.arange(4)[:, None] == plane, jnp.max(peaks, axis=(0, 2))[None, :], masked_value
    ).reshape(HEADS)
    for name, mask, size in (("c", 1, 2), ("p", 1, 4), ("p", 2, 4), ("z", 1, 4), ("z", 2, 4)):
        pairs = [(k, k ^ mask) for k in range(size)]
        maxima = jnp.maximum(maxima, lax.ppermute(maxima, name, pairs))
    limit_value = clip_threshold[0].astype(F32)
    clip_factor = jnp.sqrt(limit_value / jnp.maximum(maxima, limit_value))
    column_factor = jnp.repeat(clip_factor, HDIM)
    return (
        output,
        grad_input,
        proj[0],
        proj[1],
        proj[2],
        grad_w_output.astype(F32),
        ffn_grads[0].T,
        ffn_grads[1].T,
        ffn_grads[2],
        grad_attn_gain,
        grad_ffn_gain,
        maxima,
        clip_factor,
        w_query.astype(F32) * column_factor[None, :],
        w_key.astype(F32) * column_factor[None, :],
    )


def specs(grp, ctx):
    every = grp + ctx
    ins = [P(every, None)] * 6 + [P(grp, ctx), P(grp, ctx), P(ctx, grp), P(every), P(every)]
    ins += [P(grp, None), P(grp, None), P()]
    outs = [P(every, None)] * 6 + [P(grp, ctx), P(grp, ctx), P(ctx, grp), P(every), P(every)]
    outs += [P(), P(), P(every, None), P(every, None)]
    return tuple(ins), tuple(outs)


def solution(mesh):
    if mesh.shape["grp"] == 4 and mesh.shape["ctx"] == 8:
        mesh = Mesh(mesh.devices.reshape(4, 4, 2), ("p", "z", "c"))
        body, (in_specs, out_specs) = inner, specs(("p",), ("z", "c"))
    else:
        body, (in_specs, out_specs) = local, specs(("grp",), ("ctx",))
    return jax.shard_map(body, mesh=mesh, in_specs=in_specs, out_specs=out_specs, check_vma=False)
```

```python
import functools
import math

import jax
import jax.numpy as jnp
from jax import lax
from jax.experimental import pallas as pl
from jax.experimental.pallas import tpu as pltpu
from jax.sharding import Mesh
from jax.sharding import PartitionSpec as P

HEADS = 36
HDIM = 64
PLEN = 2048
CLEN = 256
NCONT = 8
BLK = 64
FAMTOK = 4096

F32 = jnp.float32
BF = jnp.bfloat16
NH = HEADS // 4
PART = NH * HDIM
GROUP = 3
GPART = GROUP * HDIM
QB = 256
KB = 1024
KB_FWD = 512
HEAD_STEP = 9
NT = (((1,), (1,)), ((), ()))
NN = (((1,), (0,)), ((), ()))
TN = (((0,), (0,)), ((), ()))
VMEM_ROOM = 56 * 1024 * 1024


branch_scale = 1.4 / math.sqrt(40.0)
norm_eps = 1e-05
rope_base = 10000.0
masked_value = -1e30


def rope_angles(position):
    half_dim = HDIM // 2
    frequency = rope_base ** (-(jnp.arange(half_dim, dtype=jnp.float32) * (2.0 / HDIM)))
    angles = position.astype(jnp.float32)[:, None] * frequency[None, :]
    return (jnp.cos(angles)[:, None, :], jnp.sin(angles)[:, None, :])


def rotate(values, cosine, sine_vals, turn_sign):
    row_count = values.shape[0]
    shaped = values.reshape(row_count, HEADS, HDIM)
    leading = shaped[..., : HDIM // 2]
    trailing = shaped[..., HDIM // 2 :]
    turned = jnp.concatenate(
        [
            leading * cosine - turn_sign * trailing * sine_vals,
            trailing * cosine + turn_sign * leading * sine_vals,
        ],
        axis=-1,
    )
    return turned.reshape(row_count, HEADS * HDIM)


def token_facts(logical, lengths):
    family = logical // FAMTOK
    offset = logical % FAMTOK
    prompt = offset < PLEN
    member = jnp.clip((offset - PLEN) // CLEN, 0, NCONT - 1)
    inside = offset - PLEN - member * CLEN
    seq_id = jnp.where(prompt, -1, family * NCONT + member)
    numbers = jnp.arange(lengths.shape[0], dtype=jnp.int32)
    live_len = jnp.sum(jnp.where(seq_id[:, None] == numbers[None, :], lengths[None, :], 0), axis=1)
    is_live = prompt | (inside < live_len)
    position = jnp.where(prompt, offset, PLEN + inside)
    return (family, offset, prompt, seq_id, is_live, position)


def visible(query_facts, key_part):
    same_family = query_facts[0][:, None] == key_part[0][None, :]
    causal = key_part[1][None, :] <= query_facts[1][:, None]
    reaches = (
        key_part[2][None, :]
        | (key_part[3][None, :] == query_facts[3][:, None]) & key_part[4][None, :]
    )
    return same_family & causal & reaches


def key_slice(keys_heads, values_heads, key_facts, query_facts, first_row, span_rows):
    key_block = lax.dynamic_slice_in_dim(keys_heads, first_row, span_rows, 0)
    value_block = lax.dynamic_slice_in_dim(values_heads, first_row, span_rows, 0)
    key_part = tuple(
        (
            lax.dynamic_slice_in_dim(member_array, first_row, span_rows, 0)
            for member_array in key_facts
        )
    )
    return (key_block, value_block, visible(query_facts, key_part))


def block_scores(query_heads, key_block, visible_mask):
    scores = jnp.einsum(
        "qhd,khd->hqk", query_heads, key_block, preferred_element_type=jnp.float32
    ) * HDIM ** (-0.5)
    return jnp.where(visible_mask[None], scores, masked_value)


def score_grads(
    query_heads, grad_heads, log_total, row_delta, key_block, value_block, visible_mask
):
    scores = block_scores(query_heads, key_block, visible_mask)
    prob_table = jnp.where(visible_mask[None], jnp.exp(scores - log_total[:, :, None]), 0.0)
    grad_probs = jnp.einsum(
        "qhd,khd->hqk", grad_heads, value_block, preferred_element_type=jnp.float32
    )
    grad_scores = (prob_table * (grad_probs - row_delta[:, :, None])).astype(jnp.bfloat16)
    return (prob_table.astype(jnp.bfloat16), grad_scores)


def gate_grads(grad_mixed, gate_pre, up_pre):
    sigmoid = jax.nn.sigmoid(gate_pre)
    grad_gate = grad_mixed * up_pre * sigmoid * (1.0 + gate_pre * (1.0 - sigmoid))
    grad_up = grad_mixed * gate_pre * sigmoid
    return (grad_gate.astype(jnp.bfloat16), grad_up.astype(jnp.bfloat16))


def norm_backward(grad_normed, values, inverse, gain):
    scaled = grad_normed * gain[None, :]
    grad_gain = jnp.sum(grad_normed * values * inverse, axis=0)
    grad_values = inverse * scaled - values * inverse**3 * jnp.mean(
        scaled * values, axis=-1, keepdims=True
    )
    return (grad_gain, grad_values)


def attention_weights(w_query, w_key, w_value, w_output, attn_gain, ffn_gain):
    return (
        lax.all_gather(w_query, ("grp", "ctx"), axis=0, tiled=True),
        lax.all_gather(w_key, ("grp", "ctx"), axis=0, tiled=True),
        lax.all_gather(w_value, ("grp", "ctx"), axis=0, tiled=True),
        lax.all_gather(w_output, ("grp", "ctx"), axis=0, tiled=True),
        lax.all_gather(attn_gain, ("grp", "ctx"), axis=0, tiled=True),
        lax.all_gather(ffn_gain, ("grp", "ctx"), axis=0, tiled=True),
    )


def ffn_rows_gather(w_gate, w_up, w_down):
    return (
        lax.all_gather(w_gate, "grp", axis=0, tiled=True),
        lax.all_gather(w_up, "grp", axis=0, tiled=True),
        lax.all_gather(w_down, "grp", axis=1, tiled=True),
    )


def local(
    tokens_in,
    cotangent,
    w_query,
    w_key,
    w_value,
    w_output,
    w_gate,
    w_up,
    w_down,
    attn_gain,
    ffn_gain,
    cont_len,
    deal_order,
    clip_threshold,
):
    row_count = tokens_in.shape[0]
    model_width = tokens_in.shape[1]
    tile_count = deal_order.shape[1]
    group_rows = tile_count * BLK
    lengths = cont_len[0]
    my_index = lax.axis_index("ctx")
    tile_offsets = jnp.arange(BLK, dtype=jnp.int32)
    stored_logical = (deal_order[0][:, None] * BLK + tile_offsets[None, :]).reshape(group_rows)
    key_facts = token_facts(stored_logical, lengths)
    query_facts = tuple(
        (
            lax.dynamic_slice_in_dim(member_array, my_index * row_count, row_count, 0)
            for member_array in key_facts
        )
    )
    cosine, sine_vals = rope_angles(query_facts[5])
    key_step = math.gcd(group_rows, 512)
    key_blocks = group_rows // key_step
    full_query, full_key, full_value, full_output, gain_one, gain_two = attention_weights(
        w_query, w_key, w_value, w_output, attn_gain, ffn_gain
    )
    residual = tokens_in.astype(jnp.float32)
    inverse_one = lax.rsqrt(jnp.mean(residual * residual, axis=-1, keepdims=True) + norm_eps)
    gain_one_f = gain_one.astype(jnp.float32)
    gain_two_f = gain_two.astype(jnp.float32)
    normed_one = (residual * inverse_one * gain_one_f).astype(jnp.bfloat16)
    query_rot = rotate(
        jnp.dot(normed_one, full_query, preferred_element_type=jnp.float32), cosine, sine_vals, 1.0
    ).astype(jnp.bfloat16)
    key_rot = rotate(
        jnp.dot(normed_one, full_key, preferred_element_type=jnp.float32), cosine, sine_vals, 1.0
    ).astype(jnp.bfloat16)
    value_low = jnp.dot(normed_one, full_value, preferred_element_type=jnp.float32).astype(
        jnp.bfloat16
    )
    keys_all, values_all = (
        lax.all_gather(key_rot, "ctx", axis=0, tiled=True),
        lax.all_gather(value_low, "ctx", axis=0, tiled=True),
    )
    query_heads = query_rot.reshape(row_count, HEADS, HDIM)
    keys_heads = keys_all.reshape(group_rows, HEADS, HDIM)
    values_heads = values_all.reshape(group_rows, HEADS, HDIM)

    def stats_step(block_index, state_carry):
        key_block, value_block, visible_mask = key_slice(
            keys_heads, values_heads, key_facts, query_facts, block_index * key_step, key_step
        )

        def stats_busy(carry):
            run_max, run_sum, head_max = carry
            scores = block_scores(query_heads, key_block, visible_mask)
            block_max = jnp.max(scores, axis=2)
            new_max = jnp.maximum(run_max, block_max)
            exp_table = jnp.where(visible_mask[None], jnp.exp(scores - new_max[:, :, None]), 0.0)
            new_sum = run_sum * jnp.exp(run_max - new_max) + jnp.sum(exp_table, axis=2)
            return (new_max, new_sum, jnp.maximum(head_max, jnp.max(block_max, axis=1)))

        return lax.cond(jnp.any(visible_mask), stats_busy, lambda carry: carry, state_carry)

    start_state = (
        jnp.full((HEADS, row_count), masked_value, jnp.float32),
        jnp.zeros((HEADS, row_count), jnp.float32),
        jnp.full((HEADS,), masked_value, jnp.float32),
    )
    run_max, run_sum, head_max = lax.fori_loop(0, key_blocks, stats_step, start_state)
    log_total = run_max + jnp.log(run_sum)

    def output_step(block_index, running):
        key_block, value_block, visible_mask = key_slice(
            keys_heads, values_heads, key_facts, query_facts, block_index * key_step, key_step
        )

        def output_busy(total):
            scores = block_scores(query_heads, key_block, visible_mask)
            prob_low = jnp.where(
                visible_mask[None], jnp.exp(scores - log_total[:, :, None]), 0.0
            ).astype(jnp.bfloat16)
            return total + jnp.einsum(
                "hqk,khd->qhd", prob_low, value_block, preferred_element_type=jnp.float32
            )

        return lax.cond(jnp.any(visible_mask), output_busy, lambda total: total, running)

    attended = lax.fori_loop(
        0, key_blocks, output_step, jnp.zeros((row_count, HEADS, HDIM), jnp.float32)
    )
    attn_low = attended.reshape(row_count, model_width).astype(jnp.bfloat16)
    after_attn = residual + branch_scale * jnp.dot(
        attn_low, full_output, preferred_element_type=jnp.float32
    )
    inverse_two = lax.rsqrt(jnp.mean(after_attn * after_attn, axis=-1, keepdims=True) + norm_eps)
    normed_two = (after_attn * inverse_two * gain_two_f).astype(jnp.bfloat16)
    gate_cols, up_cols, down_cols = ffn_rows_gather(w_gate, w_up, w_down)
    normed_rows = lax.all_gather(normed_two, "ctx", axis=0, tiled=True)
    gate_pre = jnp.dot(normed_rows, gate_cols, preferred_element_type=jnp.float32)
    up_pre = jnp.dot(normed_rows, up_cols, preferred_element_type=jnp.float32)
    mixed = (jax.nn.silu(gate_pre) * up_pre).astype(jnp.bfloat16)
    branch_ffn = lax.psum_scatter(
        jnp.dot(mixed, down_cols, preferred_element_type=jnp.float32).astype(jnp.bfloat16),
        "ctx",
        scatter_dimension=0,
        tiled=True,
    ).astype(jnp.float32)
    output = (after_attn + branch_scale * branch_ffn).astype(jnp.bfloat16)
    grad_out = cotangent.astype(jnp.float32)
    grad_branch = (branch_scale * grad_out).astype(jnp.bfloat16)
    gate_again, up_again, down_again = ffn_rows_gather(w_gate, w_up, w_down)
    grad_rows = lax.all_gather(grad_branch, "ctx", axis=0, tiled=True)
    grad_mixed = jnp.dot(grad_rows, down_again.T, preferred_element_type=jnp.float32)
    grad_down = jnp.dot(mixed.T, grad_rows, preferred_element_type=jnp.float32)
    grad_gate_low, grad_up_low = gate_grads(grad_mixed, gate_pre, up_pre)
    grad_gate = jnp.dot(normed_rows.T, grad_gate_low, preferred_element_type=jnp.float32)
    grad_up = jnp.dot(normed_rows.T, grad_up_low, preferred_element_type=jnp.float32)
    grad_normed_two = lax.psum_scatter(
        (
            jnp.dot(grad_gate_low, gate_again.T, preferred_element_type=jnp.float32)
            + jnp.dot(grad_up_low, up_again.T, preferred_element_type=jnp.float32)
        ).astype(jnp.bfloat16),
        "ctx",
        scatter_dimension=0,
        tiled=True,
    ).astype(jnp.float32)
    ffn_stack = jnp.stack([grad_gate, grad_up, grad_down.T], axis=0)
    ffn_summed = lax.psum_scatter(
        ffn_stack.astype(jnp.bfloat16), "grp", scatter_dimension=1, tiled=True
    ).astype(jnp.float32)
    grad_gain_two, grad_second = norm_backward(grad_normed_two, after_attn, inverse_two, gain_two_f)
    grad_resid = grad_out + grad_second
    back_query, back_key, back_value, back_output, back_gain_one, back_gain_two = attention_weights(
        w_query, w_key, w_value, w_output, attn_gain, ffn_gain
    )
    grad_branch_attn = (branch_scale * grad_resid).astype(jnp.bfloat16)
    grad_w_output = jnp.dot(attn_low.T, grad_branch_attn, preferred_element_type=jnp.float32)
    grad_attn = jnp.dot(grad_branch_attn, back_output.T, preferred_element_type=jnp.float32).astype(
        jnp.bfloat16
    )
    grad_heads = grad_attn.reshape(row_count, HEADS, HDIM)
    row_delta = jnp.sum(grad_heads.astype(jnp.float32) * attended, axis=2).T

    def back_step(grad_q, block_index):
        key_block, value_block, visible_mask = key_slice(
            keys_heads, values_heads, key_facts, query_facts, block_index * key_step, key_step
        )

        def back_busy(current):
            prob_low, grad_scores = score_grads(
                query_heads, grad_heads, log_total, row_delta, key_block, value_block, visible_mask
            )
            updated = current + jnp.einsum(
                "hqk,khd->qhd", grad_scores, key_block, preferred_element_type=jnp.float32
            )
            grad_keys = jnp.einsum(
                "hqk,qhd->khd", grad_scores, query_heads, preferred_element_type=jnp.float32
            ) * HDIM ** (-0.5)
            grad_values = jnp.einsum(
                "hqk,qhd->khd", prob_low, grad_heads, preferred_element_type=jnp.float32
            )
            return (
                updated,
                (
                    grad_keys.reshape(key_step, model_width),
                    grad_values.reshape(key_step, model_width),
                ),
            )

        def quiet(current):
            empty = jnp.zeros((key_step, model_width), jnp.float32)
            return (current, (empty, empty))

        return lax.cond(jnp.any(visible_mask), back_busy, quiet, grad_q)

    grad_q_heads, key_terms = lax.scan(
        back_step,
        jnp.zeros((row_count, HEADS, HDIM), jnp.float32),
        jnp.arange(key_blocks, dtype=jnp.int32),
    )
    key_sum, value_sum = (
        lax.psum_scatter(
            key_terms[0].reshape(group_rows, model_width).astype(jnp.bfloat16),
            "ctx",
            scatter_dimension=0,
            tiled=True,
        ).astype(jnp.float32),
        lax.psum_scatter(
            key_terms[1].reshape(group_rows, model_width).astype(jnp.bfloat16),
            "ctx",
            scatter_dimension=0,
            tiled=True,
        ).astype(jnp.float32),
    )
    grad_query_rot = grad_q_heads.reshape(row_count, model_width) * HDIM ** (-0.5)
    grad_query = rotate(grad_query_rot, cosine, sine_vals, -1.0).astype(jnp.bfloat16)
    grad_key = rotate(key_sum, cosine, sine_vals, -1.0).astype(jnp.bfloat16)
    grad_value = value_sum.astype(jnp.bfloat16)
    grad_w_query = jnp.dot(normed_one.T, grad_query, preferred_element_type=jnp.float32)
    grad_w_key = jnp.dot(normed_one.T, grad_key, preferred_element_type=jnp.float32)
    grad_w_value = jnp.dot(normed_one.T, grad_value, preferred_element_type=jnp.float32)
    grad_normed_one = (
        jnp.dot(grad_query, back_query.T, preferred_element_type=jnp.float32)
        + jnp.dot(grad_key, back_key.T, preferred_element_type=jnp.float32)
        + jnp.dot(grad_value, back_value.T, preferred_element_type=jnp.float32)
    )
    grad_gain_one, grad_first = norm_backward(grad_normed_one, residual, inverse_one, gain_one_f)
    grad_input = grad_resid + grad_first
    gain_pair = jnp.stack([grad_gain_one, grad_gain_two], axis=1)
    summed = (
        lax.psum_scatter(grad_w_query, ("grp", "ctx"), scatter_dimension=0, tiled=True),
        lax.psum_scatter(grad_w_key, ("grp", "ctx"), scatter_dimension=0, tiled=True),
        lax.psum_scatter(grad_w_value, ("grp", "ctx"), scatter_dimension=0, tiled=True),
        lax.psum_scatter(grad_w_output, ("grp", "ctx"), scatter_dimension=0, tiled=True),
        lax.psum_scatter(gain_pair, ("grp", "ctx"), scatter_dimension=0, tiled=True),
    )
    maxima = lax.pmax(head_max, ("grp", "ctx"))
    limit_value = clip_threshold[0].astype(jnp.float32)
    clip_factor = jnp.sqrt(limit_value / jnp.maximum(maxima, limit_value))
    column_factor = jnp.repeat(clip_factor, HDIM)
    clipped_query = w_query.astype(jnp.float32) * column_factor[None, :]
    clipped_key = w_key.astype(jnp.float32) * column_factor[None, :]
    return (
        output,
        grad_input,
        summed[0],
        summed[1],
        summed[2],
        summed[3],
        ffn_summed[0],
        ffn_summed[1],
        ffn_summed[2].T,
        summed[4][:, 0],
        summed[4][:, 1],
        maxima,
        clip_factor,
        clipped_query,
        clipped_key,
    )


def mul(left, right, dims=NN):
    return lax.dot_general(left, right, dims, preferred_element_type=F32)


def room():
    return pltpu.CompilerParams(vmem_limit_bytes=VMEM_ROOM)


def cost(flops, sent):
    return pl.CostEstimate(flops=int(flops), bytes_accessed=int(sent), transcendentals=0)


def straighten(w_ref, w_sc, thin):
    for i in range(4):
        for k in range(8):
            w_sc[(i * 8 + k) * thin : (i * 8 + k + 1) * thin, :] = w_ref[k, i, :thin, :]


def swing(values, cosine, sine_vals):
    lane = lax.broadcasted_iota(jnp.int32, values.shape, 1)
    other = jnp.where(
        lane % HDIM < HDIM // 2,
        pltpu.roll(values, 2 * HDIM - HDIM // 2, 1),
        pltpu.roll(values, HDIM // 2, 1),
    )
    return values * cosine + other * sine_vals


def fetch_rows(pieces, x_sc):
    step = pl.program_id(0)
    half = QB // 2
    for k in range(8):
        chunk, slot = k // 4, k % 4

        @pl.when(step == k)
        def _():
            if len(pieces) == 5 and slot < 3:
                x_sc[...] = pieces[slot][chunk * QB : (chunk + 1) * QB, :]
            elif len(pieces) == 5:
                x_sc[...] = pieces[3 + chunk][...]
            elif slot < 3:
                x_sc[...] = pieces[chunk * 5 + slot][...]
            else:
                x_sc[:half] = pieces[chunk * 5 + 3][...]
                x_sc[half:] = pieces[chunk * 5 + 4][...]


def whole(shape):
    return pl.BlockSpec(shape, lambda i: (0,) * len(shape), pipeline_mode=pl.Buffered(1))


def project_kernel(*refs):
    w_ref, cos_ref, sin_ref, q_ref, kv_ref, w_sc, x_sc = refs[5:]
    thin = w_sc.shape[0] // 32
    fetch_rows(refs[:5], x_sc)

    @pl.when(pl.program_id(0) == 0)
    def _():
        straighten(w_ref, w_sc, thin)

    y = mul(x_sc[...], w_sc[...])
    cosine, sine_vals = cos_ref[...], sin_ref[...]
    for k in range(NH):
        piece = swing(y[:, k * 128 : (k + 1) * 128], cosine, sine_vals)
        for j in range(2):
            head = 2 * k + j
            if head < NH:
                q_ref[head] = (piece[:, j * HDIM : (j + 1) * HDIM] * 0.125).astype(BF)
        if 2 * k + 1 > NH:
            kv_ref[:, k * 128 : (k + 1) * 128] = piece.astype(BF)
        elif 2 * k + 1 == NH:
            kv_ref[:, k * 128 + HDIM : (k + 1) * 128] = piece[:, HDIM:].astype(BF)
    kv_ref[:, :PART] = y[:, 2 * PART :].astype(BF)


def project(normed, w_all, cosine, sine_vals):
    rows = sum(v.shape[0] for v in normed)
    width = normed[0].shape[1]
    full = w_all.shape
    return pl.pallas_call(
        project_kernel,
        out_shape=[
            jax.ShapeDtypeStruct((NH, rows, HDIM), BF),
            jax.ShapeDtypeStruct((rows, 2 * PART), BF),
        ],
        grid=(rows // QB,),
        in_specs=[whole(v.shape) for v in normed]
        + [
            whole(full),
            pl.BlockSpec((QB, 128), lambda i: (i, 0)),
            pl.BlockSpec((QB, 128), lambda i: (i, 0)),
        ],
        out_specs=[
            pl.BlockSpec((NH, QB, HDIM), lambda i: (0, i, 0)),
            pl.BlockSpec((QB, 2 * PART), lambda i: (i, 0)),
        ],
        scratch_shapes=[pltpu.VMEM((width, full[3]), BF), pltpu.VMEM((QB, width), BF)],
        compiler_params=room(),
        cost_estimate=cost(2 * rows * width * full[3], 2 * (rows * width + width * full[3] + rows * 5 * PART)),
        name="project",
    )(*normed, w_all, cosine, sine_vals)


def sort_kernel(order_ref, *refs):
    k_ref, v_ref, kt_ref, vt_ref = refs[8:]
    first = pl.program_id(0) * 4
    for j in range(4):
        from_mine = order_ref[first + j] < 32
        tile = jnp.where(from_mine, refs[j][0], refs[4 + j][0])
        rows = slice(j * BLK, (j + 1) * BLK)
        for h in range(NH):
            v_ref[h, rows, :] = tile[:, h * HDIM : (h + 1) * HDIM]
            k_ref[h, rows, :] = tile[:, PART + h * HDIM : PART + (h + 1) * HDIM]
    for h in range(NH):
        kt_ref[h] = k_ref[h].T
        vt_ref[h] = v_ref[h].T


def sort_keys(order, mine, theirs):
    count = order.shape[0]
    shape = (1, BLK, 2 * PART)
    near = lambda j: pl.BlockSpec(shape, lambda i, o: (jnp.minimum(o[i * 4 + j], 31), 0, 0))
    far = lambda j: pl.BlockSpec(shape, lambda i, o: (jnp.maximum(o[i * 4 + j] - 32, 0), 0, 0))
    return pl.pallas_call(
        sort_kernel,
        out_shape=[jax.ShapeDtypeStruct((NH, count * BLK, HDIM), BF)] * 2
        + [jax.ShapeDtypeStruct((NH, HDIM, count * BLK), BF)] * 2,
        grid_spec=pltpu.PrefetchScalarGridSpec(
            num_scalar_prefetch=1,
            grid=(count // 4,),
            in_specs=[near(j) for j in range(4)] + [far(j) for j in range(4)],
            out_specs=[pl.BlockSpec((NH, 4 * BLK, HDIM), lambda i, o: (0, i, 0))] * 2
            + [pl.BlockSpec((NH, HDIM, 4 * BLK), lambda i, o: (0, 0, i))] * 2,
        ),
        compiler_params=room(),
        cost_estimate=cost(0, 64 * count * BLK * PART),
        name="sort_keys",
    )(order, *([mine.reshape(32, BLK, 2 * PART)] * 4), *([theirs.reshape(32, BLK, 2 * PART)] * 4))


def lane_tile(vals):
    lane = lax.broadcasted_iota(jnp.int32, (1, QB), 1)
    out = jnp.full((1, QB), vals[3], jnp.int32)
    for j in (2, 1, 0):
        out = jnp.where(lane < (j + 1) * BLK, vals[j], out)
    return out, lane & (BLK - 1)


def block_facts(tiles_ref, len_ref, block, step):
    half_tiles = PLEN // BLK
    t = [tiles_ref[block * 4 + j] for j in range(4)]
    tile, within = lane_tile(t)
    qpos = tile * BLK + within
    tmax = jnp.maximum(jnp.maximum(t[0], t[1]), jnp.maximum(t[2], t[3]))
    tmin = jnp.minimum(jnp.minimum(t[0], t[1]), jnp.minimum(t[2], t[3]))
    per = step // BLK
    is_cont = t[0] >= half_tiles
    n_all = jnp.where(is_cont, PLEN // step, tmax // per + 1)
    n_free = jnp.where(is_cont, PLEN // step, tmin // per)
    conts = [jnp.maximum(t[j] - half_tiles, 0) // 4 for j in range(4)]
    lens = lane_tile([len_ref[conts[j]] for j in range(4)])[0]
    qin = qpos - PLEN - lane_tile(conts)[0] * CLEN
    starts = [pl.multiple_of(PLEN + conts[j] * CLEN, CLEN) for j in range(4)]
    kin = lax.broadcasted_iota(jnp.int32, (CLEN, QB), 0)
    seen = lambda: (kin <= qin) & (kin < lens)
    return qpos, is_cont, n_all, n_free, starts, seen


def forward_kernel(
    tiles_ref, len_ref, q_ref, k_ref, vt_sc, o_ref, lse_ref, mx_ref, ot_sc, shift
):
    block = pl.program_id(0) + shift
    qpos, is_cont, n_all, n_free, starts, seen = block_facts(tiles_ref, len_ref, block, KB_FWD)

    def heads(group, carry):
        hs = [group * HEAD_STEP + j for j in range(HEAD_STEP)]
        qs = [q_ref[h] for h in hs]

        def update(scores, states, weigh):
            out = []
            for n, (s, (m, l, acc)) in enumerate(zip(scores, states)):
                mn = jnp.maximum(m, jnp.max(s, axis=0, keepdims=True))
                p = jnp.exp(s - mn)
                al = jnp.exp(m - mn)
                out.append(
                    (
                        mn,
                        l * al + jnp.sum(p, axis=0, keepdims=True),
                        acc * al + weigh(n, p.astype(BF)),
                    )
                )
            return tuple(out)

        def step(kb, states, masked):
            base = pl.multiple_of(kb * KB_FWD, KB_FWD)
            rows = pl.ds(base, KB_FWD)
            scores = [mul(k_ref[h, rows, :], q, NT) for h, q in zip(hs, qs)]
            if masked:
                kpos = base + lax.broadcasted_iota(jnp.int32, (KB_FWD, QB), 0)
                vis = kpos <= qpos
                scores = [jnp.where(vis, s, masked_value) for s in scores]
            return update(scores, states, lambda n, p: mul(vt_sc[hs[n], :, rows], p))

        states = tuple(
            (
                jnp.full((1, QB), masked_value, F32),
                jnp.zeros((1, QB), F32),
                jnp.zeros((HDIM, QB), F32),
            )
            for _ in hs
        )
        states = lax.fori_loop(0, n_free, functools.partial(step, masked=False), states)
        states = lax.fori_loop(n_free, n_all, functools.partial(step, masked=True), states)

        def own(states):
            vis = seen()
            cols = lambda x, j: x[:, j * BLK : (j + 1) * BLK]
            scores = []
            for h, q in zip(hs, qs):
                s = [
                    mul(k_ref[h, pl.ds(starts[j], CLEN), :], q[j * BLK : (j + 1) * BLK], NT)
                    for j in range(4)
                ]
                scores.append(jnp.where(vis, jnp.concatenate(s, axis=1), masked_value))
            return update(
                scores,
                states,
                lambda n, p: jnp.concatenate(
                    [
                        mul(vt_sc[hs[n], :, pl.ds(starts[j], CLEN)], cols(p, j))
                        for j in range(4)
                    ],
                    axis=1,
                ),
            )

        states = lax.cond(is_cont, own, lambda s: s, states)
        for h, (m, l, acc) in zip(hs, states):
            ot_sc[h] = acc / l
            lse_ref[0, pl.ds(h, 1), :] = m + jnp.log(l)
            mx_ref[0, pl.ds(h, 1), :] = m
        return carry

    lax.fori_loop(0, NH // HEAD_STEP, heads, 0)
    for h in range(NH):
        o_ref[:, h * HDIM : (h + 1) * HDIM] = ot_sc[h].T.astype(BF)


def attention_forward(tiles, lengths, queries, keys, values_t, shift, count):
    rows = count * QB
    span = keys.shape[1]
    once = lambda *shape: pl.BlockSpec(
        shape, lambda i, a, b: (0, 0, 0), pipeline_mode=pl.Buffered(1)
    )
    stat = pl.BlockSpec((1, NH, QB), lambda i, a, b: (i, 0, 0))
    return pl.pallas_call(
        functools.partial(forward_kernel, shift=shift),
        out_shape=[
            jax.ShapeDtypeStruct((rows, PART), BF),
            jax.ShapeDtypeStruct((count, NH, QB), F32),
            jax.ShapeDtypeStruct((count, NH, QB), F32),
        ],
        grid_spec=pltpu.PrefetchScalarGridSpec(
            num_scalar_prefetch=2,
            grid=(count,),
            in_specs=[
                pl.BlockSpec((NH, QB, HDIM), lambda i, a, b: (0, i + shift, 0)),
                once(NH, span, HDIM),
                once(NH, HDIM, span),
            ],
            out_specs=[pl.BlockSpec((QB, PART), lambda i, a, b: (i, 0)), stat, stat],
            scratch_shapes=[pltpu.VMEM((NH, HDIM, QB), F32)],
        ),
        compiler_params=room(),
        cost_estimate=cost(rows * PART * PLEN * 20, 16 * span * PART),
        name="attention_forward",
    )(tiles, lengths, queries, keys, values_t)


def delta_kernel(*refs):
    w_ref, o_ref, gh_ref, delta_ref, x_sc = refs[10:]
    fetch_rows(refs[:10], x_sc)
    grad = mul(x_sc[...], w_ref[...], NT).astype(BF)
    for h in range(NH):
        gh_ref[h] = grad[:, h * HDIM : (h + 1) * HDIM]
    prod = grad.astype(F32) * o_ref[...].astype(F32)
    row = lax.broadcasted_iota(jnp.int32, (16, PART), 0)
    col = lax.broadcasted_iota(jnp.int32, (16, PART), 1)
    pick = jnp.where(col // HDIM == row, 1.0, 0.0)
    total = lax.dot_general(
        pick, prod, NT, preferred_element_type=F32, precision=lax.Precision.HIGHEST
    )
    delta_ref[0] = total[:NH]


def attention_delta(grad_branch, w_out, attended):
    rows, width = attended.shape[0], w_out.shape[1]
    count = rows // QB
    return pl.pallas_call(
        delta_kernel,
        out_shape=[
            jax.ShapeDtypeStruct((NH, rows, HDIM), BF),
            jax.ShapeDtypeStruct((count, NH, QB), F32),
        ],
        grid=(count,),
        in_specs=[whole(v.shape) for v in grad_branch]
        + [whole((PART, width)), pl.BlockSpec((QB, PART), lambda i: (i, 0))],
        out_specs=[
            pl.BlockSpec((NH, QB, HDIM), lambda i: (0, i, 0)),
            pl.BlockSpec((1, NH, QB), lambda i: (i, 0, 0)),
        ],
        scratch_shapes=[pltpu.VMEM((QB, width), BF)],
        compiler_params=room(),
        cost_estimate=cost(2 * rows * width * PART, 2 * rows * width),
        name="attention_delta",
    )(*grad_branch, w_out, attended)


def backward_kernel(
    tiles_ref, len_ref, q_ref, g_ref, lse_ref, delta_ref, k_ref, v_ref, kt_ref, dq_ref, dk_out, dv_out,
    dk_ref, dv_ref, first
):
    h = pl.program_id(0) + first
    block = pl.program_id(1)

    @pl.when(block == 0)
    def _():
        dk_ref[...] = jnp.zeros_like(dk_ref)
        dv_ref[...] = jnp.zeros_like(dv_ref)

    qpos, is_cont, n_all, n_free, starts, seen = block_facts(tiles_ref, len_ref, block, KB)
    q = q_ref[0]
    g = g_ref[0]
    lse = lse_ref[0, pl.ds(h, 1), :]
    delta = delta_ref[0, pl.ds(h, 1), :]

    def step(kb, dqt, masked):
        base = pl.multiple_of(kb * KB, KB)
        rows = pl.ds(base, KB)
        s = mul(k_ref[0, rows, :], q, NT)
        dp = mul(v_ref[0, rows, :], g, NT)
        if masked:
            kpos = base + lax.broadcasted_iota(jnp.int32, (KB, QB), 0)
            s = jnp.where(kpos <= qpos, s, masked_value)
        p = jnp.exp(s - lse)
        ds = (p * (dp - delta)).astype(BF)
        dv_ref[rows, :] += mul(p.astype(BF), g)
        dk_ref[rows, :] += mul(ds, q)
        return dqt + mul(kt_ref[0, :, rows], ds)

    dqt = jnp.zeros((HDIM, QB), F32)
    dqt = lax.fori_loop(0, n_free, functools.partial(step, masked=False), dqt)
    dqt = lax.fori_loop(n_free, n_all, functools.partial(step, masked=True), dqt)
    dq_ref[0] = dqt.T * HDIM ** (-0.5)

    @pl.when(is_cont)
    def _():
        part = lambda x, j: x[j * BLK : (j + 1) * BLK]
        rows = [pl.ds(starts[j], CLEN) for j in range(4)]
        s = jnp.concatenate([mul(k_ref[0, rows[j], :], part(q, j), NT) for j in range(4)], axis=1)
        s = jnp.where(seen(), s, masked_value)
        p = jnp.exp(s - lse)
        dp = jnp.concatenate([mul(v_ref[0, rows[j], :], part(g, j), NT) for j in range(4)], axis=1)
        ds = (p * (dp - delta)).astype(BF)
        pb = p.astype(BF)
        dq = []
        for j in range(4):
            cols = slice(j * BLK, (j + 1) * BLK)
            dv_ref[rows[j], :] += mul(pb[:, cols], part(g, j))
            dk_ref[rows[j], :] += mul(ds[:, cols], part(q, j))
            dq.append(mul(kt_ref[0, :, rows[j]], ds[:, cols]))
        dq_ref[0] += jnp.concatenate(dq, axis=1).T * HDIM ** (-0.5)

    @pl.when(block == pl.num_programs(1) - 1)
    def _():
        dk_out[0] = dk_ref[...].astype(BF)
        dv_out[0] = dv_ref[...].astype(BF)


def attention_backward(tiles, lengths, queries, grads, log_total, row_delta, keys, values, keys_t, group):
    rows = queries.shape[1]
    count = rows // QB
    span = keys.shape[1]
    first = group * GROUP
    row = pl.BlockSpec((1, QB, HDIM), lambda h, i, a, b: (h + first, i, 0))
    stat = pl.BlockSpec((1, NH, QB), lambda h, i, a, b: (i, 0, 0))
    full = pl.BlockSpec((1, span, HDIM), lambda h, i, a, b: (h + first, 0, 0))
    out = pl.BlockSpec((1, span, HDIM), lambda h, i, a, b: (h, 0, 0))
    return pl.pallas_call(
        functools.partial(backward_kernel, first=first),
        out_shape=[
            jax.ShapeDtypeStruct((GROUP, rows, HDIM), F32),
            jax.ShapeDtypeStruct((GROUP, span, HDIM), BF),
            jax.ShapeDtypeStruct((GROUP, span, HDIM), BF),
        ],
        grid_spec=pltpu.PrefetchScalarGridSpec(
            num_scalar_prefetch=2,
            grid=(GROUP, count),
            in_specs=[
                row,
                row,
                stat,
                stat,
                full,
                full,
                pl.BlockSpec((1, HDIM, span), lambda h, i, a, b: (h + first, 0, 0)),
            ],
            out_specs=[pl.BlockSpec((1, QB, HDIM), lambda h, i, a, b: (h, i, 0)), out, out],
            scratch_shapes=[pltpu.VMEM((span, HDIM), F32)] * 2,
        ),
        compiler_params=room(),
        cost_estimate=cost(rows * GPART * PLEN * 40, 32 * span * GPART),
        name="attention_backward",
    )(tiles, lengths, queries, grads, log_total, row_delta, keys, values, keys_t)


def restore_kernel(tiles_ref, *refs):
    mine_ref, theirs_ref = refs[8:]

    def write(out_ref):
        for j in range(4):
            rows = slice(j * BLK, (j + 1) * BLK)
            for h in range(GROUP):
                cols = slice(h * HDIM, (h + 1) * HDIM)
                out_ref[rows, cols] = refs[4 + j][h]
                out_ref[rows, GPART + h * HDIM : GPART + (h + 1) * HDIM] = refs[j][h]

    @pl.when(pl.program_id(0) < 8)
    def _():
        write(theirs_ref)

    @pl.when(pl.program_id(0) >= 8)
    def _():
        write(mine_ref)


def restore_keys(tiles, grad_k, grad_v):
    spec = lambda j: pl.BlockSpec((GROUP, BLK, HDIM), lambda i, o: (0, o[i * 4 + j], 0))
    shape = (4 * BLK, 2 * GPART)
    return pl.pallas_call(
        restore_kernel,
        out_shape=[jax.ShapeDtypeStruct((32 * BLK, 2 * GPART), BF)] * 2,
        grid_spec=pltpu.PrefetchScalarGridSpec(
            num_scalar_prefetch=1,
            grid=(16,),
            in_specs=[spec(j) for j in range(4)] * 2,
            out_specs=[
                pl.BlockSpec(shape, lambda i, o: (jnp.maximum(i - 8, 0), 0)),
                pl.BlockSpec(shape, lambda i, o: (jnp.minimum(i, 7), 0)),
            ],
        ),
        compiler_params=room(),
        cost_estimate=cost(0, 64 * 64 * BLK * GPART),
        name="restore_keys",
    )(tiles, *([grad_k] * 4), *([grad_v] * 4))


def unturn_kernel(dq_ref, mine_ref, theirs_ref, cos_ref, sin_ref, g_ref, y_sc):
    kv = mine_ref[...].astype(F32) + theirs_ref[...].astype(F32)
    for h in range(GROUP):
        y_sc[:, h * HDIM : (h + 1) * HDIM] = dq_ref[h]
    y_sc[:, GPART:] = kv[:, GPART:]
    cosine, sine_vals = cos_ref[...], -sin_ref[...]
    for k in range(GROUP):
        cols = slice(k * 128, (k + 1) * 128)
        g_ref[:, cols] = swing(y_sc[:, cols], cosine, sine_vals).astype(BF)
    g_ref[:, 2 * GPART :] = kv[:, :GPART].astype(BF)


def unturn(grad_q, mine, theirs, cosine, sine_vals):
    rows = mine.shape[0]
    size = 2 * QB
    row = lambda n: pl.BlockSpec((size, n), lambda i: (i, 0))
    return pl.pallas_call(
        unturn_kernel,
        out_shape=jax.ShapeDtypeStruct((rows, 3 * GPART), BF),
        grid=(rows // size,),
        in_specs=[
            pl.BlockSpec((GROUP, size, HDIM), lambda i: (0, i, 0)),
            row(2 * GPART),
            row(2 * GPART),
            row(128),
            row(128),
        ],
        out_specs=row(3 * GPART),
        scratch_shapes=[pltpu.VMEM((size, 2 * GPART), F32)],
        compiler_params=room(),
        cost_estimate=cost(0, 20 * rows * GPART),
        name="unturn",
    )(grad_q, mine, theirs, cosine, sine_vals)


def unproject_kernel(a_ref, b_ref, c_ref, w_ref, x_ref, w_sc, y_sc):
    thin = w_sc.shape[0] // 32

    @pl.when(pl.program_id(0) == 0)
    def _():
        straighten(w_ref, w_sc, thin)

    for g, ref in enumerate((a_ref, b_ref, c_ref)):
        for k in range(3):
            y_sc[:, k * PART + g * GPART : k * PART + (g + 1) * GPART] = ref[
                :, k * GPART : (k + 1) * GPART
            ]
    x_ref[...] = mul(y_sc[...], w_sc[...], NT).astype(BF)


def unproject(parts, w_all, chunk):
    rows = parts[0].shape[0] // 2
    shift = chunk * (rows // QB)
    full = w_all.shape
    width = full[0] * full[1] * (full[2] - 8)
    return pl.pallas_call(
        unproject_kernel,
        out_shape=jax.ShapeDtypeStruct((rows, width), BF),
        grid=(rows // QB,),
        in_specs=[pl.BlockSpec((QB, 3 * GPART), lambda i: (i + shift, 0))] * 3
        + [pl.BlockSpec(full, lambda i: (0, 0, 0, 0), pipeline_mode=pl.Buffered(1))],
        out_specs=pl.BlockSpec((QB, width), lambda i: (i, 0)),
        scratch_shapes=[
            pltpu.VMEM((width, full[3]), BF),
            pltpu.VMEM((QB, 3 * PART), BF),
        ],
        compiler_params=room(),
        cost_estimate=cost(2 * rows * width * 3 * PART, 4 * rows * width),
        name="unproject",
    )(*parts, w_all)


def split_tiles(rows):
    blocks = rows.reshape(4, 2, rows.shape[0] // 8, rows.shape[1])
    return blocks[:, 0], blocks[:, 1]


def join_tiles(chunks):
    blocks = jnp.stack(chunks, axis=1)
    return blocks.reshape(-1, blocks.shape[-1])


def over(name, blocks):
    return lax.all_to_all(blocks, name, 0, 0, tiled=True)


def quarters(rows):
    return rows.reshape(4, rows.shape[0] // 4, rows.shape[1])


def after(value, *earlier):
    return lax.optimization_barrier((value, earlier))[0]


def flip(values, mask):
    return lax.ppermute(values, "p", [(k, k ^ mask) for k in range(4)])


def gather_near(own):
    return [own, flip(own, 1), flip(own, 2)]


def gather_far(near):
    half = near[0].shape[0] // 2
    return near + [flip(near[2][:half], 1), flip(near[1][half:], 2)]


def slots(terms):
    size = terms.shape[0] // 4
    return [terms[k * size : (k + 1) * size] for k in range(4)]


def scatter_far(terms):
    far = slots(terms)[3]
    half = far.shape[0] // 2
    return flip(far[:half], 1), flip(far[half:], 2)


def scatter_near(terms, far):
    _, first, second, _ = slots(terms)
    half = first.shape[0] // 2
    add = lambda x, y: (x.astype(F32) + y.astype(F32)).astype(BF)
    first = flip(jnp.concatenate([first[:half], add(first[half:], far[1])], axis=0), 1)
    second = flip(jnp.concatenate([add(second[:half], far[0]), second[half:]], axis=0), 2)
    return first, second


def scatter_sum(terms, near):
    return slots(terms)[0].astype(F32) + near[0].astype(F32) + near[1].astype(F32)


def scatter_far_both(terms):
    return flip(slots(terms[0])[3], 1), flip(slots(terms[1])[3], 2)


def scatter_near_both(terms, far):
    early, late = slots(terms[0]), slots(terms[1])
    add = lambda x, y: (x.astype(F32) + y.astype(F32)).astype(BF)
    first = flip(jnp.concatenate([early[1], add(late[1], far[1])], axis=0), 1)
    second = flip(jnp.concatenate([add(early[2], far[0]), late[2]], axis=0), 2)
    return first, second


def meet(*values):
    return lax.optimization_barrier(values)


def swap_blocks(name, pieces):
    return [pieces[0]] + [
        lax.ppermute(pieces[r], name, [(k, k ^ r) for k in range(4)]) for r in (1, 2, 3)
    ]


def pick(pieces, first):
    stacked = jnp.stack(pieces)
    return [
        lax.dynamic_index_in_dim(stacked, jnp.bitwise_xor(first, r), 0, keepdims=False)
        for r in range(4)
    ]


def hidden_cuts(hidden):
    steps = hidden // 8
    sizes = [8 * (steps // 4 + (k < steps % 4)) for k in range(4)]
    starts = [sum(sizes[:k]) for k in range(4)]
    return starts, sizes, max(sizes)


def inner(
    tokens_in,
    cotangent,
    w_query,
    w_key,
    w_value,
    w_output,
    w_gate,
    w_up,
    w_down,
    attn_gain,
    ffn_gain,
    cont_len,
    deal_order,
    clip_threshold,
):
    plane, depth, core = (lax.axis_index(name) for name in ("p", "z", "c"))
    line = ("z", "c")
    width = tokens_in.shape[1]
    thin = w_query.shape[0]
    hidden = w_down.shape[0]
    starts, sizes, share = hidden_cuts(hidden)
    gain_f = attn_gain.astype(F32)
    parts_of = lambda v: [v[k] for k in range(4)]
    cross = lambda v: swap_blocks("p", pick(v, plane))
    cross_whole = lambda v: jnp.stack(pick(cross(parts_of(v)), plane))
    hop_on = lambda v: swap_blocks("z", pick(v, jnp.bitwise_xor(plane, depth)))
    hop_back = lambda v: swap_blocks("z", parts_of(quarters(v)))
    hop_out = lambda v: pick(
        swap_blocks("p", pick(v, jnp.bitwise_xor(plane, depth))), plane
    )
    first_hop = cross(parts_of(quarters(tokens_in)))
    turn_over = [(g * 4 + k, k * 4 + g) for g in range(4) for k in range(4)]
    deal = lax.ppermute(deal_order[0], ("p", "z"), turn_over)
    lengths = lax.ppermute(cont_len[0], ("p", "z"), turn_over)

    scaled = [(w.astype(F32) * gain_f[:, None]).astype(BF) for w in (w_query, w_key, w_value)]
    blocks = jnp.stack(scaled).reshape(3, thin, 4, PART).transpose(2, 1, 0, 3)
    blocks = blocks.reshape(4, thin, 3 * PART)
    extra = jnp.zeros((4, 8, 3 * PART), BF).at[:, 0, :thin].set(ffn_gain[None, :])
    send = jnp.concatenate([blocks, extra], axis=1)
    first_hop, send = meet(first_hop, send)
    early = after((w_gate, w_up, w_down), first_hop)
    stacked = jnp.stack([early[0].T, early[1].T, early[2]])
    stacked = jnp.stack(
        [
            jnp.pad(stacked[:, a : a + n], ((0, 0), (0, share - n), (0, 0)))
            for a, n in zip(starts, sizes)
        ]
    )
    send, moved = meet(cross_whole(send), hop_on(first_hop))
    stacked = cross_whole(stacked)
    w_qkv = lax.all_gather(send, line, axis=0)
    gain_two = w_qkv[:, :, thin, :thin].transpose(1, 0, 2).reshape(width).astype(F32)
    w_out = lax.all_gather(w_output, line, axis=0, tiled=True)
    piece = jnp.arange(2)[:, None, None]
    slot = jnp.arange(4)[None, :, None]
    source = jnp.bitwise_xor(depth, jnp.arange(4))[None, None, :]
    quarter = jnp.bitwise_xor(plane, slot)
    held = lambda which: deal[((source * 2 + which) * 8 + quarter * 2 + piece).reshape(-1)]
    tiles, tiles_far = held(core), held(1 - core)
    both = jnp.concatenate([tiles, tiles_far])
    numbers = jnp.arange(64, dtype=jnp.int32)
    order = jnp.sum(
        jnp.where(both[None, :] == numbers[:, None], numbers[None, :], 0), axis=1
    ).astype(jnp.int32)
    logical = (tiles[:, None] * BLK + jnp.arange(BLK, dtype=jnp.int32)[None, :]).reshape(-1)
    position = jnp.where(logical < PLEN, logical, PLEN + (logical - PLEN) % CLEN)
    cosine, sine_vals = (v[:, 0, :] for v in rope_angles(position))
    cosine = jnp.concatenate([cosine] * 4, axis=1)
    sine_vals = jnp.concatenate([-sine_vals, sine_vals] * 2, axis=1)

    joined = lambda pieces: jnp.concatenate(pieces, axis=0)
    by_chunk = lambda v: [h.reshape(-1, width) for h in split_tiles(joined(v))]
    residual = [v.astype(F32) for v in by_chunk(moved)]
    inverse_of = lambda v: lax.rsqrt(jnp.mean(v * v, axis=-1, keepdims=True) + norm_eps)
    inverse_one = [inverse_of(v) for v in residual]
    pieces = gather_near(joined([(v * r).astype(BF) for v, r in zip(residual, inverse_one)]))
    pieces = gather_far(pieces)

    def in_chunks(pieces):
        size = pieces[0].shape[0] // 2
        return [
            joined([v[k * size : (k + 1) * size] for v in pieces[:3]] + [pieces[3 + k]])
            for k in range(2)
        ]

    pieces, w_qkv, grad_out = meet(pieces, w_qkv, cotangent)
    (queries, mine), grad_out = meet(
        project(pieces, w_qkv, cosine, sine_vals),
        cross(parts_of(quarters(grad_out))),
    )
    normed = joined(in_chunks(pieces))
    theirs = lax.ppermute(mine, "c", [(0, 1), (1, 0)])
    sorted_kv, grad_out, stacked = meet(
        sort_keys(order, mine, theirs), hop_on(grad_out), stacked
    )
    keys, values, keys_t, values_t = sorted_kv
    stacked = stacked.transpose(1, 2, 0, 3).reshape(3, share, width)
    w_ffn = [lax.all_gather(stacked[k], line, axis=0, tiled=True) for k in range(3)]
    attend = lambda q, k, n: attention_forward(tiles, lengths, q, keys, values_t, k, n)
    grad_out = by_chunk(grad_out)
    grad_rows = joined([(branch_scale * v.astype(F32)).astype(BF) for v in grad_out])
    queries, grad_rows = meet(queries, grad_rows)
    (low_a, total_a, peak_a), grad_rows = meet(attend(queries, 0, 4), gather_near(grad_rows))
    branch_a = mul(low_a, w_out).astype(BF)
    branch_a, grad_rows, queries_b = meet(branch_a, grad_rows, queries)
    part_b, far_a = meet(attend(queries_b, 4, 2), scatter_far(branch_a))
    rest_b, near_a, grad_rows = meet(
        attend(queries_b, 6, 2), scatter_near(branch_a, far_a), gather_far(grad_rows)
    )
    low_b, total_b, peak_b = (joined([v, w]) for v, w in zip(part_b, rest_b))
    branch_b = mul(low_b, w_out).astype(BF)
    attended = joined([low_a, low_b])
    log_total = joined([total_a, total_b])
    peaks = joined([peak_a, peak_b])
    grad_rows = in_chunks(grad_rows)

    def second_norm(k, branch):
        after_attn = residual[k] + branch_scale * branch
        inverse_two = inverse_of(after_attn)
        return after_attn, inverse_two, (after_attn * inverse_two * gain_two).astype(BF)

    def hidden_layer(grad_mixed, normed_two):
        gate_pre = mul(normed_two, w_ffn[0], NT)
        up_pre = mul(normed_two, w_ffn[1], NT)
        mixed = (jax.nn.silu(gate_pre) * up_pre).astype(BF)
        return (mixed,) + gate_grads(grad_mixed, gate_pre, up_pre)

    def hidden_back(hidden):
        return (mul(hidden[1], w_ffn[0]) + mul(hidden[2], w_ffn[1])).astype(BF)

    def second_back(k, total, state):
        grad_gain, grad_second = norm_backward(total, state[0], state[1], gain_two)
        grad_resid = grad_out[k].astype(F32) + grad_second
        return grad_gain, grad_resid, (branch_scale * grad_resid).astype(BF)

    state_a = second_norm(0, scatter_sum(branch_a, near_a))
    own, rows_a, rows_b = meet(state_a[2], grad_rows[0], grad_rows[1])
    gather, mixed_a, rows_b, branch_b = meet(
        gather_near(own), mul(rows_a, w_ffn[2], NT), rows_b, branch_b
    )
    gather, far, mixed_b = meet(
        gather_far(gather), scatter_far(branch_b), mul(rows_b, w_ffn[2], NT)
    )
    normed_a = joined(gather)
    hidden_a, near = meet(hidden_layer(mixed_a, normed_a), scatter_near(branch_b, far))
    state_b = second_norm(1, scatter_sum(branch_b, near))
    hidden_a, own = meet(hidden_a, state_b[2])
    rest_a, gather = meet(hidden_back(hidden_a), gather_near(own))
    first = mul(hidden_a[1], normed_a, TN)
    gather, far, gate_a = meet(gather_far(gather), scatter_far(rest_a), first)
    normed_b = joined(gather)
    hidden_b, near = meet(hidden_layer(mixed_b, normed_b), scatter_near(rest_a, far))
    back_a = second_back(0, scatter_sum(rest_a, near), state_a)
    hidden_b, own = meet(hidden_b, back_a[2])
    rest_b, gather_a = meet(hidden_back(hidden_b), gather_near(own))
    grad_gate = (gate_a + mul(hidden_b[1], normed_b, TN)).astype(BF)
    up_a = mul(hidden_a[2], normed_a, TN)
    gather_a, far, grad_gate, up_a = meet(
        gather_far(gather_a), scatter_far(rest_b), grad_gate, up_a
    )
    grad_up = (up_a + mul(hidden_b[2], normed_b, TN)).astype(BF)
    down_a = mul(hidden_a[0], rows_a, TN)
    near, grad_up, down_a = meet(scatter_near(rest_b, far), grad_up, down_a)
    back_b = second_back(1, scatter_sum(rest_b, near), state_b)
    own, mixed_b_rows, down_a = meet(back_b[2], hidden_b[0], down_a)
    grad_down = (down_a + mul(mixed_b_rows, rows_b, TN)).astype(BF)
    gather_b, grad_down, ffn_b = meet(
        gather_near(own), grad_down, mul(mixed_b_rows, w_ffn[2]).astype(BF)
    )
    gather_b, ffn_a = meet(gather_far(gather_b), mul(hidden_a[0], w_ffn[2]).astype(BF))
    branch_ffn = [ffn_a, ffn_b]
    sum_rows = lambda v: lax.psum_scatter(v, line, scatter_dimension=0, tiled=True)
    grad_pieces = gather_a + gather_b
    grad_gain_two = back_a[0] + back_b[0]
    grad_resid = [back_a[1], back_b[1]]

    grad_pieces, branch_ffn, grad_gate = meet(grad_pieces, branch_ffn, sum_rows(grad_gate))
    (grad_heads, row_delta), far, grad_up = meet(
        attention_delta(grad_pieces, w_out, attended),
        scatter_far_both(branch_ffn),
        sum_rows(grad_up),
    )
    grad_w_part = mul(attended, joined(grad_pieces), TN).astype(BF)

    far_order = jnp.concatenate([tiles_far, tiles])
    gain_rows = grad_gain_two.astype(BF).reshape(4, 8, 1, thin).transpose(1, 0, 2, 3)
    gain_rows = jnp.pad(gain_rows, ((0, 0), (0, 0), (0, 7), (0, 3 * GPART - thin)))

    def back_group(g, grads):
        return attention_backward(
            tiles, lengths, queries, grads, log_total, row_delta, keys, values, keys_t, g
        )

    def restore(part):
        return (part[0],) + tuple(restore_keys(far_order, part[1], part[2]))

    def weight_part(grad_qkv):
        proj = mul(normed, grad_qkv, TN).astype(BF).reshape(4, 8, thin, 3 * GPART)
        proj = jnp.concatenate([proj.transpose(1, 0, 2, 3), gain_rows], axis=2)
        return proj.reshape(8 * 4 * (thin + 8), 3 * GPART)

    def sum_line(proj):
        proj = lax.psum_scatter(proj, line, scatter_dimension=0, tiled=True)
        return proj.reshape(4, thin + 8, 3 * GPART)

    maxima = jnp.where(
        jnp.arange(4)[:, None] == plane, jnp.max(peaks, axis=(0, 2))[None, :], masked_value
    ).reshape(HEADS)
    for name, mask, size in (("c", 1, 2), ("p", 1, 4), ("p", 2, 4), ("z", 1, 4), ("z", 2, 4)):
        pairs = [(k, k ^ mask) for k in range(size)]
        maxima = jnp.maximum(maxima, lax.ppermute(maxima, name, pairs))
    trade = lambda v: lax.ppermute(v, "c", [(0, 1), (1, 0)])
    grad_heads, grad_w_part = meet(grad_heads, grad_w_part)
    part_a, grad_heads, near, grad_down, grad_w_output = meet(
        back_group(0, grad_heads),
        grad_heads,
        scatter_near_both(branch_ffn, far),
        sum_rows(grad_down),
        sum_rows(grad_w_part),
    )
    part_a = restore(part_a)
    states = (state_a, state_b)
    output = []
    for k, (state, v) in enumerate(zip(states, branch_ffn)):
        size = state[0].shape[0]
        total = scatter_sum(v, [w[k * size : (k + 1) * size] for w in near])
        output.append(quarters((state[0] + branch_scale * total).astype(BF)))
    output = join_tiles(output)
    ffn_grads = jnp.stack([grad_gate, grad_up, grad_down])
    ffn_grads = ffn_grads.reshape(3, share, 4, PART).transpose(2, 0, 1, 3)
    output, grad_heads, part_a, ffn_grads = meet(output, grad_heads, part_a, ffn_grads)
    part_b, grad_heads, hops, far_a, maxima, ffn_grads = meet(
        back_group(1, grad_heads),
        grad_heads,
        hop_back(output),
        trade(part_a[2]),
        maxima,
        cross_whole(ffn_grads),
    )
    part_b = restore(part_b)
    grads_a = unturn(part_a[0], part_a[1], far_a, cosine, sine_vals)
    weights_a = weight_part(grads_a)
    grad_heads, weights_a, hops, part_b = meet(grad_heads, weights_a, hops, part_b)
    part_c, output, far_b, weights_a = meet(
        back_group(2, grad_heads),
        hop_out(hops),
        trade(part_b[2]),
        sum_line(weights_a),
    )
    part_c = restore(part_c)
    grads_b = unturn(part_b[0], part_b[1], far_b, cosine, sine_vals)
    weights_b, far_c = meet(weight_part(grads_b), trade(part_c[2]))
    output = joined(output)
    weights_b = sum_line(weights_b)
    grads_c = unturn(part_c[0], part_c[1], far_c, cosine, sine_vals)
    grads = (grads_a, grads_b, grads_c)
    rest_a, grads = meet(unproject(grads, w_qkv, 0), grads)
    rest_b, far_a, grads_c = meet(unproject(grads, w_qkv, 1), scatter_far(rest_a), grads[2])
    weights_c, near_a, far_b = meet(
        weight_part(grads_c), scatter_near(rest_a, far_a), scatter_far(rest_b)
    )
    weights_c = sum_line(weights_c)

    def first_back(k, total):
        grad_first = inverse_one[k] * total - residual[k] * inverse_one[k] ** 3 * jnp.mean(
            total * residual[k], axis=-1, keepdims=True
        )
        return (grad_resid[k] + grad_first).astype(BF)

    near_b = scatter_near(rest_b, far_b)
    hop_a, near_b = meet(hop_back(first_back(0, scatter_sum(rest_a, near_a))), near_b)
    hop_b, hop_a = meet(hop_back(first_back(1, scatter_sum(rest_b, near_b))), hop_out(hop_a))
    grad_input = join_tiles([jnp.stack(hop_a), jnp.stack(hop_out(hop_b))]).astype(F32)
    ffn_grads = ffn_grads.astype(F32)
    ffn_grads = jnp.concatenate([ffn_grads[k, :, :n] for k, n in enumerate(sizes)], axis=1)
    proj = over("p", jnp.concatenate([weights_a, weights_b, weights_c], axis=2)).astype(F32)
    grad_ffn_gain = jnp.sum(proj[:, thin, :thin], axis=0)
    proj = proj[:, :thin].reshape(4, thin, 3, 3, GPART).transpose(3, 1, 0, 2, 4)
    proj = proj.reshape(3, thin, width)
    grad_attn_gain = sum(
        jnp.sum(w.astype(F32) * proj[k], axis=1) for k, w in enumerate((w_query, w_key, w_value))
    )
    proj = proj * gain_f[None, :, None]

    limit_value = clip_threshold[0].astype(F32)
    clip_factor = jnp.sqrt(limit_value / jnp.maximum(maxima, limit_value))
    column_factor = jnp.repeat(clip_factor, HDIM)
    return (
        output,
        grad_input,
        proj[0],
        proj[1],
        proj[2],
        grad_w_output.astype(F32),
        ffn_grads[0].T,
        ffn_grads[1].T,
        ffn_grads[2],
        grad_attn_gain,
        grad_ffn_gain,
        maxima,
        clip_factor,
        w_query.astype(F32) * column_factor[None, :],
        w_key.astype(F32) * column_factor[None, :],
    )


def specs(grp, ctx):
    every = grp + ctx
    ins = [P(every, None)] * 6 + [P(grp, ctx), P(grp, ctx), P(ctx, grp), P(every), P(every)]
    ins += [P(grp, None), P(grp, None), P()]
    outs = [P(every, None)] * 6 + [P(grp, ctx), P(grp, ctx), P(ctx, grp), P(every), P(every)]
    outs += [P(), P(), P(every, None), P(every, None)]
    return tuple(ins), tuple(outs)


def solution(mesh):
    if mesh.shape["grp"] == 4 and mesh.shape["ctx"] == 8:
        mesh = Mesh(mesh.devices.reshape(4, 4, 2), ("p", "z", "c"))
        body, (in_specs, out_specs) = inner, specs(("p",), ("z", "c"))
    else:
        body, (in_specs, out_specs) = local, specs(("grp",), ("ctx",))
    return jax.shard_map(body, mesh=mesh, in_specs=in_specs, out_specs=out_specs, check_vma=False)
```

```python
import functools
import math

import jax
import jax.numpy as jnp
from jax import lax
from jax.experimental import pallas as pl
from jax.experimental.pallas import tpu as pltpu
from jax.sharding import Mesh
from jax.sharding import PartitionSpec as P

HEADS = 36
HDIM = 64
PLEN = 2048
CLEN = 256
NCONT = 8
BLK = 64
FAMTOK = 4096

F32 = jnp.float32
BF = jnp.bfloat16
NH = HEADS // 4
PART = NH * HDIM
GROUP = 3
GPART = GROUP * HDIM
QB_BACK = 512
QB = 256
KB = 1024
KB_FWD = 1024
HEAD_STEP = 9
NT = (((1,), (1,)), ((), ()))
NN = (((1,), (0,)), ((), ()))
TN = (((0,), (0,)), ((), ()))
VMEM_ROOM = 56 * 1024 * 1024


branch_scale = 1.4 / math.sqrt(40.0)
norm_eps = 1e-05
rope_base = 10000.0
masked_value = -1e30


def rope_angles(position):
    half_dim = HDIM // 2
    frequency = rope_base ** (-(jnp.arange(half_dim, dtype=jnp.float32) * (2.0 / HDIM)))
    angles = position.astype(jnp.float32)[:, None] * frequency[None, :]
    return (jnp.cos(angles)[:, None, :], jnp.sin(angles)[:, None, :])


def rotate(values, cosine, sine_vals, turn_sign):
    row_count = values.shape[0]
    shaped = values.reshape(row_count, HEADS, HDIM)
    leading = shaped[..., : HDIM // 2]
    trailing = shaped[..., HDIM // 2 :]
    turned = jnp.concatenate(
        [
            leading * cosine - turn_sign * trailing * sine_vals,
            trailing * cosine + turn_sign * leading * sine_vals,
        ],
        axis=-1,
    )
    return turned.reshape(row_count, HEADS * HDIM)


def token_facts(logical, lengths):
    family = logical // FAMTOK
    offset = logical % FAMTOK
    prompt = offset < PLEN
    member = jnp.clip((offset - PLEN) // CLEN, 0, NCONT - 1)
    inside = offset - PLEN - member * CLEN
    seq_id = jnp.where(prompt, -1, family * NCONT + member)
    numbers = jnp.arange(lengths.shape[0], dtype=jnp.int32)
    live_len = jnp.sum(jnp.where(seq_id[:, None] == numbers[None, :], lengths[None, :], 0), axis=1)
    is_live = prompt | (inside < live_len)
    position = jnp.where(prompt, offset, PLEN + inside)
    return (family, offset, prompt, seq_id, is_live, position)


def visible(query_facts, key_part):
    same_family = query_facts[0][:, None] == key_part[0][None, :]
    causal = key_part[1][None, :] <= query_facts[1][:, None]
    reaches = (
        key_part[2][None, :]
        | (key_part[3][None, :] == query_facts[3][:, None]) & key_part[4][None, :]
    )
    return same_family & causal & reaches


def key_slice(keys_heads, values_heads, key_facts, query_facts, first_row, span_rows):
    key_block = lax.dynamic_slice_in_dim(keys_heads, first_row, span_rows, 0)
    value_block = lax.dynamic_slice_in_dim(values_heads, first_row, span_rows, 0)
    key_part = tuple(
        (
            lax.dynamic_slice_in_dim(member_array, first_row, span_rows, 0)
            for member_array in key_facts
        )
    )
    return (key_block, value_block, visible(query_facts, key_part))


def block_scores(query_heads, key_block, visible_mask):
    scores = jnp.einsum(
        "qhd,khd->hqk", query_heads, key_block, preferred_element_type=jnp.float32
    ) * HDIM ** (-0.5)
    return jnp.where(visible_mask[None], scores, masked_value)


def score_grads(
    query_heads, grad_heads, log_total, row_delta, key_block, value_block, visible_mask
):
    scores = block_scores(query_heads, key_block, visible_mask)
    prob_table = jnp.where(visible_mask[None], jnp.exp(scores - log_total[:, :, None]), 0.0)
    grad_probs = jnp.einsum(
        "qhd,khd->hqk", grad_heads, value_block, preferred_element_type=jnp.float32
    )
    grad_scores = (prob_table * (grad_probs - row_delta[:, :, None])).astype(jnp.bfloat16)
    return (prob_table.astype(jnp.bfloat16), grad_scores)


def gate_grads(grad_mixed, gate_pre, up_pre):
    sigmoid = jax.nn.sigmoid(gate_pre)
    grad_gate = grad_mixed * up_pre * sigmoid * (1.0 + gate_pre * (1.0 - sigmoid))
    grad_up = grad_mixed * gate_pre * sigmoid
    return (grad_gate.astype(jnp.bfloat16), grad_up.astype(jnp.bfloat16))


def norm_backward(grad_normed, values, inverse, gain):
    scaled = grad_normed * gain[None, :]
    grad_gain = jnp.sum(grad_normed * values * inverse, axis=0)
    grad_values = inverse * scaled - values * inverse**3 * jnp.mean(
        scaled * values, axis=-1, keepdims=True
    )
    return (grad_gain, grad_values)


def attention_weights(w_query, w_key, w_value, w_output, attn_gain, ffn_gain):
    return (
        lax.all_gather(w_query, ("grp", "ctx"), axis=0, tiled=True),
        lax.all_gather(w_key, ("grp", "ctx"), axis=0, tiled=True),
        lax.all_gather(w_value, ("grp", "ctx"), axis=0, tiled=True),
        lax.all_gather(w_output, ("grp", "ctx"), axis=0, tiled=True),
        lax.all_gather(attn_gain, ("grp", "ctx"), axis=0, tiled=True),
        lax.all_gather(ffn_gain, ("grp", "ctx"), axis=0, tiled=True),
    )


def ffn_rows_gather(w_gate, w_up, w_down):
    return (
        lax.all_gather(w_gate, "grp", axis=0, tiled=True),
        lax.all_gather(w_up, "grp", axis=0, tiled=True),
        lax.all_gather(w_down, "grp", axis=1, tiled=True),
    )


def local(
    tokens_in,
    cotangent,
    w_query,
    w_key,
    w_value,
    w_output,
    w_gate,
    w_up,
    w_down,
    attn_gain,
    ffn_gain,
    cont_len,
    deal_order,
    clip_threshold,
):
    row_count = tokens_in.shape[0]
    model_width = tokens_in.shape[1]
    tile_count = deal_order.shape[1]
    group_rows = tile_count * BLK
    lengths = cont_len[0]
    my_index = lax.axis_index("ctx")
    tile_offsets = jnp.arange(BLK, dtype=jnp.int32)
    stored_logical = (deal_order[0][:, None] * BLK + tile_offsets[None, :]).reshape(group_rows)
    key_facts = token_facts(stored_logical, lengths)
    query_facts = tuple(
        (
            lax.dynamic_slice_in_dim(member_array, my_index * row_count, row_count, 0)
            for member_array in key_facts
        )
    )
    cosine, sine_vals = rope_angles(query_facts[5])
    key_step = math.gcd(group_rows, 512)
    key_blocks = group_rows // key_step
    full_query, full_key, full_value, full_output, gain_one, gain_two = attention_weights(
        w_query, w_key, w_value, w_output, attn_gain, ffn_gain
    )
    residual = tokens_in.astype(jnp.float32)
    inverse_one = lax.rsqrt(jnp.mean(residual * residual, axis=-1, keepdims=True) + norm_eps)
    gain_one_f = gain_one.astype(jnp.float32)
    gain_two_f = gain_two.astype(jnp.float32)
    normed_one = (residual * inverse_one * gain_one_f).astype(jnp.bfloat16)
    query_rot = rotate(
        jnp.dot(normed_one, full_query, preferred_element_type=jnp.float32), cosine, sine_vals, 1.0
    ).astype(jnp.bfloat16)
    key_rot = rotate(
        jnp.dot(normed_one, full_key, preferred_element_type=jnp.float32), cosine, sine_vals, 1.0
    ).astype(jnp.bfloat16)
    value_low = jnp.dot(normed_one, full_value, preferred_element_type=jnp.float32).astype(
        jnp.bfloat16
    )
    keys_all, values_all = (
        lax.all_gather(key_rot, "ctx", axis=0, tiled=True),
        lax.all_gather(value_low, "ctx", axis=0, tiled=True),
    )
    query_heads = query_rot.reshape(row_count, HEADS, HDIM)
    keys_heads = keys_all.reshape(group_rows, HEADS, HDIM)
    values_heads = values_all.reshape(group_rows, HEADS, HDIM)

    def stats_step(block_index, state_carry):
        key_block, value_block, visible_mask = key_slice(
            keys_heads, values_heads, key_facts, query_facts, block_index * key_step, key_step
        )

        def stats_busy(carry):
            run_max, run_sum, head_max = carry
            scores = block_scores(query_heads, key_block, visible_mask)
            block_max = jnp.max(scores, axis=2)
            new_max = jnp.maximum(run_max, block_max)
            exp_table = jnp.where(visible_mask[None], jnp.exp(scores - new_max[:, :, None]), 0.0)
            new_sum = run_sum * jnp.exp(run_max - new_max) + jnp.sum(exp_table, axis=2)
            return (new_max, new_sum, jnp.maximum(head_max, jnp.max(block_max, axis=1)))

        return lax.cond(jnp.any(visible_mask), stats_busy, lambda carry: carry, state_carry)

    start_state = (
        jnp.full((HEADS, row_count), masked_value, jnp.float32),
        jnp.zeros((HEADS, row_count), jnp.float32),
        jnp.full((HEADS,), masked_value, jnp.float32),
    )
    run_max, run_sum, head_max = lax.fori_loop(0, key_blocks, stats_step, start_state)
    log_total = run_max + jnp.log(run_sum)

    def output_step(block_index, running):
        key_block, value_block, visible_mask = key_slice(
            keys_heads, values_heads, key_facts, query_facts, block_index * key_step, key_step
        )

        def output_busy(total):
            scores = block_scores(query_heads, key_block, visible_mask)
            prob_low = jnp.where(
                visible_mask[None], jnp.exp(scores - log_total[:, :, None]), 0.0
            ).astype(jnp.bfloat16)
            return total + jnp.einsum(
                "hqk,khd->qhd", prob_low, value_block, preferred_element_type=jnp.float32
            )

        return lax.cond(jnp.any(visible_mask), output_busy, lambda total: total, running)

    attended = lax.fori_loop(
        0, key_blocks, output_step, jnp.zeros((row_count, HEADS, HDIM), jnp.float32)
    )
    attn_low = attended.reshape(row_count, model_width).astype(jnp.bfloat16)
    after_attn = residual + branch_scale * jnp.dot(
        attn_low, full_output, preferred_element_type=jnp.float32
    )
    inverse_two = lax.rsqrt(jnp.mean(after_attn * after_attn, axis=-1, keepdims=True) + norm_eps)
    normed_two = (after_attn * inverse_two * gain_two_f).astype(jnp.bfloat16)
    gate_cols, up_cols, down_cols = ffn_rows_gather(w_gate, w_up, w_down)
    normed_rows = lax.all_gather(normed_two, "ctx", axis=0, tiled=True)
    gate_pre = jnp.dot(normed_rows, gate_cols, preferred_element_type=jnp.float32)
    up_pre = jnp.dot(normed_rows, up_cols, preferred_element_type=jnp.float32)
    mixed = (jax.nn.silu(gate_pre) * up_pre).astype(jnp.bfloat16)
    branch_ffn = lax.psum_scatter(
        jnp.dot(mixed, down_cols, preferred_element_type=jnp.float32).astype(jnp.bfloat16),
        "ctx",
        scatter_dimension=0,
        tiled=True,
    ).astype(jnp.float32)
    output = (after_attn + branch_scale * branch_ffn).astype(jnp.bfloat16)
    grad_out = cotangent.astype(jnp.float32)
    grad_branch = (branch_scale * grad_out).astype(jnp.bfloat16)
    gate_again, up_again, down_again = ffn_rows_gather(w_gate, w_up, w_down)
    grad_rows = lax.all_gather(grad_branch, "ctx", axis=0, tiled=True)
    grad_mixed = jnp.dot(grad_rows, down_again.T, preferred_element_type=jnp.float32)
    grad_down = jnp.dot(mixed.T, grad_rows, preferred_element_type=jnp.float32)
    grad_gate_low, grad_up_low = gate_grads(grad_mixed, gate_pre, up_pre)
    grad_gate = jnp.dot(normed_rows.T, grad_gate_low, preferred_element_type=jnp.float32)
    grad_up = jnp.dot(normed_rows.T, grad_up_low, preferred_element_type=jnp.float32)
    grad_normed_two = lax.psum_scatter(
        (
            jnp.dot(grad_gate_low, gate_again.T, preferred_element_type=jnp.float32)
            + jnp.dot(grad_up_low, up_again.T, preferred_element_type=jnp.float32)
        ).astype(jnp.bfloat16),
        "ctx",
        scatter_dimension=0,
        tiled=True,
    ).astype(jnp.float32)
    ffn_stack = jnp.stack([grad_gate, grad_up, grad_down.T], axis=0)
    ffn_summed = lax.psum_scatter(
        ffn_stack.astype(jnp.bfloat16), "grp", scatter_dimension=1, tiled=True
    ).astype(jnp.float32)
    grad_gain_two, grad_second = norm_backward(grad_normed_two, after_attn, inverse_two, gain_two_f)
    grad_resid = grad_out + grad_second
    back_query, back_key, back_value, back_output, back_gain_one, back_gain_two = attention_weights(
        w_query, w_key, w_value, w_output, attn_gain, ffn_gain
    )
    grad_branch_attn = (branch_scale * grad_resid).astype(jnp.bfloat16)
    grad_w_output = jnp.dot(attn_low.T, grad_branch_attn, preferred_element_type=jnp.float32)
    grad_attn = jnp.dot(grad_branch_attn, back_output.T, preferred_element_type=jnp.float32).astype(
        jnp.bfloat16
    )
    grad_heads = grad_attn.reshape(row_count, HEADS, HDIM)
    row_delta = jnp.sum(grad_heads.astype(jnp.float32) * attended, axis=2).T

    def back_step(grad_q, block_index):
        key_block, value_block, visible_mask = key_slice(
            keys_heads, values_heads, key_facts, query_facts, block_index * key_step, key_step
        )

        def back_busy(current):
            prob_low, grad_scores = score_grads(
                query_heads, grad_heads, log_total, row_delta, key_block, value_block, visible_mask
            )
            updated = current + jnp.einsum(
                "hqk,khd->qhd", grad_scores, key_block, preferred_element_type=jnp.float32
            )
            grad_keys = jnp.einsum(
                "hqk,qhd->khd", grad_scores, query_heads, preferred_element_type=jnp.float32
            ) * HDIM ** (-0.5)
            grad_values = jnp.einsum(
                "hqk,qhd->khd", prob_low, grad_heads, preferred_element_type=jnp.float32
            )
            return (
                updated,
                (
                    grad_keys.reshape(key_step, model_width),
                    grad_values.reshape(key_step, model_width),
                ),
            )

        def quiet(current):
            empty = jnp.zeros((key_step, model_width), jnp.float32)
            return (current, (empty, empty))

        return lax.cond(jnp.any(visible_mask), back_busy, quiet, grad_q)

    grad_q_heads, key_terms = lax.scan(
        back_step,
        jnp.zeros((row_count, HEADS, HDIM), jnp.float32),
        jnp.arange(key_blocks, dtype=jnp.int32),
    )
    key_sum, value_sum = (
        lax.psum_scatter(
            key_terms[0].reshape(group_rows, model_width).astype(jnp.bfloat16),
            "ctx",
            scatter_dimension=0,
            tiled=True,
        ).astype(jnp.float32),
        lax.psum_scatter(
            key_terms[1].reshape(group_rows, model_width).astype(jnp.bfloat16),
            "ctx",
            scatter_dimension=0,
            tiled=True,
        ).astype(jnp.float32),
    )
    grad_query_rot = grad_q_heads.reshape(row_count, model_width) * HDIM ** (-0.5)
    grad_query = rotate(grad_query_rot, cosine, sine_vals, -1.0).astype(jnp.bfloat16)
    grad_key = rotate(key_sum, cosine, sine_vals, -1.0).astype(jnp.bfloat16)
    grad_value = value_sum.astype(jnp.bfloat16)
    grad_w_query = jnp.dot(normed_one.T, grad_query, preferred_element_type=jnp.float32)
    grad_w_key = jnp.dot(normed_one.T, grad_key, preferred_element_type=jnp.float32)
    grad_w_value = jnp.dot(normed_one.T, grad_value, preferred_element_type=jnp.float32)
    grad_normed_one = (
        jnp.dot(grad_query, back_query.T, preferred_element_type=jnp.float32)
        + jnp.dot(grad_key, back_key.T, preferred_element_type=jnp.float32)
        + jnp.dot(grad_value, back_value.T, preferred_element_type=jnp.float32)
    )
    grad_gain_one, grad_first = norm_backward(grad_normed_one, residual, inverse_one, gain_one_f)
    grad_input = grad_resid + grad_first
    gain_pair = jnp.stack([grad_gain_one, grad_gain_two], axis=1)
    summed = (
        lax.psum_scatter(grad_w_query, ("grp", "ctx"), scatter_dimension=0, tiled=True),
        lax.psum_scatter(grad_w_key, ("grp", "ctx"), scatter_dimension=0, tiled=True),
        lax.psum_scatter(grad_w_value, ("grp", "ctx"), scatter_dimension=0, tiled=True),
        lax.psum_scatter(grad_w_output, ("grp", "ctx"), scatter_dimension=0, tiled=True),
        lax.psum_scatter(gain_pair, ("grp", "ctx"), scatter_dimension=0, tiled=True),
    )
    maxima = lax.pmax(head_max, ("grp", "ctx"))
    limit_value = clip_threshold[0].astype(jnp.float32)
    clip_factor = jnp.sqrt(limit_value / jnp.maximum(maxima, limit_value))
    column_factor = jnp.repeat(clip_factor, HDIM)
    clipped_query = w_query.astype(jnp.float32) * column_factor[None, :]
    clipped_key = w_key.astype(jnp.float32) * column_factor[None, :]
    return (
        output,
        grad_input,
        summed[0],
        summed[1],
        summed[2],
        summed[3],
        ffn_summed[0],
        ffn_summed[1],
        ffn_summed[2].T,
        summed[4][:, 0],
        summed[4][:, 1],
        maxima,
        clip_factor,
        clipped_query,
        clipped_key,
    )


def mul(left, right, dims=NN):
    return lax.dot_general(left, right, dims, preferred_element_type=F32)


def room():
    return pltpu.CompilerParams(vmem_limit_bytes=VMEM_ROOM)


def cost(flops, sent):
    return pl.CostEstimate(flops=int(flops), bytes_accessed=int(sent), transcendentals=0)


def straighten(w_ref, w_sc, thin):
    for i in range(4):
        for k in range(8):
            w_sc[(i * 8 + k) * thin : (i * 8 + k + 1) * thin, :] = w_ref[k, i, :thin, :]


def swing(values, cosine, sine_vals):
    lane = lax.broadcasted_iota(jnp.int32, values.shape, 1)
    other = jnp.where(
        lane % HDIM < HDIM // 2,
        pltpu.roll(values, 2 * HDIM - HDIM // 2, 1),
        pltpu.roll(values, HDIM // 2, 1),
    )
    return values * cosine + other * sine_vals


def fetch_rows(pieces, x_sc):
    step = pl.program_id(0)
    half = QB // 2
    for k in range(8):
        chunk, slot = k // 4, k % 4

        @pl.when(step == k)
        def _():
            if len(pieces) == 5 and slot < 3:
                x_sc[...] = pieces[slot][chunk * QB : (chunk + 1) * QB, :]
            elif len(pieces) == 5:
                x_sc[...] = pieces[3 + chunk][...]
            elif slot < 3:
                x_sc[...] = pieces[chunk * 5 + slot][...]
            else:
                x_sc[:half] = pieces[chunk * 5 + 3][...]
                x_sc[half:] = pieces[chunk * 5 + 4][...]


def whole(shape):
    return pl.BlockSpec(shape, lambda i: (0,) * len(shape), pipeline_mode=pl.Buffered(1))


def project_kernel(*refs):
    w_ref, cos_ref, sin_ref, q_ref, kv_ref, w_sc, x_sc = refs[5:]
    thin = w_sc.shape[0] // 32
    fetch_rows(refs[:5], x_sc)

    @pl.when(pl.program_id(0) == 0)
    def _():
        straighten(w_ref, w_sc, thin)

    y = mul(x_sc[...], w_sc[...])
    cosine, sine_vals = cos_ref[...], sin_ref[...]
    for k in range(NH):
        piece = swing(y[:, k * 128 : (k + 1) * 128], cosine, sine_vals)
        for j in range(2):
            head = 2 * k + j
            if head < NH:
                q_ref[head] = (piece[:, j * HDIM : (j + 1) * HDIM] * 0.125).astype(BF)
        if 2 * k + 1 > NH:
            kv_ref[:, k * 128 : (k + 1) * 128] = piece.astype(BF)
        elif 2 * k + 1 == NH:
            kv_ref[:, k * 128 + HDIM : (k + 1) * 128] = piece[:, HDIM:].astype(BF)
    kv_ref[:, :PART] = y[:, 2 * PART :].astype(BF)


def project(normed, w_all, cosine, sine_vals):
    rows = sum(v.shape[0] for v in normed)
    width = normed[0].shape[1]
    full = w_all.shape
    return pl.pallas_call(
        project_kernel,
        out_shape=[
            jax.ShapeDtypeStruct((NH, rows, HDIM), BF),
            jax.ShapeDtypeStruct((rows, 2 * PART), BF),
        ],
        grid=(rows // QB,),
        in_specs=[whole(v.shape) for v in normed]
        + [
            whole(full),
            pl.BlockSpec((QB, 128), lambda i: (i, 0)),
            pl.BlockSpec((QB, 128), lambda i: (i, 0)),
        ],
        out_specs=[
            pl.BlockSpec((NH, QB, HDIM), lambda i: (0, i, 0)),
            pl.BlockSpec((QB, 2 * PART), lambda i: (i, 0)),
        ],
        scratch_shapes=[pltpu.VMEM((width, full[3]), BF), pltpu.VMEM((QB, width), BF)],
        compiler_params=room(),
        cost_estimate=cost(2 * rows * width * full[3], 2 * (rows * width + width * full[3] + rows * 5 * PART)),
        name="project",
    )(*normed, w_all, cosine, sine_vals)


def sort_kernel(order_ref, *refs):
    k_ref, v_ref, kt_ref, vt_ref = refs[16:]
    first = pl.program_id(0) * 8
    for j in range(8):
        from_mine = order_ref[first + j] < 32
        tile = jnp.where(from_mine, refs[j][0], refs[8 + j][0])
        rows = slice(j * BLK, (j + 1) * BLK)
        for h in range(NH):
            v_ref[h, rows, :] = tile[:, h * HDIM : (h + 1) * HDIM]
            k_ref[h, rows, :] = tile[:, PART + h * HDIM : PART + (h + 1) * HDIM]
    for h in range(NH):
        kt_ref[h] = k_ref[h].T
        vt_ref[h] = v_ref[h].T


def sort_keys(order, mine, theirs):
    count = order.shape[0]
    shape = (1, BLK, 2 * PART)
    near = lambda j: pl.BlockSpec(shape, lambda i, o: (jnp.minimum(o[i * 8 + j], 31), 0, 0))
    far = lambda j: pl.BlockSpec(shape, lambda i, o: (jnp.maximum(o[i * 8 + j] - 32, 0), 0, 0))
    return pl.pallas_call(
        sort_kernel,
        out_shape=[jax.ShapeDtypeStruct((NH, count * BLK, HDIM), BF)] * 2
        + [jax.ShapeDtypeStruct((NH, HDIM, count * BLK), BF)] * 2,
        grid_spec=pltpu.PrefetchScalarGridSpec(
            num_scalar_prefetch=1,
            grid=(count // 8,),
            in_specs=[near(j) for j in range(8)] + [far(j) for j in range(8)],
            out_specs=[pl.BlockSpec((NH, 8 * BLK, HDIM), lambda i, o: (0, i, 0))] * 2
            + [pl.BlockSpec((NH, HDIM, 8 * BLK), lambda i, o: (0, 0, i))] * 2,
        ),
        compiler_params=room(),
        cost_estimate=cost(0, 64 * count * BLK * PART),
        name="sort_keys",
    )(order, *([mine.reshape(32, BLK, 2 * PART)] * 8), *([theirs.reshape(32, BLK, 2 * PART)] * 8))


def lane_tile(vals):
    shape = (1, len(vals) * BLK)
    lane = lax.broadcasted_iota(jnp.int32, shape, 1)
    out = jnp.full(shape, vals[-1], jnp.int32)
    for j in range(len(vals) - 2, -1, -1):
        out = jnp.where(lane < (j + 1) * BLK, vals[j], out)
    return out, lane & (BLK - 1)


def block_facts(tiles_ref, len_ref, block, step, size):
    half_tiles = PLEN // BLK
    count = size // BLK
    t = [tiles_ref[block * count + j] for j in range(count)]
    tile, within = lane_tile(t)
    qpos = tile * BLK + within
    tmax = functools.reduce(jnp.maximum, t)
    tmin = functools.reduce(jnp.minimum, t)
    per = step // BLK
    is_cont = t[0] >= half_tiles
    n_all = jnp.where(is_cont, PLEN // step, tmax // per + 1)
    n_free = jnp.where(is_cont, PLEN // step, tmin // per)
    conts = [jnp.maximum(v - half_tiles, 0) // 4 for v in t]
    lens = lane_tile([len_ref[v] for v in conts])[0]
    qin = qpos - PLEN - lane_tile(conts)[0] * CLEN
    starts = [pl.multiple_of(PLEN + v * CLEN, CLEN) for v in conts]
    kin = lax.broadcasted_iota(jnp.int32, (CLEN, size), 0)
    seen = lambda: (kin <= qin) & (kin < lens)
    return qpos, is_cont, n_all, n_free, starts, seen


def forward_kernel(
    tiles_ref, len_ref, q_ref, k_ref, vt_sc, o_ref, lse_ref, mx_ref, ot_sc, shift
):
    block = pl.program_id(0) + shift
    qpos, is_cont, n_all, n_free, starts, seen = block_facts(
        tiles_ref, len_ref, block, KB_FWD, QB
    )

    def heads(group, carry):
        hs = [group * HEAD_STEP + j for j in range(HEAD_STEP)]
        qs = [q_ref[h] for h in hs]

        def update(scores, states, weigh):
            out = []
            for n, (s, (m, l, acc)) in enumerate(zip(scores, states)):
                mn = jnp.maximum(m, jnp.max(s, axis=0, keepdims=True))
                p = jnp.exp(s - mn)
                al = jnp.exp(m - mn)
                out.append(
                    (
                        mn,
                        l * al + jnp.sum(p, axis=0, keepdims=True),
                        acc * al + weigh(n, p.astype(BF)),
                    )
                )
            return tuple(out)

        def step(kb, states, masked):
            base = pl.multiple_of(kb * KB_FWD, KB_FWD)
            rows = pl.ds(base, KB_FWD)
            scores = [mul(k_ref[h, rows, :], q, NT) for h, q in zip(hs, qs)]
            if masked:
                kpos = base + lax.broadcasted_iota(jnp.int32, (KB_FWD, QB), 0)
                vis = kpos <= qpos
                scores = [jnp.where(vis, s, masked_value) for s in scores]
            return update(scores, states, lambda n, p: mul(vt_sc[hs[n], :, rows], p))

        states = tuple(
            (
                jnp.full((1, QB), masked_value, F32),
                jnp.zeros((1, QB), F32),
                jnp.zeros((HDIM, QB), F32),
            )
            for _ in hs
        )
        states = lax.fori_loop(0, n_free, functools.partial(step, masked=False), states)
        states = lax.fori_loop(n_free, n_all, functools.partial(step, masked=True), states)

        def own(states):
            vis = seen()
            cols = lambda x, j: x[:, j * BLK : (j + 1) * BLK]
            scores = []
            for h, q in zip(hs, qs):
                s = [
                    mul(k_ref[h, pl.ds(starts[j], CLEN), :], q[j * BLK : (j + 1) * BLK], NT)
                    for j in range(4)
                ]
                scores.append(jnp.where(vis, jnp.concatenate(s, axis=1), masked_value))
            return update(
                scores,
                states,
                lambda n, p: jnp.concatenate(
                    [
                        mul(vt_sc[hs[n], :, pl.ds(starts[j], CLEN)], cols(p, j))
                        for j in range(4)
                    ],
                    axis=1,
                ),
            )

        states = lax.cond(is_cont, own, lambda s: s, states)
        for h, (m, l, acc) in zip(hs, states):
            ot_sc[h] = acc / l
            lse_ref[0, pl.ds(h, 1), :] = m + jnp.log(l)
            mx_ref[0, pl.ds(h, 1), :] = m
        return carry

    lax.fori_loop(0, NH // HEAD_STEP, heads, 0)
    for h in range(NH):
        o_ref[:, h * HDIM : (h + 1) * HDIM] = ot_sc[h].T.astype(BF)


def attention_forward(tiles, lengths, queries, keys, values_t, shift, count):
    rows = count * QB
    span = keys.shape[1]
    once = lambda *shape: pl.BlockSpec(
        shape, lambda i, a, b: (0, 0, 0), pipeline_mode=pl.Buffered(1)
    )
    stat = pl.BlockSpec((1, NH, QB), lambda i, a, b: (i, 0, 0))
    return pl.pallas_call(
        functools.partial(forward_kernel, shift=shift),
        out_shape=[
            jax.ShapeDtypeStruct((rows, PART), BF),
            jax.ShapeDtypeStruct((count, NH, QB), F32),
            jax.ShapeDtypeStruct((count, NH, QB), F32),
        ],
        grid_spec=pltpu.PrefetchScalarGridSpec(
            num_scalar_prefetch=2,
            grid=(count,),
            in_specs=[
                pl.BlockSpec((NH, QB, HDIM), lambda i, a, b: (0, i + shift, 0)),
                once(NH, span, HDIM),
                once(NH, HDIM, span),
            ],
            out_specs=[pl.BlockSpec((QB, PART), lambda i, a, b: (i, 0)), stat, stat],
            scratch_shapes=[pltpu.VMEM((NH, HDIM, QB), F32)],
        ),
        compiler_params=room(),
        cost_estimate=cost(rows * PART * PLEN * 20, 16 * span * PART),
        name="attention_forward",
    )(tiles, lengths, queries, keys, values_t)


def delta_kernel(*refs):
    w_ref, o_ref, gh_ref, delta_ref, gw_ref, x_sc = refs[10:]
    step = pl.program_id(0)
    rows = pl.ds(pl.multiple_of(step * QB, QB), QB)
    fetch_rows(refs[:10], x_sc.at[rows, :])
    grad = mul(x_sc[rows, :], w_ref[...], NT).astype(BF)
    for h in range(NH):
        gh_ref[h] = grad[:, h * HDIM : (h + 1) * HDIM]
    prod = grad.astype(F32) * o_ref[rows, :].astype(F32)
    high = prod.astype(BF)
    low = (prod - high.astype(F32)).astype(BF)
    row = lax.broadcasted_iota(jnp.int32, (16, PART), 0)
    col = lax.broadcasted_iota(jnp.int32, (16, PART), 1)
    pick_head = jnp.where(col // HDIM == row, 1.0, 0.0).astype(BF)
    total = mul(pick_head, high, NT) + mul(pick_head, low, NT)
    delta_ref[0] = total[:NH]

    @pl.when(step == pl.num_programs(0) - 1)
    def _():
        for k in range(3):
            cols = slice(k * 768, (k + 1) * 768)
            gw_ref[:, cols] = mul(o_ref[...], x_sc[:, cols], TN).astype(BF)


def attention_delta(grad_branch, w_out, attended):
    rows, width = attended.shape[0], w_out.shape[1]
    count = rows // QB
    return pl.pallas_call(
        delta_kernel,
        out_shape=[
            jax.ShapeDtypeStruct((NH, rows, HDIM), BF),
            jax.ShapeDtypeStruct((count, NH, QB), F32),
            jax.ShapeDtypeStruct((PART, width), BF),
        ],
        grid=(count,),
        in_specs=[whole(v.shape) for v in grad_branch]
        + [whole((PART, width)), whole((rows, PART))],
        out_specs=[
            pl.BlockSpec((NH, QB, HDIM), lambda i: (0, i, 0)),
            pl.BlockSpec((1, NH, QB), lambda i: (i, 0, 0)),
            pl.BlockSpec((PART, width), lambda i: (0, 0)),
        ],
        scratch_shapes=[pltpu.VMEM((rows, width), BF)],
        compiler_params=room(),
        cost_estimate=cost(2 * rows * width * PART, 2 * rows * width),
        name="attention_delta",
    )(*grad_branch, w_out, attended)


def backward_kernel(
    tiles_ref, len_ref, q_ref, g_ref, lse_ref, delta_ref, k_ref, v_ref, kt_ref, dq_ref, dk_out, dv_out,
    dk_ref, dv_ref, first
):
    h = pl.program_id(0) + first
    block = pl.program_id(1)

    @pl.when(block == 0)
    def _():
        dk_ref[...] = jnp.zeros_like(dk_ref)
        dv_ref[...] = jnp.zeros_like(dv_ref)

    qpos, is_cont, n_all, n_free, starts, seen = block_facts(
        tiles_ref, len_ref, block, KB, QB_BACK
    )
    q = q_ref[0]
    g = g_ref[0]
    stat = lambda ref: jnp.concatenate(
        [ref[j, pl.ds(h, 1), :] for j in range(QB_BACK // QB)], axis=1
    )
    lse = stat(lse_ref)
    delta = stat(delta_ref)

    def step(kb, dqt, masked):
        base = pl.multiple_of(kb * KB, KB)
        rows = pl.ds(base, KB)
        s = mul(k_ref[0, rows, :], q, NT)
        dp = mul(v_ref[0, rows, :], g, NT)
        if masked:
            kpos = base + lax.broadcasted_iota(jnp.int32, (KB, QB_BACK), 0)
            s = jnp.where(kpos <= qpos, s, masked_value)
        p = jnp.exp(s - lse)
        ds = (p * (dp - delta)).astype(BF)
        dv_ref[rows, :] += mul(p.astype(BF), g)
        dk_ref[rows, :] += mul(ds, q)
        return dqt + mul(kt_ref[0, :, rows], ds)

    dqt = jnp.zeros((HDIM, QB_BACK), F32)
    dqt = lax.fori_loop(0, n_free, functools.partial(step, masked=False), dqt)
    dqt = lax.fori_loop(n_free, n_all, functools.partial(step, masked=True), dqt)
    dq_ref[0] = dqt.T * HDIM ** (-0.5)

    @pl.when(is_cont)
    def _():
        part = lambda x, j: x[j * BLK : (j + 1) * BLK]
        rows = [pl.ds(starts[j], CLEN) for j in range(QB_BACK // BLK)]
        s = jnp.concatenate([mul(k_ref[0, rows[j], :], part(q, j), NT) for j in range(QB_BACK // BLK)], axis=1)
        s = jnp.where(seen(), s, masked_value)
        p = jnp.exp(s - lse)
        dp = jnp.concatenate([mul(v_ref[0, rows[j], :], part(g, j), NT) for j in range(QB_BACK // BLK)], axis=1)
        ds = (p * (dp - delta)).astype(BF)
        pb = p.astype(BF)
        dq = []
        for j in range(QB_BACK // BLK):
            cols = slice(j * BLK, (j + 1) * BLK)
            dv_ref[rows[j], :] += mul(pb[:, cols], part(g, j))
            dk_ref[rows[j], :] += mul(ds[:, cols], part(q, j))
            dq.append(mul(kt_ref[0, :, rows[j]], ds[:, cols]))
        dq_ref[0] += jnp.concatenate(dq, axis=1).T * HDIM ** (-0.5)

    @pl.when(block == pl.num_programs(1) - 1)
    def _():
        dk_out[0] = dk_ref[...].astype(BF)
        dv_out[0] = dv_ref[...].astype(BF)


def attention_backward(tiles, lengths, queries, grads, log_total, row_delta, keys, values, keys_t, group):
    rows = queries.shape[1]
    count = rows // QB_BACK
    span = keys.shape[1]
    first = group * GROUP
    row = pl.BlockSpec((1, QB_BACK, HDIM), lambda h, i, a, b: (h + first, i, 0))
    stat = pl.BlockSpec((QB_BACK // QB, NH, QB), lambda h, i, a, b: (i, 0, 0))
    full = pl.BlockSpec((1, span, HDIM), lambda h, i, a, b: (h + first, 0, 0))
    out = pl.BlockSpec((1, span, HDIM), lambda h, i, a, b: (h, 0, 0))
    return pl.pallas_call(
        functools.partial(backward_kernel, first=first),
        out_shape=[
            jax.ShapeDtypeStruct((GROUP, rows, HDIM), F32),
            jax.ShapeDtypeStruct((GROUP, span, HDIM), BF),
            jax.ShapeDtypeStruct((GROUP, span, HDIM), BF),
        ],
        grid_spec=pltpu.PrefetchScalarGridSpec(
            num_scalar_prefetch=2,
            grid=(GROUP, count),
            in_specs=[
                row,
                row,
                stat,
                stat,
                full,
                full,
                pl.BlockSpec((1, HDIM, span), lambda h, i, a, b: (h + first, 0, 0)),
            ],
            out_specs=[pl.BlockSpec((1, QB_BACK, HDIM), lambda h, i, a, b: (h, i, 0)), out, out],
            scratch_shapes=[pltpu.VMEM((span, HDIM), F32)] * 2,
        ),
        compiler_params=room(),
        cost_estimate=cost(rows * GPART * PLEN * 40, 32 * span * GPART),
        name="attention_backward",
    )(tiles, lengths, queries, grads, log_total, row_delta, keys, values, keys_t)


def restore_kernel(tiles_ref, *refs):
    mine_ref, theirs_ref = refs[16:]

    def write(out_ref):
        for j in range(8):
            rows = slice(j * BLK, (j + 1) * BLK)
            for h in range(GROUP):
                cols = slice(h * HDIM, (h + 1) * HDIM)
                out_ref[rows, cols] = refs[8 + j][h]
                out_ref[rows, GPART + h * HDIM : GPART + (h + 1) * HDIM] = refs[j][h]

    @pl.when(pl.program_id(0) < 4)
    def _():
        write(theirs_ref)

    @pl.when(pl.program_id(0) >= 4)
    def _():
        write(mine_ref)


def restore_keys(tiles, grad_k, grad_v):
    spec = lambda j: pl.BlockSpec((GROUP, BLK, HDIM), lambda i, o: (0, o[i * 8 + j], 0))
    shape = (8 * BLK, 2 * GPART)
    return pl.pallas_call(
        restore_kernel,
        out_shape=[jax.ShapeDtypeStruct((32 * BLK, 2 * GPART), BF)] * 2,
        grid_spec=pltpu.PrefetchScalarGridSpec(
            num_scalar_prefetch=1,
            grid=(8,),
            in_specs=[spec(j) for j in range(8)] * 2,
            out_specs=[
                pl.BlockSpec(shape, lambda i, o: (jnp.maximum(i - 4, 0), 0)),
                pl.BlockSpec(shape, lambda i, o: (jnp.minimum(i, 3), 0)),
            ],
        ),
        compiler_params=room(),
        cost_estimate=cost(0, 64 * 64 * BLK * GPART),
        name="restore_keys",
    )(tiles, *([grad_k] * 8), *([grad_v] * 8))


def unturn_kernel(dq_ref, mine_ref, theirs_ref, cos_ref, sin_ref, g_ref, y_sc):
    kv = mine_ref[...].astype(F32) + theirs_ref[...].astype(F32)
    for h in range(GROUP):
        y_sc[:, h * HDIM : (h + 1) * HDIM] = dq_ref[h]
    y_sc[:, GPART:] = kv[:, GPART:]
    cosine, sine_vals = cos_ref[...], -sin_ref[...]
    for k in range(GROUP):
        cols = slice(k * 128, (k + 1) * 128)
        g_ref[:, cols] = swing(y_sc[:, cols], cosine, sine_vals).astype(BF)
    g_ref[:, 2 * GPART :] = kv[:, :GPART].astype(BF)


def unturn(grad_q, mine, theirs, cosine, sine_vals):
    rows = mine.shape[0]
    size = QB
    row = lambda n: pl.BlockSpec((size, n), lambda i: (i, 0))
    return pl.pallas_call(
        unturn_kernel,
        out_shape=jax.ShapeDtypeStruct((rows, 3 * GPART), BF),
        grid=(rows // size,),
        in_specs=[
            pl.BlockSpec((GROUP, size, HDIM), lambda i: (0, i, 0)),
            row(2 * GPART),
            row(2 * GPART),
            row(128),
            row(128),
        ],
        out_specs=pl.BlockSpec((size, 3 * GPART), lambda i: (i % 4 * 2 + i // 4, 0)),
        scratch_shapes=[pltpu.VMEM((size, 2 * GPART), F32)],
        compiler_params=room(),
        cost_estimate=cost(0, 20 * rows * GPART),
        name="unturn",
    )(grad_q, mine, theirs, cosine, sine_vals)


def unproject_kernel(a_ref, b_ref, c_ref, w_ref, x_ref, w_sc, y_sc):
    thin = w_sc.shape[0] // 32

    @pl.when(pl.program_id(0) == 0)
    def _():
        straighten(w_ref, w_sc, thin)

    for g, ref in enumerate((a_ref, b_ref, c_ref)):
        for k in range(3):
            y_sc[:, k * PART + g * GPART : k * PART + (g + 1) * GPART] = ref[
                :, k * GPART : (k + 1) * GPART
            ]
    x_ref[...] = mul(y_sc[...], w_sc[...], NT).astype(BF)


def unproject(parts, w_all, chunk):
    rows = parts[0].shape[0] // 2
    full = w_all.shape
    width = full[0] * full[1] * (full[2] - 8)
    return pl.pallas_call(
        unproject_kernel,
        out_shape=jax.ShapeDtypeStruct((rows, width), BF),
        grid=(rows // QB,),
        in_specs=[pl.BlockSpec((QB, 3 * GPART), lambda i: (i * 2 + chunk, 0))] * 3
        + [pl.BlockSpec(full, lambda i: (0, 0, 0, 0), pipeline_mode=pl.Buffered(1))],
        out_specs=pl.BlockSpec((QB, width), lambda i: (i, 0)),
        scratch_shapes=[
            pltpu.VMEM((width, full[3]), BF),
            pltpu.VMEM((QB, 3 * PART), BF),
        ],
        compiler_params=room(),
        cost_estimate=cost(2 * rows * width * 3 * PART, 4 * rows * width),
        name="unproject",
    )(*parts, w_all)


def finish_kernel(a_ref, bc_ref, wq_ref, wk_ref, wv_ref, gain_ref, q_ref, k_ref, v_ref, sum_ref):
    thin = gain_ref.shape[0]
    gain = gain_ref[...]
    total = jnp.zeros((thin, 1), F32)
    for p in range(4):
        for g, (ref, first) in enumerate(((a_ref, 0), (bc_ref, 0), (bc_ref, PART))):
            cols = slice(p * PART + g * GPART, p * PART + (g + 1) * GPART)
            for n, (w, out) in enumerate(((wq_ref, q_ref), (wk_ref, k_ref), (wv_ref, v_ref))):
                part = slice(first + n * GPART, first + (n + 1) * GPART)
                grad = ref[p, :thin, part].astype(F32)
                out[:, cols] = grad * gain
                total += jnp.sum(grad * w[:, cols].astype(F32), axis=1, keepdims=True)
    sum_ref[...] = jnp.broadcast_to(total, sum_ref.shape)


def finish(parts, weights, gain):
    thin, width = weights[0].shape
    return pl.pallas_call(
        finish_kernel,
        out_shape=[jax.ShapeDtypeStruct((thin, width), F32)] * 3
        + [jax.ShapeDtypeStruct((thin, 128), F32)],
        compiler_params=room(),
        name="finish",
    )(*parts, *weights, gain)


def split_tiles(rows):
    blocks = rows.reshape(4, 2, rows.shape[0] // 8, rows.shape[1])
    return blocks[:, 0], blocks[:, 1]


def join_tiles(chunks):
    blocks = jnp.stack(chunks, axis=1)
    return blocks.reshape(-1, blocks.shape[-1])


def over(name, blocks):
    return lax.all_to_all(blocks, name, 0, 0, tiled=True)


def quarters(rows):
    return rows.reshape(4, rows.shape[0] // 4, rows.shape[1])


def after(value, *earlier):
    return lax.optimization_barrier((value, earlier))[0]


def flip(values, mask):
    return lax.ppermute(values, "p", [(k, k ^ mask) for k in range(4)])


def gather_near(own):
    return [own, flip(own, 1), flip(own, 2)]


def gather_far(near):
    half = near[0].shape[0] // 2
    return near + [flip(near[2][:half], 1), flip(near[1][half:], 2)]


def slots(terms):
    size = terms.shape[0] // 4
    return [terms[k * size : (k + 1) * size] for k in range(4)]


def scatter_far(terms):
    far = slots(terms)[3]
    half = far.shape[0] // 2
    return flip(far[:half], 1), flip(far[half:], 2)


def scatter_near(terms, far):
    _, first, second, _ = slots(terms)
    half = first.shape[0] // 2
    add = lambda x, y: (x.astype(F32) + y.astype(F32)).astype(BF)
    first = flip(jnp.concatenate([first[:half], add(first[half:], far[1])], axis=0), 1)
    second = flip(jnp.concatenate([add(second[:half], far[0]), second[half:]], axis=0), 2)
    return first, second


def scatter_sum(terms, near):
    return slots(terms)[0].astype(F32) + near[0].astype(F32) + near[1].astype(F32)


def scatter_far_both(terms):
    return flip(slots(terms[0])[3], 1), flip(slots(terms[1])[3], 2)


def scatter_near_both(terms, far):
    early, late = slots(terms[0]), slots(terms[1])
    add = lambda x, y: (x.astype(F32) + y.astype(F32)).astype(BF)
    first = flip(jnp.concatenate([early[1], add(late[1], far[1])], axis=0), 1)
    second = flip(jnp.concatenate([add(early[2], far[0]), late[2]], axis=0), 2)
    return first, second


def meet(*values):
    return lax.optimization_barrier(values)


def swap_blocks(name, pieces):
    return [pieces[0]] + [
        lax.ppermute(pieces[r], name, [(k, k ^ r) for k in range(4)]) for r in (1, 2, 3)
    ]


def pick(pieces, first):
    stacked = jnp.stack(pieces)
    return [
        lax.dynamic_index_in_dim(stacked, jnp.bitwise_xor(first, r), 0, keepdims=False)
        for r in range(4)
    ]


def hidden_cuts(hidden):
    steps = hidden // 8
    sizes = [8 * (steps // 4 + (k < steps % 4)) for k in range(4)]
    starts = [sum(sizes[:k]) for k in range(4)]
    return starts, sizes, max(sizes)


def inner(
    tokens_in,
    cotangent,
    w_query,
    w_key,
    w_value,
    w_output,
    w_gate,
    w_up,
    w_down,
    attn_gain,
    ffn_gain,
    cont_len,
    deal_order,
    clip_threshold,
):
    plane, depth, core = (lax.axis_index(name) for name in ("p", "z", "c"))
    line = ("z", "c")
    width = tokens_in.shape[1]
    thin = w_query.shape[0]
    hidden = w_down.shape[0]
    starts, sizes, share = hidden_cuts(hidden)
    gain_f = attn_gain.astype(F32)
    parts_of = lambda v: [v[k] for k in range(4)]
    cross = lambda v: swap_blocks("p", pick(v, plane))
    cross_whole = lambda v: jnp.stack(pick(cross(parts_of(v)), plane))
    hop_on = lambda v: swap_blocks("z", pick(v, jnp.bitwise_xor(plane, depth)))
    hop_back = lambda v: swap_blocks("z", parts_of(quarters(v)))
    hop_out = lambda v: pick(
        swap_blocks("p", pick(v, jnp.bitwise_xor(plane, depth))), plane
    )
    first_hop = cross(parts_of(quarters(tokens_in)))
    turn_over = [(g * 4 + k, k * 4 + g) for g in range(4) for k in range(4)]
    deal = lax.ppermute(deal_order[0], ("p", "z"), turn_over)
    lengths = lax.ppermute(cont_len[0], ("p", "z"), turn_over)

    scaled = [(w.astype(F32) * gain_f[:, None]).astype(BF) for w in (w_query, w_key, w_value)]
    blocks = jnp.stack(scaled).reshape(3, thin, 4, PART).transpose(2, 1, 0, 3)
    blocks = blocks.reshape(4, thin, 3 * PART)
    extra = jnp.zeros((4, 8, 3 * PART), BF).at[:, 0, :thin].set(ffn_gain[None, :])
    send = jnp.concatenate([blocks, extra], axis=1)
    first_hop, send = meet(first_hop, send)
    early = after((w_gate, w_up, w_down), first_hop)
    stacked = jnp.stack([early[0].T, early[1].T, early[2]])
    stacked = jnp.stack(
        [
            jnp.pad(stacked[:, a : a + n], ((0, 0), (0, share - n), (0, 0)))
            for a, n in zip(starts, sizes)
        ]
    )
    send, moved = meet(cross_whole(send), hop_on(first_hop))
    stacked = cross_whole(stacked)
    w_qkv = lax.all_gather(send, line, axis=0)
    gain_two = w_qkv[:, :, thin, :thin].transpose(1, 0, 2).reshape(width).astype(F32)
    w_out = lax.all_gather(w_output, line, axis=0, tiled=True)
    piece = jnp.arange(2)[:, None, None]
    slot = jnp.arange(4)[None, :, None]
    source = jnp.bitwise_xor(depth, jnp.arange(4))[None, None, :]
    quarter = jnp.bitwise_xor(plane, slot)
    held = lambda which: deal[((source * 2 + which) * 8 + quarter * 2 + piece).reshape(-1)]
    tiles, tiles_far = held(core), held(1 - core)
    both = jnp.concatenate([tiles, tiles_far])
    numbers = jnp.arange(64, dtype=jnp.int32)
    order = jnp.sum(
        jnp.where(both[None, :] == numbers[:, None], numbers[None, :], 0), axis=1
    ).astype(jnp.int32)
    logical = (tiles[:, None] * BLK + jnp.arange(BLK, dtype=jnp.int32)[None, :]).reshape(-1)
    position = jnp.where(logical < PLEN, logical, PLEN + (logical - PLEN) % CLEN)
    cosine, sine_vals = (v[:, 0, :] for v in rope_angles(position))
    cosine = jnp.concatenate([cosine] * 4, axis=1)
    sine_vals = jnp.concatenate([-sine_vals, sine_vals] * 2, axis=1)

    joined = lambda pieces: jnp.concatenate(pieces, axis=0)
    by_chunk = lambda v: [h.reshape(-1, width) for h in split_tiles(joined(v))]
    residual = [v.astype(F32) for v in by_chunk(moved)]
    inverse_of = lambda v: lax.rsqrt(jnp.mean(v * v, axis=-1, keepdims=True) + norm_eps)
    inverse_one = [inverse_of(v) for v in residual]
    pieces = gather_near(joined([(v * r).astype(BF) for v, r in zip(residual, inverse_one)]))
    pieces = gather_far(pieces)

    def in_chunks(pieces):
        size = pieces[0].shape[0] // 2
        return [
            joined([v[k * size : (k + 1) * size] for v in pieces[:3]] + [pieces[3 + k]])
            for k in range(2)
        ]

    pieces, w_qkv, grad_out = meet(pieces, w_qkv, cotangent)
    (queries, mine), grad_out = meet(
        project(pieces, w_qkv, cosine, sine_vals),
        cross(parts_of(quarters(grad_out))),
    )
    normed = joined(pieces)
    theirs = lax.ppermute(mine, "c", [(0, 1), (1, 0)])
    sorted_kv, grad_out, stacked = meet(
        sort_keys(order, mine, theirs), hop_on(grad_out), stacked
    )
    keys, values, keys_t, values_t = sorted_kv
    stacked = stacked.transpose(1, 2, 0, 3).reshape(3, share, width)
    w_ffn = [lax.all_gather(stacked[k], line, axis=0, tiled=True) for k in range(3)]
    attend = lambda q, k, n: attention_forward(tiles, lengths, q, keys, values_t, k, n)
    grad_out = by_chunk(grad_out)
    grad_rows = joined([(branch_scale * v.astype(F32)).astype(BF) for v in grad_out])
    queries, grad_rows = meet(queries, grad_rows)
    (low_a, total_a, peak_a), grad_rows = meet(attend(queries, 0, 4), gather_near(grad_rows))
    branch_a = mul(low_a, w_out).astype(BF)
    branch_a, grad_rows, queries_b = meet(branch_a, grad_rows, queries)
    part_b, far_a = meet(attend(queries_b, 4, 2), scatter_far(branch_a))
    rest_b, near_a, grad_rows = meet(
        attend(queries_b, 6, 2), scatter_near(branch_a, far_a), gather_far(grad_rows)
    )
    low_b, total_b, peak_b = (joined([v, w]) for v, w in zip(part_b, rest_b))
    branch_b = mul(low_b, w_out).astype(BF)
    attended = joined([low_a, low_b])
    log_total = joined([total_a, total_b])
    peaks = joined([peak_a, peak_b])
    grad_rows = in_chunks(grad_rows)

    def second_norm(k, branch):
        after_attn = residual[k] + branch_scale * branch
        inverse_two = inverse_of(after_attn)
        return after_attn, inverse_two, (after_attn * inverse_two * gain_two).astype(BF)

    def hidden_layer(grad_mixed, normed_two):
        gate_pre = mul(normed_two, w_ffn[0], NT)
        up_pre = mul(normed_two, w_ffn[1], NT)
        mixed = (jax.nn.silu(gate_pre) * up_pre).astype(BF)
        return (mixed,) + gate_grads(grad_mixed, gate_pre, up_pre)

    def hidden_back(hidden):
        return (mul(hidden[1], w_ffn[0]) + mul(hidden[2], w_ffn[1])).astype(BF)

    def second_back(k, total, state):
        grad_gain, grad_second = norm_backward(total, state[0], state[1], gain_two)
        grad_resid = grad_out[k].astype(F32) + grad_second
        return grad_gain, grad_resid, (branch_scale * grad_resid).astype(BF)

    state_a = second_norm(0, scatter_sum(branch_a, near_a))
    own, rows_a, rows_b = meet(state_a[2], grad_rows[0], grad_rows[1])
    gather, mixed_a, rows_b, branch_b = meet(
        gather_near(own), mul(rows_a, w_ffn[2], NT), rows_b, branch_b
    )
    gather, far, mixed_b = meet(
        gather_far(gather), scatter_far(branch_b), mul(rows_b, w_ffn[2], NT)
    )
    normed_a = joined(gather)
    hidden_a, near = meet(hidden_layer(mixed_a, normed_a), scatter_near(branch_b, far))
    state_b = second_norm(1, scatter_sum(branch_b, near))
    hidden_a, own = meet(hidden_a, state_b[2])
    rest_a, gather = meet(hidden_back(hidden_a), gather_near(own))
    first = mul(hidden_a[1], normed_a, TN)
    gather, far, gate_a = meet(gather_far(gather), scatter_far(rest_a), first)
    normed_b = joined(gather)
    hidden_b, near = meet(hidden_layer(mixed_b, normed_b), scatter_near(rest_a, far))
    back_a = second_back(0, scatter_sum(rest_a, near), state_a)
    hidden_b, own = meet(hidden_b, back_a[2])
    rest_b, gather_a = meet(hidden_back(hidden_b), gather_near(own))
    grad_gate = (gate_a + mul(hidden_b[1], normed_b, TN)).astype(BF)
    up_a = mul(hidden_a[2], normed_a, TN)
    gather_a, far, grad_gate, up_a = meet(
        gather_far(gather_a), scatter_far(rest_b), grad_gate, up_a
    )
    grad_up = (up_a + mul(hidden_b[2], normed_b, TN)).astype(BF)
    down_a = mul(hidden_a[0], rows_a, TN)
    near, grad_up, down_a = meet(scatter_near(rest_b, far), grad_up, down_a)
    back_b = second_back(1, scatter_sum(rest_b, near), state_b)
    own, mixed_b_rows, down_a = meet(back_b[2], hidden_b[0], down_a)
    grad_down = (down_a + mul(mixed_b_rows, rows_b, TN)).astype(BF)
    gather_b, grad_down, ffn_b = meet(
        gather_near(own), grad_down, mul(mixed_b_rows, w_ffn[2]).astype(BF)
    )
    gather_b, ffn_a = meet(gather_far(gather_b), mul(hidden_a[0], w_ffn[2]).astype(BF))
    branch_ffn = [ffn_a, ffn_b]
    sum_rows = lambda v: lax.psum_scatter(v, line, scatter_dimension=0, tiled=True)
    grad_pieces = gather_a + gather_b
    grad_gain_two = back_a[0] + back_b[0]
    grad_resid = [back_a[1], back_b[1]]

    grad_pieces, branch_ffn, grad_gate = meet(grad_pieces, branch_ffn, sum_rows(grad_gate))
    (grad_heads, row_delta, grad_w_part), far, grad_up = meet(
        attention_delta(grad_pieces, w_out, attended),
        scatter_far_both(branch_ffn),
        sum_rows(grad_up),
    )

    far_order = jnp.concatenate([tiles_far, tiles])
    gain_rows = grad_gain_two.astype(BF).reshape(4, 8, 1, thin).transpose(1, 0, 2, 3)
    gain_rows = jnp.pad(gain_rows, ((0, 0), (0, 0), (0, 7), (0, 3 * GPART - thin)))

    def back_group(g, grads):
        return attention_backward(
            tiles, lengths, queries, grads, log_total, row_delta, keys, values, keys_t, g
        )

    def restore(part):
        return (part[0],) + tuple(restore_keys(far_order, part[1], part[2]))

    def weight_part(grad_qkv):
        proj = mul(normed, grad_qkv, TN).astype(BF).reshape(4, 8, thin, 3 * GPART)
        proj = jnp.concatenate([proj.transpose(1, 0, 2, 3), gain_rows], axis=2)
        return proj.reshape(8 * 4 * (thin + 8), 3 * GPART)

    def sum_line(proj):
        proj = lax.psum_scatter(proj, line, scatter_dimension=0, tiled=True)
        return proj.reshape(4, thin + 8, 3 * GPART)

    maxima = jnp.where(
        jnp.arange(4)[:, None] == plane, jnp.max(peaks, axis=(0, 2))[None, :], masked_value
    ).reshape(HEADS)
    for name, mask, size in (("c", 1, 2), ("p", 1, 4), ("p", 2, 4), ("z", 1, 4), ("z", 2, 4)):
        pairs = [(k, k ^ mask) for k in range(size)]
        maxima = jnp.maximum(maxima, lax.ppermute(maxima, name, pairs))
    trade = lambda v: lax.ppermute(v, "c", [(0, 1), (1, 0)])
    grad_heads, grad_w_part = meet(grad_heads, grad_w_part)
    part_a, grad_heads, near, grad_down = meet(
        back_group(0, grad_heads),
        grad_heads,
        scatter_near_both(branch_ffn, far),
        sum_rows(grad_down),
    )
    grad_w_output = sum_rows(grad_w_part)
    part_a = restore(part_a)
    states = (state_a, state_b)
    output = []
    for k, (state, v) in enumerate(zip(states, branch_ffn)):
        size = state[0].shape[0]
        total = scatter_sum(v, [w[k * size : (k + 1) * size] for w in near])
        output.append(quarters((state[0] + branch_scale * total).astype(BF)))
    output = join_tiles(output)
    ffn_grads = jnp.stack([grad_gate, grad_up, grad_down])
    ffn_grads = ffn_grads.reshape(3, share, 4, PART).transpose(2, 0, 1, 3)
    output, grad_heads, part_a, ffn_grads = meet(output, grad_heads, part_a, ffn_grads)
    part_b, grad_heads, hops, far_a, grad_w_output = meet(
        back_group(1, grad_heads),
        grad_heads,
        hop_back(output),
        trade(part_a[2]),
        grad_w_output,
    )
    part_b = restore(part_b)
    grads_a = unturn(part_a[0], part_a[1], far_a, cosine, sine_vals)
    weights_a = weight_part(grads_a)
    grad_heads, weights_a, hops, part_b = meet(grad_heads, weights_a, hops, part_b)
    part_c, output, far_b, weights_a = meet(
        back_group(2, grad_heads),
        hop_out(hops),
        trade(part_b[2]),
        sum_line(weights_a),
    )
    part_c = restore(part_c)
    grads_b = unturn(part_b[0], part_b[1], far_b, cosine, sine_vals)
    weights_b, far_c, ffn_grads = meet(
        weight_part(grads_b), trade(part_c[2]), cross_whole(ffn_grads)
    )
    output = joined(output)
    weights_b = sum_line(weights_b)
    grads_c = unturn(part_c[0], part_c[1], far_c, cosine, sine_vals)
    grads = (grads_a, grads_b, grads_c)
    rest_a, grads, weights_a = meet(unproject(grads, w_qkv, 0), grads, cross_whole(weights_a))
    weights_c, far_a, grads = meet(weight_part(grads[2]), scatter_far(rest_a), grads)
    weights_c = sum_line(weights_c)
    rest_b, near_a = meet(unproject(grads, w_qkv, 1), scatter_near(rest_a, far_a))
    far_b = scatter_far(rest_b)

    def first_back(k, total):
        grad_first = inverse_one[k] * total - residual[k] * inverse_one[k] ** 3 * jnp.mean(
            total * residual[k], axis=-1, keepdims=True
        )
        return (grad_resid[k] + grad_first).astype(BF)

    hop_a = hop_back(first_back(0, scatter_sum(rest_a, near_a)))
    near_b = scatter_near(rest_b, far_b)
    hop_a, near_b = meet(hop_a, near_b)
    hop_b, hop_a = meet(hop_back(first_back(1, scatter_sum(rest_b, near_b))), hop_out(hop_a))
    grad_input = join_tiles([jnp.stack(hop_a), jnp.stack(hop_out(hop_b))]).astype(F32)
    ffn_grads = ffn_grads.astype(F32)
    ffn_grads = jnp.concatenate([ffn_grads[k, :, :n] for k, n in enumerate(sizes)], axis=1)
    grad_ffn_gain = jnp.sum(weights_a[:, thin, :thin].astype(F32), axis=0)
    weights_bc = over("p", jnp.concatenate([weights_b, weights_c], axis=2))
    proj = finish(
        (weights_a, weights_bc), (w_query, w_key, w_value), gain_f[:, None]
    )
    grad_attn_gain = proj[3][:, 0]

    limit_value = clip_threshold[0].astype(F32)
    clip_factor = jnp.sqrt(limit_value / jnp.maximum(maxima, limit_value))
    column_factor = jnp.repeat(clip_factor, HDIM)
    return (
        output,
        grad_input,
        proj[0],
        proj[1],
        proj[2],
        grad_w_output.astype(F32),
        ffn_grads[0].T,
        ffn_grads[1].T,
        ffn_grads[2],
        grad_attn_gain,
        grad_ffn_gain,
        maxima,
        clip_factor,
        w_query.astype(F32) * column_factor[None, :],
        w_key.astype(F32) * column_factor[None, :],
    )


def specs(grp, ctx):
    every = grp + ctx
    ins = [P(every, None)] * 6 + [P(grp, ctx), P(grp, ctx), P(ctx, grp), P(every), P(every)]
    ins += [P(grp, None), P(grp, None), P()]
    outs = [P(every, None)] * 6 + [P(grp, ctx), P(grp, ctx), P(ctx, grp), P(every), P(every)]
    outs += [P(), P(), P(every, None), P(every, None)]
    return tuple(ins), tuple(outs)


def solution(mesh):
    if mesh.shape["grp"] == 4 and mesh.shape["ctx"] == 8:
        mesh = Mesh(mesh.devices.reshape(4, 4, 2), ("p", "z", "c"))
        body, (in_specs, out_specs) = inner, specs(("p",), ("z", "c"))
    else:
        body, (in_specs, out_specs) = local, specs(("grp",), ("ctx",))
    return jax.shard_map(body, mesh=mesh, in_specs=in_specs, out_specs=out_specs, check_vma=False)
```

```python
import functools
import math

import jax
import jax.numpy as jnp
from jax import lax
from jax.experimental import pallas as pl
from jax.experimental.pallas import tpu as pltpu
from jax.sharding import Mesh
from jax.sharding import PartitionSpec as P

HEADS = 36
HDIM = 64
PLEN = 2048
CLEN = 256
NCONT = 8
BLK = 64
FAMTOK = 4096

F32 = jnp.float32
BF = jnp.bfloat16
NH = HEADS // 4
PART = NH * HDIM
GROUP = 3
GPART = GROUP * HDIM
QB_BACK = 512
QB = 256
KB = 1024
KB_FWD = 1024
HEAD_STEP = 9
NT = (((1,), (1,)), ((), ()))
NN = (((1,), (0,)), ((), ()))
TN = (((0,), (0,)), ((), ()))
VMEM_ROOM = 56 * 1024 * 1024


branch_scale = 1.4 / math.sqrt(40.0)
norm_eps = 1e-05
rope_base = 10000.0
masked_value = -1e30


def rope_angles(position):
    half_dim = HDIM // 2
    frequency = rope_base ** (-(jnp.arange(half_dim, dtype=jnp.float32) * (2.0 / HDIM)))
    angles = position.astype(jnp.float32)[:, None] * frequency[None, :]
    return (jnp.cos(angles)[:, None, :], jnp.sin(angles)[:, None, :])


def rotate(values, cosine, sine_vals, turn_sign):
    row_count = values.shape[0]
    shaped = values.reshape(row_count, HEADS, HDIM)
    leading = shaped[..., : HDIM // 2]
    trailing = shaped[..., HDIM // 2 :]
    turned = jnp.concatenate(
        [
            leading * cosine - turn_sign * trailing * sine_vals,
            trailing * cosine + turn_sign * leading * sine_vals,
        ],
        axis=-1,
    )
    return turned.reshape(row_count, HEADS * HDIM)


def token_facts(logical, lengths):
    family = logical // FAMTOK
    offset = logical % FAMTOK
    prompt = offset < PLEN
    member = jnp.clip((offset - PLEN) // CLEN, 0, NCONT - 1)
    inside = offset - PLEN - member * CLEN
    seq_id = jnp.where(prompt, -1, family * NCONT + member)
    numbers = jnp.arange(lengths.shape[0], dtype=jnp.int32)
    live_len = jnp.sum(jnp.where(seq_id[:, None] == numbers[None, :], lengths[None, :], 0), axis=1)
    is_live = prompt | (inside < live_len)
    position = jnp.where(prompt, offset, PLEN + inside)
    return (family, offset, prompt, seq_id, is_live, position)


def visible(query_facts, key_part):
    same_family = query_facts[0][:, None] == key_part[0][None, :]
    causal = key_part[1][None, :] <= query_facts[1][:, None]
    reaches = (
        key_part[2][None, :]
        | (key_part[3][None, :] == query_facts[3][:, None]) & key_part[4][None, :]
    )
    return same_family & causal & reaches


def key_slice(keys_heads, values_heads, key_facts, query_facts, first_row, span_rows):
    key_block = lax.dynamic_slice_in_dim(keys_heads, first_row, span_rows, 0)
    value_block = lax.dynamic_slice_in_dim(values_heads, first_row, span_rows, 0)
    key_part = tuple(
        (
            lax.dynamic_slice_in_dim(member_array, first_row, span_rows, 0)
            for member_array in key_facts
        )
    )
    return (key_block, value_block, visible(query_facts, key_part))


def block_scores(query_heads, key_block, visible_mask):
    scores = jnp.einsum(
        "qhd,khd->hqk", query_heads, key_block, preferred_element_type=jnp.float32
    ) * HDIM ** (-0.5)
    return jnp.where(visible_mask[None], scores, masked_value)


def score_grads(
    query_heads, grad_heads, log_total, row_delta, key_block, value_block, visible_mask
):
    scores = block_scores(query_heads, key_block, visible_mask)
    prob_table = jnp.where(visible_mask[None], jnp.exp(scores - log_total[:, :, None]), 0.0)
    grad_probs = jnp.einsum(
        "qhd,khd->hqk", grad_heads, value_block, preferred_element_type=jnp.float32
    )
    grad_scores = (prob_table * (grad_probs - row_delta[:, :, None])).astype(jnp.bfloat16)
    return (prob_table.astype(jnp.bfloat16), grad_scores)


def gate_grads(grad_mixed, gate_pre, up_pre):
    sigmoid = jax.nn.sigmoid(gate_pre)
    grad_gate = grad_mixed * up_pre * sigmoid * (1.0 + gate_pre * (1.0 - sigmoid))
    grad_up = grad_mixed * gate_pre * sigmoid
    return (grad_gate.astype(jnp.bfloat16), grad_up.astype(jnp.bfloat16))


def norm_backward(grad_normed, values, inverse, gain):
    scaled = grad_normed * gain[None, :]
    grad_gain = jnp.sum(grad_normed * values * inverse, axis=0)
    grad_values = inverse * scaled - values * inverse**3 * jnp.mean(
        scaled * values, axis=-1, keepdims=True
    )
    return (grad_gain, grad_values)


def attention_weights(w_query, w_key, w_value, w_output, attn_gain, ffn_gain):
    return (
        lax.all_gather(w_query, ("grp", "ctx"), axis=0, tiled=True),
        lax.all_gather(w_key, ("grp", "ctx"), axis=0, tiled=True),
        lax.all_gather(w_value, ("grp", "ctx"), axis=0, tiled=True),
        lax.all_gather(w_output, ("grp", "ctx"), axis=0, tiled=True),
        lax.all_gather(attn_gain, ("grp", "ctx"), axis=0, tiled=True),
        lax.all_gather(ffn_gain, ("grp", "ctx"), axis=0, tiled=True),
    )


def ffn_rows_gather(w_gate, w_up, w_down):
    return (
        lax.all_gather(w_gate, "grp", axis=0, tiled=True),
        lax.all_gather(w_up, "grp", axis=0, tiled=True),
        lax.all_gather(w_down, "grp", axis=1, tiled=True),
    )


def local(
    tokens_in,
    cotangent,
    w_query,
    w_key,
    w_value,
    w_output,
    w_gate,
    w_up,
    w_down,
    attn_gain,
    ffn_gain,
    cont_len,
    deal_order,
    clip_threshold,
):
    row_count = tokens_in.shape[0]
    model_width = tokens_in.shape[1]
    tile_count = deal_order.shape[1]
    group_rows = tile_count * BLK
    lengths = cont_len[0]
    my_index = lax.axis_index("ctx")
    tile_offsets = jnp.arange(BLK, dtype=jnp.int32)
    stored_logical = (deal_order[0][:, None] * BLK + tile_offsets[None, :]).reshape(group_rows)
    key_facts = token_facts(stored_logical, lengths)
    query_facts = tuple(
        (
            lax.dynamic_slice_in_dim(member_array, my_index * row_count, row_count, 0)
            for member_array in key_facts
        )
    )
    cosine, sine_vals = rope_angles(query_facts[5])
    key_step = math.gcd(group_rows, 512)
    key_blocks = group_rows // key_step
    full_query, full_key, full_value, full_output, gain_one, gain_two = attention_weights(
        w_query, w_key, w_value, w_output, attn_gain, ffn_gain
    )
    residual = tokens_in.astype(jnp.float32)
    inverse_one = lax.rsqrt(jnp.mean(residual * residual, axis=-1, keepdims=True) + norm_eps)
    gain_one_f = gain_one.astype(jnp.float32)
    gain_two_f = gain_two.astype(jnp.float32)
    normed_one = (residual * inverse_one * gain_one_f).astype(jnp.bfloat16)
    query_rot = rotate(
        jnp.dot(normed_one, full_query, preferred_element_type=jnp.float32), cosine, sine_vals, 1.0
    ).astype(jnp.bfloat16)
    key_rot = rotate(
        jnp.dot(normed_one, full_key, preferred_element_type=jnp.float32), cosine, sine_vals, 1.0
    ).astype(jnp.bfloat16)
    value_low = jnp.dot(normed_one, full_value, preferred_element_type=jnp.float32).astype(
        jnp.bfloat16
    )
    keys_all, values_all = (
        lax.all_gather(key_rot, "ctx", axis=0, tiled=True),
        lax.all_gather(value_low, "ctx", axis=0, tiled=True),
    )
    query_heads = query_rot.reshape(row_count, HEADS, HDIM)
    keys_heads = keys_all.reshape(group_rows, HEADS, HDIM)
    values_heads = values_all.reshape(group_rows, HEADS, HDIM)

    def stats_step(block_index, state_carry):
        key_block, value_block, visible_mask = key_slice(
            keys_heads, values_heads, key_facts, query_facts, block_index * key_step, key_step
        )

        def stats_busy(carry):
            run_max, run_sum, head_max = carry
            scores = block_scores(query_heads, key_block, visible_mask)
            block_max = jnp.max(scores, axis=2)
            new_max = jnp.maximum(run_max, block_max)
            exp_table = jnp.where(visible_mask[None], jnp.exp(scores - new_max[:, :, None]), 0.0)
            new_sum = run_sum * jnp.exp(run_max - new_max) + jnp.sum(exp_table, axis=2)
            return (new_max, new_sum, jnp.maximum(head_max, jnp.max(block_max, axis=1)))

        return lax.cond(jnp.any(visible_mask), stats_busy, lambda carry: carry, state_carry)

    start_state = (
        jnp.full((HEADS, row_count), masked_value, jnp.float32),
        jnp.zeros((HEADS, row_count), jnp.float32),
        jnp.full((HEADS,), masked_value, jnp.float32),
    )
    run_max, run_sum, head_max = lax.fori_loop(0, key_blocks, stats_step, start_state)
    log_total = run_max + jnp.log(run_sum)

    def output_step(block_index, running):
        key_block, value_block, visible_mask = key_slice(
            keys_heads, values_heads, key_facts, query_facts, block_index * key_step, key_step
        )

        def output_busy(total):
            scores = block_scores(query_heads, key_block, visible_mask)
            prob_low = jnp.where(
                visible_mask[None], jnp.exp(scores - log_total[:, :, None]), 0.0
            ).astype(jnp.bfloat16)
            return total + jnp.einsum(
                "hqk,khd->qhd", prob_low, value_block, preferred_element_type=jnp.float32
            )

        return lax.cond(jnp.any(visible_mask), output_busy, lambda total: total, running)

    attended = lax.fori_loop(
        0, key_blocks, output_step, jnp.zeros((row_count, HEADS, HDIM), jnp.float32)
    )
    attn_low = attended.reshape(row_count, model_width).astype(jnp.bfloat16)
    after_attn = residual + branch_scale * jnp.dot(
        attn_low, full_output, preferred_element_type=jnp.float32
    )
    inverse_two = lax.rsqrt(jnp.mean(after_attn * after_attn, axis=-1, keepdims=True) + norm_eps)
    normed_two = (after_attn * inverse_two * gain_two_f).astype(jnp.bfloat16)
    gate_cols, up_cols, down_cols = ffn_rows_gather(w_gate, w_up, w_down)
    normed_rows = lax.all_gather(normed_two, "ctx", axis=0, tiled=True)
    gate_pre = jnp.dot(normed_rows, gate_cols, preferred_element_type=jnp.float32)
    up_pre = jnp.dot(normed_rows, up_cols, preferred_element_type=jnp.float32)
    mixed = (jax.nn.silu(gate_pre) * up_pre).astype(jnp.bfloat16)
    branch_ffn = lax.psum_scatter(
        jnp.dot(mixed, down_cols, preferred_element_type=jnp.float32).astype(jnp.bfloat16),
        "ctx",
        scatter_dimension=0,
        tiled=True,
    ).astype(jnp.float32)
    output = (after_attn + branch_scale * branch_ffn).astype(jnp.bfloat16)
    grad_out = cotangent.astype(jnp.float32)
    grad_branch = (branch_scale * grad_out).astype(jnp.bfloat16)
    gate_again, up_again, down_again = ffn_rows_gather(w_gate, w_up, w_down)
    grad_rows = lax.all_gather(grad_branch, "ctx", axis=0, tiled=True)
    grad_mixed = jnp.dot(grad_rows, down_again.T, preferred_element_type=jnp.float32)
    grad_down = jnp.dot(mixed.T, grad_rows, preferred_element_type=jnp.float32)
    grad_gate_low, grad_up_low = gate_grads(grad_mixed, gate_pre, up_pre)
    grad_gate = jnp.dot(normed_rows.T, grad_gate_low, preferred_element_type=jnp.float32)
    grad_up = jnp.dot(normed_rows.T, grad_up_low, preferred_element_type=jnp.float32)
    grad_normed_two = lax.psum_scatter(
        (
            jnp.dot(grad_gate_low, gate_again.T, preferred_element_type=jnp.float32)
            + jnp.dot(grad_up_low, up_again.T, preferred_element_type=jnp.float32)
        ).astype(jnp.bfloat16),
        "ctx",
        scatter_dimension=0,
        tiled=True,
    ).astype(jnp.float32)
    ffn_stack = jnp.stack([grad_gate, grad_up, grad_down.T], axis=0)
    ffn_summed = lax.psum_scatter(
        ffn_stack.astype(jnp.bfloat16), "grp", scatter_dimension=1, tiled=True
    ).astype(jnp.float32)
    grad_gain_two, grad_second = norm_backward(grad_normed_two, after_attn, inverse_two, gain_two_f)
    grad_resid = grad_out + grad_second
    back_query, back_key, back_value, back_output, back_gain_one, back_gain_two = attention_weights(
        w_query, w_key, w_value, w_output, attn_gain, ffn_gain
    )
    grad_branch_attn = (branch_scale * grad_resid).astype(jnp.bfloat16)
    grad_w_output = jnp.dot(attn_low.T, grad_branch_attn, preferred_element_type=jnp.float32)
    grad_attn = jnp.dot(grad_branch_attn, back_output.T, preferred_element_type=jnp.float32).astype(
        jnp.bfloat16
    )
    grad_heads = grad_attn.reshape(row_count, HEADS, HDIM)
    row_delta = jnp.sum(grad_heads.astype(jnp.float32) * attended, axis=2).T

    def back_step(grad_q, block_index):
        key_block, value_block, visible_mask = key_slice(
            keys_heads, values_heads, key_facts, query_facts, block_index * key_step, key_step
        )

        def back_busy(current):
            prob_low, grad_scores = score_grads(
                query_heads, grad_heads, log_total, row_delta, key_block, value_block, visible_mask
            )
            updated = current + jnp.einsum(
                "hqk,khd->qhd", grad_scores, key_block, preferred_element_type=jnp.float32
            )
            grad_keys = jnp.einsum(
                "hqk,qhd->khd", grad_scores, query_heads, preferred_element_type=jnp.float32
            ) * HDIM ** (-0.5)
            grad_values = jnp.einsum(
                "hqk,qhd->khd", prob_low, grad_heads, preferred_element_type=jnp.float32
            )
            return (
                updated,
                (
                    grad_keys.reshape(key_step, model_width),
                    grad_values.reshape(key_step, model_width),
                ),
            )

        def quiet(current):
            empty = jnp.zeros((key_step, model_width), jnp.float32)
            return (current, (empty, empty))

        return lax.cond(jnp.any(visible_mask), back_busy, quiet, grad_q)

    grad_q_heads, key_terms = lax.scan(
        back_step,
        jnp.zeros((row_count, HEADS, HDIM), jnp.float32),
        jnp.arange(key_blocks, dtype=jnp.int32),
    )
    key_sum, value_sum = (
        lax.psum_scatter(
            key_terms[0].reshape(group_rows, model_width).astype(jnp.bfloat16),
            "ctx",
            scatter_dimension=0,
            tiled=True,
        ).astype(jnp.float32),
        lax.psum_scatter(
            key_terms[1].reshape(group_rows, model_width).astype(jnp.bfloat16),
            "ctx",
            scatter_dimension=0,
            tiled=True,
        ).astype(jnp.float32),
    )
    grad_query_rot = grad_q_heads.reshape(row_count, model_width) * HDIM ** (-0.5)
    grad_query = rotate(grad_query_rot, cosine, sine_vals, -1.0).astype(jnp.bfloat16)
    grad_key = rotate(key_sum, cosine, sine_vals, -1.0).astype(jnp.bfloat16)
    grad_value = value_sum.astype(jnp.bfloat16)
    grad_w_query = jnp.dot(normed_one.T, grad_query, preferred_element_type=jnp.float32)
    grad_w_key = jnp.dot(normed_one.T, grad_key, preferred_element_type=jnp.float32)
    grad_w_value = jnp.dot(normed_one.T, grad_value, preferred_element_type=jnp.float32)
    grad_normed_one = (
        jnp.dot(grad_query, back_query.T, preferred_element_type=jnp.float32)
        + jnp.dot(grad_key, back_key.T, preferred_element_type=jnp.float32)
        + jnp.dot(grad_value, back_value.T, preferred_element_type=jnp.float32)
    )
    grad_gain_one, grad_first = norm_backward(grad_normed_one, residual, inverse_one, gain_one_f)
    grad_input = grad_resid + grad_first
    gain_pair = jnp.stack([grad_gain_one, grad_gain_two], axis=1)
    summed = (
        lax.psum_scatter(grad_w_query, ("grp", "ctx"), scatter_dimension=0, tiled=True),
        lax.psum_scatter(grad_w_key, ("grp", "ctx"), scatter_dimension=0, tiled=True),
        lax.psum_scatter(grad_w_value, ("grp", "ctx"), scatter_dimension=0, tiled=True),
        lax.psum_scatter(grad_w_output, ("grp", "ctx"), scatter_dimension=0, tiled=True),
        lax.psum_scatter(gain_pair, ("grp", "ctx"), scatter_dimension=0, tiled=True),
    )
    maxima = lax.pmax(head_max, ("grp", "ctx"))
    limit_value = clip_threshold[0].astype(jnp.float32)
    clip_factor = jnp.sqrt(limit_value / jnp.maximum(maxima, limit_value))
    column_factor = jnp.repeat(clip_factor, HDIM)
    clipped_query = w_query.astype(jnp.float32) * column_factor[None, :]
    clipped_key = w_key.astype(jnp.float32) * column_factor[None, :]
    return (
        output,
        grad_input,
        summed[0],
        summed[1],
        summed[2],
        summed[3],
        ffn_summed[0],
        ffn_summed[1],
        ffn_summed[2].T,
        summed[4][:, 0],
        summed[4][:, 1],
        maxima,
        clip_factor,
        clipped_query,
        clipped_key,
    )


def mul(left, right, dims=NN):
    return lax.dot_general(left, right, dims, preferred_element_type=F32)


def room():
    return pltpu.CompilerParams(vmem_limit_bytes=VMEM_ROOM)


def cost(flops, sent):
    return pl.CostEstimate(flops=int(flops), bytes_accessed=int(sent), transcendentals=0)


def straighten(w_ref, w_sc, thin):
    for i in range(4):
        for k in range(8):
            w_sc[(i * 8 + k) * thin : (i * 8 + k + 1) * thin, :] = w_ref[k, i, :thin, :]


def swing(values, cosine, sine_vals):
    lane = lax.broadcasted_iota(jnp.int32, values.shape, 1)
    other = jnp.where(
        lane % HDIM < HDIM // 2,
        pltpu.roll(values, 2 * HDIM - HDIM // 2, 1),
        pltpu.roll(values, HDIM // 2, 1),
    )
    return values * cosine + other * sine_vals


def fetch_rows(pieces, x_sc):
    step = pl.program_id(0)
    half = QB // 2
    for k in range(8):
        chunk, slot = k // 4, k % 4

        @pl.when(step == k)
        def _():
            if len(pieces) == 5 and slot < 3:
                x_sc[...] = pieces[slot][chunk * QB : (chunk + 1) * QB, :]
            elif len(pieces) == 5:
                x_sc[...] = pieces[3 + chunk][...]
            elif slot < 3:
                x_sc[...] = pieces[chunk * 5 + slot][...]
            else:
                x_sc[:half] = pieces[chunk * 5 + 3][...]
                x_sc[half:] = pieces[chunk * 5 + 4][...]


def whole(shape):
    return pl.BlockSpec(shape, lambda i: (0,) * len(shape), pipeline_mode=pl.Buffered(1))


def project_kernel(*refs):
    w_ref, cos_ref, sin_ref, q_ref, kv_ref, x_sc, w_sc = refs[5:]
    thin = w_sc.shape[0] // 32
    fetch_rows(refs[:5], x_sc)

    @pl.when(pl.program_id(0) == 0)
    def _():
        straighten(w_ref, w_sc, thin)

    y = mul(x_sc[...], w_sc[...])
    cosine, sine_vals = cos_ref[...], sin_ref[...]
    for k in range(NH):
        piece = swing(y[:, k * 128 : (k + 1) * 128], cosine, sine_vals)
        for j in range(2):
            head = 2 * k + j
            if head < NH:
                q_ref[head] = (piece[:, j * HDIM : (j + 1) * HDIM] * 0.125).astype(BF)
        if 2 * k + 1 > NH:
            kv_ref[:, k * 128 : (k + 1) * 128] = piece.astype(BF)
        elif 2 * k + 1 == NH:
            kv_ref[:, k * 128 + HDIM : (k + 1) * 128] = piece[:, HDIM:].astype(BF)
    kv_ref[:, :PART] = y[:, 2 * PART :].astype(BF)


def project(normed, w_all, cosine, sine_vals):
    rows = sum(v.shape[0] for v in normed)
    width = normed[0].shape[1]
    full = w_all.shape
    return pl.pallas_call(
        project_kernel,
        out_shape=[
            jax.ShapeDtypeStruct((NH, rows, HDIM), BF),
            jax.ShapeDtypeStruct((rows, 2 * PART), BF),
            jax.ShapeDtypeStruct((rows, width), BF),
        ],
        grid=(rows // QB,),
        in_specs=[whole(v.shape) for v in normed]
        + [
            whole(full),
            pl.BlockSpec((QB, 128), lambda i: (i, 0)),
            pl.BlockSpec((QB, 128), lambda i: (i, 0)),
        ],
        out_specs=[
            pl.BlockSpec((NH, QB, HDIM), lambda i: (0, i, 0)),
            pl.BlockSpec((QB, 2 * PART), lambda i: (i, 0)),
            pl.BlockSpec((QB, width), lambda i: (i % 4 * 2 + i // 4, 0)),
        ],
        scratch_shapes=[pltpu.VMEM((width, full[3]), BF)],
        compiler_params=room(),
        cost_estimate=cost(2 * rows * width * full[3], 2 * (rows * width + width * full[3] + rows * 5 * PART)),
        name="project",
    )(*normed, w_all, cosine, sine_vals)


def sort_kernel(order_ref, *refs):
    k_ref, v_ref, kt_ref, vt_ref = refs[16:]
    first = pl.program_id(0) * 8
    for j in range(8):
        from_mine = order_ref[first + j] < 32
        tile = jnp.where(from_mine, refs[j][0], refs[8 + j][0])
        rows = slice(j * BLK, (j + 1) * BLK)
        for h in range(NH):
            v_ref[h, rows, :] = tile[:, h * HDIM : (h + 1) * HDIM]
            k_ref[h, rows, :] = tile[:, PART + h * HDIM : PART + (h + 1) * HDIM]
    for h in range(NH):
        kt_ref[h] = k_ref[h].T
        vt_ref[h] = v_ref[h].T


def sort_keys(order, mine, theirs):
    count = order.shape[0]
    shape = (1, BLK, 2 * PART)
    near = lambda j: pl.BlockSpec(shape, lambda i, o: (jnp.minimum(o[i * 8 + j], 31), 0, 0))
    far = lambda j: pl.BlockSpec(shape, lambda i, o: (jnp.maximum(o[i * 8 + j] - 32, 0), 0, 0))
    return pl.pallas_call(
        sort_kernel,
        out_shape=[jax.ShapeDtypeStruct((NH, count * BLK, HDIM), BF)] * 2
        + [jax.ShapeDtypeStruct((NH, HDIM, count * BLK), BF)] * 2,
        grid_spec=pltpu.PrefetchScalarGridSpec(
            num_scalar_prefetch=1,
            grid=(count // 8,),
            in_specs=[near(j) for j in range(8)] + [far(j) for j in range(8)],
            out_specs=[pl.BlockSpec((NH, 8 * BLK, HDIM), lambda i, o: (0, i, 0))] * 2
            + [pl.BlockSpec((NH, HDIM, 8 * BLK), lambda i, o: (0, 0, i))] * 2,
        ),
        compiler_params=room(),
        cost_estimate=cost(0, 64 * count * BLK * PART),
        name="sort_keys",
    )(order, *([mine.reshape(32, BLK, 2 * PART)] * 8), *([theirs.reshape(32, BLK, 2 * PART)] * 8))


def lane_tile(vals):
    shape = (1, len(vals) * BLK)
    lane = lax.broadcasted_iota(jnp.int32, shape, 1)
    out = jnp.full(shape, vals[-1], jnp.int32)
    for j in range(len(vals) - 2, -1, -1):
        out = jnp.where(lane < (j + 1) * BLK, vals[j], out)
    return out, lane & (BLK - 1)


def block_facts(tiles_ref, len_ref, block, step, size):
    half_tiles = PLEN // BLK
    count = size // BLK
    t = [tiles_ref[block * count + j] for j in range(count)]
    tile, within = lane_tile(t)
    qpos = tile * BLK + within
    tmax = functools.reduce(jnp.maximum, t)
    tmin = functools.reduce(jnp.minimum, t)
    per = step // BLK
    is_cont = t[0] >= half_tiles
    n_all = jnp.where(is_cont, PLEN // step, tmax // per + 1)
    n_free = jnp.where(is_cont, PLEN // step, tmin // per)
    conts = [jnp.maximum(v - half_tiles, 0) // 4 for v in t]
    lens = lane_tile([len_ref[v] for v in conts])[0]
    qin = qpos - PLEN - lane_tile(conts)[0] * CLEN
    starts = [pl.multiple_of(PLEN + v * CLEN, CLEN) for v in conts]
    kin = lax.broadcasted_iota(jnp.int32, (CLEN, size), 0)
    seen = lambda: (kin <= qin) & (kin < lens)
    return qpos, is_cont, n_all, n_free, starts, seen


def forward_kernel(
    tiles_ref, len_ref, q_ref, k_ref, vt_sc, o_ref, lse_ref, mx_ref, ot_sc, shift
):
    block = pl.program_id(0) + shift
    qpos, is_cont, n_all, n_free, starts, seen = block_facts(
        tiles_ref, len_ref, block, KB_FWD, QB
    )

    def heads(group, carry):
        hs = [group * HEAD_STEP + j for j in range(HEAD_STEP)]
        qs = [q_ref[h] for h in hs]

        def update(scores, states, weigh):
            out = []
            for n, (s, (m, l, acc)) in enumerate(zip(scores, states)):
                mn = jnp.maximum(m, jnp.max(s, axis=0, keepdims=True))
                p = jnp.exp(s - mn)
                al = jnp.exp(m - mn)
                out.append(
                    (
                        mn,
                        l * al + jnp.sum(p, axis=0, keepdims=True),
                        acc * al + weigh(n, p.astype(BF)),
                    )
                )
            return tuple(out)

        def step(kb, states, masked):
            base = pl.multiple_of(kb * KB_FWD, KB_FWD)
            rows = pl.ds(base, KB_FWD)
            scores = [mul(k_ref[h, rows, :], q, NT) for h, q in zip(hs, qs)]
            if masked:
                kpos = base + lax.broadcasted_iota(jnp.int32, (KB_FWD, QB), 0)
                vis = kpos <= qpos
                scores = [jnp.where(vis, s, masked_value) for s in scores]
            return update(scores, states, lambda n, p: mul(vt_sc[hs[n], :, rows], p))

        states = tuple(
            (
                jnp.full((1, QB), masked_value, F32),
                jnp.zeros((1, QB), F32),
                jnp.zeros((HDIM, QB), F32),
            )
            for _ in hs
        )
        states = lax.fori_loop(0, n_free, functools.partial(step, masked=False), states)
        states = lax.fori_loop(n_free, n_all, functools.partial(step, masked=True), states)

        def own(states):
            vis = seen()
            cols = lambda x, j: x[:, j * BLK : (j + 1) * BLK]
            scores = []
            for h, q in zip(hs, qs):
                s = [
                    mul(k_ref[h, pl.ds(starts[j], CLEN), :], q[j * BLK : (j + 1) * BLK], NT)
                    for j in range(4)
                ]
                scores.append(jnp.where(vis, jnp.concatenate(s, axis=1), masked_value))
            return update(
                scores,
                states,
                lambda n, p: jnp.concatenate(
                    [
                        mul(vt_sc[hs[n], :, pl.ds(starts[j], CLEN)], cols(p, j))
                        for j in range(4)
                    ],
                    axis=1,
                ),
            )

        states = lax.cond(is_cont, own, lambda s: s, states)
        for h, (m, l, acc) in zip(hs, states):
            ot_sc[h] = acc / l
            lse_ref[0, pl.ds(h, 1), :] = m + jnp.log(l)
            mx_ref[0, pl.ds(h, 1), :] = m
        return carry

    lax.fori_loop(0, NH // HEAD_STEP, heads, 0)
    for h in range(NH):
        o_ref[:, h * HDIM : (h + 1) * HDIM] = ot_sc[h].T.astype(BF)


def attention_forward(tiles, lengths, queries, keys, values_t, shift, count):
    rows = count * QB
    span = keys.shape[1]
    once = lambda *shape: pl.BlockSpec(
        shape, lambda i, a, b: (0, 0, 0), pipeline_mode=pl.Buffered(1)
    )
    stat = pl.BlockSpec((1, NH, QB), lambda i, a, b: (i, 0, 0))
    return pl.pallas_call(
        functools.partial(forward_kernel, shift=shift),
        out_shape=[
            jax.ShapeDtypeStruct((rows, PART), BF),
            jax.ShapeDtypeStruct((count, NH, QB), F32),
            jax.ShapeDtypeStruct((count, NH, QB), F32),
        ],
        grid_spec=pltpu.PrefetchScalarGridSpec(
            num_scalar_prefetch=2,
            grid=(count,),
            in_specs=[
                pl.BlockSpec((NH, QB, HDIM), lambda i, a, b: (0, i + shift, 0)),
                once(NH, span, HDIM),
                once(NH, HDIM, span),
            ],
            out_specs=[pl.BlockSpec((QB, PART), lambda i, a, b: (i, 0)), stat, stat],
            scratch_shapes=[pltpu.VMEM((NH, HDIM, QB), F32)],
        ),
        compiler_params=room(),
        cost_estimate=cost(rows * PART * PLEN * 20, 16 * span * PART),
        name="attention_forward",
    )(tiles, lengths, queries, keys, values_t)


def delta_kernel(*refs):
    w_ref, o_ref, gh_ref, delta_ref, gw_ref, x_sc = refs[10:]
    step = pl.program_id(0)
    rows = pl.ds(pl.multiple_of(step * QB, QB), QB)
    fetch_rows(refs[:10], x_sc.at[rows, :])
    grad = mul(x_sc[rows, :], w_ref[...], NT).astype(BF)
    for h in range(NH):
        gh_ref[h] = grad[:, h * HDIM : (h + 1) * HDIM]
    prod = grad.astype(F32) * o_ref[rows, :].astype(F32)
    high = prod.astype(BF)
    low = (prod - high.astype(F32)).astype(BF)
    row = lax.broadcasted_iota(jnp.int32, (16, PART), 0)
    col = lax.broadcasted_iota(jnp.int32, (16, PART), 1)
    pick_head = jnp.where(col // HDIM == row, 1.0, 0.0).astype(BF)
    total = mul(pick_head, high, NT) + mul(pick_head, low, NT)
    delta_ref[0] = total[:NH]

    @pl.when(step == pl.num_programs(0) - 1)
    def _():
        for k in range(3):
            cols = slice(k * 768, (k + 1) * 768)
            gw_ref[:, cols] = mul(o_ref[...], x_sc[:, cols], TN).astype(BF)


def attention_delta(grad_branch, w_out, attended):
    rows, width = attended.shape[0], w_out.shape[1]
    count = rows // QB
    return pl.pallas_call(
        delta_kernel,
        out_shape=[
            jax.ShapeDtypeStruct((NH, rows, HDIM), BF),
            jax.ShapeDtypeStruct((count, NH, QB), F32),
            jax.ShapeDtypeStruct((PART, width), BF),
        ],
        grid=(count,),
        in_specs=[whole(v.shape) for v in grad_branch]
        + [whole((PART, width)), whole((rows, PART))],
        out_specs=[
            pl.BlockSpec((NH, QB, HDIM), lambda i: (0, i, 0)),
            pl.BlockSpec((1, NH, QB), lambda i: (i, 0, 0)),
            pl.BlockSpec((PART, width), lambda i: (0, 0)),
        ],
        scratch_shapes=[pltpu.VMEM((rows, width), BF)],
        compiler_params=room(),
        cost_estimate=cost(2 * rows * width * PART, 2 * rows * width),
        name="attention_delta",
    )(*grad_branch, w_out, attended)


def backward_kernel(
    tiles_ref, len_ref, q_ref, g_ref, lse_ref, delta_ref, k_ref, v_ref, kt_ref, dq_ref, dk_out, dv_out,
    dk_ref, dv_ref, first
):
    h = pl.program_id(0) + first
    block = pl.program_id(1)

    @pl.when(block == 0)
    def _():
        dk_ref[...] = jnp.zeros_like(dk_ref)
        dv_ref[...] = jnp.zeros_like(dv_ref)

    qpos, is_cont, n_all, n_free, starts, seen = block_facts(
        tiles_ref, len_ref, block, KB, QB_BACK
    )
    q = q_ref[0]
    g = g_ref[0]
    stat = lambda ref: jnp.concatenate(
        [ref[j, pl.ds(h, 1), :] for j in range(QB_BACK // QB)], axis=1
    )
    lse = stat(lse_ref)
    delta = stat(delta_ref)

    def step(kb, dqt, masked):
        base = pl.multiple_of(kb * KB, KB)
        rows = pl.ds(base, KB)
        s = mul(k_ref[0, rows, :], q, NT)
        dp = mul(v_ref[0, rows, :], g, NT)
        if masked:
            kpos = base + lax.broadcasted_iota(jnp.int32, (KB, QB_BACK), 0)
            s = jnp.where(kpos <= qpos, s, masked_value)
        p = jnp.exp(s - lse)
        ds = (p * (dp - delta)).astype(BF)
        dv_ref[rows, :] += mul(p.astype(BF), g)
        dk_ref[rows, :] += mul(ds, q)
        return dqt + mul(kt_ref[0, :, rows], ds)

    dqt = jnp.zeros((HDIM, QB_BACK), F32)
    dqt = lax.fori_loop(0, n_free, functools.partial(step, masked=False), dqt)
    dqt = lax.fori_loop(n_free, n_all, functools.partial(step, masked=True), dqt)
    dq_ref[0] = dqt.T * HDIM ** (-0.5)

    @pl.when(is_cont)
    def _():
        part = lambda x, j: x[j * BLK : (j + 1) * BLK]
        rows = [pl.ds(starts[j], CLEN) for j in range(QB_BACK // BLK)]
        s = jnp.concatenate([mul(k_ref[0, rows[j], :], part(q, j), NT) for j in range(QB_BACK // BLK)], axis=1)
        s = jnp.where(seen(), s, masked_value)
        p = jnp.exp(s - lse)
        dp = jnp.concatenate([mul(v_ref[0, rows[j], :], part(g, j), NT) for j in range(QB_BACK // BLK)], axis=1)
        ds = (p * (dp - delta)).astype(BF)
        pb = p.astype(BF)
        dq = []
        for j in range(QB_BACK // BLK):
            cols = slice(j * BLK, (j + 1) * BLK)
            dv_ref[rows[j], :] += mul(pb[:, cols], part(g, j))
            dk_ref[rows[j], :] += mul(ds[:, cols], part(q, j))
            dq.append(mul(kt_ref[0, :, rows[j]], ds[:, cols]))
        dq_ref[0] += jnp.concatenate(dq, axis=1).T * HDIM ** (-0.5)

    @pl.when(block == pl.num_programs(1) - 1)
    def _():
        dk_out[0] = dk_ref[...].astype(BF)
        dv_out[0] = dv_ref[...].astype(BF)


def attention_backward(tiles, lengths, queries, grads, log_total, row_delta, keys, values, keys_t, group):
    rows = queries.shape[1]
    count = rows // QB_BACK
    span = keys.shape[1]
    first = group * GROUP
    row = pl.BlockSpec((1, QB_BACK, HDIM), lambda h, i, a, b: (h + first, i, 0))
    stat = pl.BlockSpec((QB_BACK // QB, NH, QB), lambda h, i, a, b: (i, 0, 0))
    full = pl.BlockSpec((1, span, HDIM), lambda h, i, a, b: (h + first, 0, 0))
    out = pl.BlockSpec((1, span, HDIM), lambda h, i, a, b: (h, 0, 0))
    return pl.pallas_call(
        functools.partial(backward_kernel, first=first),
        out_shape=[
            jax.ShapeDtypeStruct((GROUP, rows, HDIM), F32),
            jax.ShapeDtypeStruct((GROUP, span, HDIM), BF),
            jax.ShapeDtypeStruct((GROUP, span, HDIM), BF),
        ],
        grid_spec=pltpu.PrefetchScalarGridSpec(
            num_scalar_prefetch=2,
            grid=(GROUP, count),
            in_specs=[
                row,
                row,
                stat,
                stat,
                full,
                full,
                pl.BlockSpec((1, HDIM, span), lambda h, i, a, b: (h + first, 0, 0)),
            ],
            out_specs=[pl.BlockSpec((1, QB_BACK, HDIM), lambda h, i, a, b: (h, i, 0)), out, out],
            scratch_shapes=[pltpu.VMEM((span, HDIM), F32)] * 2,
        ),
        compiler_params=room(),
        cost_estimate=cost(rows * GPART * PLEN * 40, 32 * span * GPART),
        name="attention_backward",
    )(tiles, lengths, queries, grads, log_total, row_delta, keys, values, keys_t)


def restore_kernel(tiles_ref, *refs):
    mine_ref, theirs_ref = refs[16:]

    def write(out_ref):
        for j in range(8):
            rows = slice(j * BLK, (j + 1) * BLK)
            for h in range(GROUP):
                cols = slice(h * HDIM, (h + 1) * HDIM)
                out_ref[rows, cols] = refs[8 + j][h]
                out_ref[rows, GPART + h * HDIM : GPART + (h + 1) * HDIM] = refs[j][h]

    @pl.when(pl.program_id(0) < 4)
    def _():
        write(theirs_ref)

    @pl.when(pl.program_id(0) >= 4)
    def _():
        write(mine_ref)


def restore_keys(tiles, grad_k, grad_v):
    spec = lambda j: pl.BlockSpec((GROUP, BLK, HDIM), lambda i, o: (0, o[i * 8 + j], 0))
    shape = (8 * BLK, 2 * GPART)
    return pl.pallas_call(
        restore_kernel,
        out_shape=[jax.ShapeDtypeStruct((32 * BLK, 2 * GPART), BF)] * 2,
        grid_spec=pltpu.PrefetchScalarGridSpec(
            num_scalar_prefetch=1,
            grid=(8,),
            in_specs=[spec(j) for j in range(8)] * 2,
            out_specs=[
                pl.BlockSpec(shape, lambda i, o: (jnp.maximum(i - 4, 0), 0)),
                pl.BlockSpec(shape, lambda i, o: (jnp.minimum(i, 3), 0)),
            ],
        ),
        compiler_params=room(),
        cost_estimate=cost(0, 64 * 64 * BLK * GPART),
        name="restore_keys",
    )(tiles, *([grad_k] * 8), *([grad_v] * 8))


def unturn_kernel(dq_ref, mine_ref, theirs_ref, cos_ref, sin_ref, g_ref, y_sc):
    kv = mine_ref[...].astype(F32) + theirs_ref[...].astype(F32)
    for h in range(GROUP):
        y_sc[:, h * HDIM : (h + 1) * HDIM] = dq_ref[h]
    y_sc[:, GPART:] = kv[:, GPART:]
    cosine, sine_vals = cos_ref[...], -sin_ref[...]
    for k in range(GROUP):
        cols = slice(k * 128, (k + 1) * 128)
        g_ref[:, cols] = swing(y_sc[:, cols], cosine, sine_vals).astype(BF)
    g_ref[:, 2 * GPART :] = kv[:, :GPART].astype(BF)


def unturn(grad_q, mine, theirs, cosine, sine_vals):
    rows = mine.shape[0]
    size = QB
    row = lambda n: pl.BlockSpec((size, n), lambda i: (i, 0))
    return pl.pallas_call(
        unturn_kernel,
        out_shape=jax.ShapeDtypeStruct((rows, 3 * GPART), BF),
        grid=(rows // size,),
        in_specs=[
            pl.BlockSpec((GROUP, size, HDIM), lambda i: (0, i, 0)),
            row(2 * GPART),
            row(2 * GPART),
            row(128),
            row(128),
        ],
        out_specs=pl.BlockSpec((size, 3 * GPART), lambda i: (i % 4 * 2 + i // 4, 0)),
        scratch_shapes=[pltpu.VMEM((size, 2 * GPART), F32)],
        compiler_params=room(),
        cost_estimate=cost(0, 20 * rows * GPART),
        name="unturn",
    )(grad_q, mine, theirs, cosine, sine_vals)


def unproject_kernel(a_ref, b_ref, c_ref, w_ref, x_ref, w_sc, y_sc):
    thin = w_sc.shape[0] // 32

    @pl.when(pl.program_id(0) == 0)
    def _():
        straighten(w_ref, w_sc, thin)

    for g, ref in enumerate((a_ref, b_ref, c_ref)):
        for k in range(3):
            y_sc[:, k * PART + g * GPART : k * PART + (g + 1) * GPART] = ref[
                :, k * GPART : (k + 1) * GPART
            ]
    x_ref[...] = mul(y_sc[...], w_sc[...], NT).astype(BF)


def unproject(parts, w_all, chunk):
    rows = parts[0].shape[0] // 2
    full = w_all.shape
    width = full[0] * full[1] * (full[2] - 8)
    return pl.pallas_call(
        unproject_kernel,
        out_shape=jax.ShapeDtypeStruct((rows, width), BF),
        grid=(rows // QB,),
        in_specs=[pl.BlockSpec((QB, 3 * GPART), lambda i: (i * 2 + chunk, 0))] * 3
        + [pl.BlockSpec(full, lambda i: (0, 0, 0, 0), pipeline_mode=pl.Buffered(1))],
        out_specs=pl.BlockSpec((QB, width), lambda i: (i, 0)),
        scratch_shapes=[
            pltpu.VMEM((width, full[3]), BF),
            pltpu.VMEM((QB, 3 * PART), BF),
        ],
        compiler_params=room(),
        cost_estimate=cost(2 * rows * width * 3 * PART, 4 * rows * width),
        name="unproject",
    )(*parts, w_all)


def finish_kernel(a_ref, bc_ref, wq_ref, wk_ref, wv_ref, gain_ref, q_ref, k_ref, v_ref, sum_ref):
    thin = gain_ref.shape[0]
    gain = gain_ref[...]
    total = jnp.zeros((thin, 1), F32)
    for p in range(4):
        for g, (ref, first) in enumerate(((a_ref, 0), (bc_ref, 0), (bc_ref, PART))):
            cols = slice(p * PART + g * GPART, p * PART + (g + 1) * GPART)
            for n, (w, out) in enumerate(((wq_ref, q_ref), (wk_ref, k_ref), (wv_ref, v_ref))):
                part = slice(first + n * GPART, first + (n + 1) * GPART)
                grad = ref[p, :thin, part].astype(F32)
                out[:, cols] = grad * gain
                total += jnp.sum(grad * w[:, cols].astype(F32), axis=1, keepdims=True)
    sum_ref[...] = jnp.broadcast_to(total, sum_ref.shape)


def finish(parts, weights, gain):
    thin, width = weights[0].shape
    return pl.pallas_call(
        finish_kernel,
        out_shape=[jax.ShapeDtypeStruct((thin, width), F32)] * 3
        + [jax.ShapeDtypeStruct((thin, 128), F32)],
        compiler_params=room(),
        name="finish",
    )(*parts, *weights, gain)


def split_tiles(rows):
    blocks = rows.reshape(4, 2, rows.shape[0] // 8, rows.shape[1])
    return blocks[:, 0], blocks[:, 1]


def join_tiles(chunks):
    blocks = jnp.stack(chunks, axis=1)
    return blocks.reshape(-1, blocks.shape[-1])


def over(name, blocks):
    return lax.all_to_all(blocks, name, 0, 0, tiled=True)


def quarters(rows):
    return rows.reshape(4, rows.shape[0] // 4, rows.shape[1])


def after(value, *earlier):
    return lax.optimization_barrier((value, earlier))[0]


def flip(values, mask):
    return lax.ppermute(values, "p", [(k, k ^ mask) for k in range(4)])


def gather_near(own):
    return [own, flip(own, 1), flip(own, 2)]


def gather_far(near):
    half = near[0].shape[0] // 2
    return near + [flip(near[2][:half], 1), flip(near[1][half:], 2)]


def slots(terms):
    size = terms.shape[0] // 4
    return [terms[k * size : (k + 1) * size] for k in range(4)]


def scatter_far(terms):
    far = slots(terms)[3]
    half = far.shape[0] // 2
    return flip(far[:half], 1), flip(far[half:], 2)


def scatter_near(terms, far):
    _, first, second, _ = slots(terms)
    half = first.shape[0] // 2
    add = lambda x, y: (x.astype(F32) + y.astype(F32)).astype(BF)
    first = flip(jnp.concatenate([first[:half], add(first[half:], far[1])], axis=0), 1)
    second = flip(jnp.concatenate([add(second[:half], far[0]), second[half:]], axis=0), 2)
    return first, second


def scatter_sum(terms, near):
    return slots(terms)[0].astype(F32) + near[0].astype(F32) + near[1].astype(F32)


def scatter_far_both(terms):
    return flip(slots(terms[0])[3], 1), flip(slots(terms[1])[3], 2)


def scatter_near_both(terms, far):
    early, late = slots(terms[0]), slots(terms[1])
    add = lambda x, y: (x.astype(F32) + y.astype(F32)).astype(BF)
    first = flip(jnp.concatenate([early[1], add(late[1], far[1])], axis=0), 1)
    second = flip(jnp.concatenate([add(early[2], far[0]), late[2]], axis=0), 2)
    return first, second


def meet(*values):
    return lax.optimization_barrier(values)


def swap_blocks(name, pieces):
    return [pieces[0]] + [
        lax.ppermute(pieces[r], name, [(k, k ^ r) for k in range(4)]) for r in (1, 2, 3)
    ]


def pick(pieces, first):
    stacked = jnp.stack(pieces)
    return [
        lax.dynamic_index_in_dim(stacked, jnp.bitwise_xor(first, r), 0, keepdims=False)
        for r in range(4)
    ]


def hidden_cuts(hidden):
    steps = hidden // 8
    sizes = [8 * (steps // 4 + (k < steps % 4)) for k in range(4)]
    starts = [sum(sizes[:k]) for k in range(4)]
    return starts, sizes, max(sizes)


def inner(
    tokens_in,
    cotangent,
    w_query,
    w_key,
    w_value,
    w_output,
    w_gate,
    w_up,
    w_down,
    attn_gain,
    ffn_gain,
    cont_len,
    deal_order,
    clip_threshold,
):
    plane, depth, core = (lax.axis_index(name) for name in ("p", "z", "c"))
    line = ("z", "c")
    width = tokens_in.shape[1]
    thin = w_query.shape[0]
    hidden = w_down.shape[0]
    starts, sizes, share = hidden_cuts(hidden)
    gain_f = attn_gain.astype(F32)
    parts_of = lambda v: [v[k] for k in range(4)]
    cross = lambda v: swap_blocks("p", pick(v, plane))
    cross_whole = lambda v: jnp.stack(pick(cross(parts_of(v)), plane))
    hop_on = lambda v: swap_blocks("z", pick(v, jnp.bitwise_xor(plane, depth)))
    hop_back = lambda v: swap_blocks("z", parts_of(quarters(v)))
    hop_out = lambda v: pick(
        swap_blocks("p", pick(v, jnp.bitwise_xor(plane, depth))), plane
    )
    first_hop = cross(parts_of(quarters(tokens_in)))
    turn_over = [(g * 4 + k, k * 4 + g) for g in range(4) for k in range(4)]
    deal = lax.ppermute(deal_order[0], ("p", "z"), turn_over)
    lengths = lax.ppermute(cont_len[0], ("p", "z"), turn_over)

    scaled = [(w.astype(F32) * gain_f[:, None]).astype(BF) for w in (w_query, w_key, w_value)]
    blocks = jnp.stack(scaled).reshape(3, thin, 4, PART).transpose(2, 1, 0, 3)
    blocks = blocks.reshape(4, thin, 3 * PART)
    extra = jnp.zeros((4, 8, 3 * PART), BF).at[:, 0, :thin].set(ffn_gain[None, :])
    send = jnp.concatenate([blocks, extra], axis=1)
    first_hop, send = meet(first_hop, send)
    early = after((w_gate, w_up, w_down), first_hop)
    stacked = jnp.stack([early[0].T, early[1].T, early[2]])
    stacked = jnp.stack(
        [
            jnp.pad(stacked[:, a : a + n], ((0, 0), (0, share - n), (0, 0)))
            for a, n in zip(starts, sizes)
        ]
    )
    send, moved = meet(cross_whole(send), hop_on(first_hop))
    stacked = cross_whole(stacked)
    w_qkv = lax.all_gather(send, line, axis=0)
    gain_two = w_qkv[:, :, thin, :thin].transpose(1, 0, 2).reshape(width).astype(F32)
    w_out = lax.all_gather(w_output, line, axis=0, tiled=True)
    piece = jnp.arange(2)[:, None, None]
    slot = jnp.arange(4)[None, :, None]
    source = jnp.bitwise_xor(depth, jnp.arange(4))[None, None, :]
    quarter = jnp.bitwise_xor(plane, slot)
    held = lambda which: deal[((source * 2 + which) * 8 + quarter * 2 + piece).reshape(-1)]
    tiles, tiles_far = held(core), held(1 - core)
    both = jnp.concatenate([tiles, tiles_far])
    numbers = jnp.arange(64, dtype=jnp.int32)
    order = jnp.sum(
        jnp.where(both[None, :] == numbers[:, None], numbers[None, :], 0), axis=1
    ).astype(jnp.int32)
    logical = (tiles[:, None] * BLK + jnp.arange(BLK, dtype=jnp.int32)[None, :]).reshape(-1)
    position = jnp.where(logical < PLEN, logical, PLEN + (logical - PLEN) % CLEN)
    cosine, sine_vals = (v[:, 0, :] for v in rope_angles(position))
    cosine = jnp.concatenate([cosine] * 4, axis=1)
    sine_vals = jnp.concatenate([-sine_vals, sine_vals] * 2, axis=1)

    joined = lambda pieces: jnp.concatenate(pieces, axis=0)
    by_chunk = lambda v: [h.reshape(-1, width) for h in split_tiles(joined(v))]
    residual = [v.astype(F32) for v in by_chunk(moved)]
    inverse_of = lambda v: lax.rsqrt(jnp.mean(v * v, axis=-1, keepdims=True) + norm_eps)
    inverse_one = [inverse_of(v) for v in residual]
    pieces = gather_near(joined([(v * r).astype(BF) for v, r in zip(residual, inverse_one)]))
    pieces = gather_far(pieces)

    def in_chunks(pieces):
        size = pieces[0].shape[0] // 2
        return [
            joined([v[k * size : (k + 1) * size] for v in pieces[:3]] + [pieces[3 + k]])
            for k in range(2)
        ]

    pieces, w_qkv, grad_out = meet(pieces, w_qkv, cotangent)
    (queries, mine, normed), grad_out = meet(
        project(pieces, w_qkv, cosine, sine_vals),
        cross(parts_of(quarters(grad_out))),
    )
    theirs = lax.ppermute(mine, "c", [(0, 1), (1, 0)])
    sorted_kv, grad_out, stacked = meet(
        sort_keys(order, mine, theirs), hop_on(grad_out), stacked
    )
    keys, values, keys_t, values_t = sorted_kv
    stacked = stacked.transpose(1, 2, 0, 3).reshape(3, share, width)
    w_ffn = [lax.all_gather(stacked[k], line, axis=0, tiled=True) for k in range(3)]
    attend = lambda q, k, n: attention_forward(tiles, lengths, q, keys, values_t, k, n)
    grad_out = by_chunk(grad_out)
    grad_rows = joined([(branch_scale * v.astype(F32)).astype(BF) for v in grad_out])
    queries, grad_rows = meet(queries, grad_rows)
    (low_a, total_a, peak_a), grad_rows = meet(attend(queries, 0, 4), gather_near(grad_rows))
    branch_a = mul(low_a, w_out).astype(BF)
    branch_a, grad_rows, queries_b = meet(branch_a, grad_rows, queries)
    part_b, far_a = meet(attend(queries_b, 4, 2), scatter_far(branch_a))
    rest_b, near_a, grad_rows = meet(
        attend(queries_b, 6, 2), scatter_near(branch_a, far_a), gather_far(grad_rows)
    )
    low_b, total_b, peak_b = (joined([v, w]) for v, w in zip(part_b, rest_b))
    branch_b = mul(low_b, w_out).astype(BF)
    attended = joined([low_a, low_b])
    log_total = joined([total_a, total_b])
    peaks = joined([peak_a, peak_b])
    grad_rows = in_chunks(grad_rows)

    def second_norm(k, branch):
        after_attn = residual[k] + branch_scale * branch
        inverse_two = inverse_of(after_attn)
        return after_attn, inverse_two, (after_attn * inverse_two * gain_two).astype(BF)

    def hidden_layer(grad_mixed, normed_two):
        gate_pre = mul(normed_two, w_ffn[0], NT)
        up_pre = mul(normed_two, w_ffn[1], NT)
        mixed = (jax.nn.silu(gate_pre) * up_pre).astype(BF)
        return (mixed,) + gate_grads(grad_mixed, gate_pre, up_pre)

    def hidden_back(hidden):
        return (mul(hidden[1], w_ffn[0]) + mul(hidden[2], w_ffn[1])).astype(BF)

    def second_back(k, total, state):
        grad_gain, grad_second = norm_backward(total, state[0], state[1], gain_two)
        grad_resid = grad_out[k].astype(F32) + grad_second
        return grad_gain, grad_resid, (branch_scale * grad_resid).astype(BF)

    state_a = second_norm(0, scatter_sum(branch_a, near_a))
    own, rows_a, rows_b = meet(state_a[2], grad_rows[0], grad_rows[1])
    gather, mixed_a, rows_b, branch_b = meet(
        gather_near(own), mul(rows_a, w_ffn[2], NT), rows_b, branch_b
    )
    gather, far, mixed_b = meet(
        gather_far(gather), scatter_far(branch_b), mul(rows_b, w_ffn[2], NT)
    )
    normed_a = joined(gather)
    hidden_a, near = meet(hidden_layer(mixed_a, normed_a), scatter_near(branch_b, far))
    state_b = second_norm(1, scatter_sum(branch_b, near))
    hidden_a, own = meet(hidden_a, state_b[2])
    rest_a, gather = meet(hidden_back(hidden_a), gather_near(own))
    first = mul(hidden_a[1], normed_a, TN)
    gather, far, gate_a = meet(gather_far(gather), scatter_far(rest_a), first)
    normed_b = joined(gather)
    hidden_b, near = meet(hidden_layer(mixed_b, normed_b), scatter_near(rest_a, far))
    back_a = second_back(0, scatter_sum(rest_a, near), state_a)
    hidden_b, own = meet(hidden_b, back_a[2])
    rest_b, gather_a = meet(hidden_back(hidden_b), gather_near(own))
    grad_gate = (gate_a + mul(hidden_b[1], normed_b, TN)).astype(BF)
    up_a = mul(hidden_a[2], normed_a, TN)
    gather_a, far, grad_gate, up_a = meet(
        gather_far(gather_a), scatter_far(rest_b), grad_gate, up_a
    )
    grad_up = (up_a + mul(hidden_b[2], normed_b, TN)).astype(BF)
    down_a = mul(hidden_a[0], rows_a, TN)
    near, grad_up, down_a = meet(scatter_near(rest_b, far), grad_up, down_a)
    back_b = second_back(1, scatter_sum(rest_b, near), state_b)
    own, mixed_b_rows, down_a = meet(back_b[2], hidden_b[0], down_a)
    grad_down = (down_a + mul(mixed_b_rows, rows_b, TN)).astype(BF)
    gather_b, grad_down, ffn_b = meet(
        gather_near(own), grad_down, mul(mixed_b_rows, w_ffn[2]).astype(BF)
    )
    gather_b, ffn_a = meet(gather_far(gather_b), mul(hidden_a[0], w_ffn[2]).astype(BF))
    branch_ffn = [ffn_a, ffn_b]
    sum_rows = lambda v: lax.psum_scatter(v, line, scatter_dimension=0, tiled=True)
    grad_pieces = gather_a + gather_b
    grad_gain_two = back_a[0] + back_b[0]
    grad_resid = [back_a[1], back_b[1]]

    grad_pieces, branch_ffn, grad_gate = meet(grad_pieces, branch_ffn, sum_rows(grad_gate))
    (grad_heads, row_delta, grad_w_part), far, grad_up = meet(
        attention_delta(grad_pieces, w_out, attended),
        scatter_far_both(branch_ffn),
        sum_rows(grad_up),
    )

    far_order = jnp.concatenate([tiles_far, tiles])
    gain_rows = grad_gain_two.astype(BF).reshape(4, 8, 1, thin).transpose(1, 0, 2, 3)
    peak = jnp.max(peaks, axis=(0, 2))
    peak_high = lax.reduce_precision(peak, 8, 7)
    peak_rows = jnp.stack([peak_high.astype(BF), (peak - peak_high).astype(BF)])
    mine_slot = (jnp.arange(8) == depth * 2 + core)[None, :, None]
    peak_rows = jnp.where(mine_slot, peak_rows[:, None, :], 0).reshape(2, 8 * NH)
    widen = lambda v: jnp.pad(v, ((0, 0), (0, 0), (0, 0), (0, 3 * GPART - v.shape[3])))
    gain_rows = jnp.concatenate(
        [
            widen(gain_rows),
            widen(jnp.broadcast_to(peak_rows, (8, 4, 2, 8 * NH))),
            jnp.zeros((8, 4, 5, 3 * GPART), BF),
        ],
        axis=2,
    )

    def back_group(g, grads):
        return attention_backward(
            tiles, lengths, queries, grads, log_total, row_delta, keys, values, keys_t, g
        )

    def restore(part):
        return (part[0],) + tuple(restore_keys(far_order, part[1], part[2]))

    def weight_part(grad_qkv):
        proj = mul(normed, grad_qkv, TN).astype(BF).reshape(4, 8, thin, 3 * GPART)
        proj = jnp.concatenate([proj.transpose(1, 0, 2, 3), gain_rows], axis=2)
        return proj.reshape(8 * 4 * (thin + 8), 3 * GPART)

    def sum_line(proj):
        proj = lax.psum_scatter(proj, line, scatter_dimension=0, tiled=True)
        return proj.reshape(4, thin + 8, 3 * GPART)

    trade = lambda v: lax.ppermute(v, "c", [(0, 1), (1, 0)])
    grad_heads, grad_w_part = meet(grad_heads, grad_w_part)
    grad_down = sum_rows(grad_down)
    part_a, grad_heads, near = meet(
        back_group(0, grad_heads),
        grad_heads,
        scatter_near_both(branch_ffn, far),
    )
    grad_w_output = sum_rows(grad_w_part)
    part_a = restore(part_a)
    states = (state_a, state_b)
    output = []
    for k, (state, v) in enumerate(zip(states, branch_ffn)):
        size = state[0].shape[0]
        total = scatter_sum(v, [w[k * size : (k + 1) * size] for w in near])
        output.append(quarters((state[0] + branch_scale * total).astype(BF)))
    output = join_tiles(output)
    output, grad_heads, part_a = meet(output, grad_heads, part_a)
    part_b, grad_heads, hops, far_a, grad_down = meet(
        back_group(1, grad_heads),
        grad_heads,
        hop_back(output),
        trade(part_a[2]),
        grad_down,
    )
    ffn_grads = jnp.stack([grad_gate, grad_up, grad_down])
    ffn_grads = ffn_grads.reshape(3, share, 4, PART).transpose(2, 0, 1, 3)
    part_b = restore(part_b)
    grads_a = unturn(part_a[0], part_a[1], far_a, cosine, sine_vals)
    weights_a = weight_part(grads_a)
    grad_heads, weights_a, hops, part_b, ffn_grads = meet(
        grad_heads, weights_a, hops, part_b, ffn_grads
    )
    part_c, output, far_b, weights_a, grad_w_output = meet(
        back_group(2, grad_heads),
        hop_out(hops),
        trade(part_b[2]),
        sum_line(weights_a),
        grad_w_output,
    )
    part_c, far_b = meet(restore(part_c), far_b)
    grads_b = unturn(part_b[0], part_b[1], far_b, cosine, sine_vals)
    weights_b, far_c, ffn_grads = meet(
        weight_part(grads_b), trade(part_c[2]), cross_whole(ffn_grads)
    )
    output = joined(output)
    grads_c = unturn(part_c[0], part_c[1], far_c, cosine, sine_vals)
    grads = (grads_a, grads_b, grads_c)
    rest_a, grads, weights_a, weights_b = meet(
        unproject(grads, w_qkv, 0), grads, cross_whole(weights_a), sum_line(weights_b)
    )
    weights_c, far_a, grads = meet(weight_part(grads[2]), scatter_far(rest_a), grads)
    weights_c = sum_line(weights_c)
    rest_b, near_a = meet(unproject(grads, w_qkv, 1), scatter_near(rest_a, far_a))
    far_b = scatter_far(rest_b)

    def first_back(k, total):
        grad_first = inverse_one[k] * total - residual[k] * inverse_one[k] ** 3 * jnp.mean(
            total * residual[k], axis=-1, keepdims=True
        )
        return (grad_resid[k] + grad_first).astype(BF)

    hop_a = hop_back(first_back(0, scatter_sum(rest_a, near_a)))
    near_b = scatter_near(rest_b, far_b)
    hop_a, near_b = meet(hop_a, near_b)
    hop_b, hop_a = meet(hop_back(first_back(1, scatter_sum(rest_b, near_b))), hop_out(hop_a))
    grad_input = join_tiles([jnp.stack(hop_a), jnp.stack(hop_out(hop_b))]).astype(F32)
    ffn_grads = ffn_grads.astype(F32)
    ffn_grads = jnp.concatenate([ffn_grads[k, :, :n] for k, n in enumerate(sizes)], axis=1)
    grad_ffn_gain = jnp.sum(weights_a[:, thin, :thin].astype(F32), axis=0)
    weights_bc = over("p", jnp.concatenate([weights_b, weights_c], axis=2))
    proj = finish(
        (weights_a, weights_bc), (w_query, w_key, w_value), gain_f[:, None]
    )
    grad_attn_gain = proj[3][:, 0]

    maxima = jnp.sum(weights_a[:, thin + 1 : thin + 3, : 8 * NH].astype(F32), axis=1)
    maxima = jnp.max(maxima.reshape(4, 8, NH), axis=1).reshape(HEADS)
    limit_value = clip_threshold[0].astype(F32)
    clip_factor = jnp.sqrt(limit_value / jnp.maximum(maxima, limit_value))
    column_factor = jnp.repeat(clip_factor, HDIM)
    return (
        output,
        grad_input,
        proj[0],
        proj[1],
        proj[2],
        grad_w_output.astype(F32),
        ffn_grads[0].T,
        ffn_grads[1].T,
        ffn_grads[2],
        grad_attn_gain,
        grad_ffn_gain,
        maxima,
        clip_factor,
        w_query.astype(F32) * column_factor[None, :],
        w_key.astype(F32) * column_factor[None, :],
    )


def specs(grp, ctx):
    every = grp + ctx
    ins = [P(every, None)] * 6 + [P(grp, ctx), P(grp, ctx), P(ctx, grp), P(every), P(every)]
    ins += [P(grp, None), P(grp, None), P()]
    outs = [P(every, None)] * 6 + [P(grp, ctx), P(grp, ctx), P(ctx, grp), P(every), P(every)]
    outs += [P(), P(), P(every, None), P(every, None)]
    return tuple(ins), tuple(outs)


def solution(mesh):
    if mesh.shape["grp"] == 4 and mesh.shape["ctx"] == 8:
        mesh = Mesh(mesh.devices.reshape(4, 4, 2), ("p", "z", "c"))
        body, (in_specs, out_specs) = inner, specs(("p",), ("z", "c"))
    else:
        body, (in_specs, out_specs) = local, specs(("grp",), ("ctx",))
    return jax.shard_map(body, mesh=mesh, in_specs=in_specs, out_specs=out_specs, check_vma=False)
```

```python
import functools
import math

import jax
import jax.numpy as jnp
from jax import lax
from jax.experimental import pallas as pl
from jax.experimental.pallas import tpu as pltpu
from jax.sharding import Mesh
from jax.sharding import PartitionSpec as P

HEADS = 36
HDIM = 64
PLEN = 2048
CLEN = 256
NCONT = 8
BLK = 64
FAMTOK = 4096

F32 = jnp.float32
BF = jnp.bfloat16
NH = HEADS // 4
PART = NH * HDIM
GROUP = 3
GPART = GROUP * HDIM
QB_BACK = 512
QB = 256
KB = 1024
KB_FWD = 1024
HEAD_STEP = 9
NT = (((1,), (1,)), ((), ()))
NN = (((1,), (0,)), ((), ()))
TN = (((0,), (0,)), ((), ()))
VMEM_ROOM = 56 * 1024 * 1024


branch_scale = 1.4 / math.sqrt(40.0)
norm_eps = 1e-05
rope_base = 10000.0
masked_value = -1e30


def rope_angles(position):
    half_dim = HDIM // 2
    frequency = rope_base ** (-(jnp.arange(half_dim, dtype=jnp.float32) * (2.0 / HDIM)))
    angles = position.astype(jnp.float32)[:, None] * frequency[None, :]
    return (jnp.cos(angles)[:, None, :], jnp.sin(angles)[:, None, :])


def rotate(values, cosine, sine_vals, turn_sign):
    row_count = values.shape[0]
    shaped = values.reshape(row_count, HEADS, HDIM)
    leading = shaped[..., : HDIM // 2]
    trailing = shaped[..., HDIM // 2 :]
    turned = jnp.concatenate(
        [
            leading * cosine - turn_sign * trailing * sine_vals,
            trailing * cosine + turn_sign * leading * sine_vals,
        ],
        axis=-1,
    )
    return turned.reshape(row_count, HEADS * HDIM)


def token_facts(logical, lengths):
    family = logical // FAMTOK
    offset = logical % FAMTOK
    prompt = offset < PLEN
    member = jnp.clip((offset - PLEN) // CLEN, 0, NCONT - 1)
    inside = offset - PLEN - member * CLEN
    seq_id = jnp.where(prompt, -1, family * NCONT + member)
    numbers = jnp.arange(lengths.shape[0], dtype=jnp.int32)
    live_len = jnp.sum(jnp.where(seq_id[:, None] == numbers[None, :], lengths[None, :], 0), axis=1)
    is_live = prompt | (inside < live_len)
    position = jnp.where(prompt, offset, PLEN + inside)
    return (family, offset, prompt, seq_id, is_live, position)


def visible(query_facts, key_part):
    same_family = query_facts[0][:, None] == key_part[0][None, :]
    causal = key_part[1][None, :] <= query_facts[1][:, None]
    reaches = (
        key_part[2][None, :]
        | (key_part[3][None, :] == query_facts[3][:, None]) & key_part[4][None, :]
    )
    return same_family & causal & reaches


def key_slice(keys_heads, values_heads, key_facts, query_facts, first_row, span_rows):
    key_block = lax.dynamic_slice_in_dim(keys_heads, first_row, span_rows, 0)
    value_block = lax.dynamic_slice_in_dim(values_heads, first_row, span_rows, 0)
    key_part = tuple(
        (
            lax.dynamic_slice_in_dim(member_array, first_row, span_rows, 0)
            for member_array in key_facts
        )
    )
    return (key_block, value_block, visible(query_facts, key_part))


def block_scores(query_heads, key_block, visible_mask):
    scores = jnp.einsum(
        "qhd,khd->hqk", query_heads, key_block, preferred_element_type=jnp.float32
    ) * HDIM ** (-0.5)
    return jnp.where(visible_mask[None], scores, masked_value)


def score_grads(
    query_heads, grad_heads, log_total, row_delta, key_block, value_block, visible_mask
):
    scores = block_scores(query_heads, key_block, visible_mask)
    prob_table = jnp.where(visible_mask[None], jnp.exp(scores - log_total[:, :, None]), 0.0)
    grad_probs = jnp.einsum(
        "qhd,khd->hqk", grad_heads, value_block, preferred_element_type=jnp.float32
    )
    grad_scores = (prob_table * (grad_probs - row_delta[:, :, None])).astype(jnp.bfloat16)
    return (prob_table.astype(jnp.bfloat16), grad_scores)


def gate_grads(grad_mixed, gate_pre, up_pre):
    sigmoid = jax.nn.sigmoid(gate_pre)
    grad_gate = grad_mixed * up_pre * sigmoid * (1.0 + gate_pre * (1.0 - sigmoid))
    grad_up = grad_mixed * gate_pre * sigmoid
    return (grad_gate.astype(jnp.bfloat16), grad_up.astype(jnp.bfloat16))


def norm_backward(grad_normed, values, inverse, gain):
    scaled = grad_normed * gain[None, :]
    grad_gain = jnp.sum(grad_normed * values * inverse, axis=0)
    grad_values = inverse * scaled - values * inverse**3 * jnp.mean(
        scaled * values, axis=-1, keepdims=True
    )
    return (grad_gain, grad_values)


def attention_weights(w_query, w_key, w_value, w_output, attn_gain, ffn_gain):
    return (
        lax.all_gather(w_query, ("grp", "ctx"), axis=0, tiled=True),
        lax.all_gather(w_key, ("grp", "ctx"), axis=0, tiled=True),
        lax.all_gather(w_value, ("grp", "ctx"), axis=0, tiled=True),
        lax.all_gather(w_output, ("grp", "ctx"), axis=0, tiled=True),
        lax.all_gather(attn_gain, ("grp", "ctx"), axis=0, tiled=True),
        lax.all_gather(ffn_gain, ("grp", "ctx"), axis=0, tiled=True),
    )


def ffn_rows_gather(w_gate, w_up, w_down):
    return (
        lax.all_gather(w_gate, "grp", axis=0, tiled=True),
        lax.all_gather(w_up, "grp", axis=0, tiled=True),
        lax.all_gather(w_down, "grp", axis=1, tiled=True),
    )


def local(
    tokens_in,
    cotangent,
    w_query,
    w_key,
    w_value,
    w_output,
    w_gate,
    w_up,
    w_down,
    attn_gain,
    ffn_gain,
    cont_len,
    deal_order,
    clip_threshold,
):
    row_count = tokens_in.shape[0]
    model_width = tokens_in.shape[1]
    tile_count = deal_order.shape[1]
    group_rows = tile_count * BLK
    lengths = cont_len[0]
    my_index = lax.axis_index("ctx")
    tile_offsets = jnp.arange(BLK, dtype=jnp.int32)
    stored_logical = (deal_order[0][:, None] * BLK + tile_offsets[None, :]).reshape(group_rows)
    key_facts = token_facts(stored_logical, lengths)
    query_facts = tuple(
        (
            lax.dynamic_slice_in_dim(member_array, my_index * row_count, row_count, 0)
            for member_array in key_facts
        )
    )
    cosine, sine_vals = rope_angles(query_facts[5])
    key_step = math.gcd(group_rows, 512)
    key_blocks = group_rows // key_step
    full_query, full_key, full_value, full_output, gain_one, gain_two = attention_weights(
        w_query, w_key, w_value, w_output, attn_gain, ffn_gain
    )
    residual = tokens_in.astype(jnp.float32)
    inverse_one = lax.rsqrt(jnp.mean(residual * residual, axis=-1, keepdims=True) + norm_eps)
    gain_one_f = gain_one.astype(jnp.float32)
    gain_two_f = gain_two.astype(jnp.float32)
    normed_one = (residual * inverse_one * gain_one_f).astype(jnp.bfloat16)
    query_rot = rotate(
        jnp.dot(normed_one, full_query, preferred_element_type=jnp.float32), cosine, sine_vals, 1.0
    ).astype(jnp.bfloat16)
    key_rot = rotate(
        jnp.dot(normed_one, full_key, preferred_element_type=jnp.float32), cosine, sine_vals, 1.0
    ).astype(jnp.bfloat16)
    value_low = jnp.dot(normed_one, full_value, preferred_element_type=jnp.float32).astype(
        jnp.bfloat16
    )
    keys_all, values_all = (
        lax.all_gather(key_rot, "ctx", axis=0, tiled=True),
        lax.all_gather(value_low, "ctx", axis=0, tiled=True),
    )
    query_heads = query_rot.reshape(row_count, HEADS, HDIM)
    keys_heads = keys_all.reshape(group_rows, HEADS, HDIM)
    values_heads = values_all.reshape(group_rows, HEADS, HDIM)

    def stats_step(block_index, state_carry):
        key_block, value_block, visible_mask = key_slice(
            keys_heads, values_heads, key_facts, query_facts, block_index * key_step, key_step
        )

        def stats_busy(carry):
            run_max, run_sum, head_max = carry
            scores = block_scores(query_heads, key_block, visible_mask)
            block_max = jnp.max(scores, axis=2)
            new_max = jnp.maximum(run_max, block_max)
            exp_table = jnp.where(visible_mask[None], jnp.exp(scores - new_max[:, :, None]), 0.0)
            new_sum = run_sum * jnp.exp(run_max - new_max) + jnp.sum(exp_table, axis=2)
            return (new_max, new_sum, jnp.maximum(head_max, jnp.max(block_max, axis=1)))

        return lax.cond(jnp.any(visible_mask), stats_busy, lambda carry: carry, state_carry)

    start_state = (
        jnp.full((HEADS, row_count), masked_value, jnp.float32),
        jnp.zeros((HEADS, row_count), jnp.float32),
        jnp.full((HEADS,), masked_value, jnp.float32),
    )
    run_max, run_sum, head_max = lax.fori_loop(0, key_blocks, stats_step, start_state)
    log_total = run_max + jnp.log(run_sum)

    def output_step(block_index, running):
        key_block, value_block, visible_mask = key_slice(
            keys_heads, values_heads, key_facts, query_facts, block_index * key_step, key_step
        )

        def output_busy(total):
            scores = block_scores(query_heads, key_block, visible_mask)
            prob_low = jnp.where(
                visible_mask[None], jnp.exp(scores - log_total[:, :, None]), 0.0
            ).astype(jnp.bfloat16)
            return total + jnp.einsum(
                "hqk,khd->qhd", prob_low, value_block, preferred_element_type=jnp.float32
            )

        return lax.cond(jnp.any(visible_mask), output_busy, lambda total: total, running)

    attended = lax.fori_loop(
        0, key_blocks, output_step, jnp.zeros((row_count, HEADS, HDIM), jnp.float32)
    )
    attn_low = attended.reshape(row_count, model_width).astype(jnp.bfloat16)
    after_attn = residual + branch_scale * jnp.dot(
        attn_low, full_output, preferred_element_type=jnp.float32
    )
    inverse_two = lax.rsqrt(jnp.mean(after_attn * after_attn, axis=-1, keepdims=True) + norm_eps)
    normed_two = (after_attn * inverse_two * gain_two_f).astype(jnp.bfloat16)
    gate_cols, up_cols, down_cols = ffn_rows_gather(w_gate, w_up, w_down)
    normed_rows = lax.all_gather(normed_two, "ctx", axis=0, tiled=True)
    gate_pre = jnp.dot(normed_rows, gate_cols, preferred_element_type=jnp.float32)
    up_pre = jnp.dot(normed_rows, up_cols, preferred_element_type=jnp.float32)
    mixed = (jax.nn.silu(gate_pre) * up_pre).astype(jnp.bfloat16)
    branch_ffn = lax.psum_scatter(
        jnp.dot(mixed, down_cols, preferred_element_type=jnp.float32).astype(jnp.bfloat16),
        "ctx",
        scatter_dimension=0,
        tiled=True,
    ).astype(jnp.float32)
    output = (after_attn + branch_scale * branch_ffn).astype(jnp.bfloat16)
    grad_out = cotangent.astype(jnp.float32)
    grad_branch = (branch_scale * grad_out).astype(jnp.bfloat16)
    gate_again, up_again, down_again = ffn_rows_gather(w_gate, w_up, w_down)
    grad_rows = lax.all_gather(grad_branch, "ctx", axis=0, tiled=True)
    grad_mixed = jnp.dot(grad_rows, down_again.T, preferred_element_type=jnp.float32)
    grad_down = jnp.dot(mixed.T, grad_rows, preferred_element_type=jnp.float32)
    grad_gate_low, grad_up_low = gate_grads(grad_mixed, gate_pre, up_pre)
    grad_gate = jnp.dot(normed_rows.T, grad_gate_low, preferred_element_type=jnp.float32)
    grad_up = jnp.dot(normed_rows.T, grad_up_low, preferred_element_type=jnp.float32)
    grad_normed_two = lax.psum_scatter(
        (
            jnp.dot(grad_gate_low, gate_again.T, preferred_element_type=jnp.float32)
            + jnp.dot(grad_up_low, up_again.T, preferred_element_type=jnp.float32)
        ).astype(jnp.bfloat16),
        "ctx",
        scatter_dimension=0,
        tiled=True,
    ).astype(jnp.float32)
    ffn_stack = jnp.stack([grad_gate, grad_up, grad_down.T], axis=0)
    ffn_summed = lax.psum_scatter(
        ffn_stack.astype(jnp.bfloat16), "grp", scatter_dimension=1, tiled=True
    ).astype(jnp.float32)
    grad_gain_two, grad_second = norm_backward(grad_normed_two, after_attn, inverse_two, gain_two_f)
    grad_resid = grad_out + grad_second
    back_query, back_key, back_value, back_output, back_gain_one, back_gain_two = attention_weights(
        w_query, w_key, w_value, w_output, attn_gain, ffn_gain
    )
    grad_branch_attn = (branch_scale * grad_resid).astype(jnp.bfloat16)
    grad_w_output = jnp.dot(attn_low.T, grad_branch_attn, preferred_element_type=jnp.float32)
    grad_attn = jnp.dot(grad_branch_attn, back_output.T, preferred_element_type=jnp.float32).astype(
        jnp.bfloat16
    )
    grad_heads = grad_attn.reshape(row_count, HEADS, HDIM)
    row_delta = jnp.sum(grad_heads.astype(jnp.float32) * attended, axis=2).T

    def back_step(grad_q, block_index):
        key_block, value_block, visible_mask = key_slice(
            keys_heads, values_heads, key_facts, query_facts, block_index * key_step, key_step
        )

        def back_busy(current):
            prob_low, grad_scores = score_grads(
                query_heads, grad_heads, log_total, row_delta, key_block, value_block, visible_mask
            )
            updated = current + jnp.einsum(
                "hqk,khd->qhd", grad_scores, key_block, preferred_element_type=jnp.float32
            )
            grad_keys = jnp.einsum(
                "hqk,qhd->khd", grad_scores, query_heads, preferred_element_type=jnp.float32
            ) * HDIM ** (-0.5)
            grad_values = jnp.einsum(
                "hqk,qhd->khd", prob_low, grad_heads, preferred_element_type=jnp.float32
            )
            return (
                updated,
                (
                    grad_keys.reshape(key_step, model_width),
                    grad_values.reshape(key_step, model_width),
                ),
            )

        def quiet(current):
            empty = jnp.zeros((key_step, model_width), jnp.float32)
            return (current, (empty, empty))

        return lax.cond(jnp.any(visible_mask), back_busy, quiet, grad_q)

    grad_q_heads, key_terms = lax.scan(
        back_step,
        jnp.zeros((row_count, HEADS, HDIM), jnp.float32),
        jnp.arange(key_blocks, dtype=jnp.int32),
    )
    key_sum, value_sum = (
        lax.psum_scatter(
            key_terms[0].reshape(group_rows, model_width).astype(jnp.bfloat16),
            "ctx",
            scatter_dimension=0,
            tiled=True,
        ).astype(jnp.float32),
        lax.psum_scatter(
            key_terms[1].reshape(group_rows, model_width).astype(jnp.bfloat16),
            "ctx",
            scatter_dimension=0,
            tiled=True,
        ).astype(jnp.float32),
    )
    grad_query_rot = grad_q_heads.reshape(row_count, model_width) * HDIM ** (-0.5)
    grad_query = rotate(grad_query_rot, cosine, sine_vals, -1.0).astype(jnp.bfloat16)
    grad_key = rotate(key_sum, cosine, sine_vals, -1.0).astype(jnp.bfloat16)
    grad_value = value_sum.astype(jnp.bfloat16)
    grad_w_query = jnp.dot(normed_one.T, grad_query, preferred_element_type=jnp.float32)
    grad_w_key = jnp.dot(normed_one.T, grad_key, preferred_element_type=jnp.float32)
    grad_w_value = jnp.dot(normed_one.T, grad_value, preferred_element_type=jnp.float32)
    grad_normed_one = (
        jnp.dot(grad_query, back_query.T, preferred_element_type=jnp.float32)
        + jnp.dot(grad_key, back_key.T, preferred_element_type=jnp.float32)
        + jnp.dot(grad_value, back_value.T, preferred_element_type=jnp.float32)
    )
    grad_gain_one, grad_first = norm_backward(grad_normed_one, residual, inverse_one, gain_one_f)
    grad_input = grad_resid + grad_first
    gain_pair = jnp.stack([grad_gain_one, grad_gain_two], axis=1)
    summed = (
        lax.psum_scatter(grad_w_query, ("grp", "ctx"), scatter_dimension=0, tiled=True),
        lax.psum_scatter(grad_w_key, ("grp", "ctx"), scatter_dimension=0, tiled=True),
        lax.psum_scatter(grad_w_value, ("grp", "ctx"), scatter_dimension=0, tiled=True),
        lax.psum_scatter(grad_w_output, ("grp", "ctx"), scatter_dimension=0, tiled=True),
        lax.psum_scatter(gain_pair, ("grp", "ctx"), scatter_dimension=0, tiled=True),
    )
    maxima = lax.pmax(head_max, ("grp", "ctx"))
    limit_value = clip_threshold[0].astype(jnp.float32)
    clip_factor = jnp.sqrt(limit_value / jnp.maximum(maxima, limit_value))
    column_factor = jnp.repeat(clip_factor, HDIM)
    clipped_query = w_query.astype(jnp.float32) * column_factor[None, :]
    clipped_key = w_key.astype(jnp.float32) * column_factor[None, :]
    return (
        output,
        grad_input,
        summed[0],
        summed[1],
        summed[2],
        summed[3],
        ffn_summed[0],
        ffn_summed[1],
        ffn_summed[2].T,
        summed[4][:, 0],
        summed[4][:, 1],
        maxima,
        clip_factor,
        clipped_query,
        clipped_key,
    )


def mul(left, right, dims=NN):
    return lax.dot_general(left, right, dims, preferred_element_type=F32)


def room():
    return pltpu.CompilerParams(vmem_limit_bytes=VMEM_ROOM)


def cost(flops, sent):
    return pl.CostEstimate(flops=int(flops), bytes_accessed=int(sent), transcendentals=0)


def straighten(w_ref, w_sc, thin):
    for i in range(4):
        for k in range(8):
            w_sc[(i * 8 + k) * thin : (i * 8 + k + 1) * thin, :] = w_ref[k, i, :thin, :]


def swing(values, cosine, sine_vals):
    lane = lax.broadcasted_iota(jnp.int32, values.shape, 1)
    other = jnp.where(
        lane % HDIM < HDIM // 2,
        pltpu.roll(values, 2 * HDIM - HDIM // 2, 1),
        pltpu.roll(values, HDIM // 2, 1),
    )
    return values * cosine + other * sine_vals


def fetch_rows(pieces, x_sc):
    step = pl.program_id(0)
    half = QB // 2
    for k in range(8):
        chunk, slot = k // 4, k % 4

        @pl.when(step == k)
        def _():
            if len(pieces) == 5 and slot < 3:
                x_sc[...] = pieces[slot][chunk * QB : (chunk + 1) * QB, :]
            elif len(pieces) == 5:
                x_sc[...] = pieces[3 + chunk][...]
            elif slot < 3:
                x_sc[...] = pieces[chunk * 5 + slot][...]
            else:
                x_sc[:half] = pieces[chunk * 5 + 3][...]
                x_sc[half:] = pieces[chunk * 5 + 4][...]


def whole(shape):
    return pl.BlockSpec(shape, lambda i: (0,) * len(shape), pipeline_mode=pl.Buffered(1))


def project_kernel(*refs):
    w_ref, cos_ref, sin_ref, q_ref, kv_ref, x_sc, w_sc = refs[5:]
    thin = w_sc.shape[0] // 32
    fetch_rows(refs[:5], x_sc)

    @pl.when(pl.program_id(0) == 0)
    def _():
        straighten(w_ref, w_sc, thin)

    y = mul(x_sc[...], w_sc[...])
    cosine, sine_vals = cos_ref[...], sin_ref[...]
    for k in range(NH):
        piece = swing(y[:, k * 128 : (k + 1) * 128], cosine, sine_vals)
        for j in range(2):
            head = 2 * k + j
            if head < NH:
                q_ref[head] = (piece[:, j * HDIM : (j + 1) * HDIM] * 0.125).astype(BF)
        if 2 * k + 1 > NH:
            kv_ref[:, k * 128 : (k + 1) * 128] = piece.astype(BF)
        elif 2 * k + 1 == NH:
            kv_ref[:, k * 128 + HDIM : (k + 1) * 128] = piece[:, HDIM:].astype(BF)
    kv_ref[:, :PART] = y[:, 2 * PART :].astype(BF)


def project(normed, w_all, cosine, sine_vals):
    rows = sum(v.shape[0] for v in normed)
    width = normed[0].shape[1]
    full = w_all.shape
    return pl.pallas_call(
        project_kernel,
        out_shape=[
            jax.ShapeDtypeStruct((NH, rows, HDIM), BF),
            jax.ShapeDtypeStruct((rows, 2 * PART), BF),
            jax.ShapeDtypeStruct((rows, width), BF),
        ],
        grid=(rows // QB,),
        in_specs=[whole(v.shape) for v in normed]
        + [
            whole(full),
            pl.BlockSpec((QB, 128), lambda i: (i, 0)),
            pl.BlockSpec((QB, 128), lambda i: (i, 0)),
        ],
        out_specs=[
            pl.BlockSpec((NH, QB, HDIM), lambda i: (0, i, 0)),
            pl.BlockSpec((QB, 2 * PART), lambda i: (i, 0)),
            pl.BlockSpec((QB, width), lambda i: (i % 4 * 2 + i // 4, 0)),
        ],
        scratch_shapes=[pltpu.VMEM((width, full[3]), BF)],
        compiler_params=room(),
        cost_estimate=cost(2 * rows * width * full[3], 2 * (rows * width + width * full[3] + rows * 5 * PART)),
        name="project",
    )(*normed, w_all, cosine, sine_vals)


def sort_kernel(order_ref, *refs):
    k_ref, v_ref, kt_ref, vt_ref = refs[16:]
    first = pl.program_id(0) * 8
    for j in range(8):
        from_mine = order_ref[first + j] < 32
        tile = jnp.where(from_mine, refs[j][0], refs[8 + j][0])
        rows = slice(j * BLK, (j + 1) * BLK)
        for h in range(NH):
            v_ref[h, rows, :] = tile[:, h * HDIM : (h + 1) * HDIM]
            k_ref[h, rows, :] = tile[:, PART + h * HDIM : PART + (h + 1) * HDIM]
    for h in range(NH):
        kt_ref[h] = k_ref[h].T
        vt_ref[h] = v_ref[h].T


def sort_keys(order, mine, theirs):
    count = order.shape[0]
    shape = (1, BLK, 2 * PART)
    near = lambda j: pl.BlockSpec(shape, lambda i, o: (jnp.minimum(o[i * 8 + j], 31), 0, 0))
    far = lambda j: pl.BlockSpec(shape, lambda i, o: (jnp.maximum(o[i * 8 + j] - 32, 0), 0, 0))
    return pl.pallas_call(
        sort_kernel,
        out_shape=[jax.ShapeDtypeStruct((NH, count * BLK, HDIM), BF)] * 2
        + [jax.ShapeDtypeStruct((NH, HDIM, count * BLK), BF)] * 2,
        grid_spec=pltpu.PrefetchScalarGridSpec(
            num_scalar_prefetch=1,
            grid=(count // 8,),
            in_specs=[near(j) for j in range(8)] + [far(j) for j in range(8)],
            out_specs=[pl.BlockSpec((NH, 8 * BLK, HDIM), lambda i, o: (0, i, 0))] * 2
            + [pl.BlockSpec((NH, HDIM, 8 * BLK), lambda i, o: (0, 0, i))] * 2,
        ),
        compiler_params=room(),
        cost_estimate=cost(0, 64 * count * BLK * PART),
        name="sort_keys",
    )(order, *([mine.reshape(32, BLK, 2 * PART)] * 8), *([theirs.reshape(32, BLK, 2 * PART)] * 8))


def lane_tile(vals):
    shape = (1, len(vals) * BLK)
    lane = lax.broadcasted_iota(jnp.int32, shape, 1)
    out = jnp.full(shape, vals[-1], jnp.int32)
    for j in range(len(vals) - 2, -1, -1):
        out = jnp.where(lane < (j + 1) * BLK, vals[j], out)
    return out, lane & (BLK - 1)


def block_facts(tiles_ref, len_ref, block, step, size):
    half_tiles = PLEN // BLK
    count = size // BLK
    t = [tiles_ref[block * count + j] for j in range(count)]
    tile, within = lane_tile(t)
    qpos = tile * BLK + within
    tmax = functools.reduce(jnp.maximum, t)
    tmin = functools.reduce(jnp.minimum, t)
    per = step // BLK
    is_cont = t[0] >= half_tiles
    n_all = jnp.where(is_cont, PLEN // step, tmax // per + 1)
    n_free = jnp.where(is_cont, PLEN // step, tmin // per)
    conts = [jnp.maximum(v - half_tiles, 0) // 4 for v in t]
    lens = lane_tile([len_ref[v] for v in conts])[0]
    qin = qpos - PLEN - lane_tile(conts)[0] * CLEN
    starts = [pl.multiple_of(PLEN + v * CLEN, CLEN) for v in conts]
    kin = lax.broadcasted_iota(jnp.int32, (CLEN, size), 0)
    seen = lambda: (kin <= qin) & (kin < lens)
    return qpos, is_cont, n_all, n_free, starts, seen


def forward_kernel(
    tiles_ref, len_ref, q_ref, k_ref, vt_sc, o_ref, lse_ref, mx_ref, ot_sc, shift
):
    block = pl.program_id(0) + shift
    qpos, is_cont, n_all, n_free, starts, seen = block_facts(
        tiles_ref, len_ref, block, KB_FWD, QB
    )

    def heads(group, carry):
        hs = [group * HEAD_STEP + j for j in range(HEAD_STEP)]
        qs = [q_ref[h] for h in hs]

        def update(scores, states, weigh):
            out = []
            for n, (s, (m, l, acc)) in enumerate(zip(scores, states)):
                mn = jnp.maximum(m, jnp.max(s, axis=0, keepdims=True))
                p = jnp.exp(s - mn)
                al = jnp.exp(m - mn)
                out.append(
                    (
                        mn,
                        l * al + jnp.sum(p, axis=0, keepdims=True),
                        acc * al + weigh(n, p.astype(BF)),
                    )
                )
            return tuple(out)

        def step(kb, states, masked):
            base = pl.multiple_of(kb * KB_FWD, KB_FWD)
            rows = pl.ds(base, KB_FWD)
            scores = [mul(k_ref[h, rows, :], q, NT) for h, q in zip(hs, qs)]
            if masked:
                kpos = base + lax.broadcasted_iota(jnp.int32, (KB_FWD, QB), 0)
                vis = kpos <= qpos
                scores = [jnp.where(vis, s, masked_value) for s in scores]
            return update(scores, states, lambda n, p: mul(vt_sc[hs[n], :, rows], p))

        states = tuple(
            (
                jnp.full((1, QB), masked_value, F32),
                jnp.zeros((1, QB), F32),
                jnp.zeros((HDIM, QB), F32),
            )
            for _ in hs
        )
        states = lax.fori_loop(0, n_free, functools.partial(step, masked=False), states)
        states = lax.fori_loop(n_free, n_all, functools.partial(step, masked=True), states)

        def own(states):
            vis = seen()
            cols = lambda x, j: x[:, j * BLK : (j + 1) * BLK]
            scores = []
            for h, q in zip(hs, qs):
                s = [
                    mul(k_ref[h, pl.ds(starts[j], CLEN), :], q[j * BLK : (j + 1) * BLK], NT)
                    for j in range(4)
                ]
                scores.append(jnp.where(vis, jnp.concatenate(s, axis=1), masked_value))
            return update(
                scores,
                states,
                lambda n, p: jnp.concatenate(
                    [
                        mul(vt_sc[hs[n], :, pl.ds(starts[j], CLEN)], cols(p, j))
                        for j in range(4)
                    ],
                    axis=1,
                ),
            )

        states = lax.cond(is_cont, own, lambda s: s, states)
        for h, (m, l, acc) in zip(hs, states):
            ot_sc[h] = acc / l
            lse_ref[0, pl.ds(h, 1), :] = m + jnp.log(l)
            mx_ref[0, pl.ds(h, 1), :] = m
        return carry

    lax.fori_loop(0, NH // HEAD_STEP, heads, 0)
    for h in range(NH):
        o_ref[:, h * HDIM : (h + 1) * HDIM] = ot_sc[h].T.astype(BF)


def attention_forward(tiles, lengths, queries, keys, values_t, shift, count):
    rows = count * QB
    span = keys.shape[1]
    once = lambda *shape: pl.BlockSpec(
        shape, lambda i, a, b: (0, 0, 0), pipeline_mode=pl.Buffered(1)
    )
    stat = pl.BlockSpec((1, NH, QB), lambda i, a, b: (i, 0, 0))
    return pl.pallas_call(
        functools.partial(forward_kernel, shift=shift),
        out_shape=[
            jax.ShapeDtypeStruct((rows, PART), BF),
            jax.ShapeDtypeStruct((count, NH, QB), F32),
            jax.ShapeDtypeStruct((count, NH, QB), F32),
        ],
        grid_spec=pltpu.PrefetchScalarGridSpec(
            num_scalar_prefetch=2,
            grid=(count,),
            in_specs=[
                pl.BlockSpec((NH, QB, HDIM), lambda i, a, b: (0, i + shift, 0)),
                once(NH, span, HDIM),
                once(NH, HDIM, span),
            ],
            out_specs=[pl.BlockSpec((QB, PART), lambda i, a, b: (i, 0)), stat, stat],
            scratch_shapes=[pltpu.VMEM((NH, HDIM, QB), F32)],
        ),
        compiler_params=room(),
        cost_estimate=cost(rows * PART * PLEN * 20, 16 * span * PART),
        name="attention_forward",
    )(tiles, lengths, queries, keys, values_t)


def delta_kernel(*refs):
    w_ref, o_ref, gh_ref, delta_ref, gw_ref, x_sc = refs[10:]
    step = pl.program_id(0)
    rows = pl.ds(pl.multiple_of(step * QB, QB), QB)
    fetch_rows(refs[:10], x_sc.at[rows, :])
    grad = mul(x_sc[rows, :], w_ref[...], NT).astype(BF)
    for h in range(NH):
        gh_ref[h] = grad[:, h * HDIM : (h + 1) * HDIM]
    prod = grad.astype(F32) * o_ref[rows, :].astype(F32)
    high = prod.astype(BF)
    low = (prod - high.astype(F32)).astype(BF)
    row = lax.broadcasted_iota(jnp.int32, (16, PART), 0)
    col = lax.broadcasted_iota(jnp.int32, (16, PART), 1)
    pick_head = jnp.where(col // HDIM == row, 1.0, 0.0).astype(BF)
    total = mul(pick_head, high, NT) + mul(pick_head, low, NT)
    delta_ref[0] = total[:NH]

    @pl.when(step == pl.num_programs(0) - 1)
    def _():
        for k in range(3):
            cols = slice(k * 768, (k + 1) * 768)
            gw_ref[:, cols] = mul(o_ref[...], x_sc[:, cols], TN).astype(BF)


def attention_delta(grad_branch, w_out, attended):
    rows, width = attended.shape[0], w_out.shape[1]
    count = rows // QB
    return pl.pallas_call(
        delta_kernel,
        out_shape=[
            jax.ShapeDtypeStruct((NH, rows, HDIM), BF),
            jax.ShapeDtypeStruct((count, NH, QB), F32),
            jax.ShapeDtypeStruct((PART, width), BF),
        ],
        grid=(count,),
        in_specs=[whole(v.shape) for v in grad_branch]
        + [whole((PART, width)), whole((rows, PART))],
        out_specs=[
            pl.BlockSpec((NH, QB, HDIM), lambda i: (0, i, 0)),
            pl.BlockSpec((1, NH, QB), lambda i: (i, 0, 0)),
            pl.BlockSpec((PART, width), lambda i: (0, 0)),
        ],
        scratch_shapes=[pltpu.VMEM((rows, width), BF)],
        compiler_params=room(),
        cost_estimate=cost(2 * rows * width * PART, 2 * rows * width),
        name="attention_delta",
    )(*grad_branch, w_out, attended)


def backward_kernel(
    tiles_ref, len_ref, q_ref, g_ref, lse_ref, delta_ref, k_ref, v_ref, kt_ref, dq_ref, dk_out, dv_out,
    dk_ref, dv_ref, first
):
    h = pl.program_id(0) + first
    block = pl.program_id(1)

    @pl.when(block == 0)
    def _():
        dk_ref[...] = jnp.zeros_like(dk_ref)
        dv_ref[...] = jnp.zeros_like(dv_ref)

    qpos, is_cont, n_all, n_free, starts, seen = block_facts(
        tiles_ref, len_ref, block, KB, QB_BACK
    )
    q = q_ref[0]
    g = g_ref[0]
    stat = lambda ref: jnp.concatenate(
        [ref[j, pl.ds(h, 1), :] for j in range(QB_BACK // QB)], axis=1
    )
    lse = stat(lse_ref)
    delta = stat(delta_ref)

    def step(kb, dqt, masked):
        base = pl.multiple_of(kb * KB, KB)
        rows = pl.ds(base, KB)
        s = mul(k_ref[0, rows, :], q, NT)
        dp = mul(v_ref[0, rows, :], g, NT)
        if masked:
            kpos = base + lax.broadcasted_iota(jnp.int32, (KB, QB_BACK), 0)
            s = jnp.where(kpos <= qpos, s, masked_value)
        p = jnp.exp(s - lse)
        ds = (p * (dp - delta)).astype(BF)
        dv_ref[rows, :] += mul(p.astype(BF), g)
        dk_ref[rows, :] += mul(ds, q)
        return dqt + mul(kt_ref[0, :, rows], ds)

    dqt = jnp.zeros((HDIM, QB_BACK), F32)
    dqt = lax.fori_loop(0, n_free, functools.partial(step, masked=False), dqt)
    dqt = lax.fori_loop(n_free, n_all, functools.partial(step, masked=True), dqt)
    dq_ref[0] = dqt.T * HDIM ** (-0.5)

    @pl.when(is_cont)
    def _():
        part = lambda x, j: x[j * BLK : (j + 1) * BLK]
        rows = [pl.ds(starts[j], CLEN) for j in range(QB_BACK // BLK)]
        s = jnp.concatenate([mul(k_ref[0, rows[j], :], part(q, j), NT) for j in range(QB_BACK // BLK)], axis=1)
        s = jnp.where(seen(), s, masked_value)
        p = jnp.exp(s - lse)
        dp = jnp.concatenate([mul(v_ref[0, rows[j], :], part(g, j), NT) for j in range(QB_BACK // BLK)], axis=1)
        ds = (p * (dp - delta)).astype(BF)
        pb = p.astype(BF)
        dq = []
        for j in range(QB_BACK // BLK):
            cols = slice(j * BLK, (j + 1) * BLK)
            dv_ref[rows[j], :] += mul(pb[:, cols], part(g, j))
            dk_ref[rows[j], :] += mul(ds[:, cols], part(q, j))
            dq.append(mul(kt_ref[0, :, rows[j]], ds[:, cols]))
        dq_ref[0] += jnp.concatenate(dq, axis=1).T * HDIM ** (-0.5)

    @pl.when(block == pl.num_programs(1) - 1)
    def _():
        dk_out[0] = dk_ref[...].astype(BF)
        dv_out[0] = dv_ref[...].astype(BF)


def attention_backward(tiles, lengths, queries, grads, log_total, row_delta, keys, values, keys_t, group):
    rows = queries.shape[1]
    count = rows // QB_BACK
    span = keys.shape[1]
    first = group * GROUP
    row = pl.BlockSpec((1, QB_BACK, HDIM), lambda h, i, a, b: (h + first, i, 0))
    stat = pl.BlockSpec((QB_BACK // QB, NH, QB), lambda h, i, a, b: (i, 0, 0))
    full = pl.BlockSpec((1, span, HDIM), lambda h, i, a, b: (h + first, 0, 0))
    out = pl.BlockSpec((1, span, HDIM), lambda h, i, a, b: (h, 0, 0))
    return pl.pallas_call(
        functools.partial(backward_kernel, first=first),
        out_shape=[
            jax.ShapeDtypeStruct((GROUP, rows, HDIM), F32),
            jax.ShapeDtypeStruct((GROUP, span, HDIM), BF),
            jax.ShapeDtypeStruct((GROUP, span, HDIM), BF),
        ],
        grid_spec=pltpu.PrefetchScalarGridSpec(
            num_scalar_prefetch=2,
            grid=(GROUP, count),
            in_specs=[
                row,
                row,
                stat,
                stat,
                full,
                full,
                pl.BlockSpec((1, HDIM, span), lambda h, i, a, b: (h + first, 0, 0)),
            ],
            out_specs=[pl.BlockSpec((1, QB_BACK, HDIM), lambda h, i, a, b: (h, i, 0)), out, out],
            scratch_shapes=[pltpu.VMEM((span, HDIM), F32)] * 2,
        ),
        compiler_params=room(),
        cost_estimate=cost(rows * GPART * PLEN * 40, 32 * span * GPART),
        name="attention_backward",
    )(tiles, lengths, queries, grads, log_total, row_delta, keys, values, keys_t)


def restore_kernel(tiles_ref, *refs):
    mine_ref, theirs_ref = refs[16:]

    def write(out_ref):
        for j in range(8):
            rows = slice(j * BLK, (j + 1) * BLK)
            for h in range(GROUP):
                cols = slice(h * HDIM, (h + 1) * HDIM)
                out_ref[rows, cols] = refs[8 + j][h]
                out_ref[rows, GPART + h * HDIM : GPART + (h + 1) * HDIM] = refs[j][h]

    @pl.when(pl.program_id(0) < 4)
    def _():
        write(theirs_ref)

    @pl.when(pl.program_id(0) >= 4)
    def _():
        write(mine_ref)


def restore_keys(tiles, grad_k, grad_v):
    spec = lambda j: pl.BlockSpec((GROUP, BLK, HDIM), lambda i, o: (0, o[i * 8 + j], 0))
    shape = (8 * BLK, 2 * GPART)
    return pl.pallas_call(
        restore_kernel,
        out_shape=[jax.ShapeDtypeStruct((32 * BLK, 2 * GPART), BF)] * 2,
        grid_spec=pltpu.PrefetchScalarGridSpec(
            num_scalar_prefetch=1,
            grid=(8,),
            in_specs=[spec(j) for j in range(8)] * 2,
            out_specs=[
                pl.BlockSpec(shape, lambda i, o: (jnp.maximum(i - 4, 0), 0)),
                pl.BlockSpec(shape, lambda i, o: (jnp.minimum(i, 3), 0)),
            ],
        ),
        compiler_params=room(),
        cost_estimate=cost(0, 64 * 64 * BLK * GPART),
        name="restore_keys",
    )(tiles, *([grad_k] * 8), *([grad_v] * 8))


def unturn_kernel(dq_ref, mine_ref, theirs_ref, cos_ref, sin_ref, g_ref, y_sc):
    kv = mine_ref[...].astype(F32) + theirs_ref[...].astype(F32)
    for h in range(GROUP):
        y_sc[:, h * HDIM : (h + 1) * HDIM] = dq_ref[h]
    y_sc[:, GPART:] = kv[:, GPART:]
    cosine, sine_vals = cos_ref[...], -sin_ref[...]
    for k in range(GROUP):
        cols = slice(k * 128, (k + 1) * 128)
        g_ref[:, cols] = swing(y_sc[:, cols], cosine, sine_vals).astype(BF)
    g_ref[:, 2 * GPART :] = kv[:, :GPART].astype(BF)


def unturn(grad_q, mine, theirs, cosine, sine_vals):
    rows = mine.shape[0]
    size = QB
    row = lambda n: pl.BlockSpec((size, n), lambda i: (i, 0))
    return pl.pallas_call(
        unturn_kernel,
        out_shape=jax.ShapeDtypeStruct((rows, 3 * GPART), BF),
        grid=(rows // size,),
        in_specs=[
            pl.BlockSpec((GROUP, size, HDIM), lambda i: (0, i, 0)),
            row(2 * GPART),
            row(2 * GPART),
            row(128),
            row(128),
        ],
        out_specs=pl.BlockSpec((size, 3 * GPART), lambda i: (i % 4 * 2 + i // 4, 0)),
        scratch_shapes=[pltpu.VMEM((size, 2 * GPART), F32)],
        compiler_params=room(),
        cost_estimate=cost(0, 20 * rows * GPART),
        name="unturn",
    )(grad_q, mine, theirs, cosine, sine_vals)


def unproject_kernel(a_ref, b_ref, c_ref, w_ref, x_ref, w_sc, y_sc):
    thin = w_sc.shape[0] // 32

    @pl.when(pl.program_id(0) == 0)
    def _():
        straighten(w_ref, w_sc, thin)

    for g, ref in enumerate((a_ref, b_ref, c_ref)):
        for k in range(3):
            y_sc[:, k * PART + g * GPART : k * PART + (g + 1) * GPART] = ref[
                :, k * GPART : (k + 1) * GPART
            ]
    x_ref[...] = mul(y_sc[...], w_sc[...], NT).astype(BF)


def unproject(parts, w_all, chunk):
    rows = parts[0].shape[0] // 2
    full = w_all.shape
    width = full[0] * full[1] * (full[2] - 8)
    return pl.pallas_call(
        unproject_kernel,
        out_shape=jax.ShapeDtypeStruct((rows, width), BF),
        grid=(rows // QB,),
        in_specs=[pl.BlockSpec((QB, 3 * GPART), lambda i: (i * 2 + chunk, 0))] * 3
        + [pl.BlockSpec(full, lambda i: (0, 0, 0, 0), pipeline_mode=pl.Buffered(1))],
        out_specs=pl.BlockSpec((QB, width), lambda i: (i, 0)),
        scratch_shapes=[
            pltpu.VMEM((width, full[3]), BF),
            pltpu.VMEM((QB, 3 * PART), BF),
        ],
        compiler_params=room(),
        cost_estimate=cost(2 * rows * width * 3 * PART, 4 * rows * width),
        name="unproject",
    )(*parts, w_all)


def finish_kernel(a_ref, bc_ref, wq_ref, wk_ref, wv_ref, gain_ref, q_ref, k_ref, v_ref, sum_ref):
    thin = gain_ref.shape[0]
    gain = gain_ref[...]
    total = jnp.zeros((thin, 1), F32)
    for p in range(4):
        for g, (ref, first) in enumerate(((a_ref, 0), (bc_ref, 0), (bc_ref, PART))):
            cols = slice(p * PART + g * GPART, p * PART + (g + 1) * GPART)
            for n, (w, out) in enumerate(((wq_ref, q_ref), (wk_ref, k_ref), (wv_ref, v_ref))):
                part = slice(first + n * GPART, first + (n + 1) * GPART)
                grad = ref[p, :thin, part].astype(F32)
                out[:, cols] = grad * gain
                total += jnp.sum(grad * w[:, cols].astype(F32), axis=1, keepdims=True)
    sum_ref[...] = jnp.broadcast_to(total, sum_ref.shape)


def finish(parts, weights, gain):
    thin, width = weights[0].shape
    return pl.pallas_call(
        finish_kernel,
        out_shape=[jax.ShapeDtypeStruct((thin, width), F32)] * 3
        + [jax.ShapeDtypeStruct((thin, 128), F32)],
        compiler_params=room(),
        name="finish",
    )(*parts, *weights, gain)


def split_tiles(rows):
    blocks = rows.reshape(4, 2, rows.shape[0] // 8, rows.shape[1])
    return blocks[:, 0], blocks[:, 1]


def join_tiles(chunks):
    blocks = jnp.stack(chunks, axis=1)
    return blocks.reshape(-1, blocks.shape[-1])


def over(name, blocks):
    return lax.all_to_all(blocks, name, 0, 0, tiled=True)


def quarters(rows):
    return rows.reshape(4, rows.shape[0] // 4, rows.shape[1])


def after(value, *earlier):
    return lax.optimization_barrier((value, earlier))[0]


def flip(values, mask):
    return lax.ppermute(values, "p", [(k, k ^ mask) for k in range(4)])


def gather_near(own):
    return [own, flip(own, 1), flip(own, 2)]


def gather_far(near):
    half = near[0].shape[0] // 2
    return near + [flip(near[2][:half], 1), flip(near[1][half:], 2)]


def slots(terms):
    size = terms.shape[0] // 4
    return [terms[k * size : (k + 1) * size] for k in range(4)]


def scatter_far(terms):
    far = slots(terms)[3]
    half = far.shape[0] // 2
    return flip(far[:half], 1), flip(far[half:], 2)


def scatter_near(terms, far):
    _, first, second, _ = slots(terms)
    half = first.shape[0] // 2
    add = lambda x, y: (x.astype(F32) + y.astype(F32)).astype(BF)
    first = flip(jnp.concatenate([first[:half], add(first[half:], far[1])], axis=0), 1)
    second = flip(jnp.concatenate([add(second[:half], far[0]), second[half:]], axis=0), 2)
    return first, second


def scatter_sum(terms, near):
    return slots(terms)[0].astype(F32) + near[0].astype(F32) + near[1].astype(F32)


def scatter_far_both(terms):
    return flip(slots(terms[0])[3], 1), flip(slots(terms[1])[3], 2)


def scatter_near_both(terms, far):
    early, late = slots(terms[0]), slots(terms[1])
    add = lambda x, y: (x.astype(F32) + y.astype(F32)).astype(BF)
    first = flip(jnp.concatenate([early[1], add(late[1], far[1])], axis=0), 1)
    second = flip(jnp.concatenate([add(early[2], far[0]), late[2]], axis=0), 2)
    return first, second


def meet(*values):
    return lax.optimization_barrier(values)


def swap_blocks(name, pieces):
    return [pieces[0]] + [
        lax.ppermute(pieces[r], name, [(k, k ^ r) for k in range(4)]) for r in (1, 2, 3)
    ]


def pick(pieces, first):
    stacked = jnp.stack(pieces)
    return [
        lax.dynamic_index_in_dim(stacked, jnp.bitwise_xor(first, r), 0, keepdims=False)
        for r in range(4)
    ]


def hidden_cuts(hidden):
    steps = hidden // 8
    sizes = [8 * (steps // 4 + (k < steps % 4)) for k in range(4)]
    starts = [sum(sizes[:k]) for k in range(4)]
    return starts, sizes, max(sizes)


def inner(
    tokens_in,
    cotangent,
    w_query,
    w_key,
    w_value,
    w_output,
    w_gate,
    w_up,
    w_down,
    attn_gain,
    ffn_gain,
    cont_len,
    deal_order,
    clip_threshold,
):
    plane, depth, core = (lax.axis_index(name) for name in ("p", "z", "c"))
    line = ("z", "c")
    width = tokens_in.shape[1]
    thin = w_query.shape[0]
    hidden = w_down.shape[0]
    starts, sizes, share = hidden_cuts(hidden)
    gain_f = attn_gain.astype(F32)
    parts_of = lambda v: [v[k] for k in range(4)]
    cross = lambda v: swap_blocks("p", pick(v, plane))
    cross_whole = lambda v: jnp.stack(pick(cross(parts_of(v)), plane))
    hop_on = lambda v: swap_blocks("z", pick(v, jnp.bitwise_xor(plane, depth)))
    hop_back = lambda v: swap_blocks("z", parts_of(quarters(v)))
    hop_out = lambda v: pick(
        swap_blocks("p", pick(v, jnp.bitwise_xor(plane, depth))), plane
    )
    first_hop = cross(parts_of(quarters(tokens_in)))
    turn_over = [(g * 4 + k, k * 4 + g) for g in range(4) for k in range(4)]
    deal = lax.ppermute(deal_order[0], ("p", "z"), turn_over)
    lengths = lax.ppermute(cont_len[0], ("p", "z"), turn_over)

    scaled = [(w.astype(F32) * gain_f[:, None]).astype(BF) for w in (w_query, w_key, w_value)]
    blocks = jnp.stack(scaled).reshape(3, thin, 4, PART).transpose(2, 1, 0, 3)
    blocks = blocks.reshape(4, thin, 3 * PART)
    extra = jnp.zeros((4, 8, 3 * PART), BF).at[:, 0, :thin].set(ffn_gain[None, :])
    send = jnp.concatenate([blocks, extra], axis=1)
    first_hop, send = meet(first_hop, send)
    early = after((w_gate, w_up, w_down), first_hop)
    stacked = jnp.stack([early[0].T, early[1].T, early[2]])
    stacked = jnp.stack(
        [
            jnp.pad(stacked[:, a : a + n], ((0, 0), (0, share - n), (0, 0)))
            for a, n in zip(starts, sizes)
        ]
    )
    send, moved = meet(cross_whole(send), hop_on(first_hop))
    stacked = cross_whole(stacked)
    w_qkv = lax.all_gather(send, line, axis=0)
    gain_two = w_qkv[:, :, thin, :thin].transpose(1, 0, 2).reshape(width).astype(F32)
    w_out = lax.all_gather(w_output, line, axis=0, tiled=True)
    piece = jnp.arange(2)[:, None, None]
    slot = jnp.arange(4)[None, :, None]
    source = jnp.bitwise_xor(depth, jnp.arange(4))[None, None, :]
    quarter = jnp.bitwise_xor(plane, slot)
    held = lambda which: deal[((source * 2 + which) * 8 + quarter * 2 + piece).reshape(-1)]
    tiles, tiles_far = held(core), held(1 - core)
    both = jnp.concatenate([tiles, tiles_far])
    numbers = jnp.arange(64, dtype=jnp.int32)
    order = jnp.sum(
        jnp.where(both[None, :] == numbers[:, None], numbers[None, :], 0), axis=1
    ).astype(jnp.int32)
    logical = (tiles[:, None] * BLK + jnp.arange(BLK, dtype=jnp.int32)[None, :]).reshape(-1)
    position = jnp.where(logical < PLEN, logical, PLEN + (logical - PLEN) % CLEN)
    cosine, sine_vals = (v[:, 0, :] for v in rope_angles(position))
    cosine = jnp.concatenate([cosine] * 4, axis=1)
    sine_vals = jnp.concatenate([-sine_vals, sine_vals] * 2, axis=1)

    joined = lambda pieces: jnp.concatenate(pieces, axis=0)
    by_chunk = lambda v: [h.reshape(-1, width) for h in split_tiles(joined(v))]
    residual = [v.astype(F32) for v in by_chunk(moved)]
    inverse_of = lambda v: lax.rsqrt(jnp.mean(v * v, axis=-1, keepdims=True) + norm_eps)
    inverse_one = [inverse_of(v) for v in residual]
    pieces = gather_near(joined([(v * r).astype(BF) for v, r in zip(residual, inverse_one)]))
    pieces = gather_far(pieces)

    def in_chunks(pieces):
        size = pieces[0].shape[0] // 2
        return [
            joined([v[k * size : (k + 1) * size] for v in pieces[:3]] + [pieces[3 + k]])
            for k in range(2)
        ]

    pieces, w_qkv, grad_out = meet(pieces, w_qkv, cotangent)
    (queries, mine, normed), grad_out = meet(
        project(pieces, w_qkv, cosine, sine_vals),
        cross(parts_of(quarters(grad_out))),
    )
    theirs = lax.ppermute(mine, "c", [(0, 1), (1, 0)])
    sorted_kv, grad_out, stacked = meet(
        sort_keys(order, mine, theirs), hop_on(grad_out), stacked
    )
    keys, values, keys_t, values_t = sorted_kv
    stacked = stacked.transpose(1, 2, 0, 3).reshape(3, share, width)
    w_ffn = [lax.all_gather(stacked[k], line, axis=0, tiled=True) for k in range(3)]
    attend = lambda q, k, n: attention_forward(tiles, lengths, q, keys, values_t, k, n)
    grad_out = by_chunk(grad_out)
    grad_rows = joined([(branch_scale * v.astype(F32)).astype(BF) for v in grad_out])
    queries, grad_rows = meet(queries, grad_rows)
    (low_a, total_a, peak_a), grad_rows = meet(attend(queries, 0, 4), gather_near(grad_rows))
    branch_a = mul(low_a, w_out).astype(BF)
    branch_a, grad_rows, queries_b = meet(branch_a, grad_rows, queries)
    part_b, far_a = meet(attend(queries_b, 4, 2), scatter_far(branch_a))
    rest_b, near_a, grad_rows = meet(
        attend(queries_b, 6, 2), scatter_near(branch_a, far_a), gather_far(grad_rows)
    )
    low_b, total_b, peak_b = (joined([v, w]) for v, w in zip(part_b, rest_b))
    branch_b = mul(low_b, w_out).astype(BF)
    attended = joined([low_a, low_b])
    log_total = joined([total_a, total_b])
    peaks = joined([peak_a, peak_b])
    grad_rows = in_chunks(grad_rows)

    def second_norm(k, branch):
        after_attn = residual[k] + branch_scale * branch
        inverse_two = inverse_of(after_attn)
        return after_attn, inverse_two, (after_attn * inverse_two * gain_two).astype(BF)

    def hidden_layer(grad_mixed, normed_two):
        gate_pre = mul(normed_two, w_ffn[0], NT)
        up_pre = mul(normed_two, w_ffn[1], NT)
        mixed = (jax.nn.silu(gate_pre) * up_pre).astype(BF)
        return (mixed,) + gate_grads(grad_mixed, gate_pre, up_pre)

    def hidden_back(hidden):
        return (mul(hidden[1], w_ffn[0]) + mul(hidden[2], w_ffn[1])).astype(BF)

    def second_back(k, total, state):
        grad_gain, grad_second = norm_backward(total, state[0], state[1], gain_two)
        grad_resid = grad_out[k].astype(F32) + grad_second
        return grad_gain, grad_resid, (branch_scale * grad_resid).astype(BF)

    state_a = second_norm(0, scatter_sum(branch_a, near_a))
    own, rows_a, rows_b = meet(state_a[2], grad_rows[0], grad_rows[1])
    gather, mixed_a, rows_b, branch_b = meet(
        gather_near(own), mul(rows_a, w_ffn[2], NT), rows_b, branch_b
    )
    gather, far, mixed_b = meet(
        gather_far(gather), scatter_far(branch_b), mul(rows_b, w_ffn[2], NT)
    )
    normed_a = joined(gather)
    hidden_a, near = meet(hidden_layer(mixed_a, normed_a), scatter_near(branch_b, far))
    state_b = second_norm(1, scatter_sum(branch_b, near))
    hidden_a, own = meet(hidden_a, state_b[2])
    rest_a, gather = meet(hidden_back(hidden_a), gather_near(own))
    first = mul(hidden_a[1], normed_a, TN)
    gather, far, gate_a = meet(gather_far(gather), scatter_far(rest_a), first)
    normed_b = joined(gather)
    hidden_b, near = meet(hidden_layer(mixed_b, normed_b), scatter_near(rest_a, far))
    back_a = second_back(0, scatter_sum(rest_a, near), state_a)
    hidden_b, own = meet(hidden_b, back_a[2])
    rest_b, gather_a = meet(hidden_back(hidden_b), gather_near(own))
    grad_gate = (gate_a + mul(hidden_b[1], normed_b, TN)).astype(BF)
    up_a = mul(hidden_a[2], normed_a, TN)
    gather_a, far, grad_gate, up_a = meet(
        gather_far(gather_a), scatter_far(rest_b), grad_gate, up_a
    )
    grad_up = (up_a + mul(hidden_b[2], normed_b, TN)).astype(BF)
    down_a = mul(hidden_a[0], rows_a, TN)
    near, grad_up, down_a = meet(scatter_near(rest_b, far), grad_up, down_a)
    back_b = second_back(1, scatter_sum(rest_b, near), state_b)
    own, mixed_b_rows, down_a = meet(back_b[2], hidden_b[0], down_a)
    grad_down = (down_a + mul(mixed_b_rows, rows_b, TN)).astype(BF)
    gather_b, grad_down, ffn_b = meet(
        gather_near(own), grad_down, mul(mixed_b_rows, w_ffn[2]).astype(BF)
    )
    gather_b, ffn_a = meet(gather_far(gather_b), mul(hidden_a[0], w_ffn[2]).astype(BF))
    branch_ffn = [ffn_a, ffn_b]
    sum_rows = lambda v: lax.psum_scatter(v, line, scatter_dimension=0, tiled=True)
    grad_pieces = gather_a + gather_b
    grad_gain_two = back_a[0] + back_b[0]
    grad_resid = [back_a[1], back_b[1]]

    grad_pieces, branch_ffn = meet(grad_pieces, branch_ffn)
    (grad_heads, row_delta, grad_w_part), far, grad_gate = meet(
        attention_delta(grad_pieces, w_out, attended),
        scatter_far_both(branch_ffn),
        sum_rows(grad_gate),
    )
    far_order = jnp.concatenate([tiles_far, tiles])
    gain_rows = grad_gain_two.astype(BF).reshape(4, 8, 1, thin).transpose(1, 0, 2, 3)
    peak = jnp.max(peaks, axis=(0, 2))
    peak_high = lax.reduce_precision(peak, 8, 7)
    peak_rows = jnp.stack([peak_high.astype(BF), (peak - peak_high).astype(BF)])
    mine_slot = (jnp.arange(8) == depth * 2 + core)[None, :, None]
    peak_rows = jnp.where(mine_slot, peak_rows[:, None, :], 0).reshape(2, 8 * NH)
    widen = lambda v: jnp.pad(v, ((0, 0), (0, 0), (0, 0), (0, 3 * GPART - v.shape[3])))
    gain_rows = jnp.concatenate(
        [
            widen(gain_rows),
            widen(jnp.broadcast_to(peak_rows, (8, 4, 2, 8 * NH))),
            jnp.zeros((8, 4, 5, 3 * GPART), BF),
        ],
        axis=2,
    )

    def back_group(g, grads):
        return attention_backward(
            tiles, lengths, queries, grads, log_total, row_delta, keys, values, keys_t, g
        )

    def restore(part):
        return (part[0],) + tuple(restore_keys(far_order, part[1], part[2]))

    def weight_part(grad_qkv):
        proj = mul(normed, grad_qkv, TN).astype(BF).reshape(4, 8, thin, 3 * GPART)
        proj = jnp.concatenate([proj.transpose(1, 0, 2, 3), gain_rows], axis=2)
        return proj.reshape(8 * 4 * (thin + 8), 3 * GPART)

    def sum_line(proj):
        proj = lax.psum_scatter(proj, line, scatter_dimension=0, tiled=True)
        return proj.reshape(4, thin + 8, 3 * GPART)

    trade = lambda v: lax.ppermute(v, "c", [(0, 1), (1, 0)])
    grad_heads, grad_w_part = meet(grad_heads, grad_w_part)
    grad_down = sum_rows(grad_down)
    part_a, grad_heads, near, grad_up = meet(
        back_group(0, grad_heads),
        grad_heads,
        scatter_near_both(branch_ffn, far),
        sum_rows(grad_up),
    )
    grad_w_output = sum_rows(grad_w_part)
    part_a = restore(part_a)
    states = (state_a, state_b)
    output = []
    for k, (state, v) in enumerate(zip(states, branch_ffn)):
        size = state[0].shape[0]
        total = scatter_sum(v, [w[k * size : (k + 1) * size] for w in near])
        output.append(quarters((state[0] + branch_scale * total).astype(BF)))
    output = join_tiles(output)
    output, grad_heads, part_a = meet(output, grad_heads, part_a)
    part_b, grad_heads, hops, far_a, grad_down = meet(
        back_group(1, grad_heads),
        grad_heads,
        hop_back(output),
        trade(part_a[2]),
        grad_down,
    )
    ffn_grads = jnp.stack([grad_gate, grad_up, grad_down])
    ffn_grads = ffn_grads.reshape(3, share, 4, PART).transpose(2, 0, 1, 3)
    part_b = restore(part_b)
    grads_a = unturn(part_a[0], part_a[1], far_a, cosine, sine_vals)
    weights_a = weight_part(grads_a)
    grad_heads, weights_a, hops, part_b, ffn_grads = meet(
        grad_heads, weights_a, hops, part_b, ffn_grads
    )
    part_c, output, far_b = meet(back_group(2, grad_heads), hop_out(hops), trade(part_b[2]))
    weights_a = sum_line(weights_a)
    part_c, far_b = meet(restore(part_c), far_b)
    grads_b = unturn(part_b[0], part_b[1], far_b, cosine, sine_vals)
    weights_b, far_c, ffn_grads = meet(
        weight_part(grads_b), trade(part_c[2]), cross_whole(ffn_grads)
    )
    output = joined(output)
    grads_c, weights_a = meet(
        unturn(part_c[0], part_c[1], far_c, cosine, sine_vals), weights_a
    )
    grads = (grads_a, grads_b, grads_c)
    rest_a, grads, weights_a = meet(unproject(grads, w_qkv, 0), grads, cross_whole(weights_a))
    weights_c, far_a, grads = meet(weight_part(grads[2]), scatter_far(rest_a), grads)
    weights_c = sum_line(weights_c)
    rest_b, near_a, weights_b, grad_w_output = meet(
        unproject(grads, w_qkv, 1),
        scatter_near(rest_a, far_a),
        sum_line(weights_b),
        grad_w_output,
    )
    far_b = scatter_far(rest_b)

    def first_back(k, total):
        grad_first = inverse_one[k] * total - residual[k] * inverse_one[k] ** 3 * jnp.mean(
            total * residual[k], axis=-1, keepdims=True
        )
        return (grad_resid[k] + grad_first).astype(BF)

    hop_a = hop_back(first_back(0, scatter_sum(rest_a, near_a)))
    near_b = scatter_near(rest_b, far_b)
    hop_a, near_b = meet(hop_a, near_b)
    hop_b, hop_a = meet(hop_back(first_back(1, scatter_sum(rest_b, near_b))), hop_out(hop_a))
    grad_input = join_tiles([jnp.stack(hop_a), jnp.stack(hop_out(hop_b))]).astype(F32)
    ffn_grads = ffn_grads.astype(F32)
    ffn_grads = jnp.concatenate([ffn_grads[k, :, :n] for k, n in enumerate(sizes)], axis=1)
    grad_ffn_gain = jnp.sum(weights_a[:, thin, :thin].astype(F32), axis=0)
    weights_bc = over("p", jnp.concatenate([weights_b, weights_c], axis=2))
    proj = finish(
        (weights_a, weights_bc), (w_query, w_key, w_value), gain_f[:, None]
    )
    grad_attn_gain = proj[3][:, 0]

    maxima = jnp.sum(weights_a[:, thin + 1 : thin + 3, : 8 * NH].astype(F32), axis=1)
    maxima = jnp.max(maxima.reshape(4, 8, NH), axis=1).reshape(HEADS)
    limit_value = clip_threshold[0].astype(F32)
    clip_factor = jnp.sqrt(limit_value / jnp.maximum(maxima, limit_value))
    column_factor = jnp.repeat(clip_factor, HDIM)
    return (
        output,
        grad_input,
        proj[0],
        proj[1],
        proj[2],
        grad_w_output.astype(F32),
        ffn_grads[0].T,
        ffn_grads[1].T,
        ffn_grads[2],
        grad_attn_gain,
        grad_ffn_gain,
        maxima,
        clip_factor,
        w_query.astype(F32) * column_factor[None, :],
        w_key.astype(F32) * column_factor[None, :],
    )


def specs(grp, ctx):
    every = grp + ctx
    ins = [P(every, None)] * 6 + [P(grp, ctx), P(grp, ctx), P(ctx, grp), P(every), P(every)]
    ins += [P(grp, None), P(grp, None), P()]
    outs = [P(every, None)] * 6 + [P(grp, ctx), P(grp, ctx), P(ctx, grp), P(every), P(every)]
    outs += [P(), P(), P(every, None), P(every, None)]
    return tuple(ins), tuple(outs)


def solution(mesh):
    if mesh.shape["grp"] == 4 and mesh.shape["ctx"] == 8:
        mesh = Mesh(mesh.devices.reshape(4, 4, 2), ("p", "z", "c"))
        body, (in_specs, out_specs) = inner, specs(("p",), ("z", "c"))
    else:
        body, (in_specs, out_specs) = local, specs(("grp",), ("ctx",))
    return jax.shard_map(body, mesh=mesh, in_specs=in_specs, out_specs=out_specs, check_vma=False)
```

```python
import functools
import math

import jax
import jax.numpy as jnp
from jax import lax
from jax.experimental import pallas as pl
from jax.experimental.pallas import tpu as pltpu
from jax.sharding import Mesh
from jax.sharding import PartitionSpec as P

HEADS = 36
HDIM = 64
PLEN = 2048
CLEN = 256
NCONT = 8
BLK = 64
FAMTOK = 4096

F32 = jnp.float32
BF = jnp.bfloat16
NH = HEADS // 4
PART = NH * HDIM
GROUP = 3
GPART = GROUP * HDIM
QB_BACK = 512
QB = 256
KB = 1024
KB_FWD = 1024
HEAD_STEP = 9
NT = (((1,), (1,)), ((), ()))
NN = (((1,), (0,)), ((), ()))
TN = (((0,), (0,)), ((), ()))
VMEM_ROOM = 56 * 1024 * 1024


branch_scale = 1.4 / math.sqrt(40.0)
norm_eps = 1e-05
rope_base = 10000.0
masked_value = -1e30


def rope_angles(position):
    half_dim = HDIM // 2
    frequency = rope_base ** (-(jnp.arange(half_dim, dtype=jnp.float32) * (2.0 / HDIM)))
    angles = position.astype(jnp.float32)[:, None] * frequency[None, :]
    return (jnp.cos(angles)[:, None, :], jnp.sin(angles)[:, None, :])


def rotate(values, cosine, sine_vals, turn_sign):
    row_count = values.shape[0]
    shaped = values.reshape(row_count, HEADS, HDIM)
    leading = shaped[..., : HDIM // 2]
    trailing = shaped[..., HDIM // 2 :]
    turned = jnp.concatenate(
        [
            leading * cosine - turn_sign * trailing * sine_vals,
            trailing * cosine + turn_sign * leading * sine_vals,
        ],
        axis=-1,
    )
    return turned.reshape(row_count, HEADS * HDIM)


def token_facts(logical, lengths):
    family = logical // FAMTOK
    offset = logical % FAMTOK
    prompt = offset < PLEN
    member = jnp.clip((offset - PLEN) // CLEN, 0, NCONT - 1)
    inside = offset - PLEN - member * CLEN
    seq_id = jnp.where(prompt, -1, family * NCONT + member)
    numbers = jnp.arange(lengths.shape[0], dtype=jnp.int32)
    live_len = jnp.sum(jnp.where(seq_id[:, None] == numbers[None, :], lengths[None, :], 0), axis=1)
    is_live = prompt | (inside < live_len)
    position = jnp.where(prompt, offset, PLEN + inside)
    return (family, offset, prompt, seq_id, is_live, position)


def visible(query_facts, key_part):
    same_family = query_facts[0][:, None] == key_part[0][None, :]
    causal = key_part[1][None, :] <= query_facts[1][:, None]
    reaches = (
        key_part[2][None, :]
        | (key_part[3][None, :] == query_facts[3][:, None]) & key_part[4][None, :]
    )
    return same_family & causal & reaches


def key_slice(keys_heads, values_heads, key_facts, query_facts, first_row, span_rows):
    key_block = lax.dynamic_slice_in_dim(keys_heads, first_row, span_rows, 0)
    value_block = lax.dynamic_slice_in_dim(values_heads, first_row, span_rows, 0)
    key_part = tuple(
        (
            lax.dynamic_slice_in_dim(member_array, first_row, span_rows, 0)
            for member_array in key_facts
        )
    )
    return (key_block, value_block, visible(query_facts, key_part))


def block_scores(query_heads, key_block, visible_mask):
    scores = jnp.einsum(
        "qhd,khd->hqk", query_heads, key_block, preferred_element_type=jnp.float32
    ) * HDIM ** (-0.5)
    return jnp.where(visible_mask[None], scores, masked_value)


def score_grads(
    query_heads, grad_heads, log_total, row_delta, key_block, value_block, visible_mask
):
    scores = block_scores(query_heads, key_block, visible_mask)
    prob_table = jnp.where(visible_mask[None], jnp.exp(scores - log_total[:, :, None]), 0.0)
    grad_probs = jnp.einsum(
        "qhd,khd->hqk", grad_heads, value_block, preferred_element_type=jnp.float32
    )
    grad_scores = (prob_table * (grad_probs - row_delta[:, :, None])).astype(jnp.bfloat16)
    return (prob_table.astype(jnp.bfloat16), grad_scores)


def gate_grads(grad_mixed, gate_pre, up_pre):
    sigmoid = jax.nn.sigmoid(gate_pre)
    grad_gate = grad_mixed * up_pre * sigmoid * (1.0 + gate_pre * (1.0 - sigmoid))
    grad_up = grad_mixed * gate_pre * sigmoid
    return (grad_gate.astype(jnp.bfloat16), grad_up.astype(jnp.bfloat16))


def norm_backward(grad_normed, values, inverse, gain):
    scaled = grad_normed * gain[None, :]
    grad_gain = jnp.sum(grad_normed * values * inverse, axis=0)
    grad_values = inverse * scaled - values * inverse**3 * jnp.mean(
        scaled * values, axis=-1, keepdims=True
    )
    return (grad_gain, grad_values)


def attention_weights(w_query, w_key, w_value, w_output, attn_gain, ffn_gain):
    return (
        lax.all_gather(w_query, ("grp", "ctx"), axis=0, tiled=True),
        lax.all_gather(w_key, ("grp", "ctx"), axis=0, tiled=True),
        lax.all_gather(w_value, ("grp", "ctx"), axis=0, tiled=True),
        lax.all_gather(w_output, ("grp", "ctx"), axis=0, tiled=True),
        lax.all_gather(attn_gain, ("grp", "ctx"), axis=0, tiled=True),
        lax.all_gather(ffn_gain, ("grp", "ctx"), axis=0, tiled=True),
    )


def ffn_rows_gather(w_gate, w_up, w_down):
    return (
        lax.all_gather(w_gate, "grp", axis=0, tiled=True),
        lax.all_gather(w_up, "grp", axis=0, tiled=True),
        lax.all_gather(w_down, "grp", axis=1, tiled=True),
    )


def local(
    tokens_in,
    cotangent,
    w_query,
    w_key,
    w_value,
    w_output,
    w_gate,
    w_up,
    w_down,
    attn_gain,
    ffn_gain,
    cont_len,
    deal_order,
    clip_threshold,
):
    row_count = tokens_in.shape[0]
    model_width = tokens_in.shape[1]
    tile_count = deal_order.shape[1]
    group_rows = tile_count * BLK
    lengths = cont_len[0]
    my_index = lax.axis_index("ctx")
    tile_offsets = jnp.arange(BLK, dtype=jnp.int32)
    stored_logical = (deal_order[0][:, None] * BLK + tile_offsets[None, :]).reshape(group_rows)
    key_facts = token_facts(stored_logical, lengths)
    query_facts = tuple(
        (
            lax.dynamic_slice_in_dim(member_array, my_index * row_count, row_count, 0)
            for member_array in key_facts
        )
    )
    cosine, sine_vals = rope_angles(query_facts[5])
    key_step = math.gcd(group_rows, 512)
    key_blocks = group_rows // key_step
    full_query, full_key, full_value, full_output, gain_one, gain_two = attention_weights(
        w_query, w_key, w_value, w_output, attn_gain, ffn_gain
    )
    residual = tokens_in.astype(jnp.float32)
    inverse_one = lax.rsqrt(jnp.mean(residual * residual, axis=-1, keepdims=True) + norm_eps)
    gain_one_f = gain_one.astype(jnp.float32)
    gain_two_f = gain_two.astype(jnp.float32)
    normed_one = (residual * inverse_one * gain_one_f).astype(jnp.bfloat16)
    query_rot = rotate(
        jnp.dot(normed_one, full_query, preferred_element_type=jnp.float32), cosine, sine_vals, 1.0
    ).astype(jnp.bfloat16)
    key_rot = rotate(
        jnp.dot(normed_one, full_key, preferred_element_type=jnp.float32), cosine, sine_vals, 1.0
    ).astype(jnp.bfloat16)
    value_low = jnp.dot(normed_one, full_value, preferred_element_type=jnp.float32).astype(
        jnp.bfloat16
    )
    keys_all, values_all = (
        lax.all_gather(key_rot, "ctx", axis=0, tiled=True),
        lax.all_gather(value_low, "ctx", axis=0, tiled=True),
    )
    query_heads = query_rot.reshape(row_count, HEADS, HDIM)
    keys_heads = keys_all.reshape(group_rows, HEADS, HDIM)
    values_heads = values_all.reshape(group_rows, HEADS, HDIM)

    def stats_step(block_index, state_carry):
        key_block, value_block, visible_mask = key_slice(
            keys_heads, values_heads, key_facts, query_facts, block_index * key_step, key_step
        )

        def stats_busy(carry):
            run_max, run_sum, head_max = carry
            scores = block_scores(query_heads, key_block, visible_mask)
            block_max = jnp.max(scores, axis=2)
            new_max = jnp.maximum(run_max, block_max)
            exp_table = jnp.where(visible_mask[None], jnp.exp(scores - new_max[:, :, None]), 0.0)
            new_sum = run_sum * jnp.exp(run_max - new_max) + jnp.sum(exp_table, axis=2)
            return (new_max, new_sum, jnp.maximum(head_max, jnp.max(block_max, axis=1)))

        return lax.cond(jnp.any(visible_mask), stats_busy, lambda carry: carry, state_carry)

    start_state = (
        jnp.full((HEADS, row_count), masked_value, jnp.float32),
        jnp.zeros((HEADS, row_count), jnp.float32),
        jnp.full((HEADS,), masked_value, jnp.float32),
    )
    run_max, run_sum, head_max = lax.fori_loop(0, key_blocks, stats_step, start_state)
    log_total = run_max + jnp.log(run_sum)

    def output_step(block_index, running):
        key_block, value_block, visible_mask = key_slice(
            keys_heads, values_heads, key_facts, query_facts, block_index * key_step, key_step
        )

        def output_busy(total):
            scores = block_scores(query_heads, key_block, visible_mask)
            prob_low = jnp.where(
                visible_mask[None], jnp.exp(scores - log_total[:, :, None]), 0.0
            ).astype(jnp.bfloat16)
            return total + jnp.einsum(
                "hqk,khd->qhd", prob_low, value_block, preferred_element_type=jnp.float32
            )

        return lax.cond(jnp.any(visible_mask), output_busy, lambda total: total, running)

    attended = lax.fori_loop(
        0, key_blocks, output_step, jnp.zeros((row_count, HEADS, HDIM), jnp.float32)
    )
    attn_low = attended.reshape(row_count, model_width).astype(jnp.bfloat16)
    after_attn = residual + branch_scale * jnp.dot(
        attn_low, full_output, preferred_element_type=jnp.float32
    )
    inverse_two = lax.rsqrt(jnp.mean(after_attn * after_attn, axis=-1, keepdims=True) + norm_eps)
    normed_two = (after_attn * inverse_two * gain_two_f).astype(jnp.bfloat16)
    gate_cols, up_cols, down_cols = ffn_rows_gather(w_gate, w_up, w_down)
    normed_rows = lax.all_gather(normed_two, "ctx", axis=0, tiled=True)
    gate_pre = jnp.dot(normed_rows, gate_cols, preferred_element_type=jnp.float32)
    up_pre = jnp.dot(normed_rows, up_cols, preferred_element_type=jnp.float32)
    mixed = (jax.nn.silu(gate_pre) * up_pre).astype(jnp.bfloat16)
    branch_ffn = lax.psum_scatter(
        jnp.dot(mixed, down_cols, preferred_element_type=jnp.float32).astype(jnp.bfloat16),
        "ctx",
        scatter_dimension=0,
        tiled=True,
    ).astype(jnp.float32)
    output = (after_attn + branch_scale * branch_ffn).astype(jnp.bfloat16)
    grad_out = cotangent.astype(jnp.float32)
    grad_branch = (branch_scale * grad_out).astype(jnp.bfloat16)
    gate_again, up_again, down_again = ffn_rows_gather(w_gate, w_up, w_down)
    grad_rows = lax.all_gather(grad_branch, "ctx", axis=0, tiled=True)
    grad_mixed = jnp.dot(grad_rows, down_again.T, preferred_element_type=jnp.float32)
    grad_down = jnp.dot(mixed.T, grad_rows, preferred_element_type=jnp.float32)
    grad_gate_low, grad_up_low = gate_grads(grad_mixed, gate_pre, up_pre)
    grad_gate = jnp.dot(normed_rows.T, grad_gate_low, preferred_element_type=jnp.float32)
    grad_up = jnp.dot(normed_rows.T, grad_up_low, preferred_element_type=jnp.float32)
    grad_normed_two = lax.psum_scatter(
        (
            jnp.dot(grad_gate_low, gate_again.T, preferred_element_type=jnp.float32)
            + jnp.dot(grad_up_low, up_again.T, preferred_element_type=jnp.float32)
        ).astype(jnp.bfloat16),
        "ctx",
        scatter_dimension=0,
        tiled=True,
    ).astype(jnp.float32)
    ffn_stack = jnp.stack([grad_gate, grad_up, grad_down.T], axis=0)
    ffn_summed = lax.psum_scatter(
        ffn_stack.astype(jnp.bfloat16), "grp", scatter_dimension=1, tiled=True
    ).astype(jnp.float32)
    grad_gain_two, grad_second = norm_backward(grad_normed_two, after_attn, inverse_two, gain_two_f)
    grad_resid = grad_out + grad_second
    back_query, back_key, back_value, back_output, back_gain_one, back_gain_two = attention_weights(
        w_query, w_key, w_value, w_output, attn_gain, ffn_gain
    )
    grad_branch_attn = (branch_scale * grad_resid).astype(jnp.bfloat16)
    grad_w_output = jnp.dot(attn_low.T, grad_branch_attn, preferred_element_type=jnp.float32)
    grad_attn = jnp.dot(grad_branch_attn, back_output.T, preferred_element_type=jnp.float32).astype(
        jnp.bfloat16
    )
    grad_heads = grad_attn.reshape(row_count, HEADS, HDIM)
    row_delta = jnp.sum(grad_heads.astype(jnp.float32) * attended, axis=2).T

    def back_step(grad_q, block_index):
        key_block, value_block, visible_mask = key_slice(
            keys_heads, values_heads, key_facts, query_facts, block_index * key_step, key_step
        )

        def back_busy(current):
            prob_low, grad_scores = score_grads(
                query_heads, grad_heads, log_total, row_delta, key_block, value_block, visible_mask
            )
            updated = current + jnp.einsum(
                "hqk,khd->qhd", grad_scores, key_block, preferred_element_type=jnp.float32
            )
            grad_keys = jnp.einsum(
                "hqk,qhd->khd", grad_scores, query_heads, preferred_element_type=jnp.float32
            ) * HDIM ** (-0.5)
            grad_values = jnp.einsum(
                "hqk,qhd->khd", prob_low, grad_heads, preferred_element_type=jnp.float32
            )
            return (
                updated,
                (
                    grad_keys.reshape(key_step, model_width),
                    grad_values.reshape(key_step, model_width),
                ),
            )

        def quiet(current):
            empty = jnp.zeros((key_step, model_width), jnp.float32)
            return (current, (empty, empty))

        return lax.cond(jnp.any(visible_mask), back_busy, quiet, grad_q)

    grad_q_heads, key_terms = lax.scan(
        back_step,
        jnp.zeros((row_count, HEADS, HDIM), jnp.float32),
        jnp.arange(key_blocks, dtype=jnp.int32),
    )
    key_sum, value_sum = (
        lax.psum_scatter(
            key_terms[0].reshape(group_rows, model_width).astype(jnp.bfloat16),
            "ctx",
            scatter_dimension=0,
            tiled=True,
        ).astype(jnp.float32),
        lax.psum_scatter(
            key_terms[1].reshape(group_rows, model_width).astype(jnp.bfloat16),
            "ctx",
            scatter_dimension=0,
            tiled=True,
        ).astype(jnp.float32),
    )
    grad_query_rot = grad_q_heads.reshape(row_count, model_width) * HDIM ** (-0.5)
    grad_query = rotate(grad_query_rot, cosine, sine_vals, -1.0).astype(jnp.bfloat16)
    grad_key = rotate(key_sum, cosine, sine_vals, -1.0).astype(jnp.bfloat16)
    grad_value = value_sum.astype(jnp.bfloat16)
    grad_w_query = jnp.dot(normed_one.T, grad_query, preferred_element_type=jnp.float32)
    grad_w_key = jnp.dot(normed_one.T, grad_key, preferred_element_type=jnp.float32)
    grad_w_value = jnp.dot(normed_one.T, grad_value, preferred_element_type=jnp.float32)
    grad_normed_one = (
        jnp.dot(grad_query, back_query.T, preferred_element_type=jnp.float32)
        + jnp.dot(grad_key, back_key.T, preferred_element_type=jnp.float32)
        + jnp.dot(grad_value, back_value.T, preferred_element_type=jnp.float32)
    )
    grad_gain_one, grad_first = norm_backward(grad_normed_one, residual, inverse_one, gain_one_f)
    grad_input = grad_resid + grad_first
    gain_pair = jnp.stack([grad_gain_one, grad_gain_two], axis=1)
    summed = (
        lax.psum_scatter(grad_w_query, ("grp", "ctx"), scatter_dimension=0, tiled=True),
        lax.psum_scatter(grad_w_key, ("grp", "ctx"), scatter_dimension=0, tiled=True),
        lax.psum_scatter(grad_w_value, ("grp", "ctx"), scatter_dimension=0, tiled=True),
        lax.psum_scatter(grad_w_output, ("grp", "ctx"), scatter_dimension=0, tiled=True),
        lax.psum_scatter(gain_pair, ("grp", "ctx"), scatter_dimension=0, tiled=True),
    )
    maxima = lax.pmax(head_max, ("grp", "ctx"))
    limit_value = clip_threshold[0].astype(jnp.float32)
    clip_factor = jnp.sqrt(limit_value / jnp.maximum(maxima, limit_value))
    column_factor = jnp.repeat(clip_factor, HDIM)
    clipped_query = w_query.astype(jnp.float32) * column_factor[None, :]
    clipped_key = w_key.astype(jnp.float32) * column_factor[None, :]
    return (
        output,
        grad_input,
        summed[0],
        summed[1],
        summed[2],
        summed[3],
        ffn_summed[0],
        ffn_summed[1],
        ffn_summed[2].T,
        summed[4][:, 0],
        summed[4][:, 1],
        maxima,
        clip_factor,
        clipped_query,
        clipped_key,
    )


def mul(left, right, dims=NN):
    return lax.dot_general(left, right, dims, preferred_element_type=F32)


def room():
    return pltpu.CompilerParams(vmem_limit_bytes=VMEM_ROOM)


def cost(flops, sent):
    return pl.CostEstimate(flops=int(flops), bytes_accessed=int(sent), transcendentals=0)


def straighten(w_ref, w_sc, thin):
    for i in range(4):
        for k in range(8):
            w_sc[(i * 8 + k) * thin : (i * 8 + k + 1) * thin, :] = w_ref[k, i, :thin, :]


def swing(values, cosine, sine_vals):
    lane = lax.broadcasted_iota(jnp.int32, values.shape, 1)
    other = jnp.where(
        lane % HDIM < HDIM // 2,
        pltpu.roll(values, 2 * HDIM - HDIM // 2, 1),
        pltpu.roll(values, HDIM // 2, 1),
    )
    return values * cosine + other * sine_vals


def fetch_rows(pieces, x_sc):
    step = pl.program_id(0)
    half = QB // 2
    for k in range(8):
        chunk, slot = k // 4, k % 4

        @pl.when(step == k)
        def _():
            if len(pieces) == 5 and slot < 3:
                x_sc[...] = pieces[slot][chunk * QB : (chunk + 1) * QB, :]
            elif len(pieces) == 5:
                x_sc[...] = pieces[3 + chunk][...]
            elif slot < 3:
                x_sc[...] = pieces[chunk * 5 + slot][...]
            else:
                x_sc[:half] = pieces[chunk * 5 + 3][...]
                x_sc[half:] = pieces[chunk * 5 + 4][...]


def whole(shape):
    return pl.BlockSpec(shape, lambda i: (0,) * len(shape), pipeline_mode=pl.Buffered(1))


def project_kernel(*refs):
    w_ref, cos_ref, sin_ref, q_ref, kv_ref, x_sc, w_sc = refs[5:]
    thin = w_sc.shape[0] // 32
    fetch_rows(refs[:5], x_sc)

    @pl.when(pl.program_id(0) == 0)
    def _():
        straighten(w_ref, w_sc, thin)

    y = mul(x_sc[...], w_sc[...])
    cosine, sine_vals = cos_ref[...], sin_ref[...]
    for k in range(NH):
        piece = swing(y[:, k * 128 : (k + 1) * 128], cosine, sine_vals)
        for j in range(2):
            head = 2 * k + j
            if head < NH:
                q_ref[head] = (piece[:, j * HDIM : (j + 1) * HDIM] * 0.125).astype(BF)
        if 2 * k + 1 > NH:
            kv_ref[:, k * 128 : (k + 1) * 128] = piece.astype(BF)
        elif 2 * k + 1 == NH:
            kv_ref[:, k * 128 + HDIM : (k + 1) * 128] = piece[:, HDIM:].astype(BF)
    kv_ref[:, :PART] = y[:, 2 * PART :].astype(BF)


def project(normed, w_all, cosine, sine_vals):
    rows = sum(v.shape[0] for v in normed)
    width = normed[0].shape[1]
    full = w_all.shape
    return pl.pallas_call(
        project_kernel,
        out_shape=[
            jax.ShapeDtypeStruct((NH, rows, HDIM), BF),
            jax.ShapeDtypeStruct((rows, 2 * PART), BF),
            jax.ShapeDtypeStruct((rows, width), BF),
        ],
        grid=(rows // QB,),
        in_specs=[whole(v.shape) for v in normed]
        + [
            whole(full),
            pl.BlockSpec((QB, 128), lambda i: (i, 0)),
            pl.BlockSpec((QB, 128), lambda i: (i, 0)),
        ],
        out_specs=[
            pl.BlockSpec((NH, QB, HDIM), lambda i: (0, i, 0)),
            pl.BlockSpec((QB, 2 * PART), lambda i: (i, 0)),
            pl.BlockSpec((QB, width), lambda i: (i % 4 * 2 + i // 4, 0)),
        ],
        scratch_shapes=[pltpu.VMEM((width, full[3]), BF)],
        compiler_params=room(),
        cost_estimate=cost(2 * rows * width * full[3], 2 * (rows * width + width * full[3] + rows * 5 * PART)),
        name="project",
    )(*normed, w_all, cosine, sine_vals)


def sort_kernel(order_ref, *refs):
    k_ref, v_ref, kt_ref, vt_ref = refs[16:]
    first = pl.program_id(0) * 8
    for j in range(8):
        from_mine = order_ref[first + j] < 32
        tile = jnp.where(from_mine, refs[j][0], refs[8 + j][0])
        rows = slice(j * BLK, (j + 1) * BLK)
        for h in range(NH):
            v_ref[h, rows, :] = tile[:, h * HDIM : (h + 1) * HDIM]
            k_ref[h, rows, :] = tile[:, PART + h * HDIM : PART + (h + 1) * HDIM]
    for h in range(NH):
        kt_ref[h] = k_ref[h].T
        vt_ref[h] = v_ref[h].T


def sort_keys(order, mine, theirs):
    count = order.shape[0]
    shape = (1, BLK, 2 * PART)
    near = lambda j: pl.BlockSpec(shape, lambda i, o: (jnp.minimum(o[i * 8 + j], 31), 0, 0))
    far = lambda j: pl.BlockSpec(shape, lambda i, o: (jnp.maximum(o[i * 8 + j] - 32, 0), 0, 0))
    return pl.pallas_call(
        sort_kernel,
        out_shape=[jax.ShapeDtypeStruct((NH, count * BLK, HDIM), BF)] * 2
        + [jax.ShapeDtypeStruct((NH, HDIM, count * BLK), BF)] * 2,
        grid_spec=pltpu.PrefetchScalarGridSpec(
            num_scalar_prefetch=1,
            grid=(count // 8,),
            in_specs=[near(j) for j in range(8)] + [far(j) for j in range(8)],
            out_specs=[pl.BlockSpec((NH, 8 * BLK, HDIM), lambda i, o: (0, i, 0))] * 2
            + [pl.BlockSpec((NH, HDIM, 8 * BLK), lambda i, o: (0, 0, i))] * 2,
        ),
        compiler_params=room(),
        cost_estimate=cost(0, 64 * count * BLK * PART),
        name="sort_keys",
    )(order, *([mine.reshape(32, BLK, 2 * PART)] * 8), *([theirs.reshape(32, BLK, 2 * PART)] * 8))


def lane_tile(vals):
    shape = (1, len(vals) * BLK)
    lane = lax.broadcasted_iota(jnp.int32, shape, 1)
    out = jnp.full(shape, vals[-1], jnp.int32)
    for j in range(len(vals) - 2, -1, -1):
        out = jnp.where(lane < (j + 1) * BLK, vals[j], out)
    return out, lane & (BLK - 1)


def block_facts(tiles_ref, len_ref, block, step, size):
    half_tiles = PLEN // BLK
    count = size // BLK
    t = [tiles_ref[block * count + j] for j in range(count)]
    tile, within = lane_tile(t)
    qpos = tile * BLK + within
    tmax = functools.reduce(jnp.maximum, t)
    tmin = functools.reduce(jnp.minimum, t)
    per = step // BLK
    is_cont = t[0] >= half_tiles
    n_all = jnp.where(is_cont, PLEN // step, tmax // per + 1)
    n_free = jnp.where(is_cont, PLEN // step, tmin // per)
    conts = [jnp.maximum(v - half_tiles, 0) // 4 for v in t]
    lens = lane_tile([len_ref[v] for v in conts])[0]
    qin = qpos - PLEN - lane_tile(conts)[0] * CLEN
    starts = [pl.multiple_of(PLEN + v * CLEN, CLEN) for v in conts]
    kin = lax.broadcasted_iota(jnp.int32, (CLEN, size), 0)
    seen = lambda: (kin <= qin) & (kin < lens)
    return qpos, is_cont, n_all, n_free, starts, seen


def forward_kernel(
    tiles_ref, len_ref, q_ref, k_ref, vt_sc, o_ref, lse_ref, mx_ref, ot_sc, shift
):
    block = pl.program_id(0) + shift
    qpos, is_cont, n_all, n_free, starts, seen = block_facts(
        tiles_ref, len_ref, block, KB_FWD, QB
    )

    def heads(group, carry):
        hs = [group * HEAD_STEP + j for j in range(HEAD_STEP)]
        qs = [q_ref[h] for h in hs]

        def update(scores, states, weigh):
            out = []
            for n, (s, (m, l, acc)) in enumerate(zip(scores, states)):
                mn = jnp.maximum(m, jnp.max(s, axis=0, keepdims=True))
                p = jnp.exp(s - mn)
                al = jnp.exp(m - mn)
                out.append(
                    (
                        mn,
                        l * al + jnp.sum(p, axis=0, keepdims=True),
                        acc * al + weigh(n, p.astype(BF)),
                    )
                )
            return tuple(out)

        def step(kb, states, masked):
            base = pl.multiple_of(kb * KB_FWD, KB_FWD)
            rows = pl.ds(base, KB_FWD)
            scores = [mul(k_ref[h, rows, :], q, NT) for h, q in zip(hs, qs)]
            if masked:
                kpos = base + lax.broadcasted_iota(jnp.int32, (KB_FWD, QB), 0)
                vis = kpos <= qpos
                scores = [jnp.where(vis, s, masked_value) for s in scores]
            return update(scores, states, lambda n, p: mul(vt_sc[hs[n], :, rows], p))

        states = tuple(
            (
                jnp.full((1, QB), masked_value, F32),
                jnp.zeros((1, QB), F32),
                jnp.zeros((HDIM, QB), F32),
            )
            for _ in hs
        )
        states = lax.fori_loop(0, n_free, functools.partial(step, masked=False), states)
        states = lax.fori_loop(n_free, n_all, functools.partial(step, masked=True), states)

        def own(states):
            vis = seen()
            cols = lambda x, j: x[:, j * BLK : (j + 1) * BLK]
            scores = []
            for h, q in zip(hs, qs):
                s = [
                    mul(k_ref[h, pl.ds(starts[j], CLEN), :], q[j * BLK : (j + 1) * BLK], NT)
                    for j in range(4)
                ]
                scores.append(jnp.where(vis, jnp.concatenate(s, axis=1), masked_value))
            return update(
                scores,
                states,
                lambda n, p: jnp.concatenate(
                    [
                        mul(vt_sc[hs[n], :, pl.ds(starts[j], CLEN)], cols(p, j))
                        for j in range(4)
                    ],
                    axis=1,
                ),
            )

        states = lax.cond(is_cont, own, lambda s: s, states)
        for h, (m, l, acc) in zip(hs, states):
            ot_sc[h] = acc / l
            lse_ref[0, pl.ds(h, 1), :] = m + jnp.log(l)
            mx_ref[0, pl.ds(h, 1), :] = m
        return carry

    lax.fori_loop(0, NH // HEAD_STEP, heads, 0)
    for h in range(NH):
        o_ref[:, h * HDIM : (h + 1) * HDIM] = ot_sc[h].T.astype(BF)


def attention_forward(tiles, lengths, queries, keys, values_t, shift, count):
    rows = count * QB
    span = keys.shape[1]
    once = lambda *shape: pl.BlockSpec(
        shape, lambda i, a, b: (0, 0, 0), pipeline_mode=pl.Buffered(1)
    )
    stat = pl.BlockSpec((1, NH, QB), lambda i, a, b: (i, 0, 0))
    return pl.pallas_call(
        functools.partial(forward_kernel, shift=shift),
        out_shape=[
            jax.ShapeDtypeStruct((rows, PART), BF),
            jax.ShapeDtypeStruct((count, NH, QB), F32),
            jax.ShapeDtypeStruct((count, NH, QB), F32),
        ],
        grid_spec=pltpu.PrefetchScalarGridSpec(
            num_scalar_prefetch=2,
            grid=(count,),
            in_specs=[
                pl.BlockSpec((NH, QB, HDIM), lambda i, a, b: (0, i + shift, 0)),
                once(NH, span, HDIM),
                once(NH, HDIM, span),
            ],
            out_specs=[pl.BlockSpec((QB, PART), lambda i, a, b: (i, 0)), stat, stat],
            scratch_shapes=[pltpu.VMEM((NH, HDIM, QB), F32)],
        ),
        compiler_params=room(),
        cost_estimate=cost(rows * PART * PLEN * 20, 16 * span * PART),
        name="attention_forward",
    )(tiles, lengths, queries, keys, values_t)


def delta_kernel(*refs):
    w_ref, o_ref, gh_ref, delta_ref, gw_ref, x_sc = refs[10:]
    step = pl.program_id(0)
    rows = pl.ds(pl.multiple_of(step * QB, QB), QB)
    fetch_rows(refs[:10], x_sc.at[rows, :])
    grad = mul(x_sc[rows, :], w_ref[...], NT).astype(BF)
    for h in range(NH):
        gh_ref[h] = grad[:, h * HDIM : (h + 1) * HDIM]
    prod = grad.astype(F32) * o_ref[rows, :].astype(F32)
    high = prod.astype(BF)
    low = (prod - high.astype(F32)).astype(BF)
    row = lax.broadcasted_iota(jnp.int32, (16, PART), 0)
    col = lax.broadcasted_iota(jnp.int32, (16, PART), 1)
    pick_head = jnp.where(col // HDIM == row, 1.0, 0.0).astype(BF)
    total = mul(pick_head, high, NT) + mul(pick_head, low, NT)
    delta_ref[0] = total[:NH]

    @pl.when(step == pl.num_programs(0) - 1)
    def _():
        for k in range(3):
            cols = slice(k * 768, (k + 1) * 768)
            gw_ref[:, cols] = mul(o_ref[...], x_sc[:, cols], TN).astype(BF)


def attention_delta(grad_branch, w_out, attended):
    rows, width = attended.shape[0], w_out.shape[1]
    count = rows // QB
    return pl.pallas_call(
        delta_kernel,
        out_shape=[
            jax.ShapeDtypeStruct((NH, rows, HDIM), BF),
            jax.ShapeDtypeStruct((count, NH, QB), F32),
            jax.ShapeDtypeStruct((PART, width), BF),
        ],
        grid=(count,),
        in_specs=[whole(v.shape) for v in grad_branch]
        + [whole((PART, width)), whole((rows, PART))],
        out_specs=[
            pl.BlockSpec((NH, QB, HDIM), lambda i: (0, i, 0)),
            pl.BlockSpec((1, NH, QB), lambda i: (i, 0, 0)),
            pl.BlockSpec((PART, width), lambda i: (0, 0)),
        ],
        scratch_shapes=[pltpu.VMEM((rows, width), BF)],
        compiler_params=room(),
        cost_estimate=cost(2 * rows * width * PART, 2 * rows * width),
        name="attention_delta",
    )(*grad_branch, w_out, attended)


def backward_kernel(
    tiles_ref, len_ref, q_ref, g_ref, lse_ref, delta_ref, k_ref, v_ref, kt_ref, dq_ref, dk_out, dv_out,
    dk_ref, dv_ref, first
):
    h = pl.program_id(0) + first
    block = pl.program_id(1)

    @pl.when(block == 0)
    def _():
        dk_ref[...] = jnp.zeros_like(dk_ref)
        dv_ref[...] = jnp.zeros_like(dv_ref)

    qpos, is_cont, n_all, n_free, starts, seen = block_facts(
        tiles_ref, len_ref, block, KB, QB_BACK
    )
    q = q_ref[0]
    g = g_ref[0]
    stat = lambda ref: jnp.concatenate(
        [ref[j, pl.ds(h, 1), :] for j in range(QB_BACK // QB)], axis=1
    )
    lse = stat(lse_ref)
    delta = stat(delta_ref)

    def step(kb, dqt, masked):
        base = pl.multiple_of(kb * KB, KB)
        rows = pl.ds(base, KB)
        s = mul(k_ref[0, rows, :], q, NT)
        dp = mul(v_ref[0, rows, :], g, NT)
        if masked:
            kpos = base + lax.broadcasted_iota(jnp.int32, (KB, QB_BACK), 0)
            s = jnp.where(kpos <= qpos, s, masked_value)
        p = jnp.exp(s - lse)
        ds = (p * (dp - delta)).astype(BF)
        dv_ref[rows, :] += mul(p.astype(BF), g)
        dk_ref[rows, :] += mul(ds, q)
        return dqt + mul(kt_ref[0, :, rows], ds)

    dqt = jnp.zeros((HDIM, QB_BACK), F32)
    dqt = lax.fori_loop(0, n_free, functools.partial(step, masked=False), dqt)
    dqt = lax.fori_loop(n_free, n_all, functools.partial(step, masked=True), dqt)
    dq_ref[0] = dqt.T * HDIM ** (-0.5)

    @pl.when(is_cont)
    def _():
        part = lambda x, j: x[j * BLK : (j + 1) * BLK]
        rows = [pl.ds(starts[j], CLEN) for j in range(QB_BACK // BLK)]
        s = jnp.concatenate([mul(k_ref[0, rows[j], :], part(q, j), NT) for j in range(QB_BACK // BLK)], axis=1)
        s = jnp.where(seen(), s, masked_value)
        p = jnp.exp(s - lse)
        dp = jnp.concatenate([mul(v_ref[0, rows[j], :], part(g, j), NT) for j in range(QB_BACK // BLK)], axis=1)
        ds = (p * (dp - delta)).astype(BF)
        pb = p.astype(BF)
        dq = []
        for j in range(QB_BACK // BLK):
            cols = slice(j * BLK, (j + 1) * BLK)
            dv_ref[rows[j], :] += mul(pb[:, cols], part(g, j))
            dk_ref[rows[j], :] += mul(ds[:, cols], part(q, j))
            dq.append(mul(kt_ref[0, :, rows[j]], ds[:, cols]))
        dq_ref[0] += jnp.concatenate(dq, axis=1).T * HDIM ** (-0.5)

    @pl.when(block == pl.num_programs(1) - 1)
    def _():
        dk_out[0] = dk_ref[...].astype(BF)
        dv_out[0] = dv_ref[...].astype(BF)


def attention_backward(tiles, lengths, queries, grads, log_total, row_delta, keys, values, keys_t, group):
    rows = queries.shape[1]
    count = rows // QB_BACK
    span = keys.shape[1]
    first = group * GROUP
    row = pl.BlockSpec((1, QB_BACK, HDIM), lambda h, i, a, b: (h + first, i, 0))
    stat = pl.BlockSpec((QB_BACK // QB, NH, QB), lambda h, i, a, b: (i, 0, 0))
    full = pl.BlockSpec((1, span, HDIM), lambda h, i, a, b: (h + first, 0, 0))
    out = pl.BlockSpec((1, span, HDIM), lambda h, i, a, b: (h, 0, 0))
    return pl.pallas_call(
        functools.partial(backward_kernel, first=first),
        out_shape=[
            jax.ShapeDtypeStruct((GROUP, rows, HDIM), F32),
            jax.ShapeDtypeStruct((GROUP, span, HDIM), BF),
            jax.ShapeDtypeStruct((GROUP, span, HDIM), BF),
        ],
        grid_spec=pltpu.PrefetchScalarGridSpec(
            num_scalar_prefetch=2,
            grid=(GROUP, count),
            in_specs=[
                row,
                row,
                stat,
                stat,
                full,
                full,
                pl.BlockSpec((1, HDIM, span), lambda h, i, a, b: (h + first, 0, 0)),
            ],
            out_specs=[pl.BlockSpec((1, QB_BACK, HDIM), lambda h, i, a, b: (h, i, 0)), out, out],
            scratch_shapes=[pltpu.VMEM((span, HDIM), F32)] * 2,
        ),
        compiler_params=room(),
        cost_estimate=cost(rows * GPART * PLEN * 40, 32 * span * GPART),
        name="attention_backward",
    )(tiles, lengths, queries, grads, log_total, row_delta, keys, values, keys_t)


def restore_kernel(tiles_ref, *refs):
    mine_ref, theirs_ref = refs[16:]

    def write(out_ref):
        for j in range(8):
            rows = slice(j * BLK, (j + 1) * BLK)
            for h in range(GROUP):
                cols = slice(h * HDIM, (h + 1) * HDIM)
                out_ref[rows, cols] = refs[8 + j][h]
                out_ref[rows, GPART + h * HDIM : GPART + (h + 1) * HDIM] = refs[j][h]

    @pl.when(pl.program_id(0) < 4)
    def _():
        write(theirs_ref)

    @pl.when(pl.program_id(0) >= 4)
    def _():
        write(mine_ref)


def restore_keys(tiles, grad_k, grad_v):
    spec = lambda j: pl.BlockSpec((GROUP, BLK, HDIM), lambda i, o: (0, o[i * 8 + j], 0))
    shape = (8 * BLK, 2 * GPART)
    return pl.pallas_call(
        restore_kernel,
        out_shape=[jax.ShapeDtypeStruct((32 * BLK, 2 * GPART), BF)] * 2,
        grid_spec=pltpu.PrefetchScalarGridSpec(
            num_scalar_prefetch=1,
            grid=(8,),
            in_specs=[spec(j) for j in range(8)] * 2,
            out_specs=[
                pl.BlockSpec(shape, lambda i, o: (jnp.maximum(i - 4, 0), 0)),
                pl.BlockSpec(shape, lambda i, o: (jnp.minimum(i, 3), 0)),
            ],
        ),
        compiler_params=room(),
        cost_estimate=cost(0, 64 * 64 * BLK * GPART),
        name="restore_keys",
    )(tiles, *([grad_k] * 8), *([grad_v] * 8))


def unturn_kernel(dq_ref, mine_ref, theirs_ref, cos_ref, sin_ref, g_ref, y_sc):
    kv = mine_ref[...].astype(F32) + theirs_ref[...].astype(F32)
    for h in range(GROUP):
        y_sc[:, h * HDIM : (h + 1) * HDIM] = dq_ref[h]
    y_sc[:, GPART:] = kv[:, GPART:]
    cosine, sine_vals = cos_ref[...], -sin_ref[...]
    for k in range(GROUP):
        cols = slice(k * 128, (k + 1) * 128)
        g_ref[:, cols] = swing(y_sc[:, cols], cosine, sine_vals).astype(BF)
    g_ref[:, 2 * GPART :] = kv[:, :GPART].astype(BF)


def unturn(grad_q, mine, theirs, cosine, sine_vals):
    rows = mine.shape[0]
    size = QB
    row = lambda n: pl.BlockSpec((size, n), lambda i: (i, 0))
    return pl.pallas_call(
        unturn_kernel,
        out_shape=jax.ShapeDtypeStruct((rows, 3 * GPART), BF),
        grid=(rows // size,),
        in_specs=[
            pl.BlockSpec((GROUP, size, HDIM), lambda i: (0, i, 0)),
            row(2 * GPART),
            row(2 * GPART),
            row(128),
            row(128),
        ],
        out_specs=pl.BlockSpec((size, 3 * GPART), lambda i: (i % 4 * 2 + i // 4, 0)),
        scratch_shapes=[pltpu.VMEM((size, 2 * GPART), F32)],
        compiler_params=room(),
        cost_estimate=cost(0, 20 * rows * GPART),
        name="unturn",
    )(grad_q, mine, theirs, cosine, sine_vals)


def unproject_kernel(a_ref, b_ref, c_ref, w_ref, x_ref, w_sc, y_sc):
    thin = w_sc.shape[0] // 32

    @pl.when(pl.program_id(0) == 0)
    def _():
        straighten(w_ref, w_sc, thin)

    for g, ref in enumerate((a_ref, b_ref, c_ref)):
        for k in range(3):
            y_sc[:, k * PART + g * GPART : k * PART + (g + 1) * GPART] = ref[
                :, k * GPART : (k + 1) * GPART
            ]
    x_ref[...] = mul(y_sc[...], w_sc[...], NT).astype(BF)


def unproject(parts, w_all, chunk):
    rows = parts[0].shape[0] // 2
    full = w_all.shape
    width = full[0] * full[1] * (full[2] - 8)
    return pl.pallas_call(
        unproject_kernel,
        out_shape=jax.ShapeDtypeStruct((rows, width), BF),
        grid=(rows // QB,),
        in_specs=[pl.BlockSpec((QB, 3 * GPART), lambda i: (i * 2 + chunk, 0))] * 3
        + [pl.BlockSpec(full, lambda i: (0, 0, 0, 0), pipeline_mode=pl.Buffered(1))],
        out_specs=pl.BlockSpec((QB, width), lambda i: (i, 0)),
        scratch_shapes=[
            pltpu.VMEM((width, full[3]), BF),
            pltpu.VMEM((QB, 3 * PART), BF),
        ],
        compiler_params=room(),
        cost_estimate=cost(2 * rows * width * 3 * PART, 4 * rows * width),
        name="unproject",
    )(*parts, w_all)


def finish_kernel(a_ref, bc_ref, wq_ref, wk_ref, wv_ref, gain_ref, q_ref, k_ref, v_ref, sum_ref):
    thin = gain_ref.shape[0]
    gain = gain_ref[...]
    total = jnp.zeros((thin, 1), F32)
    for p in range(4):
        for g, (ref, first) in enumerate(((a_ref, 0), (bc_ref, 0), (bc_ref, PART))):
            cols = slice(p * PART + g * GPART, p * PART + (g + 1) * GPART)
            for n, (w, out) in enumerate(((wq_ref, q_ref), (wk_ref, k_ref), (wv_ref, v_ref))):
                part = slice(first + n * GPART, first + (n + 1) * GPART)
                grad = ref[p, :thin, part].astype(F32)
                out[:, cols] = grad * gain
                total += jnp.sum(grad * w[:, cols].astype(F32), axis=1, keepdims=True)
    sum_ref[...] = jnp.broadcast_to(total, sum_ref.shape)


def finish(parts, weights, gain):
    thin, width = weights[0].shape
    return pl.pallas_call(
        finish_kernel,
        out_shape=[jax.ShapeDtypeStruct((thin, width), F32)] * 3
        + [jax.ShapeDtypeStruct((thin, 128), F32)],
        compiler_params=room(),
        name="finish",
    )(*parts, *weights, gain)


def split_tiles(rows):
    blocks = rows.reshape(4, 2, rows.shape[0] // 8, rows.shape[1])
    return blocks[:, 0], blocks[:, 1]


def join_tiles(chunks):
    blocks = jnp.stack(chunks, axis=1)
    return blocks.reshape(-1, blocks.shape[-1])


def over(name, blocks):
    return lax.all_to_all(blocks, name, 0, 0, tiled=True)


def quarters(rows):
    return rows.reshape(4, rows.shape[0] // 4, rows.shape[1])


def after(value, *earlier):
    return lax.optimization_barrier((value, earlier))[0]


def flip(values, mask):
    return lax.ppermute(values, "p", [(k, k ^ mask) for k in range(4)])


def gather_near(own):
    return [own, flip(own, 1), flip(own, 2)]


def gather_far(near):
    half = near[0].shape[0] // 2
    return near + [flip(near[2][:half], 1), flip(near[1][half:], 2)]


def slots(terms):
    size = terms.shape[0] // 4
    return [terms[k * size : (k + 1) * size] for k in range(4)]


def scatter_far(terms):
    far = slots(terms)[3]
    half = far.shape[0] // 2
    return flip(far[:half], 1), flip(far[half:], 2)


def scatter_near(terms, far):
    _, first, second, _ = slots(terms)
    half = first.shape[0] // 2
    add = lambda x, y: (x.astype(F32) + y.astype(F32)).astype(BF)
    first = flip(jnp.concatenate([first[:half], add(first[half:], far[1])], axis=0), 1)
    second = flip(jnp.concatenate([add(second[:half], far[0]), second[half:]], axis=0), 2)
    return first, second


def scatter_sum(terms, near):
    return slots(terms)[0].astype(F32) + near[0].astype(F32) + near[1].astype(F32)


def scatter_far_both(terms):
    return flip(slots(terms[0])[3], 1), flip(slots(terms[1])[3], 2)


def scatter_near_both(terms, far):
    early, late = slots(terms[0]), slots(terms[1])
    add = lambda x, y: (x.astype(F32) + y.astype(F32)).astype(BF)
    first = flip(jnp.concatenate([early[1], add(late[1], far[1])], axis=0), 1)
    second = flip(jnp.concatenate([add(early[2], far[0]), late[2]], axis=0), 2)
    return first, second


def meet(*values):
    return lax.optimization_barrier(values)


def swap_blocks(name, pieces):
    return [pieces[0]] + [
        lax.ppermute(pieces[r], name, [(k, k ^ r) for k in range(4)]) for r in (1, 2, 3)
    ]


def pick(pieces, first):
    stacked = jnp.stack(pieces)
    return [
        lax.dynamic_index_in_dim(stacked, jnp.bitwise_xor(first, r), 0, keepdims=False)
        for r in range(4)
    ]


def hidden_cuts(hidden):
    steps = hidden // 8
    sizes = [8 * (steps // 4 + (k < steps % 4)) for k in range(4)]
    starts = [sum(sizes[:k]) for k in range(4)]
    return starts, sizes, max(sizes)


def inner(
    tokens_in,
    cotangent,
    w_query,
    w_key,
    w_value,
    w_output,
    w_gate,
    w_up,
    w_down,
    attn_gain,
    ffn_gain,
    cont_len,
    deal_order,
    clip_threshold,
):
    plane, depth, core = (lax.axis_index(name) for name in ("p", "z", "c"))
    line = ("z", "c")
    width = tokens_in.shape[1]
    thin = w_query.shape[0]
    hidden = w_down.shape[0]
    starts, sizes, share = hidden_cuts(hidden)
    gain_f = attn_gain.astype(F32)
    parts_of = lambda v: [v[k] for k in range(4)]
    cross = lambda v: swap_blocks("p", pick(v, plane))
    cross_whole = lambda v: jnp.stack(pick(cross(parts_of(v)), plane))
    hop_on = lambda v: swap_blocks("z", pick(v, jnp.bitwise_xor(plane, depth)))
    hop_back = lambda v: swap_blocks("z", parts_of(quarters(v)))
    hop_out = lambda v: pick(
        swap_blocks("p", pick(v, jnp.bitwise_xor(plane, depth))), plane
    )
    first_hop = cross(parts_of(quarters(tokens_in)))
    turn_over = [(g * 4 + k, k * 4 + g) for g in range(4) for k in range(4)]
    deal = lax.ppermute(deal_order[0], ("p", "z"), turn_over)
    lengths = lax.ppermute(cont_len[0], ("p", "z"), turn_over)

    scaled = [(w.astype(F32) * gain_f[:, None]).astype(BF) for w in (w_query, w_key, w_value)]
    blocks = jnp.stack(scaled).reshape(3, thin, 4, PART).transpose(2, 1, 0, 3)
    blocks = blocks.reshape(4, thin, 3 * PART)
    extra = jnp.zeros((4, 8, 3 * PART), BF).at[:, 0, :thin].set(ffn_gain[None, :])
    send = jnp.concatenate([blocks, extra], axis=1)
    first_hop, send = meet(first_hop, send)
    early = after((w_gate, w_up, w_down), first_hop)
    stacked = jnp.stack([early[0].T, early[1].T, early[2]])
    stacked = jnp.stack(
        [
            jnp.pad(stacked[:, a : a + n], ((0, 0), (0, share - n), (0, 0)))
            for a, n in zip(starts, sizes)
        ]
    )
    send, moved = meet(cross_whole(send), hop_on(first_hop))
    stacked = cross_whole(stacked)
    w_qkv = lax.all_gather(send, line, axis=0)
    gain_two = w_qkv[:, :, thin, :thin].transpose(1, 0, 2).reshape(width).astype(F32)
    w_out = lax.all_gather(w_output, line, axis=0, tiled=True)
    piece = jnp.arange(2)[:, None, None]
    slot = jnp.arange(4)[None, :, None]
    source = jnp.bitwise_xor(depth, jnp.arange(4))[None, None, :]
    quarter = jnp.bitwise_xor(plane, slot)
    held = lambda which: deal[((source * 2 + which) * 8 + quarter * 2 + piece).reshape(-1)]
    tiles, tiles_far = held(core), held(1 - core)
    both = jnp.concatenate([tiles, tiles_far])
    numbers = jnp.arange(64, dtype=jnp.int32)
    order = jnp.sum(
        jnp.where(both[None, :] == numbers[:, None], numbers[None, :], 0), axis=1
    ).astype(jnp.int32)
    logical = (tiles[:, None] * BLK + jnp.arange(BLK, dtype=jnp.int32)[None, :]).reshape(-1)
    position = jnp.where(logical < PLEN, logical, PLEN + (logical - PLEN) % CLEN)
    cosine, sine_vals = (v[:, 0, :] for v in rope_angles(position))
    cosine = jnp.concatenate([cosine] * 4, axis=1)
    sine_vals = jnp.concatenate([-sine_vals, sine_vals] * 2, axis=1)

    joined = lambda pieces: jnp.concatenate(pieces, axis=0)
    by_chunk = lambda v: [h.reshape(-1, width) for h in split_tiles(joined(v))]
    residual = [v.astype(F32) for v in by_chunk(moved)]
    inverse_of = lambda v: lax.rsqrt(jnp.mean(v * v, axis=-1, keepdims=True) + norm_eps)
    inverse_one = [inverse_of(v) for v in residual]
    pieces = gather_near(joined([(v * r).astype(BF) for v, r in zip(residual, inverse_one)]))
    pieces = gather_far(pieces)

    def in_chunks(pieces):
        size = pieces[0].shape[0] // 2
        return [
            joined([v[k * size : (k + 1) * size] for v in pieces[:3]] + [pieces[3 + k]])
            for k in range(2)
        ]

    pieces, w_qkv, grad_out = meet(pieces, w_qkv, cotangent)
    (queries, mine, normed), grad_out = meet(
        project(pieces, w_qkv, cosine, sine_vals),
        cross(parts_of(quarters(grad_out))),
    )
    theirs = lax.ppermute(mine, "c", [(0, 1), (1, 0)])
    sorted_kv, grad_out, stacked = meet(
        sort_keys(order, mine, theirs), hop_on(grad_out), stacked
    )
    keys, values, keys_t, values_t = sorted_kv
    stacked = stacked.transpose(1, 2, 0, 3).reshape(3, share, width)
    w_ffn = [lax.all_gather(stacked[k], line, axis=0, tiled=True) for k in range(3)]
    attend = lambda q, k, n: attention_forward(tiles, lengths, q, keys, values_t, k, n)
    grad_out = by_chunk(grad_out)
    grad_rows = joined([(branch_scale * v.astype(F32)).astype(BF) for v in grad_out])
    queries, grad_rows = meet(queries, grad_rows)
    (low_a, total_a, peak_a), grad_rows = meet(attend(queries, 0, 4), gather_near(grad_rows))
    branch_a = mul(low_a, w_out).astype(BF)
    branch_a, grad_rows, queries_b = meet(branch_a, grad_rows, queries)
    part_b, far_a = meet(attend(queries_b, 4, 2), scatter_far(branch_a))
    rest_b, near_a, grad_rows = meet(
        attend(queries_b, 6, 2), scatter_near(branch_a, far_a), gather_far(grad_rows)
    )
    low_b, total_b, peak_b = (joined([v, w]) for v, w in zip(part_b, rest_b))
    branch_b = mul(low_b, w_out).astype(BF)
    attended = joined([low_a, low_b])
    log_total = joined([total_a, total_b])
    peaks = joined([peak_a, peak_b])
    grad_rows = in_chunks(grad_rows)

    def second_norm(k, branch):
        after_attn = residual[k] + branch_scale * branch
        inverse_two = inverse_of(after_attn)
        return after_attn, inverse_two, (after_attn * inverse_two * gain_two).astype(BF)

    def hidden_layer(grad_mixed, normed_two):
        gate_pre = mul(normed_two, w_ffn[0], NT)
        up_pre = mul(normed_two, w_ffn[1], NT)
        mixed = (jax.nn.silu(gate_pre) * up_pre).astype(BF)
        return (mixed,) + gate_grads(grad_mixed, gate_pre, up_pre)

    def hidden_back(hidden):
        return (mul(hidden[1], w_ffn[0]) + mul(hidden[2], w_ffn[1])).astype(BF)

    def second_back(k, total, state):
        grad_gain, grad_second = norm_backward(total, state[0], state[1], gain_two)
        grad_resid = grad_out[k].astype(F32) + grad_second
        return grad_gain, grad_resid, (branch_scale * grad_resid).astype(BF)

    state_a = second_norm(0, scatter_sum(branch_a, near_a))
    own, rows_a, rows_b = meet(state_a[2], grad_rows[0], grad_rows[1])
    gather, mixed_a, rows_b, branch_b = meet(
        gather_near(own), mul(rows_a, w_ffn[2], NT), rows_b, branch_b
    )
    gather, far, mixed_b = meet(
        gather_far(gather), scatter_far(branch_b), mul(rows_b, w_ffn[2], NT)
    )
    normed_a = joined(gather)
    hidden_a, near = meet(hidden_layer(mixed_a, normed_a), scatter_near(branch_b, far))
    state_b = second_norm(1, scatter_sum(branch_b, near))
    hidden_a, own = meet(hidden_a, state_b[2])
    rest_a, gather = meet(hidden_back(hidden_a), gather_near(own))
    first = mul(hidden_a[1], normed_a, TN)
    gather, far, gate_a = meet(gather_far(gather), scatter_far(rest_a), first)
    normed_b = joined(gather)
    hidden_b, near = meet(hidden_layer(mixed_b, normed_b), scatter_near(rest_a, far))
    back_a = second_back(0, scatter_sum(rest_a, near), state_a)
    hidden_b, own = meet(hidden_b, back_a[2])
    rest_b, gather_a = meet(hidden_back(hidden_b), gather_near(own))
    grad_gate = (gate_a + mul(hidden_b[1], normed_b, TN)).astype(BF)
    up_a = mul(hidden_a[2], normed_a, TN)
    gather_a, far, grad_gate, up_a = meet(
        gather_far(gather_a), scatter_far(rest_b), grad_gate, up_a
    )
    grad_up = (up_a + mul(hidden_b[2], normed_b, TN)).astype(BF)
    down_a = mul(hidden_a[0], rows_a, TN)
    near, grad_up, down_a = meet(scatter_near(rest_b, far), grad_up, down_a)
    back_b = second_back(1, scatter_sum(rest_b, near), state_b)
    own, mixed_b_rows, down_a = meet(back_b[2], hidden_b[0], down_a)
    grad_down = (down_a + mul(mixed_b_rows, rows_b, TN)).astype(BF)
    gather_b, grad_down, ffn_b = meet(
        gather_near(own), grad_down, mul(mixed_b_rows, w_ffn[2]).astype(BF)
    )
    gather_b, ffn_a = meet(gather_far(gather_b), mul(hidden_a[0], w_ffn[2]).astype(BF))
    branch_ffn = [ffn_a, ffn_b]
    sum_rows = lambda v: lax.psum_scatter(v, line, scatter_dimension=0, tiled=True)
    grad_pieces = gather_a + gather_b
    grad_gain_two = back_a[0] + back_b[0]
    grad_resid = [back_a[1], back_b[1]]

    grad_pieces, branch_ffn = meet(grad_pieces, branch_ffn)
    (grad_heads, row_delta, grad_w_part), far, grad_gate = meet(
        attention_delta(grad_pieces, w_out, attended),
        scatter_far_both(branch_ffn),
        sum_rows(grad_gate),
    )
    far_order = jnp.concatenate([tiles_far, tiles])
    gain_rows = grad_gain_two.astype(BF).reshape(4, 8, 1, thin).transpose(1, 0, 2, 3)
    peak = jnp.max(peaks, axis=(0, 2))
    peak_high = lax.reduce_precision(peak, 8, 7)
    peak_rows = jnp.stack([peak_high.astype(BF), (peak - peak_high).astype(BF)])
    mine_slot = (jnp.arange(8) == depth * 2 + core)[None, :, None]
    peak_rows = jnp.where(mine_slot, peak_rows[:, None, :], 0).reshape(2, 8 * NH)
    widen = lambda v: jnp.pad(v, ((0, 0), (0, 0), (0, 0), (0, 3 * GPART - v.shape[3])))
    gain_rows = jnp.concatenate(
        [
            widen(gain_rows),
            widen(jnp.broadcast_to(peak_rows, (8, 4, 2, 8 * NH))),
            jnp.zeros((8, 4, 5, 3 * GPART), BF),
        ],
        axis=2,
    )

    def back_group(g, grads):
        return attention_backward(
            tiles, lengths, queries, grads, log_total, row_delta, keys, values, keys_t, g
        )

    def restore(part):
        return (part[0],) + tuple(restore_keys(far_order, part[1], part[2]))

    def weight_part(grad_qkv):
        proj = mul(normed, grad_qkv, TN).astype(BF).reshape(4, 8, thin, 3 * GPART)
        proj = jnp.concatenate([proj.transpose(1, 0, 2, 3), gain_rows], axis=2)
        return proj.reshape(8 * 4 * (thin + 8), 3 * GPART)

    def sum_line(proj):
        proj = lax.psum_scatter(proj, line, scatter_dimension=0, tiled=True)
        return proj.reshape(4, thin + 8, 3 * GPART)

    trade = lambda v: lax.ppermute(v, "c", [(0, 1), (1, 0)])
    grad_heads, grad_w_part = meet(grad_heads, grad_w_part)
    grad_down = sum_rows(grad_down)
    part_a, grad_heads, near, grad_up = meet(
        back_group(0, grad_heads),
        grad_heads,
        scatter_near_both(branch_ffn, far),
        sum_rows(grad_up),
    )
    grad_w_output = sum_rows(grad_w_part)
    part_a = restore(part_a)
    states = (state_a, state_b)
    output = []
    for k, (state, v) in enumerate(zip(states, branch_ffn)):
        size = state[0].shape[0]
        total = scatter_sum(v, [w[k * size : (k + 1) * size] for w in near])
        output.append(quarters((state[0] + branch_scale * total).astype(BF)))
    output = join_tiles(output)
    output, grad_heads, part_a = meet(output, grad_heads, part_a)
    part_b, grad_heads, hops, far_a, grad_down = meet(
        back_group(1, grad_heads),
        grad_heads,
        hop_back(output),
        trade(part_a[2]),
        grad_down,
    )
    ffn_grads = jnp.stack([grad_gate, grad_up, grad_down])
    ffn_grads = ffn_grads.reshape(3, share, 4, PART).transpose(2, 0, 1, 3)
    part_b = restore(part_b)
    grads_a = unturn(part_a[0], part_a[1], far_a, cosine, sine_vals)
    weights_a = weight_part(grads_a)
    grad_heads, weights_a, hops, part_b, ffn_grads = meet(
        grad_heads, weights_a, hops, part_b, ffn_grads
    )
    part_c, hops, ffn_grads, far_b = meet(
        back_group(2, grad_heads), hops, cross_whole(ffn_grads), trade(part_b[2])
    )
    weights_a = sum_line(weights_a)
    part_c, far_b = meet(restore(part_c), far_b)
    grads_b = unturn(part_b[0], part_b[1], far_b, cosine, sine_vals)
    weights_b, far_c, output = meet(weight_part(grads_b), trade(part_c[2]), hop_out(hops))
    output = joined(output)
    grads_c, weights_a = meet(
        unturn(part_c[0], part_c[1], far_c, cosine, sine_vals), weights_a
    )
    grads = (grads_a, grads_b, grads_c)
    rest_a, grads, weights_a = meet(unproject(grads, w_qkv, 0), grads, cross_whole(weights_a))
    weights_c, far_a, grads = meet(weight_part(grads[2]), scatter_far(rest_a), grads)
    weights_c = sum_line(weights_c)
    rest_b, near_a, weights_b, grad_w_output = meet(
        unproject(grads, w_qkv, 1),
        scatter_near(rest_a, far_a),
        sum_line(weights_b),
        grad_w_output,
    )
    far_b = scatter_far(rest_b)

    def first_back(k, total):
        grad_first = inverse_one[k] * total - residual[k] * inverse_one[k] ** 3 * jnp.mean(
            total * residual[k], axis=-1, keepdims=True
        )
        return (grad_resid[k] + grad_first).astype(BF)

    hop_a = hop_back(first_back(0, scatter_sum(rest_a, near_a)))
    near_b = scatter_near(rest_b, far_b)
    hop_a, near_b = meet(hop_a, near_b)
    hop_b, hop_a = meet(hop_back(first_back(1, scatter_sum(rest_b, near_b))), hop_out(hop_a))
    grad_input = join_tiles([jnp.stack(hop_a), jnp.stack(hop_out(hop_b))]).astype(F32)
    ffn_grads = ffn_grads.astype(F32)
    ffn_grads = jnp.concatenate([ffn_grads[k, :, :n] for k, n in enumerate(sizes)], axis=1)
    grad_ffn_gain = jnp.sum(weights_a[:, thin, :thin].astype(F32), axis=0)
    weights_bc = over("p", jnp.concatenate([weights_b, weights_c], axis=2))
    proj = finish(
        (weights_a, weights_bc), (w_query, w_key, w_value), gain_f[:, None]
    )
    grad_attn_gain = proj[3][:, 0]

    maxima = jnp.sum(weights_a[:, thin + 1 : thin + 3, : 8 * NH].astype(F32), axis=1)
    maxima = jnp.max(maxima.reshape(4, 8, NH), axis=1).reshape(HEADS)
    limit_value = clip_threshold[0].astype(F32)
    clip_factor = jnp.sqrt(limit_value / jnp.maximum(maxima, limit_value))
    column_factor = jnp.repeat(clip_factor, HDIM)
    return (
        output,
        grad_input,
        proj[0],
        proj[1],
        proj[2],
        grad_w_output.astype(F32),
        ffn_grads[0].T,
        ffn_grads[1].T,
        ffn_grads[2],
        grad_attn_gain,
        grad_ffn_gain,
        maxima,
        clip_factor,
        w_query.astype(F32) * column_factor[None, :],
        w_key.astype(F32) * column_factor[None, :],
    )


def specs(grp, ctx):
    every = grp + ctx
    ins = [P(every, None)] * 6 + [P(grp, ctx), P(grp, ctx), P(ctx, grp), P(every), P(every)]
    ins += [P(grp, None), P(grp, None), P()]
    outs = [P(every, None)] * 6 + [P(grp, ctx), P(grp, ctx), P(ctx, grp), P(every), P(every)]
    outs += [P(), P(), P(every, None), P(every, None)]
    return tuple(ins), tuple(outs)


def solution(mesh):
    if mesh.shape["grp"] == 4 and mesh.shape["ctx"] == 8:
        mesh = Mesh(mesh.devices.reshape(4, 4, 2), ("p", "z", "c"))
        body, (in_specs, out_specs) = inner, specs(("p",), ("z", "c"))
    else:
        body, (in_specs, out_specs) = local, specs(("grp",), ("ctx",))
    return jax.shard_map(body, mesh=mesh, in_specs=in_specs, out_specs=out_specs, check_vma=False)
```

```python
import functools
import math

import jax
import jax.numpy as jnp
from jax import lax
from jax.experimental import pallas as pl
from jax.experimental.pallas import tpu as pltpu
from jax.sharding import Mesh
from jax.sharding import PartitionSpec as P

HEADS = 36
HDIM = 64
PLEN = 2048
CLEN = 256
NCONT = 8
BLK = 64
FAMTOK = 4096

F32 = jnp.float32
BF = jnp.bfloat16
NH = HEADS // 4
PART = NH * HDIM
GROUP = 3
GPART = GROUP * HDIM
QB_BACK = 512
QB = 256
KB = 1024
KB_FWD = 1024
HEAD_STEP = 9
NT = (((1,), (1,)), ((), ()))
NN = (((1,), (0,)), ((), ()))
TN = (((0,), (0,)), ((), ()))
VMEM_ROOM = 56 * 1024 * 1024


branch_scale = 1.4 / math.sqrt(40.0)
norm_eps = 1e-05
rope_base = 10000.0
masked_value = -1e30


def rope_angles(position):
    half_dim = HDIM // 2
    frequency = rope_base ** (-(jnp.arange(half_dim, dtype=jnp.float32) * (2.0 / HDIM)))
    angles = position.astype(jnp.float32)[:, None] * frequency[None, :]
    return (jnp.cos(angles)[:, None, :], jnp.sin(angles)[:, None, :])


def rotate(values, cosine, sine_vals, turn_sign):
    row_count = values.shape[0]
    shaped = values.reshape(row_count, HEADS, HDIM)
    leading = shaped[..., : HDIM // 2]
    trailing = shaped[..., HDIM // 2 :]
    turned = jnp.concatenate(
        [
            leading * cosine - turn_sign * trailing * sine_vals,
            trailing * cosine + turn_sign * leading * sine_vals,
        ],
        axis=-1,
    )
    return turned.reshape(row_count, HEADS * HDIM)


def token_facts(logical, lengths):
    family = logical // FAMTOK
    offset = logical % FAMTOK
    prompt = offset < PLEN
    member = jnp.clip((offset - PLEN) // CLEN, 0, NCONT - 1)
    inside = offset - PLEN - member * CLEN
    seq_id = jnp.where(prompt, -1, family * NCONT + member)
    numbers = jnp.arange(lengths.shape[0], dtype=jnp.int32)
    live_len = jnp.sum(jnp.where(seq_id[:, None] == numbers[None, :], lengths[None, :], 0), axis=1)
    is_live = prompt | (inside < live_len)
    position = jnp.where(prompt, offset, PLEN + inside)
    return (family, offset, prompt, seq_id, is_live, position)


def visible(query_facts, key_part):
    same_family = query_facts[0][:, None] == key_part[0][None, :]
    causal = key_part[1][None, :] <= query_facts[1][:, None]
    reaches = (
        key_part[2][None, :]
        | (key_part[3][None, :] == query_facts[3][:, None]) & key_part[4][None, :]
    )
    return same_family & causal & reaches


def key_slice(keys_heads, values_heads, key_facts, query_facts, first_row, span_rows):
    key_block = lax.dynamic_slice_in_dim(keys_heads, first_row, span_rows, 0)
    value_block = lax.dynamic_slice_in_dim(values_heads, first_row, span_rows, 0)
    key_part = tuple(
        (
            lax.dynamic_slice_in_dim(member_array, first_row, span_rows, 0)
            for member_array in key_facts
        )
    )
    return (key_block, value_block, visible(query_facts, key_part))


def block_scores(query_heads, key_block, visible_mask):
    scores = jnp.einsum(
        "qhd,khd->hqk", query_heads, key_block, preferred_element_type=jnp.float32
    ) * HDIM ** (-0.5)
    return jnp.where(visible_mask[None], scores, masked_value)


def score_grads(
    query_heads, grad_heads, log_total, row_delta, key_block, value_block, visible_mask
):
    scores = block_scores(query_heads, key_block, visible_mask)
    prob_table = jnp.where(visible_mask[None], jnp.exp(scores - log_total[:, :, None]), 0.0)
    grad_probs = jnp.einsum(
        "qhd,khd->hqk", grad_heads, value_block, preferred_element_type=jnp.float32
    )
    grad_scores = (prob_table * (grad_probs - row_delta[:, :, None])).astype(jnp.bfloat16)
    return (prob_table.astype(jnp.bfloat16), grad_scores)


def gate_grads(grad_mixed, gate_pre, up_pre):
    sigmoid = jax.nn.sigmoid(gate_pre)
    grad_gate = grad_mixed * up_pre * sigmoid * (1.0 + gate_pre * (1.0 - sigmoid))
    grad_up = grad_mixed * gate_pre * sigmoid
    return (grad_gate.astype(jnp.bfloat16), grad_up.astype(jnp.bfloat16))


def norm_backward(grad_normed, values, inverse, gain):
    scaled = grad_normed * gain[None, :]
    grad_gain = jnp.sum(grad_normed * values * inverse, axis=0)
    grad_values = inverse * scaled - values * inverse**3 * jnp.mean(
        scaled * values, axis=-1, keepdims=True
    )
    return (grad_gain, grad_values)


def attention_weights(w_query, w_key, w_value, w_output, attn_gain, ffn_gain):
    return (
        lax.all_gather(w_query, ("grp", "ctx"), axis=0, tiled=True),
        lax.all_gather(w_key, ("grp", "ctx"), axis=0, tiled=True),
        lax.all_gather(w_value, ("grp", "ctx"), axis=0, tiled=True),
        lax.all_gather(w_output, ("grp", "ctx"), axis=0, tiled=True),
        lax.all_gather(attn_gain, ("grp", "ctx"), axis=0, tiled=True),
        lax.all_gather(ffn_gain, ("grp", "ctx"), axis=0, tiled=True),
    )


def ffn_rows_gather(w_gate, w_up, w_down):
    return (
        lax.all_gather(w_gate, "grp", axis=0, tiled=True),
        lax.all_gather(w_up, "grp", axis=0, tiled=True),
        lax.all_gather(w_down, "grp", axis=1, tiled=True),
    )


def local(
    tokens_in,
    cotangent,
    w_query,
    w_key,
    w_value,
    w_output,
    w_gate,
    w_up,
    w_down,
    attn_gain,
    ffn_gain,
    cont_len,
    deal_order,
    clip_threshold,
):
    row_count = tokens_in.shape[0]
    model_width = tokens_in.shape[1]
    tile_count = deal_order.shape[1]
    group_rows = tile_count * BLK
    lengths = cont_len[0]
    my_index = lax.axis_index("ctx")
    tile_offsets = jnp.arange(BLK, dtype=jnp.int32)
    stored_logical = (deal_order[0][:, None] * BLK + tile_offsets[None, :]).reshape(group_rows)
    key_facts = token_facts(stored_logical, lengths)
    query_facts = tuple(
        (
            lax.dynamic_slice_in_dim(member_array, my_index * row_count, row_count, 0)
            for member_array in key_facts
        )
    )
    cosine, sine_vals = rope_angles(query_facts[5])
    key_step = math.gcd(group_rows, 512)
    key_blocks = group_rows // key_step
    full_query, full_key, full_value, full_output, gain_one, gain_two = attention_weights(
        w_query, w_key, w_value, w_output, attn_gain, ffn_gain
    )
    residual = tokens_in.astype(jnp.float32)
    inverse_one = lax.rsqrt(jnp.mean(residual * residual, axis=-1, keepdims=True) + norm_eps)
    gain_one_f = gain_one.astype(jnp.float32)
    gain_two_f = gain_two.astype(jnp.float32)
    normed_one = (residual * inverse_one * gain_one_f).astype(jnp.bfloat16)
    query_rot = rotate(
        jnp.dot(normed_one, full_query, preferred_element_type=jnp.float32), cosine, sine_vals, 1.0
    ).astype(jnp.bfloat16)
    key_rot = rotate(
        jnp.dot(normed_one, full_key, preferred_element_type=jnp.float32), cosine, sine_vals, 1.0
    ).astype(jnp.bfloat16)
    value_low = jnp.dot(normed_one, full_value, preferred_element_type=jnp.float32).astype(
        jnp.bfloat16
    )
    keys_all, values_all = (
        lax.all_gather(key_rot, "ctx", axis=0, tiled=True),
        lax.all_gather(value_low, "ctx", axis=0, tiled=True),
    )
    query_heads = query_rot.reshape(row_count, HEADS, HDIM)
    keys_heads = keys_all.reshape(group_rows, HEADS, HDIM)
    values_heads = values_all.reshape(group_rows, HEADS, HDIM)

    def stats_step(block_index, state_carry):
        key_block, value_block, visible_mask = key_slice(
            keys_heads, values_heads, key_facts, query_facts, block_index * key_step, key_step
        )

        def stats_busy(carry):
            run_max, run_sum, head_max = carry
            scores = block_scores(query_heads, key_block, visible_mask)
            block_max = jnp.max(scores, axis=2)
            new_max = jnp.maximum(run_max, block_max)
            exp_table = jnp.where(visible_mask[None], jnp.exp(scores - new_max[:, :, None]), 0.0)
            new_sum = run_sum * jnp.exp(run_max - new_max) + jnp.sum(exp_table, axis=2)
            return (new_max, new_sum, jnp.maximum(head_max, jnp.max(block_max, axis=1)))

        return lax.cond(jnp.any(visible_mask), stats_busy, lambda carry: carry, state_carry)

    start_state = (
        jnp.full((HEADS, row_count), masked_value, jnp.float32),
        jnp.zeros((HEADS, row_count), jnp.float32),
        jnp.full((HEADS,), masked_value, jnp.float32),
    )
    run_max, run_sum, head_max = lax.fori_loop(0, key_blocks, stats_step, start_state)
    log_total = run_max + jnp.log(run_sum)

    def output_step(block_index, running):
        key_block, value_block, visible_mask = key_slice(
            keys_heads, values_heads, key_facts, query_facts, block_index * key_step, key_step
        )

        def output_busy(total):
            scores = block_scores(query_heads, key_block, visible_mask)
            prob_low = jnp.where(
                visible_mask[None], jnp.exp(scores - log_total[:, :, None]), 0.0
            ).astype(jnp.bfloat16)
            return total + jnp.einsum(
                "hqk,khd->qhd", prob_low, value_block, preferred_element_type=jnp.float32
            )

        return lax.cond(jnp.any(visible_mask), output_busy, lambda total: total, running)

    attended = lax.fori_loop(
        0, key_blocks, output_step, jnp.zeros((row_count, HEADS, HDIM), jnp.float32)
    )
    attn_low = attended.reshape(row_count, model_width).astype(jnp.bfloat16)
    after_attn = residual + branch_scale * jnp.dot(
        attn_low, full_output, preferred_element_type=jnp.float32
    )
    inverse_two = lax.rsqrt(jnp.mean(after_attn * after_attn, axis=-1, keepdims=True) + norm_eps)
    normed_two = (after_attn * inverse_two * gain_two_f).astype(jnp.bfloat16)
    gate_cols, up_cols, down_cols = ffn_rows_gather(w_gate, w_up, w_down)
    normed_rows = lax.all_gather(normed_two, "ctx", axis=0, tiled=True)
    gate_pre = jnp.dot(normed_rows, gate_cols, preferred_element_type=jnp.float32)
    up_pre = jnp.dot(normed_rows, up_cols, preferred_element_type=jnp.float32)
    mixed = (jax.nn.silu(gate_pre) * up_pre).astype(jnp.bfloat16)
    branch_ffn = lax.psum_scatter(
        jnp.dot(mixed, down_cols, preferred_element_type=jnp.float32).astype(jnp.bfloat16),
        "ctx",
        scatter_dimension=0,
        tiled=True,
    ).astype(jnp.float32)
    output = (after_attn + branch_scale * branch_ffn).astype(jnp.bfloat16)
    grad_out = cotangent.astype(jnp.float32)
    grad_branch = (branch_scale * grad_out).astype(jnp.bfloat16)
    gate_again, up_again, down_again = ffn_rows_gather(w_gate, w_up, w_down)
    grad_rows = lax.all_gather(grad_branch, "ctx", axis=0, tiled=True)
    grad_mixed = jnp.dot(grad_rows, down_again.T, preferred_element_type=jnp.float32)
    grad_down = jnp.dot(mixed.T, grad_rows, preferred_element_type=jnp.float32)
    grad_gate_low, grad_up_low = gate_grads(grad_mixed, gate_pre, up_pre)
    grad_gate = jnp.dot(normed_rows.T, grad_gate_low, preferred_element_type=jnp.float32)
    grad_up = jnp.dot(normed_rows.T, grad_up_low, preferred_element_type=jnp.float32)
    grad_normed_two = lax.psum_scatter(
        (
            jnp.dot(grad_gate_low, gate_again.T, preferred_element_type=jnp.float32)
            + jnp.dot(grad_up_low, up_again.T, preferred_element_type=jnp.float32)
        ).astype(jnp.bfloat16),
        "ctx",
        scatter_dimension=0,
        tiled=True,
    ).astype(jnp.float32)
    ffn_stack = jnp.stack([grad_gate, grad_up, grad_down.T], axis=0)
    ffn_summed = lax.psum_scatter(
        ffn_stack.astype(jnp.bfloat16), "grp", scatter_dimension=1, tiled=True
    ).astype(jnp.float32)
    grad_gain_two, grad_second = norm_backward(grad_normed_two, after_attn, inverse_two, gain_two_f)
    grad_resid = grad_out + grad_second
    back_query, back_key, back_value, back_output, back_gain_one, back_gain_two = attention_weights(
        w_query, w_key, w_value, w_output, attn_gain, ffn_gain
    )
    grad_branch_attn = (branch_scale * grad_resid).astype(jnp.bfloat16)
    grad_w_output = jnp.dot(attn_low.T, grad_branch_attn, preferred_element_type=jnp.float32)
    grad_attn = jnp.dot(grad_branch_attn, back_output.T, preferred_element_type=jnp.float32).astype(
        jnp.bfloat16
    )
    grad_heads = grad_attn.reshape(row_count, HEADS, HDIM)
    row_delta = jnp.sum(grad_heads.astype(jnp.float32) * attended, axis=2).T

    def back_step(grad_q, block_index):
        key_block, value_block, visible_mask = key_slice(
            keys_heads, values_heads, key_facts, query_facts, block_index * key_step, key_step
        )

        def back_busy(current):
            prob_low, grad_scores = score_grads(
                query_heads, grad_heads, log_total, row_delta, key_block, value_block, visible_mask
            )
            updated = current + jnp.einsum(
                "hqk,khd->qhd", grad_scores, key_block, preferred_element_type=jnp.float32
            )
            grad_keys = jnp.einsum(
                "hqk,qhd->khd", grad_scores, query_heads, preferred_element_type=jnp.float32
            ) * HDIM ** (-0.5)
            grad_values = jnp.einsum(
                "hqk,qhd->khd", prob_low, grad_heads, preferred_element_type=jnp.float32
            )
            return (
                updated,
                (
                    grad_keys.reshape(key_step, model_width),
                    grad_values.reshape(key_step, model_width),
                ),
            )

        def quiet(current):
            empty = jnp.zeros((key_step, model_width), jnp.float32)
            return (current, (empty, empty))

        return lax.cond(jnp.any(visible_mask), back_busy, quiet, grad_q)

    grad_q_heads, key_terms = lax.scan(
        back_step,
        jnp.zeros((row_count, HEADS, HDIM), jnp.float32),
        jnp.arange(key_blocks, dtype=jnp.int32),
    )
    key_sum, value_sum = (
        lax.psum_scatter(
            key_terms[0].reshape(group_rows, model_width).astype(jnp.bfloat16),
            "ctx",
            scatter_dimension=0,
            tiled=True,
        ).astype(jnp.float32),
        lax.psum_scatter(
            key_terms[1].reshape(group_rows, model_width).astype(jnp.bfloat16),
            "ctx",
            scatter_dimension=0,
            tiled=True,
        ).astype(jnp.float32),
    )
    grad_query_rot = grad_q_heads.reshape(row_count, model_width) * HDIM ** (-0.5)
    grad_query = rotate(grad_query_rot, cosine, sine_vals, -1.0).astype(jnp.bfloat16)
    grad_key = rotate(key_sum, cosine, sine_vals, -1.0).astype(jnp.bfloat16)
    grad_value = value_sum.astype(jnp.bfloat16)
    grad_w_query = jnp.dot(normed_one.T, grad_query, preferred_element_type=jnp.float32)
    grad_w_key = jnp.dot(normed_one.T, grad_key, preferred_element_type=jnp.float32)
    grad_w_value = jnp.dot(normed_one.T, grad_value, preferred_element_type=jnp.float32)
    grad_normed_one = (
        jnp.dot(grad_query, back_query.T, preferred_element_type=jnp.float32)
        + jnp.dot(grad_key, back_key.T, preferred_element_type=jnp.float32)
        + jnp.dot(grad_value, back_value.T, preferred_element_type=jnp.float32)
    )
    grad_gain_one, grad_first = norm_backward(grad_normed_one, residual, inverse_one, gain_one_f)
    grad_input = grad_resid + grad_first
    gain_pair = jnp.stack([grad_gain_one, grad_gain_two], axis=1)
    summed = (
        lax.psum_scatter(grad_w_query, ("grp", "ctx"), scatter_dimension=0, tiled=True),
        lax.psum_scatter(grad_w_key, ("grp", "ctx"), scatter_dimension=0, tiled=True),
        lax.psum_scatter(grad_w_value, ("grp", "ctx"), scatter_dimension=0, tiled=True),
        lax.psum_scatter(grad_w_output, ("grp", "ctx"), scatter_dimension=0, tiled=True),
        lax.psum_scatter(gain_pair, ("grp", "ctx"), scatter_dimension=0, tiled=True),
    )
    maxima = lax.pmax(head_max, ("grp", "ctx"))
    limit_value = clip_threshold[0].astype(jnp.float32)
    clip_factor = jnp.sqrt(limit_value / jnp.maximum(maxima, limit_value))
    column_factor = jnp.repeat(clip_factor, HDIM)
    clipped_query = w_query.astype(jnp.float32) * column_factor[None, :]
    clipped_key = w_key.astype(jnp.float32) * column_factor[None, :]
    return (
        output,
        grad_input,
        summed[0],
        summed[1],
        summed[2],
        summed[3],
        ffn_summed[0],
        ffn_summed[1],
        ffn_summed[2].T,
        summed[4][:, 0],
        summed[4][:, 1],
        maxima,
        clip_factor,
        clipped_query,
        clipped_key,
    )


def mul(left, right, dims=NN):
    return lax.dot_general(left, right, dims, preferred_element_type=F32)


def room():
    return pltpu.CompilerParams(vmem_limit_bytes=VMEM_ROOM)


def cost(flops, sent):
    return pl.CostEstimate(flops=int(flops), bytes_accessed=int(sent), transcendentals=0)


def straighten(w_ref, w_sc, thin):
    for i in range(4):
        for k in range(8):
            w_sc[(i * 8 + k) * thin : (i * 8 + k + 1) * thin, :] = w_ref[k, i, :thin, :]


def swing(values, cosine, sine_vals):
    lane = lax.broadcasted_iota(jnp.int32, values.shape, 1)
    other = jnp.where(
        lane % HDIM < HDIM // 2,
        pltpu.roll(values, 2 * HDIM - HDIM // 2, 1),
        pltpu.roll(values, HDIM // 2, 1),
    )
    return values * cosine + other * sine_vals


def fetch_rows(pieces, x_sc):
    step = pl.program_id(0)
    half = QB // 2
    for k in range(8):
        chunk, slot = k // 4, k % 4

        @pl.when(step == k)
        def _():
            if len(pieces) == 5 and slot < 3:
                x_sc[...] = pieces[slot][chunk * QB : (chunk + 1) * QB, :]
            elif len(pieces) == 5:
                x_sc[...] = pieces[3 + chunk][...]
            elif slot < 3:
                x_sc[...] = pieces[chunk * 5 + slot][...]
            else:
                x_sc[:half] = pieces[chunk * 5 + 3][...]
                x_sc[half:] = pieces[chunk * 5 + 4][...]


def whole(shape):
    return pl.BlockSpec(shape, lambda i: (0,) * len(shape), pipeline_mode=pl.Buffered(1))


def project_kernel(*refs):
    w_ref, cos_ref, sin_ref, q_ref, kv_ref, x_sc, w_sc = refs[5:]
    thin = w_sc.shape[0] // 32
    fetch_rows(refs[:5], x_sc)

    @pl.when(pl.program_id(0) == 0)
    def _():
        straighten(w_ref, w_sc, thin)

    y = mul(x_sc[...], w_sc[...])
    cosine, sine_vals = cos_ref[...], sin_ref[...]
    for k in range(NH):
        piece = swing(y[:, k * 128 : (k + 1) * 128], cosine, sine_vals)
        for j in range(2):
            head = 2 * k + j
            if head < NH:
                q_ref[head] = (piece[:, j * HDIM : (j + 1) * HDIM] * 0.125).astype(BF)
        if 2 * k + 1 > NH:
            kv_ref[:, k * 128 : (k + 1) * 128] = piece.astype(BF)
        elif 2 * k + 1 == NH:
            kv_ref[:, k * 128 + HDIM : (k + 1) * 128] = piece[:, HDIM:].astype(BF)
    kv_ref[:, :PART] = y[:, 2 * PART :].astype(BF)


def project(normed, w_all, cosine, sine_vals):
    rows = sum(v.shape[0] for v in normed)
    width = normed[0].shape[1]
    full = w_all.shape
    return pl.pallas_call(
        project_kernel,
        out_shape=[
            jax.ShapeDtypeStruct((NH, rows, HDIM), BF),
            jax.ShapeDtypeStruct((rows, 2 * PART), BF),
            jax.ShapeDtypeStruct((rows, width), BF),
        ],
        grid=(rows // QB,),
        in_specs=[whole(v.shape) for v in normed]
        + [
            whole(full),
            pl.BlockSpec((QB, 128), lambda i: (i, 0)),
            pl.BlockSpec((QB, 128), lambda i: (i, 0)),
        ],
        out_specs=[
            pl.BlockSpec((NH, QB, HDIM), lambda i: (0, i, 0)),
            pl.BlockSpec((QB, 2 * PART), lambda i: (i, 0)),
            pl.BlockSpec((QB, width), lambda i: (i % 4 * 2 + i // 4, 0)),
        ],
        scratch_shapes=[pltpu.VMEM((width, full[3]), BF)],
        compiler_params=room(),
        cost_estimate=cost(2 * rows * width * full[3], 2 * (rows * width + width * full[3] + rows * 5 * PART)),
        name="project",
    )(*normed, w_all, cosine, sine_vals)


def sort_kernel(order_ref, *refs):
    k_ref, v_ref, kt_ref, vt_ref = refs[16:]
    first = pl.program_id(0) * 8
    for j in range(8):
        from_mine = order_ref[first + j] < 32
        tile = jnp.where(from_mine, refs[j][0], refs[8 + j][0])
        rows = slice(j * BLK, (j + 1) * BLK)
        for h in range(NH):
            v_ref[h, rows, :] = tile[:, h * HDIM : (h + 1) * HDIM]
            k_ref[h, rows, :] = tile[:, PART + h * HDIM : PART + (h + 1) * HDIM]
    for h in range(NH):
        kt_ref[h] = k_ref[h].T
        vt_ref[h] = v_ref[h].T


def sort_keys(order, mine, theirs):
    count = order.shape[0]
    shape = (1, BLK, 2 * PART)
    near = lambda j: pl.BlockSpec(shape, lambda i, o: (jnp.minimum(o[i * 8 + j], 31), 0, 0))
    far = lambda j: pl.BlockSpec(shape, lambda i, o: (jnp.maximum(o[i * 8 + j] - 32, 0), 0, 0))
    return pl.pallas_call(
        sort_kernel,
        out_shape=[jax.ShapeDtypeStruct((NH, count * BLK, HDIM), BF)] * 2
        + [jax.ShapeDtypeStruct((NH, HDIM, count * BLK), BF)] * 2,
        grid_spec=pltpu.PrefetchScalarGridSpec(
            num_scalar_prefetch=1,
            grid=(count // 8,),
            in_specs=[near(j) for j in range(8)] + [far(j) for j in range(8)],
            out_specs=[pl.BlockSpec((NH, 8 * BLK, HDIM), lambda i, o: (0, i, 0))] * 2
            + [pl.BlockSpec((NH, HDIM, 8 * BLK), lambda i, o: (0, 0, i))] * 2,
        ),
        compiler_params=room(),
        cost_estimate=cost(0, 64 * count * BLK * PART),
        name="sort_keys",
    )(order, *([mine.reshape(32, BLK, 2 * PART)] * 8), *([theirs.reshape(32, BLK, 2 * PART)] * 8))


def lane_tile(vals):
    shape = (1, len(vals) * BLK)
    lane = lax.broadcasted_iota(jnp.int32, shape, 1)
    out = jnp.full(shape, vals[-1], jnp.int32)
    for j in range(len(vals) - 2, -1, -1):
        out = jnp.where(lane < (j + 1) * BLK, vals[j], out)
    return out, lane & (BLK - 1)


def block_facts(tiles_ref, len_ref, block, step, size):
    half_tiles = PLEN // BLK
    count = size // BLK
    t = [tiles_ref[block * count + j] for j in range(count)]
    tile, within = lane_tile(t)
    qpos = tile * BLK + within
    tmax = functools.reduce(jnp.maximum, t)
    tmin = functools.reduce(jnp.minimum, t)
    per = step // BLK
    is_cont = t[0] >= half_tiles
    n_all = jnp.where(is_cont, PLEN // step, tmax // per + 1)
    n_free = jnp.where(is_cont, PLEN // step, tmin // per)
    conts = [jnp.maximum(v - half_tiles, 0) // 4 for v in t]
    lens = lane_tile([len_ref[v] for v in conts])[0]
    qin = qpos - PLEN - lane_tile(conts)[0] * CLEN
    starts = [pl.multiple_of(PLEN + v * CLEN, CLEN) for v in conts]
    kin = lax.broadcasted_iota(jnp.int32, (CLEN, size), 0)
    seen = lambda: (kin <= qin) & (kin < lens)
    return qpos, is_cont, n_all, n_free, starts, seen


def forward_kernel(
    tiles_ref, len_ref, q_ref, k_ref, vt_sc, o_ref, lse_ref, mx_ref, ot_sc, shift
):
    block = pl.program_id(0) + shift
    qpos, is_cont, n_all, n_free, starts, seen = block_facts(
        tiles_ref, len_ref, block, KB_FWD, QB
    )

    def heads(group, carry):
        hs = [group * HEAD_STEP + j for j in range(HEAD_STEP)]
        qs = [q_ref[h] for h in hs]

        def update(scores, states, weigh):
            out = []
            for n, (s, (m, l, acc)) in enumerate(zip(scores, states)):
                mn = jnp.maximum(m, jnp.max(s, axis=0, keepdims=True))
                p = jnp.exp(s - mn)
                al = jnp.exp(m - mn)
                out.append(
                    (
                        mn,
                        l * al + jnp.sum(p, axis=0, keepdims=True),
                        acc * al + weigh(n, p.astype(BF)),
                    )
                )
            return tuple(out)

        def step(kb, states, masked):
            base = pl.multiple_of(kb * KB_FWD, KB_FWD)
            rows = pl.ds(base, KB_FWD)
            scores = [mul(k_ref[h, rows, :], q, NT) for h, q in zip(hs, qs)]
            if masked:
                kpos = base + lax.broadcasted_iota(jnp.int32, (KB_FWD, QB), 0)
                vis = kpos <= qpos
                scores = [jnp.where(vis, s, masked_value) for s in scores]
            return update(scores, states, lambda n, p: mul(vt_sc[hs[n], :, rows], p))

        states = tuple(
            (
                jnp.full((1, QB), masked_value, F32),
                jnp.zeros((1, QB), F32),
                jnp.zeros((HDIM, QB), F32),
            )
            for _ in hs
        )
        states = lax.fori_loop(0, n_free, functools.partial(step, masked=False), states)
        states = lax.fori_loop(n_free, n_all, functools.partial(step, masked=True), states)

        def own(states):
            vis = seen()
            cols = lambda x, j: x[:, j * BLK : (j + 1) * BLK]
            scores = []
            for h, q in zip(hs, qs):
                s = [
                    mul(k_ref[h, pl.ds(starts[j], CLEN), :], q[j * BLK : (j + 1) * BLK], NT)
                    for j in range(4)
                ]
                scores.append(jnp.where(vis, jnp.concatenate(s, axis=1), masked_value))
            return update(
                scores,
                states,
                lambda n, p: jnp.concatenate(
                    [
                        mul(vt_sc[hs[n], :, pl.ds(starts[j], CLEN)], cols(p, j))
                        for j in range(4)
                    ],
                    axis=1,
                ),
            )

        states = lax.cond(is_cont, own, lambda s: s, states)
        for h, (m, l, acc) in zip(hs, states):
            ot_sc[h] = acc / l
            lse_ref[0, pl.ds(h, 1), :] = m + jnp.log(l)
            mx_ref[0, pl.ds(h, 1), :] = m
        return carry

    lax.fori_loop(0, NH // HEAD_STEP, heads, 0)
    for h in range(NH):
        o_ref[:, h * HDIM : (h + 1) * HDIM] = ot_sc[h].T.astype(BF)


def attention_forward(tiles, lengths, queries, keys, values_t, shift, count):
    rows = count * QB
    span = keys.shape[1]
    once = lambda *shape: pl.BlockSpec(
        shape, lambda i, a, b: (0, 0, 0), pipeline_mode=pl.Buffered(1)
    )
    stat = pl.BlockSpec((1, NH, QB), lambda i, a, b: (i, 0, 0))
    return pl.pallas_call(
        functools.partial(forward_kernel, shift=shift),
        out_shape=[
            jax.ShapeDtypeStruct((rows, PART), BF),
            jax.ShapeDtypeStruct((count, NH, QB), F32),
            jax.ShapeDtypeStruct((count, NH, QB), F32),
        ],
        grid_spec=pltpu.PrefetchScalarGridSpec(
            num_scalar_prefetch=2,
            grid=(count,),
            in_specs=[
                pl.BlockSpec((NH, QB, HDIM), lambda i, a, b: (0, i + shift, 0)),
                once(NH, span, HDIM),
                once(NH, HDIM, span),
            ],
            out_specs=[pl.BlockSpec((QB, PART), lambda i, a, b: (i, 0)), stat, stat],
            scratch_shapes=[pltpu.VMEM((NH, HDIM, QB), F32)],
        ),
        compiler_params=room(),
        cost_estimate=cost(rows * PART * PLEN * 20, 16 * span * PART),
        name="attention_forward",
    )(tiles, lengths, queries, keys, values_t)


def delta_kernel(*refs):
    w_ref, o_ref, gh_ref, delta_ref, gw_ref, x_sc = refs[10:]
    step = pl.program_id(0)
    rows = pl.ds(pl.multiple_of(step * QB, QB), QB)
    fetch_rows(refs[:10], x_sc.at[rows, :])
    grad = mul(x_sc[rows, :], w_ref[...], NT).astype(BF)
    for h in range(NH):
        gh_ref[h] = grad[:, h * HDIM : (h + 1) * HDIM]
    prod = grad.astype(F32) * o_ref[rows, :].astype(F32)
    high = prod.astype(BF)
    low = (prod - high.astype(F32)).astype(BF)
    row = lax.broadcasted_iota(jnp.int32, (16, PART), 0)
    col = lax.broadcasted_iota(jnp.int32, (16, PART), 1)
    pick_head = jnp.where(col // HDIM == row, 1.0, 0.0).astype(BF)
    total = mul(pick_head, high, NT) + mul(pick_head, low, NT)
    delta_ref[0] = total[:NH]

    @pl.when(step == pl.num_programs(0) - 1)
    def _():
        for k in range(3):
            cols = slice(k * 768, (k + 1) * 768)
            gw_ref[:, cols] = mul(o_ref[...], x_sc[:, cols], TN).astype(BF)


def attention_delta(grad_branch, w_out, attended):
    rows, width = attended.shape[0], w_out.shape[1]
    count = rows // QB
    return pl.pallas_call(
        delta_kernel,
        out_shape=[
            jax.ShapeDtypeStruct((NH, rows, HDIM), BF),
            jax.ShapeDtypeStruct((count, NH, QB), F32),
            jax.ShapeDtypeStruct((PART, width), BF),
        ],
        grid=(count,),
        in_specs=[whole(v.shape) for v in grad_branch]
        + [whole((PART, width)), whole((rows, PART))],
        out_specs=[
            pl.BlockSpec((NH, QB, HDIM), lambda i: (0, i, 0)),
            pl.BlockSpec((1, NH, QB), lambda i: (i, 0, 0)),
            pl.BlockSpec((PART, width), lambda i: (0, 0)),
        ],
        scratch_shapes=[pltpu.VMEM((rows, width), BF)],
        compiler_params=room(),
        cost_estimate=cost(2 * rows * width * PART, 2 * rows * width),
        name="attention_delta",
    )(*grad_branch, w_out, attended)


def backward_kernel(
    tiles_ref, len_ref, q_ref, g_ref, lse_ref, delta_ref, k_ref, v_ref, kt_ref, dq_ref, dk_out, dv_out,
    dk_ref, dv_ref, first
):
    h = pl.program_id(0) + first
    block = pl.program_id(1)

    @pl.when(block == 0)
    def _():
        dk_ref[...] = jnp.zeros_like(dk_ref)
        dv_ref[...] = jnp.zeros_like(dv_ref)

    qpos, is_cont, n_all, n_free, starts, seen = block_facts(
        tiles_ref, len_ref, block, KB, QB_BACK
    )
    q = q_ref[0]
    g = g_ref[0]
    stat = lambda ref: jnp.concatenate(
        [ref[j, pl.ds(h, 1), :] for j in range(QB_BACK // QB)], axis=1
    )
    lse = stat(lse_ref)
    delta = stat(delta_ref)

    def step(kb, dqt, masked):
        base = pl.multiple_of(kb * KB, KB)
        rows = pl.ds(base, KB)
        s = mul(k_ref[0, rows, :], q, NT)
        dp = mul(v_ref[0, rows, :], g, NT)
        if masked:
            kpos = base + lax.broadcasted_iota(jnp.int32, (KB, QB_BACK), 0)
            s = jnp.where(kpos <= qpos, s, masked_value)
        p = jnp.exp(s - lse)
        ds = (p * (dp - delta)).astype(BF)
        dv_ref[rows, :] += mul(p.astype(BF), g)
        dk_ref[rows, :] += mul(ds, q)
        return dqt + mul(kt_ref[0, :, rows], ds)

    dqt = jnp.zeros((HDIM, QB_BACK), F32)
    dqt = lax.fori_loop(0, n_free, functools.partial(step, masked=False), dqt)
    dqt = lax.fori_loop(n_free, n_all, functools.partial(step, masked=True), dqt)
    dq_ref[0] = dqt.T * HDIM ** (-0.5)

    @pl.when(is_cont)
    def _():
        part = lambda x, j: x[j * BLK : (j + 1) * BLK]
        rows = [pl.ds(starts[j], CLEN) for j in range(QB_BACK // BLK)]
        s = jnp.concatenate([mul(k_ref[0, rows[j], :], part(q, j), NT) for j in range(QB_BACK // BLK)], axis=1)
        s = jnp.where(seen(), s, masked_value)
        p = jnp.exp(s - lse)
        dp = jnp.concatenate([mul(v_ref[0, rows[j], :], part(g, j), NT) for j in range(QB_BACK // BLK)], axis=1)
        ds = (p * (dp - delta)).astype(BF)
        pb = p.astype(BF)
        dq = []
        for j in range(QB_BACK // BLK):
            cols = slice(j * BLK, (j + 1) * BLK)
            dv_ref[rows[j], :] += mul(pb[:, cols], part(g, j))
            dk_ref[rows[j], :] += mul(ds[:, cols], part(q, j))
            dq.append(mul(kt_ref[0, :, rows[j]], ds[:, cols]))
        dq_ref[0] += jnp.concatenate(dq, axis=1).T * HDIM ** (-0.5)

    @pl.when(block == pl.num_programs(1) - 1)
    def _():
        dk_out[0] = dk_ref[...].astype(BF)
        dv_out[0] = dv_ref[...].astype(BF)


def attention_backward(tiles, lengths, queries, grads, log_total, row_delta, keys, values, keys_t, group):
    rows = queries.shape[1]
    count = rows // QB_BACK
    span = keys.shape[1]
    first = group * GROUP
    row = pl.BlockSpec((1, QB_BACK, HDIM), lambda h, i, a, b: (h + first, i, 0))
    stat = pl.BlockSpec((QB_BACK // QB, NH, QB), lambda h, i, a, b: (i, 0, 0))
    full = pl.BlockSpec((1, span, HDIM), lambda h, i, a, b: (h + first, 0, 0))
    out = pl.BlockSpec((1, span, HDIM), lambda h, i, a, b: (h, 0, 0))
    return pl.pallas_call(
        functools.partial(backward_kernel, first=first),
        out_shape=[
            jax.ShapeDtypeStruct((GROUP, rows, HDIM), F32),
            jax.ShapeDtypeStruct((GROUP, span, HDIM), BF),
            jax.ShapeDtypeStruct((GROUP, span, HDIM), BF),
        ],
        grid_spec=pltpu.PrefetchScalarGridSpec(
            num_scalar_prefetch=2,
            grid=(GROUP, count),
            in_specs=[
                row,
                row,
                stat,
                stat,
                full,
                full,
                pl.BlockSpec((1, HDIM, span), lambda h, i, a, b: (h + first, 0, 0)),
            ],
            out_specs=[pl.BlockSpec((1, QB_BACK, HDIM), lambda h, i, a, b: (h, i, 0)), out, out],
            scratch_shapes=[pltpu.VMEM((span, HDIM), F32)] * 2,
        ),
        compiler_params=room(),
        cost_estimate=cost(rows * GPART * PLEN * 40, 32 * span * GPART),
        name="attention_backward",
    )(tiles, lengths, queries, grads, log_total, row_delta, keys, values, keys_t)


def restore_kernel(tiles_ref, *refs):
    mine_ref, theirs_ref = refs[16:]

    def write(out_ref):
        for j in range(8):
            rows = slice(j * BLK, (j + 1) * BLK)
            for h in range(GROUP):
                cols = slice(h * HDIM, (h + 1) * HDIM)
                out_ref[rows, cols] = refs[8 + j][h]
                out_ref[rows, GPART + h * HDIM : GPART + (h + 1) * HDIM] = refs[j][h]

    @pl.when(pl.program_id(0) < 4)
    def _():
        write(theirs_ref)

    @pl.when(pl.program_id(0) >= 4)
    def _():
        write(mine_ref)


def restore_keys(tiles, grad_k, grad_v):
    spec = lambda j: pl.BlockSpec((GROUP, BLK, HDIM), lambda i, o: (0, o[i * 8 + j], 0))
    shape = (8 * BLK, 2 * GPART)
    return pl.pallas_call(
        restore_kernel,
        out_shape=[jax.ShapeDtypeStruct((32 * BLK, 2 * GPART), BF)] * 2,
        grid_spec=pltpu.PrefetchScalarGridSpec(
            num_scalar_prefetch=1,
            grid=(8,),
            in_specs=[spec(j) for j in range(8)] * 2,
            out_specs=[
                pl.BlockSpec(shape, lambda i, o: (jnp.maximum(i - 4, 0), 0)),
                pl.BlockSpec(shape, lambda i, o: (jnp.minimum(i, 3), 0)),
            ],
        ),
        compiler_params=room(),
        cost_estimate=cost(0, 64 * 64 * BLK * GPART),
        name="restore_keys",
    )(tiles, *([grad_k] * 8), *([grad_v] * 8))


def unturn_kernel(dq_ref, mine_ref, theirs_ref, cos_ref, sin_ref, g_ref, y_sc):
    kv = mine_ref[...].astype(F32) + theirs_ref[...].astype(F32)
    for h in range(GROUP):
        y_sc[:, h * HDIM : (h + 1) * HDIM] = dq_ref[h]
    y_sc[:, GPART:] = kv[:, GPART:]
    cosine, sine_vals = cos_ref[...], -sin_ref[...]
    for k in range(GROUP):
        cols = slice(k * 128, (k + 1) * 128)
        g_ref[:, cols] = swing(y_sc[:, cols], cosine, sine_vals).astype(BF)
    g_ref[:, 2 * GPART :] = kv[:, :GPART].astype(BF)


def unturn(grad_q, mine, theirs, cosine, sine_vals):
    rows = mine.shape[0]
    size = QB
    row = lambda n: pl.BlockSpec((size, n), lambda i: (i, 0))
    return pl.pallas_call(
        unturn_kernel,
        out_shape=jax.ShapeDtypeStruct((rows, 3 * GPART), BF),
        grid=(rows // size,),
        in_specs=[
            pl.BlockSpec((GROUP, size, HDIM), lambda i: (0, i, 0)),
            row(2 * GPART),
            row(2 * GPART),
            row(128),
            row(128),
        ],
        out_specs=pl.BlockSpec((size, 3 * GPART), lambda i: (i % 4 * 2 + i // 4, 0)),
        scratch_shapes=[pltpu.VMEM((size, 2 * GPART), F32)],
        compiler_params=room(),
        cost_estimate=cost(0, 20 * rows * GPART),
        name="unturn",
    )(grad_q, mine, theirs, cosine, sine_vals)


def unproject_kernel(a_ref, b_ref, c_ref, w_ref, x_ref, w_sc, y_sc):
    thin = w_sc.shape[0] // 32

    @pl.when(pl.program_id(0) == 0)
    def _():
        straighten(w_ref, w_sc, thin)

    for g, ref in enumerate((a_ref, b_ref, c_ref)):
        for k in range(3):
            y_sc[:, k * PART + g * GPART : k * PART + (g + 1) * GPART] = ref[
                :, k * GPART : (k + 1) * GPART
            ]
    x_ref[...] = mul(y_sc[...], w_sc[...], NT).astype(BF)


def unproject(parts, w_all, chunk):
    rows = parts[0].shape[0] // 2
    full = w_all.shape
    width = full[0] * full[1] * (full[2] - 8)
    return pl.pallas_call(
        unproject_kernel,
        out_shape=jax.ShapeDtypeStruct((rows, width), BF),
        grid=(rows // QB,),
        in_specs=[pl.BlockSpec((QB, 3 * GPART), lambda i: (i * 2 + chunk, 0))] * 3
        + [pl.BlockSpec(full, lambda i: (0, 0, 0, 0), pipeline_mode=pl.Buffered(1))],
        out_specs=pl.BlockSpec((QB, width), lambda i: (i, 0)),
        scratch_shapes=[
            pltpu.VMEM((width, full[3]), BF),
            pltpu.VMEM((QB, 3 * PART), BF),
        ],
        compiler_params=room(),
        cost_estimate=cost(2 * rows * width * 3 * PART, 4 * rows * width),
        name="unproject",
    )(*parts, w_all)


def finish_kernel(a_ref, bc_ref, wq_ref, wk_ref, wv_ref, gain_ref, q_ref, k_ref, v_ref, sum_ref):
    thin = gain_ref.shape[0]
    gain = gain_ref[...]
    total = jnp.zeros((thin, 1), F32)
    for p in range(4):
        for g, (ref, first) in enumerate(((a_ref, 0), (bc_ref, 0), (bc_ref, PART))):
            cols = slice(p * PART + g * GPART, p * PART + (g + 1) * GPART)
            for n, (w, out) in enumerate(((wq_ref, q_ref), (wk_ref, k_ref), (wv_ref, v_ref))):
                part = slice(first + n * GPART, first + (n + 1) * GPART)
                grad = ref[p, :thin, part].astype(F32)
                out[:, cols] = grad * gain
                total += jnp.sum(grad * w[:, cols].astype(F32), axis=1, keepdims=True)
    sum_ref[...] = jnp.broadcast_to(total, sum_ref.shape)


def finish(parts, weights, gain):
    thin, width = weights[0].shape
    return pl.pallas_call(
        finish_kernel,
        out_shape=[jax.ShapeDtypeStruct((thin, width), F32)] * 3
        + [jax.ShapeDtypeStruct((thin, 128), F32)],
        compiler_params=room(),
        name="finish",
    )(*parts, *weights, gain)


def split_tiles(rows):
    blocks = rows.reshape(4, 2, rows.shape[0] // 8, rows.shape[1])
    return blocks[:, 0], blocks[:, 1]


def join_tiles(chunks):
    blocks = jnp.stack(chunks, axis=1)
    return blocks.reshape(-1, blocks.shape[-1])


def over(name, blocks):
    return lax.all_to_all(blocks, name, 0, 0, tiled=True)


def quarters(rows):
    return rows.reshape(4, rows.shape[0] // 4, rows.shape[1])


def after(value, *earlier):
    return lax.optimization_barrier((value, earlier))[0]


def flip(values, mask):
    return lax.ppermute(values, "p", [(k, k ^ mask) for k in range(4)])


def gather_near(own):
    return [own, flip(own, 1), flip(own, 2)]


def gather_far(near):
    half = near[0].shape[0] // 2
    return near + [flip(near[2][:half], 1), flip(near[1][half:], 2)]


def slots(terms):
    size = terms.shape[0] // 4
    return [terms[k * size : (k + 1) * size] for k in range(4)]


def scatter_far(terms):
    far = slots(terms)[3]
    half = far.shape[0] // 2
    return flip(far[:half], 1), flip(far[half:], 2)


def scatter_near(terms, far):
    _, first, second, _ = slots(terms)
    half = first.shape[0] // 2
    add = lambda x, y: (x.astype(F32) + y.astype(F32)).astype(BF)
    first = flip(jnp.concatenate([first[:half], add(first[half:], far[1])], axis=0), 1)
    second = flip(jnp.concatenate([add(second[:half], far[0]), second[half:]], axis=0), 2)
    return first, second


def scatter_sum(terms, near):
    return slots(terms)[0].astype(F32) + near[0].astype(F32) + near[1].astype(F32)


def scatter_far_both(terms):
    return flip(slots(terms[0])[3], 1), flip(slots(terms[1])[3], 2)


def scatter_near_both(terms, far):
    early, late = slots(terms[0]), slots(terms[1])
    add = lambda x, y: (x.astype(F32) + y.astype(F32)).astype(BF)
    first = flip(jnp.concatenate([early[1], add(late[1], far[1])], axis=0), 1)
    second = flip(jnp.concatenate([add(early[2], far[0]), late[2]], axis=0), 2)
    return first, second


def meet(*values):
    return lax.optimization_barrier(values)


def swap_blocks(name, pieces):
    return [pieces[0]] + [
        lax.ppermute(pieces[r], name, [(k, k ^ r) for k in range(4)]) for r in (1, 2, 3)
    ]


def pick(pieces, first):
    stacked = jnp.stack(pieces)
    return [
        lax.dynamic_index_in_dim(stacked, jnp.bitwise_xor(first, r), 0, keepdims=False)
        for r in range(4)
    ]


def hidden_cuts(hidden):
    steps = hidden // 8
    sizes = [8 * (steps // 4 + (k < steps % 4)) for k in range(4)]
    starts = [sum(sizes[:k]) for k in range(4)]
    return starts, sizes, max(sizes)


def inner(
    tokens_in,
    cotangent,
    w_query,
    w_key,
    w_value,
    w_output,
    w_gate,
    w_up,
    w_down,
    attn_gain,
    ffn_gain,
    cont_len,
    deal_order,
    clip_threshold,
):
    plane, depth, core = (lax.axis_index(name) for name in ("p", "z", "c"))
    line = ("z", "c")
    width = tokens_in.shape[1]
    thin = w_query.shape[0]
    hidden = w_down.shape[0]
    starts, sizes, share = hidden_cuts(hidden)
    gain_f = attn_gain.astype(F32)
    parts_of = lambda v: [v[k] for k in range(4)]
    cross = lambda v: swap_blocks("p", pick(v, plane))
    cross_whole = lambda v: jnp.stack(pick(cross(parts_of(v)), plane))
    hop_on = lambda v: swap_blocks("z", pick(v, jnp.bitwise_xor(plane, depth)))
    hop_back = lambda v: swap_blocks("z", parts_of(quarters(v)))
    hop_out = lambda v: pick(
        swap_blocks("p", pick(v, jnp.bitwise_xor(plane, depth))), plane
    )
    first_hop = cross(parts_of(quarters(tokens_in)))
    turn_over = [(g * 4 + k, k * 4 + g) for g in range(4) for k in range(4)]
    deal = lax.ppermute(deal_order[0], ("p", "z"), turn_over)
    lengths = lax.ppermute(cont_len[0], ("p", "z"), turn_over)

    scaled = [(w.astype(F32) * gain_f[:, None]).astype(BF) for w in (w_query, w_key, w_value)]
    blocks = jnp.stack(scaled).reshape(3, thin, 4, PART).transpose(2, 1, 0, 3)
    blocks = blocks.reshape(4, thin, 3 * PART)
    extra = jnp.zeros((4, 8, 3 * PART), BF).at[:, 0, :thin].set(ffn_gain[None, :])
    send = jnp.concatenate([blocks, extra], axis=1)
    first_hop, send = meet(first_hop, send)
    early = after((w_gate, w_up, w_down), first_hop)
    stacked = jnp.stack([early[0].T, early[1].T, early[2]])
    stacked = jnp.stack(
        [
            jnp.pad(stacked[:, a : a + n], ((0, 0), (0, share - n), (0, 0)))
            for a, n in zip(starts, sizes)
        ]
    )
    send, moved = meet(cross_whole(send), hop_on(first_hop))
    stacked = cross_whole(stacked)
    w_qkv = lax.all_gather(send, line, axis=0)
    gain_two = w_qkv[:, :, thin, :thin].transpose(1, 0, 2).reshape(width).astype(F32)
    w_out = lax.all_gather(w_output, line, axis=0, tiled=True)
    piece = jnp.arange(2)[:, None, None]
    slot = jnp.arange(4)[None, :, None]
    source = jnp.bitwise_xor(depth, jnp.arange(4))[None, None, :]
    quarter = jnp.bitwise_xor(plane, slot)
    held = lambda which: deal[((source * 2 + which) * 8 + quarter * 2 + piece).reshape(-1)]
    tiles, tiles_far = held(core), held(1 - core)
    both = jnp.concatenate([tiles, tiles_far])
    numbers = jnp.arange(64, dtype=jnp.int32)
    order = jnp.sum(
        jnp.where(both[None, :] == numbers[:, None], numbers[None, :], 0), axis=1
    ).astype(jnp.int32)
    logical = (tiles[:, None] * BLK + jnp.arange(BLK, dtype=jnp.int32)[None, :]).reshape(-1)
    position = jnp.where(logical < PLEN, logical, PLEN + (logical - PLEN) % CLEN)
    cosine, sine_vals = (v[:, 0, :] for v in rope_angles(position))
    cosine = jnp.concatenate([cosine] * 4, axis=1)
    sine_vals = jnp.concatenate([-sine_vals, sine_vals] * 2, axis=1)

    joined = lambda pieces: jnp.concatenate(pieces, axis=0)
    by_chunk = lambda v: [h.reshape(-1, width) for h in split_tiles(joined(v))]
    residual = [v.astype(F32) for v in by_chunk(moved)]
    inverse_of = lambda v: lax.rsqrt(jnp.mean(v * v, axis=-1, keepdims=True) + norm_eps)
    inverse_one = [inverse_of(v) for v in residual]
    pieces = gather_near(joined([(v * r).astype(BF) for v, r in zip(residual, inverse_one)]))
    pieces = gather_far(pieces)

    def in_chunks(pieces):
        size = pieces[0].shape[0] // 2
        return [
            joined([v[k * size : (k + 1) * size] for v in pieces[:3]] + [pieces[3 + k]])
            for k in range(2)
        ]

    pieces, w_qkv, grad_out = meet(pieces, w_qkv, cotangent)
    (queries, mine, normed), grad_out = meet(
        project(pieces, w_qkv, cosine, sine_vals),
        cross(parts_of(quarters(grad_out))),
    )
    theirs = lax.ppermute(mine, "c", [(0, 1), (1, 0)])
    sorted_kv, grad_out, stacked = meet(
        sort_keys(order, mine, theirs), hop_on(grad_out), stacked
    )
    keys, values, keys_t, values_t = sorted_kv
    stacked = stacked.transpose(1, 2, 0, 3).reshape(3, share, width)
    w_ffn = [lax.all_gather(stacked[k], line, axis=0, tiled=True) for k in range(3)]
    attend = lambda q, k, n: attention_forward(tiles, lengths, q, keys, values_t, k, n)
    grad_out = by_chunk(grad_out)
    grad_rows = joined([(branch_scale * v.astype(F32)).astype(BF) for v in grad_out])
    queries, grad_rows = meet(queries, grad_rows)
    (low_a, total_a, peak_a), grad_rows = meet(attend(queries, 0, 4), gather_near(grad_rows))
    branch_a = mul(low_a, w_out).astype(BF)
    branch_a, grad_rows, queries_b = meet(branch_a, grad_rows, queries)
    part_b, far_a = meet(attend(queries_b, 4, 2), scatter_far(branch_a))
    rest_b, near_a, grad_rows = meet(
        attend(queries_b, 6, 2), scatter_near(branch_a, far_a), gather_far(grad_rows)
    )
    low_b, total_b, peak_b = (joined([v, w]) for v, w in zip(part_b, rest_b))
    branch_b = mul(low_b, w_out).astype(BF)
    attended = joined([low_a, low_b])
    log_total = joined([total_a, total_b])
    peaks = joined([peak_a, peak_b])
    grad_rows = in_chunks(grad_rows)

    def second_norm(k, branch):
        after_attn = residual[k] + branch_scale * branch
        inverse_two = inverse_of(after_attn)
        return after_attn, inverse_two, (after_attn * inverse_two * gain_two).astype(BF)

    def hidden_layer(grad_mixed, normed_two):
        gate_pre = mul(normed_two, w_ffn[0], NT)
        up_pre = mul(normed_two, w_ffn[1], NT)
        mixed = (jax.nn.silu(gate_pre) * up_pre).astype(BF)
        return (mixed,) + gate_grads(grad_mixed, gate_pre, up_pre)

    def hidden_back(hidden):
        return (mul(hidden[1], w_ffn[0]) + mul(hidden[2], w_ffn[1])).astype(BF)

    def second_back(k, total, state):
        grad_gain, grad_second = norm_backward(total, state[0], state[1], gain_two)
        grad_resid = grad_out[k].astype(F32) + grad_second
        return grad_gain, grad_resid, (branch_scale * grad_resid).astype(BF)

    state_a = second_norm(0, scatter_sum(branch_a, near_a))
    own, rows_a, rows_b = meet(state_a[2], grad_rows[0], grad_rows[1])
    gather, mixed_a, rows_b, branch_b = meet(
        gather_near(own), mul(rows_a, w_ffn[2], NT), rows_b, branch_b
    )
    gather, far, mixed_b = meet(
        gather_far(gather), scatter_far(branch_b), mul(rows_b, w_ffn[2], NT)
    )
    normed_a = joined(gather)
    hidden_a, near = meet(hidden_layer(mixed_a, normed_a), scatter_near(branch_b, far))
    state_b = second_norm(1, scatter_sum(branch_b, near))
    hidden_a, own = meet(hidden_a, state_b[2])
    rest_a, gather = meet(hidden_back(hidden_a), gather_near(own))
    first = mul(hidden_a[1], normed_a, TN)
    gather, far, gate_a = meet(gather_far(gather), scatter_far(rest_a), first)
    normed_b = joined(gather)
    hidden_b, near = meet(hidden_layer(mixed_b, normed_b), scatter_near(rest_a, far))
    back_a = second_back(0, scatter_sum(rest_a, near), state_a)
    hidden_b, own = meet(hidden_b, back_a[2])
    rest_b, gather_a = meet(hidden_back(hidden_b), gather_near(own))
    grad_gate = (gate_a + mul(hidden_b[1], normed_b, TN)).astype(BF)
    up_a = mul(hidden_a[2], normed_a, TN)
    gather_a, far, grad_gate, up_a = meet(
        gather_far(gather_a), scatter_far(rest_b), grad_gate, up_a
    )
    grad_up = (up_a + mul(hidden_b[2], normed_b, TN)).astype(BF)
    down_a = mul(hidden_a[0], rows_a, TN)
    near, grad_up, down_a = meet(scatter_near(rest_b, far), grad_up, down_a)
    back_b = second_back(1, scatter_sum(rest_b, near), state_b)
    own, mixed_b_rows, down_a = meet(back_b[2], hidden_b[0], down_a)
    grad_down = (down_a + mul(mixed_b_rows, rows_b, TN)).astype(BF)
    gather_b, grad_down, ffn_b = meet(
        gather_near(own), grad_down, mul(mixed_b_rows, w_ffn[2]).astype(BF)
    )
    gather_b, ffn_a = meet(gather_far(gather_b), mul(hidden_a[0], w_ffn[2]).astype(BF))
    branch_ffn = [ffn_a, ffn_b]
    sum_rows = lambda v: lax.psum_scatter(v, line, scatter_dimension=0, tiled=True)
    grad_pieces = gather_a + gather_b
    grad_gain_two = back_a[0] + back_b[0]
    grad_resid = [back_a[1], back_b[1]]

    grad_pieces, branch_ffn = meet(grad_pieces, branch_ffn)
    (grad_heads, row_delta, grad_w_part), far, grad_gate = meet(
        attention_delta(grad_pieces, w_out, attended),
        scatter_far_both(branch_ffn),
        sum_rows(grad_gate),
    )
    far_order = jnp.concatenate([tiles_far, tiles])
    gain_rows = grad_gain_two.astype(BF).reshape(4, 8, 1, thin).transpose(1, 0, 2, 3)
    peak = jnp.max(peaks, axis=(0, 2))
    peak_high = lax.reduce_precision(peak, 8, 7)
    peak_rows = jnp.stack([peak_high.astype(BF), (peak - peak_high).astype(BF)])
    mine_slot = (jnp.arange(8) == depth * 2 + core)[None, :, None]
    peak_rows = jnp.where(mine_slot, peak_rows[:, None, :], 0).reshape(2, 8 * NH)
    widen = lambda v: jnp.pad(v, ((0, 0), (0, 0), (0, 0), (0, 3 * GPART - v.shape[3])))
    gain_rows = jnp.concatenate(
        [
            widen(gain_rows),
            widen(jnp.broadcast_to(peak_rows, (8, 4, 2, 8 * NH))),
            jnp.zeros((8, 4, 5, 3 * GPART), BF),
        ],
        axis=2,
    )

    def back_group(g, grads):
        return attention_backward(
            tiles, lengths, queries, grads, log_total, row_delta, keys, values, keys_t, g
        )

    def restore(part):
        return (part[0],) + tuple(restore_keys(far_order, part[1], part[2]))

    def weight_part(grad_qkv):
        proj = mul(normed, grad_qkv, TN).astype(BF).reshape(4, 8, thin, 3 * GPART)
        proj = jnp.concatenate([proj.transpose(1, 0, 2, 3), gain_rows], axis=2)
        return proj.reshape(8 * 4 * (thin + 8), 3 * GPART)

    def sum_line(proj):
        proj = lax.psum_scatter(proj, line, scatter_dimension=0, tiled=True)
        return proj.reshape(4, thin + 8, 3 * GPART)

    trade = lambda v: lax.ppermute(v, "c", [(0, 1), (1, 0)])
    grad_heads, grad_w_part = meet(grad_heads, grad_w_part)
    grad_down = sum_rows(grad_down)
    part_a, grad_heads, near, grad_up = meet(
        back_group(0, grad_heads),
        grad_heads,
        scatter_near_both(branch_ffn, far),
        sum_rows(grad_up),
    )
    grad_w_output = sum_rows(grad_w_part)
    part_a = restore(part_a)
    states = (state_a, state_b)
    output = []
    for k, (state, v) in enumerate(zip(states, branch_ffn)):
        size = state[0].shape[0]
        total = scatter_sum(v, [w[k * size : (k + 1) * size] for w in near])
        output.append(quarters((state[0] + branch_scale * total).astype(BF)))
    output = join_tiles(output)
    output, grad_heads, part_a = meet(output, grad_heads, part_a)
    part_b, grad_heads, hops, far_a, grad_down = meet(
        back_group(1, grad_heads),
        grad_heads,
        hop_back(output),
        trade(part_a[2]),
        grad_down,
    )
    ffn_grads = jnp.stack([grad_gate, grad_up, grad_down])
    ffn_grads = ffn_grads.reshape(3, share, 4, PART).transpose(2, 0, 1, 3)
    part_b = restore(part_b)
    grads_a = unturn(part_a[0], part_a[1], far_a, cosine, sine_vals)
    weights_a = weight_part(grads_a)
    grad_heads, weights_a, hops, part_b, ffn_grads = meet(
        grad_heads, weights_a, hops, part_b, ffn_grads
    )
    part_c, output, far_b = meet(back_group(2, grad_heads), hop_out(hops), trade(part_b[2]))
    weights_a = sum_line(weights_a)
    part_c, far_b = meet(restore(part_c), far_b)
    grads_b = unturn(part_b[0], part_b[1], far_b, cosine, sine_vals)
    weights_b, far_c, ffn_grads = meet(
        weight_part(grads_b), trade(part_c[2]), cross_whole(ffn_grads)
    )
    output = joined(output)
    grads_c, weights_a = meet(
        unturn(part_c[0], part_c[1], far_c, cosine, sine_vals), weights_a
    )
    grads = (grads_a, grads_b, grads_c)
    rest_a, grads, weights_a = meet(unproject(grads, w_qkv, 0), grads, cross_whole(weights_a))
    weights_c, far_a, grads = meet(weight_part(grads[2]), scatter_far(rest_a), grads)
    weights_c = sum_line(weights_c)
    rest_b, near_a, weights_b, grad_w_output = meet(
        unproject(grads, w_qkv, 1),
        scatter_near(rest_a, far_a),
        sum_line(weights_b),
        grad_w_output,
    )
    far_b = scatter_far(rest_b)

    def first_back(k, total):
        grad_first = inverse_one[k] * total - residual[k] * inverse_one[k] ** 3 * jnp.mean(
            total * residual[k], axis=-1, keepdims=True
        )
        return (grad_resid[k] + grad_first).astype(BF)

    hop_a = hop_back(first_back(0, scatter_sum(rest_a, near_a)))
    near_b = scatter_near(rest_b, far_b)
    hop_a, near_b = meet(hop_a, near_b)
    hop_b, hop_a = meet(hop_back(first_back(1, scatter_sum(rest_b, near_b))), hop_out(hop_a))
    grad_input = join_tiles([jnp.stack(hop_a), jnp.stack(hop_out(hop_b))]).astype(F32)
    ffn_grads, late = after((ffn_grads, weights_a), rest_b)
    ffn_grads = ffn_grads.astype(F32)
    ffn_grads = jnp.concatenate([ffn_grads[k, :, :n] for k, n in enumerate(sizes)], axis=1)
    grad_ffn_gain = jnp.sum(weights_a[:, thin, :thin].astype(F32), axis=0)
    weights_bc = over("p", jnp.concatenate([weights_b, weights_c], axis=2))
    proj = finish(
        (weights_a, weights_bc), (w_query, w_key, w_value), gain_f[:, None]
    )
    grad_attn_gain = proj[3][:, 0]

    maxima = jnp.sum(late[:, thin + 1 : thin + 3, : 8 * NH].astype(F32), axis=1)
    maxima = jnp.max(maxima.reshape(4, 8, NH), axis=1).reshape(HEADS)
    limit_value = clip_threshold[0].astype(F32)
    clip_factor = jnp.sqrt(limit_value / jnp.maximum(maxima, limit_value))
    column_factor = jnp.repeat(clip_factor, HDIM)
    return (
        output,
        grad_input,
        proj[0],
        proj[1],
        proj[2],
        grad_w_output.astype(F32),
        ffn_grads[0].T,
        ffn_grads[1].T,
        ffn_grads[2],
        grad_attn_gain,
        grad_ffn_gain,
        maxima,
        clip_factor,
        w_query.astype(F32) * column_factor[None, :],
        w_key.astype(F32) * column_factor[None, :],
    )


def specs(grp, ctx):
    every = grp + ctx
    ins = [P(every, None)] * 6 + [P(grp, ctx), P(grp, ctx), P(ctx, grp), P(every), P(every)]
    ins += [P(grp, None), P(grp, None), P()]
    outs = [P(every, None)] * 6 + [P(grp, ctx), P(grp, ctx), P(ctx, grp), P(every), P(every)]
    outs += [P(), P(), P(every, None), P(every, None)]
    return tuple(ins), tuple(outs)


def solution(mesh):
    if mesh.shape["grp"] == 4 and mesh.shape["ctx"] == 8:
        mesh = Mesh(mesh.devices.reshape(4, 4, 2), ("p", "z", "c"))
        body, (in_specs, out_specs) = inner, specs(("p",), ("z", "c"))
    else:
        body, (in_specs, out_specs) = local, specs(("grp",), ("ctx",))
    return jax.shard_map(body, mesh=mesh, in_specs=in_specs, out_specs=out_specs, check_vma=False)
```
